32 devices in a mesh: fsdp: 4 (over y, x), ctx: 8 (over z, core).
Axes of the slice: x: 2, y: 2, z: 4, core: 2. Of those that a mesh axis runs over, the one named last changes fastest.
Arguments:
- tokens: bfloat16 [4096, 2048], P(('fsdp', 'ctx')), may hold values from -6 to 6
- w_qkv: bfloat16 [2048, 6144], P(('fsdp', 'ctx')), may hold values from -0.125 to 0.125
- w_out: bfloat16 [2048, 2048], P(('fsdp', 'ctx')), may hold values from -1 to 1
- w_gate_up: bfloat16 [2048, 16384], P(('fsdp', 'ctx')), may hold values from -0.125 to 0.125
- w_down: bfloat16 [8192, 2048], P(('fsdp', 'ctx')), may hold values from -0.0625 to 0.0625
- seq_lengths: int32 [4, 2], P('fsdp'), may hold values from 1 to 768, 1024 in all within a row
- block_order: int32 [4, 8], P('fsdp'), may hold values from 0 to 7, as said below
- cotangent: bfloat16 [4096, 2048], P(('fsdp', 'ctx')), may hold values from -6 to 6
Outputs:
- layer_out: bfloat16 [4096, 2048], P(('fsdp', 'ctx'))
- tokens_grad: float32 [4096, 2048], P(('fsdp', 'ctx'))
- qkv_grad: float32 [2048, 6144], P(('fsdp', 'ctx'))
- out_grad: float32 [2048, 2048], P(('fsdp', 'ctx'))
- gate_up_grad: float32 [2048, 16384], P(('fsdp', 'ctx'))
- down_grad: float32 [8192, 2048], P(('fsdp', 'ctx'))
The draws below stay inside these ranges and needn't reach their ends.
Inputs may be any that keep to these rules, and one draw needn't show every extreme that they name: `seq_lengths`: the lengths of each group sum to 1024, and none is longer than 768. `block_order`: each row names every block of its group exactly once.
All inputs are finite; a program needn't handle non-finite values.
Results may differ from the reference program's by a relative error of at most 0.018.
Values may be sent and summed in bfloat16 or wider, within the bound.
A program may use at most 704 MiB of HBM per device.

```python
import math
import jax
import jax.numpy as jnp
import numpy as np
from jax import lax

D = 2048
HEADS = 16
HEAD_DIM = 128
FF = 8192
BLOCK = 128
GROUP_TOK = 1024
GROUP_BLOCKS = 8
LONGEST = 768
SEQS = 2
TOKENS = 4096
N_FSDP = 4


def draw_block_order(key, part):
    group_keys = jax.random.split(jax.random.fold_in(key, 17), N_FSDP)
    return jax.vmap(lambda one_key: jax.random.permutation(one_key, GROUP_BLOCKS))(group_keys).astype(jnp.int32)


def level_of(stream_key, extent, cuts, least, largest):
    factor_of, own = 1.0, jax.random.fold_in(stream_key, 6)
    for dim, shards_of in cuts:
        steps = jnp.exp(jax.random.uniform(jax.random.fold_in(own, dim), (shards_of,), jnp.float32, least / len(cuts), largest / len(cuts)))
        factor_of = factor_of * jnp.repeat(steps, extent[dim] // shards_of).reshape([-1 if axis == dim else 1 for axis in range(len(extent))])
    return factor_of


def length_profile(count, total, limit, skew):
    weights = [(1 << 20) // math.isqrt(standing ** skew) + 1 for standing in range(2, count + 1)]
    surplus, holding = total - limit - (count - 1), [1] * (count - 1)
    while surplus > 0:
        free = [i for i in range(count - 1) if holding[i] < limit]
        pool, remaining = sum([weights[i] for i in free]), surplus
        for i in free:
            addition = min(limit - holding[i], max(1, remaining * weights[i] // pool), surplus)
            holding[i] = holding[i] + addition
            surplus = surplus - addition
    return np.array([limit] + holding)


def ragged_sizes(rng, amount, total, most, slope):
    if amount == 2:
        one = jax.random.randint(rng, (), max(1, total - most), min(most, total - 1) + 1)
        return jnp.stack([one, total - one])
    tallies = jnp.asarray(length_profile(amount, total, most, slope), jnp.int32)
    twos = (amount - 1) // 2
    source_of, sink = tallies[1:1 + 2 * twos:2], tallies[2:2 + 2 * twos:2]
    room = jnp.minimum(source_of - 1, most - sink)
    passed = jax.random.randint(jax.random.fold_in(rng, 1), (twos,), 0, 1 << 20) % (room + 1)
    tallies = tallies.at[1:1 + 2 * twos:2].set(source_of - passed).at[2:2 + 2 * twos:2].set(sink + passed)
    return tallies[jax.random.permutation(jax.random.fold_in(rng, 2), amount)]


def scatter_about(stream_key, shape, deviation, limit, pieces=(), held_as=jnp.bfloat16):
    factor_of = level_of(stream_key, shape, pieces, -0.22, 0.18) if pieces else 1.0
    values = jax.random.normal(stream_key, shape, jnp.float32) * deviation * factor_of
    return jnp.minimum(jnp.maximum(values, -limit), limit).astype(held_as)


def setup_inputs(seed: int = 0) -> dict:
    keys = jax.random.split(jax.random.key(seed), 9)
    return {
        "tokens": scatter_about(keys[0], (TOKENS, D), 1.0, 6.0, ((0, 32),)),
        "w_qkv": scatter_about(keys[1], (D, 3 * D), D ** -0.5, 0.125, ((0, 32),)),
        "w_out": scatter_about(keys[2], (D, D), (D // 64) ** -0.5, 1.0, ((0, 32),)),
        "w_gate_up": scatter_about(keys[3], (D, 2 * FF), D ** -0.5, 0.125, ((0, 32),)),
        "w_down": scatter_about(keys[4], (FF, D), FF ** -0.5, 0.0625, ((0, 32),)),
        "seq_lengths": jax.vmap(lambda own: ragged_sizes(own, SEQS, GROUP_TOK, LONGEST, 0))(jax.random.split(keys[5], N_FSDP)).reshape((N_FSDP, SEQS)).astype(jnp.int32),
        "block_order": draw_block_order(jax.random.fold_in(keys[8], 71), 0),
        "cotangent": scatter_about(keys[7], (TOKENS, D), 1.0, 6.0, ((0, 32),)),
    }


@jax.custom_vjp
def low(v):
    return lax.optimization_barrier(v.astype(jnp.bfloat16)).astype(jnp.float32)

@jax.custom_vjp
def low_back(v):
    return v

def low_keep(v):
    return (low(v), None)

def low_pass(kept, grad):
    return (grad,)

def back_keep(v):
    return (v, None)

def back_low(kept, grad):
    return (low(grad),)
low.defvjp(low_keep, low_pass)
low_back.defvjp(back_keep, back_low)

def matmul(left, right):
    return jnp.dot(left, right, precision=lax.Precision.HIGHEST, preferred_element_type=jnp.float32)

def normalize(values):
    average = lax.optimization_barrier(jnp.mean(values, axis=-1, keepdims=True))
    centered = values - average
    variance = lax.optimization_barrier(jnp.mean(centered * centered, axis=-1, keepdims=True))
    return centered * lax.rsqrt(variance + 1e-05)

def places(token_index, lengths):
    seq_ends = jnp.cumsum(lengths).astype(jnp.int32)
    sequence = lax.optimization_barrier(jnp.sum((token_index[:, None] >= seq_ends[None, :]).astype(jnp.int32), axis=1)).astype(jnp.int32)
    before = jnp.arange(lengths.shape[0], dtype=jnp.int32)
    seq_start = lax.optimization_barrier(jnp.sum(jnp.where(before[None, :] < sequence[:, None], lengths[None, :], 0), axis=1)).astype(jnp.int32)
    return (sequence, (token_index - seq_start).astype(jnp.int32))

def group_places(lengths, order):
    row_index = jnp.arange(GROUP_TOK, dtype=jnp.int32)
    initial = (order[row_index // BLOCK] * BLOCK + row_index % BLOCK).astype(jnp.int32)
    return places(initial, lengths)

def angle_tables(position):
    half_dim = HEAD_DIM // 2
    frequency = 10000.0 ** (-jnp.arange(half_dim, dtype=jnp.float32) * 2.0 / HEAD_DIM)
    angle_table = position.astype(jnp.float32)[:, None] * frequency[None, :]
    angle_table = jnp.concatenate([angle_table, angle_table], axis=-1)
    return (jnp.cos(angle_table)[:, None, :], jnp.sin(angle_table)[:, None, :])

def rotate(values, cosine_table, sine_table):
    half_dim = values.shape[-1] // 2
    turned = jnp.concatenate([-values[..., half_dim:], values[..., :half_dim]], axis=-1)
    return values * cosine_table + turned * sine_table

def score_block(query_block, query_seq, query_pos, key_rows, value_rows, key_seq, key_pos):
    scores = low_back(jnp.einsum('qhd,khd->hqk', query_block, key_rows, precision=lax.Precision.HIGHEST))
    scores = scores * HEAD_DIM ** (-0.5)
    allowed = (query_seq[:, None] == key_seq[None, :]) & (key_pos[None, :] <= query_pos[:, None])
    scores = jnp.where(allowed[None], scores, -1e+30)
    probs = low(jax.nn.softmax(scores, axis=-1))
    return jnp.einsum('hqk,khd->qhd', probs, value_rows, precision=lax.Precision.HIGHEST)

def reference(tokens, w_qkv, w_out, w_gate_up, w_down, seq_lengths, block_order, cotangent):
    seq_ids, positions = jax.vmap(group_places)(seq_lengths, block_order)
    cosine_table, sine_table = angle_tables(positions.reshape(TOKENS))
    half_rows = GROUP_TOK // 2

    def group_attention(group_args):
        queries, key_rows, value_rows, group_seq, group_pos = group_args
        query_blocks = queries.reshape(2, half_rows, HEADS, HEAD_DIM)
        seq_blocks = group_seq.reshape(2, half_rows)
        pos_blocks = group_pos.reshape(2, half_rows)
        checked = jax.checkpoint(score_block)
        mixed = lax.map(lambda parts: checked(parts[0], parts[1], parts[2], key_rows, value_rows, group_seq, group_pos), (query_blocks, seq_blocks, pos_blocks))
        return mixed.reshape(GROUP_TOK, HEADS, HEAD_DIM)

    def forward(inputs, qkv_weight, out_weight, gate_up_weight, down_weight):
        normed_in = low(normalize(inputs))
        qkv = low_back(matmul(normed_in, qkv_weight))
        queries = qkv[:, :D].reshape(TOKENS, HEADS, HEAD_DIM)
        key_rows = qkv[:, D:2 * D].reshape(TOKENS, HEADS, HEAD_DIM)
        value_rows = low(qkv[:, 2 * D:].reshape(TOKENS, HEADS, HEAD_DIM))
        queries = low(rotate(queries, cosine_table, sine_table))
        key_rows = low(rotate(key_rows, cosine_table, sine_table))
        shape_four = (N_FSDP, GROUP_TOK, HEADS, HEAD_DIM)
        mixed = lax.map(group_attention, (queries.reshape(shape_four), key_rows.reshape(shape_four), value_rows.reshape(shape_four), seq_ids, positions))
        attn_mix = low(low_back(mixed.reshape(TOKENS, D)))
        residual = inputs + low_back(matmul(attn_mix, out_weight))
        normed_mid = low(normalize(residual))
        gate_up = low_back(matmul(normed_mid, gate_up_weight))
        gate_part = gate_up[:, :FF]
        up_part = gate_up[:, FF:]
        activated = low(gate_part * jax.nn.sigmoid(gate_part) * up_part)
        return residual + low_back(matmul(activated, down_weight))
    inputs = tokens.astype(jnp.float32)
    result, pullback = jax.vjp(forward, inputs, w_qkv.astype(jnp.float32), w_out.astype(jnp.float32), w_gate_up.astype(jnp.float32), w_down.astype(jnp.float32))
    grads = pullback(cotangent.astype(jnp.float32))
    return (result.astype(jnp.bfloat16), grads[0], grads[1], grads[2], grads[3], grads[4])
```

```python
import jax
import jax.numpy as jnp
from jax import lax
from jax.sharding import PartitionSpec as P

HEADS = 16
HEAD_DIM = 128
BLOCK = 128


def normalize(values):
    average = jnp.mean(values, axis=-1, keepdims=True)
    centered = values - average
    variance = jnp.mean(centered * centered, axis=-1, keepdims=True)
    inv_root = lax.rsqrt(variance + 1e-05)
    return (centered * inv_root, inv_root)


def norm_back(upstream, normed, inv_root):
    first_mean = jnp.mean(upstream, axis=-1, keepdims=True)
    second_mean = jnp.mean(upstream * normed, axis=-1, keepdims=True)
    return inv_root * (upstream - first_mean - normed * second_mean)


def places(token_index, lengths):
    seq_ends = jnp.cumsum(lengths)
    sequence = jnp.sum((token_index[:, None] >= seq_ends[None, :]).astype(jnp.int32), axis=1)
    before = jnp.arange(lengths.shape[0], dtype=jnp.int32)
    seq_start = jnp.sum(jnp.where(before[None, :] < sequence[:, None], lengths[None, :], 0), axis=1)
    return (sequence, token_index - seq_start)


def initial_index(row_index, order_row):
    slot_index = row_index // BLOCK
    slot_table = jnp.arange(order_row.shape[0], dtype=jnp.int32)
    picked = jnp.sum(
        jnp.where(slot_table[None, :] == slot_index[:, None], order_row[None, :], 0), axis=1
    )
    return picked * BLOCK + row_index % BLOCK


def angle_tables(position):
    half_dim = HEAD_DIM // 2
    frequency = 10000.0 ** (-jnp.arange(half_dim, dtype=jnp.float32) * 2.0 / HEAD_DIM)
    angle_table = position.astype(jnp.float32)[:, None] * frequency[None, :]
    angle_table = jnp.concatenate([angle_table, angle_table], axis=-1)
    return (jnp.cos(angle_table)[:, None, :], jnp.sin(angle_table)[:, None, :])


def rotate(values, cosine_table, sine_table):
    half_dim = values.shape[-1] // 2
    turned = jnp.concatenate([-values[..., half_dim:], values[..., :half_dim]], axis=-1)
    return values * cosine_table + turned * sine_table


def unrotate(values, cosine_table, sine_table):
    half_dim = values.shape[-1] // 2
    scaled = values * sine_table
    turned = jnp.concatenate([scaled[..., half_dim:], -scaled[..., :half_dim]], axis=-1)
    return values * cosine_table + turned


def dot(left, right):
    return jnp.dot(left, right, preferred_element_type=jnp.float32)


def times_transposed(left, right):
    return lax.dot_general(
        left, right, (((1,), (1,)), ((), ())), preferred_element_type=jnp.float32
    )


def column_product(left, right):
    return lax.dot_general(
        left, right, (((0,), (0,)), ((), ())), preferred_element_type=jnp.float32
    )


def gather(values, axes):
    return lax.all_gather(values, axes, axis=0, tiled=True)


def scatter(values, axes):
    return lax.psum_scatter(values, axes, scatter_dimension=0, tiled=True)


def spread_columns(weight, outer, parts):
    rows, columns = weight.shape
    inner = columns // (outer * parts)
    pieces = weight.reshape(rows, outer, parts, inner).transpose(2, 0, 1, 3)
    pieces = lax.all_to_all(pieces, "ctx", split_axis=0, concat_axis=0, tiled=True)
    return pieces.reshape(parts * rows, outer * inner)


def collect_rows(grad, outer, parts):
    rows, columns = grad.shape
    inner = columns // outer
    pieces = grad.reshape(parts, rows // parts, columns)
    pieces = lax.all_to_all(pieces, "ctx", split_axis=0, concat_axis=0, tiled=True)
    pieces = pieces.reshape(parts, rows // parts, outer, inner).transpose(1, 2, 0, 3)
    return pieces.reshape(rows // parts, outer * parts * inner).astype(jnp.float32)


def per_device(tokens, w_qkv, w_out, w_gate_up, w_down, seq_lengths, block_order, cotangent):
    lengths = seq_lengths[0]
    order_row = block_order[0]
    parts = lax.axis_size("ctx")
    groups = lax.axis_size("fsdp")
    rows, width = tokens.shape
    length = rows * parts
    heads = HEADS // parts
    head_width = heads * HEAD_DIM
    low = jnp.bfloat16
    score_scale = HEAD_DIM ** (-0.5)

    qkv_cols = gather(spread_columns(w_qkv, 3, parts), "fsdp")
    out_full = gather(w_out, ("fsdp", "ctx"))
    gate_up_cols = gather(spread_columns(w_gate_up, 2 * groups, parts), "fsdp")
    down_rows = gather(w_down, "fsdp")
    cot_full = gather(cotangent, "ctx")

    inputs = tokens.astype(jnp.float32)
    normed_in, root_in = normalize(inputs)
    normed_in_full = gather(normed_in.astype(low), "ctx")

    row_index = jnp.arange(length, dtype=jnp.int32)
    seq, pos = places(initial_index(row_index, order_row), lengths)
    cosine_table, sine_table = angle_tables(pos)
    allowed = ((seq[:, None] == seq[None, :]) & (pos[None, :] <= pos[:, None]))[None]

    qkv = dot(normed_in_full, qkv_cols)
    head_shape = (length, heads, HEAD_DIM)
    queries = rotate(qkv[:, :head_width].reshape(head_shape), cosine_table, sine_table).astype(low)
    keys = rotate(
        qkv[:, head_width : 2 * head_width].reshape(head_shape), cosine_table, sine_table
    ).astype(low)
    values = qkv[:, 2 * head_width :].astype(low).reshape(head_shape)
    scores = jnp.einsum("qhd,khd->hqk", queries, keys, preferred_element_type=jnp.float32)
    scores = jnp.where(allowed, scores * score_scale, -1e30)
    row_max = jnp.max(scores, axis=-1)
    weights = jnp.where(allowed, jnp.exp(scores - row_max[..., None]), 0.0)
    row_total = jnp.sum(weights, axis=-1)
    mixed = jnp.einsum("hqk,khd->qhd", weights.astype(low), values, preferred_element_type=jnp.float32)
    log_total = row_max + jnp.log(row_total)
    attn_heads = mixed / jnp.transpose(row_total)[..., None]

    mix_pieces = attn_heads.astype(low).reshape(parts, rows, head_width)
    mix_pieces = lax.all_to_all(mix_pieces, "ctx", split_axis=0, concat_axis=0, tiled=True)
    mix_low = mix_pieces.transpose(1, 0, 2).reshape(rows, width)
    residual = inputs + dot(mix_low, out_full)
    normed_mid, root_mid = normalize(residual)
    normed_mid_full = gather(normed_mid.astype(low), "ctx")

    gate_up = dot(normed_mid_full, gate_up_cols)
    units = gate_up.shape[1] // 2
    gate_part = gate_up[:, :units]
    up_part = gate_up[:, units:]
    sigmoid_gate = jax.nn.sigmoid(gate_part)
    silu_gate = gate_part * sigmoid_gate
    activated = (silu_gate * up_part).astype(low)
    down_out = scatter(dot(activated, down_rows).astype(low), "ctx")
    layer_out = (residual + down_out.astype(jnp.float32)).astype(low)

    down_grad = scatter(column_product(activated, cot_full).astype(low), "fsdp").astype(jnp.float32)

    act_grad = times_transposed(cot_full, down_rows)
    gate_grad = act_grad * up_part * sigmoid_gate * (1.0 + gate_part * (1.0 - sigmoid_gate))
    up_grad = act_grad * silu_gate
    gate_up_back = jnp.concatenate([gate_grad, up_grad], axis=1).astype(low)
    mid_back = scatter(times_transposed(gate_up_back, gate_up_cols).astype(low), "ctx")
    gate_up_grad = scatter(column_product(normed_mid_full, gate_up_back).astype(low), "fsdp")

    residual_back = cotangent.astype(jnp.float32) + norm_back(
        mid_back.astype(jnp.float32), normed_mid, root_mid
    )
    proj_back = residual_back.astype(low)
    mix_back = times_transposed(proj_back, out_full).astype(low)
    out_grad = scatter(column_product(mix_low, proj_back).astype(low), ("fsdp", "ctx"))

    back_pieces = mix_back.reshape(rows, parts, head_width).transpose(1, 0, 2)
    back_pieces = lax.all_to_all(back_pieces, "ctx", split_axis=0, concat_axis=0, tiled=True)
    back_heads = back_pieces.reshape(head_shape)

    delta = jnp.einsum("qhd,qhd->hq", back_heads.astype(jnp.float32), attn_heads)
    probs = jnp.where(allowed, jnp.exp(scores - log_total[..., None]), 0.0)
    value_back = jnp.einsum(
        "hqk,qhd->khd", probs.astype(low), back_heads, preferred_element_type=jnp.float32
    )
    prob_back = jnp.einsum("qhd,khd->hqk", back_heads, values, preferred_element_type=jnp.float32)
    score_back = (score_scale * probs * (prob_back - delta[..., None])).astype(low)
    query_back = jnp.einsum("hqk,khd->qhd", score_back, keys, preferred_element_type=jnp.float32)
    key_back = jnp.einsum("hqk,qhd->khd", score_back, queries, preferred_element_type=jnp.float32)
    qkv_back = jnp.concatenate(
        [
            unrotate(query_back, cosine_table, sine_table).reshape(length, head_width),
            unrotate(key_back, cosine_table, sine_table).reshape(length, head_width),
            value_back.reshape(length, head_width),
        ],
        axis=1,
    ).astype(low)
    in_back = scatter(times_transposed(qkv_back, qkv_cols).astype(low), "ctx")
    tokens_grad = residual_back + norm_back(in_back.astype(jnp.float32), normed_in, root_in)
    qkv_grad = scatter(column_product(normed_in_full, qkv_back).astype(low), "fsdp")

    return (
        layer_out,
        tokens_grad,
        collect_rows(qkv_grad, 3, parts),
        out_grad.astype(jnp.float32),
        collect_rows(gate_up_grad, 2 * groups, parts),
        down_grad,
    )


def solution(mesh):
    both = P(("fsdp", "ctx"), None)
    one = P("fsdp", None)
    return jax.shard_map(
        per_device,
        mesh=mesh,
        in_specs=(both, both, both, both, both, one, one, both),
        out_specs=(both,) * 6,
        check_vma=False,
    )
```

```python
import jax
import jax.numpy as jnp
from jax import lax
from jax.experimental import pallas as pl
from jax.experimental.pallas import tpu as pltpu
from jax.sharding import PartitionSpec as P

HEADS = 16
HEAD_DIM = 128
BLOCK = 128
LOW = jnp.bfloat16


def normalize(values):
    average = jnp.mean(values, axis=-1, keepdims=True)
    centered = values - average
    variance = jnp.mean(centered * centered, axis=-1, keepdims=True)
    inv_root = lax.rsqrt(variance + 1e-05)
    return (centered * inv_root, inv_root)


def norm_back(upstream, normed, inv_root):
    first_mean = jnp.mean(upstream, axis=-1, keepdims=True)
    second_mean = jnp.mean(upstream * normed, axis=-1, keepdims=True)
    return inv_root * (upstream - first_mean - normed * second_mean)


def places(token_index, lengths):
    seq_ends = jnp.cumsum(lengths)
    sequence = jnp.sum((token_index[:, None] >= seq_ends[None, :]).astype(jnp.int32), axis=1)
    before = jnp.arange(lengths.shape[0], dtype=jnp.int32)
    seq_start = jnp.sum(jnp.where(before[None, :] < sequence[:, None], lengths[None, :], 0), axis=1)
    return (sequence, token_index - seq_start)


def initial_index(row_index, order_row):
    slot_index = row_index // BLOCK
    slot_table = jnp.arange(order_row.shape[0], dtype=jnp.int32)
    picked = jnp.sum(
        jnp.where(slot_table[None, :] == slot_index[:, None], order_row[None, :], 0), axis=1
    )
    return picked * BLOCK + row_index % BLOCK


def angle_tables(position):
    half_dim = HEAD_DIM // 2
    frequency = 10000.0 ** (-jnp.arange(half_dim, dtype=jnp.float32) * 2.0 / HEAD_DIM)
    angle_table = position.astype(jnp.float32)[:, None] * frequency[None, :]
    angle_table = jnp.concatenate([angle_table, angle_table], axis=-1)
    return (jnp.cos(angle_table)[:, None, :], jnp.sin(angle_table)[:, None, :])


def rotate(values, cosine_table, sine_table):
    half_dim = values.shape[-1] // 2
    turned = jnp.concatenate([-values[..., half_dim:], values[..., :half_dim]], axis=-1)
    return values * cosine_table + turned * sine_table


def unrotate(values, cosine_table, sine_table):
    half_dim = values.shape[-1] // 2
    scaled = values * sine_table
    turned = jnp.concatenate([scaled[..., half_dim:], -scaled[..., :half_dim]], axis=-1)
    return values * cosine_table + turned


def dot(left, right):
    return jnp.dot(left, right, preferred_element_type=jnp.float32)


def times_transposed(left, right):
    return lax.dot_general(
        left, right, (((1,), (1,)), ((), ())), preferred_element_type=jnp.float32
    )


def column_product(left, right):
    return lax.dot_general(
        left, right, (((0,), (0,)), ((), ())), preferred_element_type=jnp.float32
    )


def gather(values, axes):
    return lax.all_gather(values, axes, axis=0, tiled=True)


def scatter(values, axes):
    return lax.psum_scatter(values, axes, scatter_dimension=0, tiled=True)


def by_part(weight, outer, parts):
    rows, columns = weight.shape
    inner = columns // (outer * parts)
    pieces = weight.reshape(rows, outer, parts, inner).transpose(2, 0, 1, 3)
    return pieces.reshape(parts, rows, outer * inner)


def from_parts(pieces, outer):
    parts, rows, columns = pieces.shape
    pieces = pieces.reshape(parts, rows, outer, columns // outer).transpose(1, 2, 0, 3)
    return pieces.reshape(rows, parts * columns).astype(jnp.float32)


def enter(axes):
    barrier = pltpu.get_barrier_semaphore()
    count = 0
    for axis, size in axes:
        me = lax.axis_index(axis)
        for step in range(1, size):
            pl.semaphore_signal(barrier, inc=1, device_id={axis: lax.rem(me + step, size)})
        count += size - 1
    pl.semaphore_wait(barrier, count)


def remote(src, dst, send, recv, axis, peer):
    return pltpu.make_async_remote_copy(
        src_ref=src, dst_ref=dst, send_sem=send, recv_sem=recv, device_id={axis: peer}
    )


class Exchange:
    def __init__(self, parts, shape):
        self.parts = parts
        self.out = jax.ShapeDtypeStruct((parts,) + shape, LOW)
        self.scratch = [
            pltpu.SemaphoreType.DMA((parts - 1,)),
            pltpu.SemaphoreType.DMA((parts - 1,)),
            pltpu.SemaphoreType.DMA,
        ]

    def run(self, src, dst, send, recv, local):
        me = lax.axis_index("ctx")
        copies = []
        for step in range(1, self.parts):
            peer = lax.rem(me + step, self.parts)
            copies.append(
                remote(src.at[peer], dst.at[me], send.at[step - 1], recv.at[step - 1], "ctx", peer)
            )
            copies[-1].start()
        own = pltpu.make_async_copy(src.at[me], dst.at[me], local)
        own.start()
        yield
        for copy in copies:
            copy.wait()
        own.wait()


class Gather:
    def __init__(self, parts, shape):
        self.parts = parts
        self.out = jax.ShapeDtypeStruct((parts,) + shape, LOW)
        chips = parts // 2
        self.scratch = [
            pltpu.SemaphoreType.DMA((2, chips)),
            pltpu.SemaphoreType.DMA((chips,)),
            pltpu.SemaphoreType.DMA((chips,)),
            pltpu.SemaphoreType.DMA((chips,)),
            pltpu.SemaphoreType.DMA,
        ]

    def run(self, src, dst, send, recv, pair_send, pair_recv, local):
        chips = self.parts // 2
        me = lax.axis_index("ctx")
        chip, core = me // 2, lax.rem(me, 2)
        partner = me + 1 - 2 * core

        def line(block, slot, origin, way):
            return remote(
                block, slot, send.at[way, origin], recv.at[origin], "ctx", me + 2 - 4 * way
            )

        def across(block, slot, origin):
            return remote(block, slot, pair_send.at[origin], pair_recv.at[origin], "ctx", partner)

        mine = dst.at[me]

        @pl.when(chip < chips - 1)
        def _():
            line(src, mine, chip, 0).start()

        @pl.when(chip > 0)
        def _():
            line(src, mine, chip, 1).start()

        across(src, mine, chip).start()
        own = pltpu.make_async_copy(src, mine, local)
        own.start()
        yield
        for step in range(1, chips):
            for way in range(2):
                origin = chip - step if way == 0 else chip + step

                @pl.when((origin >= 0) & (origin < chips))
                def _():
                    slot = dst.at[2 * origin + core]
                    line(slot, slot, origin, way).wait_recv()

                    @pl.when((chip < chips - 1) if way == 0 else (chip > 0))
                    def _():
                        line(slot, slot, origin, way).start()

                    across(slot, slot, origin).start()

            yield
        for step in range(chips):
            for way in range(2):
                origin = chip - step if way == 0 else chip + step
                ahead = (chip < chips - 1) if way == 0 else (chip > 0)

                @pl.when((origin >= 0) & (origin < chips) & ahead)
                def _():
                    slot = dst.at[2 * origin + core]
                    line(slot, slot, origin, way).wait_send()

        for origin in range(chips):
            across(dst.at[2 * origin + core], dst.at[2 * origin + core], origin).wait_send()
            other = dst.at[2 * origin + 1 - core]
            across(other, other, origin).wait_recv()
        own.wait()


class Scatter:
    def __init__(self, parts, shape):
        self.parts, self.shape = parts, shape
        self.out = jax.ShapeDtypeStruct(shape, jnp.float32)
        chips = parts // 2
        self.scratch = [
            pltpu.VMEM((chips,) + shape, LOW),
            pltpu.VMEM((2, chips) + shape, LOW),
            pltpu.VMEM((chips,) + shape, LOW),
            pltpu.SemaphoreType.DMA((chips,)),
            pltpu.SemaphoreType.DMA((chips,)),
            pltpu.SemaphoreType.DMA((chips,)),
            pltpu.SemaphoreType.DMA((2, chips)),
        ]

    def run(self, src, out, pair, come, stage, pair_send, pair_recv, send, recv):
        chips = self.parts // 2
        me = lax.axis_index("ctx")
        chip, core = me // 2, lax.rem(me, 2)
        partner = me + 1 - 2 * core
        rows = self.shape[0]
        slab = min(rows, 16)

        def across(goal):
            return remote(
                src.at[2 * goal + 1 - core],
                pair.at[goal],
                pair_send.at[goal],
                pair_recv.at[goal],
                "ctx",
                partner,
            )

        def line(goal, way):
            return remote(
                stage.at[goal],
                come.at[way, goal],
                send.at[goal],
                recv.at[way, goal],
                "ctx",
                me + 2 - 4 * way,
            )

        def wide(ref, *index):
            return ref[index].astype(jnp.float32)

        def slabs(part):
            def one(index, carry):
                part(pl.ds(pl.multiple_of(index * slab, slab), slab))
                return carry

            lax.fori_loop(0, rows // slab, one, 0)

        order = []
        for step in range((chips + 1) // 2):
            order += sorted({step, chips - 1 - step})
        for goal in order:
            across(goal).start()
        yield
        for step in range(chips - 1):
            for way in range(2):
                goal = chips - 1 - step if way == 0 else step
                first = (chip == 0) if way == 0 else (chip == chips - 1)

                def begin(at):
                    value = wide(src, 2 * goal + core, at) + wide(pair, goal, at)
                    stage[goal, at, :] = value.astype(LOW)

                def middle(at):
                    value = wide(src, 2 * goal + core, at) + wide(pair, goal, at)
                    value += wide(come, way, goal, at)
                    stage[goal, at, :] = value.astype(LOW)

                @pl.when((chip < goal) if way == 0 else (chip > goal))
                def _():
                    across(goal).wait_recv()

                    @pl.when(first)
                    def _():
                        slabs(begin)

                    @pl.when(jnp.logical_not(first))
                    def _():
                        line(goal, way).wait_recv()
                        slabs(middle)

                    line(goal, way).start()

            yield

        def own(at):
            out[at, :] = wide(src, me, at) + wide(pair, chip, at)

        across(chip).wait_recv()
        slabs(own)
        for way in range(2):

            def last(at):
                out[at, :] += wide(come, way, chip, at)

            @pl.when((chip > 0) if way == 0 else (chip < chips - 1))
            def _():
                line(chip, way).wait_recv()
                slabs(last)

            yield
        for goal in range(chips):
            across(goal).wait_send()

            @pl.when(chip != goal)
            def _():
                line(goal, 0).wait_send()


class Spread:
    def __init__(self, parts, groups, shape):
        self.parts, self.groups = parts, groups
        self.out = jax.ShapeDtypeStruct((groups, parts) + shape, LOW)
        self.scratch = [
            pltpu.SemaphoreType.DMA((parts - 1,)),
            pltpu.SemaphoreType.DMA((parts - 1,)),
            pltpu.SemaphoreType.DMA((groups - 1, parts)),
            pltpu.SemaphoreType.DMA((groups - 1, parts)),
            pltpu.SemaphoreType.DMA,
        ]

    def run(self, src, dst, send, recv, far_send, far_recv, local):
        parts, groups = self.parts, self.groups
        me, group = lax.axis_index("ctx"), lax.axis_index("fsdp")
        copies = []
        for step in range(1, parts):
            peer = lax.rem(me + step, parts)
            copies.append(
                remote(
                    src.at[peer],
                    dst.at[group, me],
                    send.at[step - 1],
                    recv.at[step - 1],
                    "ctx",
                    peer,
                )
            )
            copies[-1].start()
        own = pltpu.make_async_copy(src.at[me], dst.at[group, me], local)
        own.start()

        def pass_on(block, origin, step):
            out = []
            for hop in range(1, groups):
                copy = remote(
                    block,
                    dst.at[group, origin],
                    far_send.at[hop - 1, step],
                    far_recv.at[hop - 1, step],
                    "fsdp",
                    lax.rem(group + hop, groups),
                )
                copy.start()
                out.append(copy)
            return out

        far = pass_on(src.at[me], me, 0)
        yield
        for step in range(1, parts):
            copies[step - 1].wait_recv()
            origin = lax.rem(me - step + parts, parts)
            far += pass_on(dst.at[group, origin], origin, step)
            yield
        for copy in far:
            copy.wait()
            yield
        for copy in copies:
            copy.wait_send()
        own.wait()


def call(jobs, operands, name, identity, axes, body=None):
    counts = [len(job.scratch) for job in jobs]

    def kernel(*refs):
        n = len(jobs)
        ins, outs, rest = refs[:n], refs[n : 2 * n], refs[2 * n :]
        enter(axes)
        runs, at = [], 0
        for job, src, dst, count in zip(jobs, ins, outs, counts):
            runs.append(job.run(src, dst, *rest[at : at + count]))
            at += count
        while runs:
            going = []
            for run in runs:
                try:
                    next(run)
                    going.append(run)
                except StopIteration:
                    pass
            runs = going

    vmem = pl.BlockSpec(memory_space=pltpu.VMEM)
    return pl.pallas_call(
        kernel,
        out_shape=tuple(job.out for job in jobs),
        in_specs=[vmem] * len(jobs),
        out_specs=(vmem,) * len(jobs),
        scratch_shapes=[shape for job in jobs for shape in job.scratch],
        compiler_params=pltpu.CompilerParams(
            collective_id=identity, has_side_effects=True, vmem_limit_bytes=60 << 20
        ),
        name=name,
    )(*operands)


def per_device(tokens, w_qkv, w_out, w_gate_up, w_down, seq_lengths, block_order, cotangent):
    lengths = seq_lengths[0]
    order_row = block_order[0]
    parts = lax.axis_size("ctx")
    groups = lax.axis_size("fsdp")
    rows, width = tokens.shape
    length = rows * parts
    heads = HEADS // parts
    head_width = heads * HEAD_DIM
    score_scale = HEAD_DIM ** (-0.5)

    line = (("ctx", parts),)
    plane = (("ctx", parts), ("fsdp", groups))
    block = (rows, width)

    out_full = gather(w_out, ("fsdp", "ctx"))
    down_rows = gather(w_down, "fsdp")
    inputs = tokens.astype(jnp.float32)
    normed_in, root_in = normalize(inputs)
    qkv_pieces = by_part(w_qkv, 3, parts)
    gate_up_pieces = by_part(w_gate_up, 2 * groups, parts)
    qkv_cols, normed_in_full, gate_up_cols = call(
        [
            Spread(parts, groups, qkv_pieces.shape[1:]),
            Gather(parts, block),
            Exchange(parts, gate_up_pieces.shape[1:]),
        ],
        [qkv_pieces, normed_in.astype(LOW), gate_up_pieces],
        "start",
        1,
        plane,
    )
    qkv_cols = qkv_cols.reshape(width, 3 * head_width)
    normed_in_full = normed_in_full.reshape(length, width)
    gate_up_cols = gather(gate_up_cols.reshape(width // groups, -1), "fsdp")

    row_index = jnp.arange(length, dtype=jnp.int32)
    seq, pos = places(initial_index(row_index, order_row), lengths)
    cosine_table, sine_table = angle_tables(pos)
    allowed = ((seq[:, None] == seq[None, :]) & (pos[None, :] <= pos[:, None]))[None]

    qkv = dot(normed_in_full, qkv_cols)
    head_shape = (length, heads, HEAD_DIM)
    queries = rotate(qkv[:, :head_width].reshape(head_shape), cosine_table, sine_table).astype(LOW)
    keys = rotate(
        qkv[:, head_width : 2 * head_width].reshape(head_shape), cosine_table, sine_table
    ).astype(LOW)
    values = qkv[:, 2 * head_width :].astype(LOW).reshape(head_shape)
    scores = jnp.einsum("qhd,khd->hqk", queries, keys, preferred_element_type=jnp.float32)
    scores = jnp.where(allowed, scores * score_scale, -1e30)
    row_max = jnp.max(scores, axis=-1)
    weights = jnp.where(allowed, jnp.exp(scores - row_max[..., None]), 0.0)
    row_total = jnp.sum(weights, axis=-1)
    mixed = jnp.einsum("hqk,khd->qhd", weights.astype(LOW), values, preferred_element_type=jnp.float32)
    log_total = row_max + jnp.log(row_total)
    attn_heads = mixed / jnp.transpose(row_total)[..., None]

    mix_pieces = attn_heads.astype(LOW).reshape(parts, rows, head_width)
    (mix_pieces,) = call(
        [Exchange(parts, mix_pieces.shape[1:])], [mix_pieces], "mix", 2, line
    )
    mix_low = mix_pieces.transpose(1, 0, 2).reshape(rows, width)
    residual = inputs + dot(mix_low, out_full)
    normed_mid, root_mid = normalize(residual)
    normed_mid_full, cot_full = call(
        [Gather(parts, block), Gather(parts, block)],
        [normed_mid.astype(LOW), cotangent],
        "mid",
        3,
        line,
    )
    normed_mid_full = normed_mid_full.reshape(length, width)
    cot_full = cot_full.reshape(length, width)

    gate_up = dot(normed_mid_full, gate_up_cols)
    units = gate_up.shape[1] // 2
    gate_part = gate_up[:, :units]
    up_part = gate_up[:, units:]
    sigmoid_gate = jax.nn.sigmoid(gate_part)
    silu_gate = gate_part * sigmoid_gate
    activated = (silu_gate * up_part).astype(LOW)
    down_out = scatter(dot(activated, down_rows).astype(LOW), "ctx")
    layer_out = (residual + down_out.astype(jnp.float32)).astype(LOW)

    down_grad = scatter(column_product(activated, cot_full).astype(LOW), "fsdp").astype(jnp.float32)

    act_grad = times_transposed(cot_full, down_rows)
    gate_grad = act_grad * up_part * sigmoid_gate * (1.0 + gate_part * (1.0 - sigmoid_gate))
    up_grad = act_grad * silu_gate
    gate_up_back = jnp.concatenate([gate_grad, up_grad], axis=1).astype(LOW)
    mid_back_terms = times_transposed(gate_up_back, gate_up_cols).astype(LOW)
    gate_up_grad = scatter(column_product(normed_mid_full, gate_up_back).astype(LOW), "fsdp")

    (mid_back,) = call(
        [Scatter(parts, block)],
        [mid_back_terms.reshape((parts,) + block)],
        "mid_back",
        4,
        line,
    )
    residual_back = cotangent.astype(jnp.float32) + norm_back(mid_back, normed_mid, root_mid)
    proj_back = residual_back.astype(LOW)
    mix_back = times_transposed(proj_back, out_full).astype(LOW)

    back_pieces = mix_back.reshape(rows, parts, head_width).transpose(1, 0, 2)
    (back_pieces,) = call(
        [Exchange(parts, back_pieces.shape[1:])], [back_pieces], "mix_back", 5, line
    )
    back_heads = back_pieces.reshape(head_shape)

    delta = jnp.einsum("qhd,qhd->hq", back_heads.astype(jnp.float32), attn_heads)
    probs = jnp.where(allowed, jnp.exp(scores - log_total[..., None]), 0.0)
    value_back = jnp.einsum(
        "hqk,qhd->khd", probs.astype(LOW), back_heads, preferred_element_type=jnp.float32
    )
    prob_back = jnp.einsum("qhd,khd->hqk", back_heads, values, preferred_element_type=jnp.float32)
    score_back = (score_scale * probs * (prob_back - delta[..., None])).astype(LOW)
    query_back = jnp.einsum("hqk,khd->qhd", score_back, keys, preferred_element_type=jnp.float32)
    key_back = jnp.einsum("hqk,qhd->khd", score_back, queries, preferred_element_type=jnp.float32)
    qkv_back = jnp.concatenate(
        [
            unrotate(query_back, cosine_table, sine_table).reshape(length, head_width),
            unrotate(key_back, cosine_table, sine_table).reshape(length, head_width),
            value_back.reshape(length, head_width),
        ],
        axis=1,
    ).astype(LOW)
    in_back_terms = times_transposed(qkv_back, qkv_cols).astype(LOW)
    qkv_grad = scatter(column_product(normed_in_full, qkv_back).astype(LOW), "fsdp")
    shard = width // (parts * groups)
    mix_columns = mix_low.reshape(rows, groups, parts, shard).transpose(2, 0, 1, 3)
    in_back, proj_back_full, mix_columns, gate_up_grad = call(
        [
            Scatter(parts, block),
            Gather(parts, block),
            Exchange(parts, (rows, groups * shard)),
            Exchange(parts, gate_up_pieces.shape[1:]),
        ],
        [
            in_back_terms.reshape((parts,) + block),
            proj_back,
            mix_columns.reshape(parts, rows, groups * shard),
            gate_up_grad.reshape(gate_up_pieces.shape),
        ],
        "in_back",
        6,
        line,
    )
    out_grad = scatter(
        column_product(
            mix_columns.reshape(length, groups * shard), proj_back_full.reshape(length, width)
        ).astype(LOW),
        "fsdp",
    )
    tokens_grad = residual_back + norm_back(in_back, normed_in, root_in)
    (qkv_grad,) = call(
        [Exchange(parts, qkv_pieces.shape[1:])],
        [qkv_grad.reshape(qkv_pieces.shape)],
        "last",
        7,
        line,
    )

    return (
        layer_out,
        tokens_grad,
        from_parts(qkv_grad, 3),
        out_grad.astype(jnp.float32),
        from_parts(gate_up_grad, 2 * groups),
        down_grad,
    )


def solution(mesh):
    both = P(("fsdp", "ctx"), None)
    one = P("fsdp", None)
    return jax.shard_map(
        per_device,
        mesh=mesh,
        in_specs=(both, both, both, both, both, one, one, both),
        out_specs=(both,) * 6,
        check_vma=False,
    )
```

```python
import jax
import jax.numpy as jnp
from jax import lax
from jax.experimental import pallas as pl
from jax.experimental.pallas import tpu as pltpu
from jax.sharding import PartitionSpec as P

HEADS = 16
HEAD_DIM = 128
BLOCK = 128
LOW = jnp.bfloat16


def normalize(values):
    average = jnp.mean(values, axis=-1, keepdims=True)
    centered = values - average
    variance = jnp.mean(centered * centered, axis=-1, keepdims=True)
    inv_root = lax.rsqrt(variance + 1e-05)
    return (centered * inv_root, inv_root)


def norm_back(upstream, normed, inv_root):
    first_mean = jnp.mean(upstream, axis=-1, keepdims=True)
    second_mean = jnp.mean(upstream * normed, axis=-1, keepdims=True)
    return inv_root * (upstream - first_mean - normed * second_mean)


def places(token_index, lengths):
    seq_ends = jnp.cumsum(lengths)
    sequence = jnp.sum((token_index[:, None] >= seq_ends[None, :]).astype(jnp.int32), axis=1)
    before = jnp.arange(lengths.shape[0], dtype=jnp.int32)
    seq_start = jnp.sum(jnp.where(before[None, :] < sequence[:, None], lengths[None, :], 0), axis=1)
    return (sequence, token_index - seq_start)


def initial_index(row_index, order_row):
    slot_index = row_index // BLOCK
    slot_table = jnp.arange(order_row.shape[0], dtype=jnp.int32)
    picked = jnp.sum(
        jnp.where(slot_table[None, :] == slot_index[:, None], order_row[None, :], 0), axis=1
    )
    return picked * BLOCK + row_index % BLOCK


def angle_tables(position):
    half_dim = HEAD_DIM // 2
    frequency = 10000.0 ** (-jnp.arange(half_dim, dtype=jnp.float32) * 2.0 / HEAD_DIM)
    angle_table = position.astype(jnp.float32)[:, None] * frequency[None, :]
    angle_table = jnp.concatenate([angle_table, angle_table], axis=-1)
    return (jnp.cos(angle_table)[:, None, :], jnp.sin(angle_table)[:, None, :])


def rotate(values, cosine_table, sine_table):
    half_dim = values.shape[-1] // 2
    turned = jnp.concatenate([-values[..., half_dim:], values[..., :half_dim]], axis=-1)
    return values * cosine_table + turned * sine_table


def unrotate(values, cosine_table, sine_table):
    half_dim = values.shape[-1] // 2
    scaled = values * sine_table
    turned = jnp.concatenate([scaled[..., half_dim:], -scaled[..., :half_dim]], axis=-1)
    return values * cosine_table + turned


def dot(left, right):
    return jnp.dot(left, right, preferred_element_type=jnp.float32)


def times_transposed(left, right):
    return lax.dot_general(
        left, right, (((1,), (1,)), ((), ())), preferred_element_type=jnp.float32
    )


def column_product(left, right):
    return lax.dot_general(
        left, right, (((0,), (0,)), ((), ())), preferred_element_type=jnp.float32
    )


def gather(values, axes):
    return lax.all_gather(values, axes, axis=0, tiled=True)


def scatter(values, axes):
    return lax.psum_scatter(values, axes, scatter_dimension=0, tiled=True)


def enter(axes):
    barrier = pltpu.get_barrier_semaphore()
    count = 0
    for axis, size in axes:
        me = lax.axis_index(axis)
        for step in range(1, size):
            pl.semaphore_signal(barrier, inc=1, device_id={axis: lax.rem(me + step, size)})
        count += size - 1
    pl.semaphore_wait(barrier, count)


def remote(src, dst, send, recv, axis, peer):
    return pltpu.make_async_remote_copy(
        src_ref=src, dst_ref=dst, send_sem=send, recv_sem=recv, device_id={axis: peer}
    )


class Exchange:
    def __init__(self, parts, shape):
        self.parts = parts
        self.out = jax.ShapeDtypeStruct((parts,) + shape, LOW)
        self.scratch = [
            pltpu.SemaphoreType.DMA((parts - 1,)),
            pltpu.SemaphoreType.DMA((parts - 1,)),
            pltpu.SemaphoreType.DMA,
        ]

    def run(self, src, dst, send, recv, local):
        place = lax.axis_index("ctx")
        me = lax.rem(place, self.parts)
        copies = []
        for step in range(1, self.parts):
            peer = lax.rem(me + step, self.parts)
            copies.append(
                remote(
                    src.at[peer],
                    dst.at[me],
                    send.at[step - 1],
                    recv.at[step - 1],
                    "ctx",
                    place - me + peer,
                )
            )
            copies[-1].start()
        own = pltpu.make_async_copy(src.at[me], dst.at[me], local)
        own.start()
        yield
        for copy in copies:
            copy.wait()
            yield
        own.wait()


class Gather:
    def __init__(self, parts, shape):
        self.parts = parts
        self.out = jax.ShapeDtypeStruct((parts,) + shape, LOW)
        chips = parts // 2
        self.scratch = [
            pltpu.SemaphoreType.DMA((2, chips)),
            pltpu.SemaphoreType.DMA((chips,)),
            pltpu.SemaphoreType.DMA((chips,)),
            pltpu.SemaphoreType.DMA((chips,)),
            pltpu.SemaphoreType.DMA,
        ]

    def run(self, src, dst, send, recv, pair_send, pair_recv, local):
        chips = self.parts // 2
        me = lax.axis_index("ctx")
        chip, core = me // 2, lax.rem(me, 2)
        partner = me + 1 - 2 * core

        def line(block, slot, origin, way):
            return remote(
                block, slot, send.at[way, origin], recv.at[origin], "ctx", me + 2 - 4 * way
            )

        def across(block, slot, origin):
            return remote(block, slot, pair_send.at[origin], pair_recv.at[origin], "ctx", partner)

        mine = dst.at[me]

        @pl.when(chip < chips - 1)
        def _():
            line(src, mine, chip, 0).start()

        @pl.when(chip > 0)
        def _():
            line(src, mine, chip, 1).start()

        across(src, mine, chip).start()
        own = pltpu.make_async_copy(src, mine, local)
        own.start()
        yield
        for step in range(1, chips):
            for way in range(2):
                origin = chip - step if way == 0 else chip + step

                @pl.when((origin >= 0) & (origin < chips))
                def _():
                    slot = dst.at[2 * origin + core]
                    line(slot, slot, origin, way).wait_recv()

                    @pl.when((chip < chips - 1) if way == 0 else (chip > 0))
                    def _():
                        line(slot, slot, origin, way).start()

                    across(slot, slot, origin).start()

            yield
        for step in range(chips):
            for way in range(2):
                origin = chip - step if way == 0 else chip + step
                ahead = (chip < chips - 1) if way == 0 else (chip > 0)

                @pl.when((origin >= 0) & (origin < chips) & ahead)
                def _():
                    slot = dst.at[2 * origin + core]
                    line(slot, slot, origin, way).wait_send()

        for origin in range(chips):
            across(dst.at[2 * origin + core], dst.at[2 * origin + core], origin).wait_send()
            other = dst.at[2 * origin + 1 - core]
            across(other, other, origin).wait_recv()
        own.wait()


class Scatter:
    cuts = 2

    def __init__(self, parts, shape):
        self.parts, self.shape = parts, shape
        self.out = jax.ShapeDtypeStruct(shape, jnp.float32)
        chips = parts // 2
        piece = (self.cuts, shape[0] // self.cuts, shape[1])
        self.scratch = [
            pltpu.VMEM((chips,) + shape, LOW),
            pltpu.VMEM((2, chips) + piece, LOW),
            pltpu.VMEM((chips,) + piece, LOW),
            pltpu.SemaphoreType.DMA((chips,)),
            pltpu.SemaphoreType.DMA((chips,)),
            pltpu.SemaphoreType.DMA((chips, self.cuts)),
            pltpu.SemaphoreType.DMA((2, chips, self.cuts)),
        ]

    def run(self, src, out, pair, come, stage, pair_send, pair_recv, send, recv):
        chips, cuts = self.parts // 2, self.cuts
        me = lax.axis_index("ctx")
        chip, core = me // 2, lax.rem(me, 2)
        partner = me + 1 - 2 * core
        rows = self.shape[0] // cuts
        slab = min(rows, 16)
        last = chips - 1

        def across(goal):
            return remote(
                src.at[2 * goal + 1 - core],
                pair.at[goal],
                pair_send.at[goal],
                pair_recv.at[goal],
                "ctx",
                partner,
            )

        def line(goal, cut, way):
            return remote(
                stage.at[goal, cut],
                come.at[way, goal, cut],
                send.at[goal, cut],
                recv.at[way, goal, cut],
                "ctx",
                me + 2 - 4 * way,
            )

        def wide(ref, *index):
            return ref[index].astype(jnp.float32)

        def slabs(part):
            def one(index, carry):
                part(pl.multiple_of(index * slab, slab))
                return carry

            lax.fori_loop(0, rows // slab, one, 0)

        def both(goal, cut, at):
            at = pl.ds(cut * rows + at, slab)
            return wide(src, 2 * goal + core, at) + wide(pair, goal, at)

        order = []
        for step in range((chips + 1) // 2):
            order += sorted({step, last - step})
        for goal in order:
            across(goal).start()
        yield
        for step in range(last * cuts):
            for way in range(2):
                turn = step - (chip if way == 0 else last - chip)
                goal = (last - turn // cuts) if way == 0 else turn // cuts
                cut = step - (chip if way == 0 else last - chip) - (turn // cuts) * cuts
                first = (chip == 0) if way == 0 else (chip == last)
                ahead = last - chip if way == 0 else chip

                def begin(at):
                    value = both(goal, cut, at)
                    stage[goal, cut, pl.ds(at, slab), :] = value.astype(LOW)

                def middle(at):
                    value = both(goal, cut, at) + wide(come, way, goal, cut, pl.ds(at, slab))
                    stage[goal, cut, pl.ds(at, slab), :] = value.astype(LOW)

                @pl.when((turn >= 0) & (turn < ahead * cuts))
                def _():
                    @pl.when(cut == 0)
                    def _():
                        across(goal).wait_recv()

                    @pl.when(first)
                    def _():
                        slabs(begin)

                    @pl.when(jnp.logical_not(first))
                    def _():
                        line(goal, cut, way).wait_recv()
                        slabs(middle)

                    line(goal, cut, way).start()

            yield
        across(chip).wait_recv()
        for cut in range(cuts):

            def own(at):
                out[pl.ds(cut * rows + at, slab), :] = both(chip, cut, at)

            slabs(own)
        yield
        for cut in range(cuts):
            for way in range(2):

                def final(at):
                    out[pl.ds(cut * rows + at, slab), :] += wide(
                        come, way, chip, cut, pl.ds(at, slab)
                    )

                @pl.when((chip > 0) if way == 0 else (chip < last))
                def _():
                    line(chip, cut, way).wait_recv()
                    slabs(final)

            yield
        for goal in range(chips):
            across(goal).wait_send()

            @pl.when(chip != goal)
            def _():
                for cut in range(cuts):
                    line(goal, cut, 0).wait_send()


class Spread:
    def __init__(self, parts, groups, shape):
        self.parts, self.groups = parts, groups
        self.out = jax.ShapeDtypeStruct((groups, parts) + shape, LOW)
        self.scratch = [
            pltpu.SemaphoreType.DMA((parts - 1,)),
            pltpu.SemaphoreType.DMA((parts - 1,)),
            pltpu.SemaphoreType.DMA((groups - 1, parts)),
            pltpu.SemaphoreType.DMA((groups - 1, parts)),
            pltpu.SemaphoreType.DMA,
        ]

    def run(self, src, dst, send, recv, far_send, far_recv, local):
        parts, groups = self.parts, self.groups
        me, group = lax.axis_index("ctx"), lax.axis_index("fsdp")
        copies = []
        for step in range(1, parts):
            peer = lax.rem(me + step, parts)
            copies.append(
                remote(
                    src.at[peer],
                    dst.at[group, me],
                    send.at[step - 1],
                    recv.at[step - 1],
                    "ctx",
                    peer,
                )
            )
            copies[-1].start()
        own = pltpu.make_async_copy(src.at[me], dst.at[group, me], local)
        own.start()

        def pass_on(block, origin, step):
            out = []
            for hop in range(1, groups):
                copy = remote(
                    block,
                    dst.at[group, origin],
                    far_send.at[hop - 1, step],
                    far_recv.at[hop - 1, step],
                    "fsdp",
                    lax.rem(group + hop, groups),
                )
                copy.start()
                out.append(copy)
            return out

        far = pass_on(src.at[me], me, 0)
        yield
        for step in range(1, parts):
            copies[step - 1].wait_recv()
            origin = lax.rem(me - step + parts, parts)
            far += pass_on(dst.at[group, origin], origin, step)
            yield
        for copy in far:
            copy.wait()
            yield
        for copy in copies:
            copy.wait_send()
        own.wait()


def call(jobs, operands, name, identity, axes, work=None):
    counts = [len(job.scratch) for job in jobs]
    jobs_n = len(jobs)
    extra = work.operands if work else []
    extra_out = work.outs if work else []
    extra_scratch = work.scratch if work else []

    def kernel(*refs):
        refs = list(refs)

        def take(count):
            taken = refs[:count]
            del refs[:count]
            return taken

        ins, more = take(jobs_n), take(len(extra))
        outs, more_outs = take(jobs_n), take(len(extra_out))
        runs = []
        for job, src, dst, count in zip(jobs, ins, outs, counts):
            runs.append(job.run(src, dst, *take(count)))
        if work:
            runs.append(work.run(*more, *more_outs, *refs))
        enter(axes)
        while runs:
            going = []
            for run in runs:
                try:
                    next(run)
                    going.append(run)
                except StopIteration:
                    pass
            runs = going

    vmem = pl.BlockSpec(memory_space=pltpu.VMEM)
    anywhere = pl.BlockSpec(memory_space=pl.ANY)
    return pl.pallas_call(
        kernel,
        out_shape=tuple(job.out for job in jobs) + tuple(extra_out),
        in_specs=[vmem] * jobs_n + [anywhere] * len(extra),
        out_specs=(vmem,) * jobs_n + (anywhere,) * len(extra_out),
        scratch_shapes=[shape for job in jobs for shape in job.scratch] + list(extra_scratch),
        compiler_params=pltpu.CompilerParams(
            collective_id=identity, has_side_effects=True, vmem_limit_bytes=62 << 20
        ),
        name=name,
    )(*operands, *extra)


class Grads:
    tile = 256

    def __init__(self, pairs):
        self.pairs = pairs
        length, wide = pairs[0][0].shape[0], max(right.shape[1] for _, right in pairs)
        self.operands = [array for pair in pairs for array in pair]
        self.outs = [jax.ShapeDtypeStruct((l.shape[1], r.shape[1]), LOW) for l, r in pairs]
        self.scratch = [pltpu.VMEM(array.shape, LOW) for array in self.operands]
        self.scratch += [
            pltpu.VMEM((self.tile, length), LOW),
            pltpu.VMEM((2, self.tile, wide), LOW),
            pltpu.SemaphoreType.DMA((2 * len(pairs),)),
            pltpu.SemaphoreType.DMA((2,)),
        ]

    def run(self, *refs):
        n, tile = len(self.pairs), self.tile
        sources, outs = refs[: 2 * n], refs[2 * n : 3 * n]
        held = refs[3 * n : 5 * n]
        turned, made, get, put = refs[5 * n :]
        gets = [pltpu.make_async_copy(s, h, get.at[i]) for i, (s, h) in enumerate(zip(sources, held))]
        for copy in gets:
            copy.start()
        yield
        puts = []
        for which in range(n):
            left, right, out = held[2 * which], held[2 * which + 1], outs[which]
            gets[2 * which].wait()
            gets[2 * which + 1].wait()
            columns = right.shape[1]
            step = min(columns, 512)
            for at in range(0, left.shape[1], tile):
                slot = len(puts) % 2
                if len(puts) >= 2:
                    puts[-2].wait()
                turned[...] = left[:, at : at + tile].T

                def one(index, carry):
                    where = pl.ds(pl.multiple_of(index * step, step), step)
                    made[slot, :, where] = jnp.dot(
                        turned[...], right[:, where], preferred_element_type=jnp.float32
                    ).astype(LOW)
                    return carry

                lax.fori_loop(0, columns // step, one, 0)
                part = made.at[slot] if columns == made.shape[2] else made.at[slot, :, :columns]
                puts.append(pltpu.make_async_copy(part, out.at[at : at + tile, :], put.at[slot]))
                puts[-1].start()
                yield
        for copy in puts[-2:]:
            copy.wait()


class Plan:
    def __init__(self, parts, groups, width):
        self.parts, self.groups = parts, groups
        self.shard = width // (parts * groups)
        self.run = HEAD_DIM // self.shard
        self.heads = HEADS // parts
        self.qkv_dims = (3, self.run, self.heads, parts // self.run, HEAD_DIM)

    def qkv_pieces(self, weight):
        rows = weight.shape[0]
        pieces = weight.reshape((rows,) + self.qkv_dims).transpose(4, 2, 0, 1, 3, 5)
        return pieces.reshape(self.parts, rows, 3 * self.heads * HEAD_DIM)

    def qkv_rows(self, pieces):
        parts, rows, columns = pieces.shape
        runs = parts // self.run
        pieces = pieces.reshape(runs, self.run, rows, 3, self.heads, HEAD_DIM)
        return pieces.transpose(2, 3, 1, 4, 0, 5).reshape(rows, parts * columns).astype(jnp.float32)

    def unit_pieces(self, weight):
        rows, columns = weight.shape
        inner = columns // (2 * self.groups * self.parts)
        pieces = weight.reshape(rows, 2 * self.groups, self.parts, inner).transpose(2, 0, 1, 3)
        return pieces.reshape(self.parts, rows, 2 * self.groups * inner)

    def unit_rows(self, pieces):
        parts, rows, columns = pieces.shape
        outer = 2 * self.groups
        pieces = pieces.reshape(parts, rows, outer, columns // outer).transpose(1, 2, 0, 3)
        return pieces.reshape(rows, parts * columns).astype(jnp.float32)


def per_device(tokens, w_qkv, w_out, w_gate_up, w_down, seq_lengths, block_order, cotangent):
    lengths = seq_lengths[0]
    order_row = block_order[0]
    parts = lax.axis_size("ctx")
    groups = lax.axis_size("fsdp")
    rows, width = tokens.shape
    length = rows * parts
    plan = Plan(parts, groups, width)
    heads, shard, run = plan.heads, plan.shard, plan.run
    head_width = heads * HEAD_DIM
    score_scale = HEAD_DIM ** (-0.5)
    line = (("ctx", parts),)
    plane = (("ctx", parts), ("fsdp", groups))
    block = (rows, width)

    out_rows = gather(w_out, "fsdp")
    down_rows = gather(w_down, "fsdp")
    gate_up_pieces = plan.unit_pieces(w_gate_up)
    (gate_up_cols,) = call(
        [Exchange(parts, gate_up_pieces.shape[1:])], [gate_up_pieces], "units", 1, line
    )
    gate_up_cols = gather(gate_up_cols.reshape(width // groups, -1), "fsdp")
    inputs = tokens.astype(jnp.float32)
    normed_in, root_in = normalize(inputs)
    qkv_pieces = plan.qkv_pieces(w_qkv)
    qkv_cols, normed_in_full, out_cols = call(
        [
            Spread(parts, groups, qkv_pieces.shape[1:]),
            Gather(parts, block),
            Exchange(run, (heads * shard, width)),
        ],
        [qkv_pieces, normed_in.astype(LOW), out_rows.reshape(run, heads * shard, width)],
        "start",
        2,
        plane,
    )
    qkv_cols = qkv_cols.reshape(width, 3 * head_width)
    normed_in_full = normed_in_full.reshape(length, width)
    out_cols = out_cols.reshape(run, heads, shard, width).transpose(1, 0, 2, 3)
    out_cols = out_cols.reshape(head_width, width)

    row_index = jnp.arange(length, dtype=jnp.int32)
    seq, pos = places(initial_index(row_index, order_row), lengths)
    cosine_table, sine_table = angle_tables(pos)
    allowed = ((seq[:, None] == seq[None, :]) & (pos[None, :] <= pos[:, None]))[None]

    qkv = dot(normed_in_full, qkv_cols)
    head_shape = (length, heads, HEAD_DIM)
    queries = rotate(qkv[:, :head_width].reshape(head_shape), cosine_table, sine_table).astype(LOW)
    keys = rotate(
        qkv[:, head_width : 2 * head_width].reshape(head_shape), cosine_table, sine_table
    ).astype(LOW)
    values = qkv[:, 2 * head_width :].astype(LOW).reshape(head_shape)
    scores = jnp.einsum("qhd,khd->hqk", queries, keys, preferred_element_type=jnp.float32)
    scores = jnp.where(allowed, scores * score_scale, -1e30)
    row_max = jnp.max(scores, axis=-1)
    weights = jnp.where(allowed, jnp.exp(scores - row_max[..., None]), 0.0)
    row_total = jnp.sum(weights, axis=-1)
    mixed = jnp.einsum("hqk,khd->qhd", weights.astype(LOW), values, preferred_element_type=jnp.float32)
    log_total = row_max + jnp.log(row_total)
    attn_heads = mixed / jnp.transpose(row_total)[..., None]
    mix_low = attn_heads.astype(LOW).reshape(length, head_width)

    out_terms = dot(mix_low, out_cols).astype(LOW)
    attn_out, cot_full = call(
        [Scatter(parts, block), Gather(parts, block)],
        [out_terms.reshape((parts,) + block), cotangent],
        "out",
        3,
        line,
    )
    cot_full = cot_full.reshape(length, width)
    residual = inputs + attn_out
    normed_mid, root_mid = normalize(residual)
    (normed_mid_full,) = call([Gather(parts, block)], [normed_mid.astype(LOW)], "mid", 4, line)
    normed_mid_full = normed_mid_full.reshape(length, width)

    gate_up = dot(normed_mid_full, gate_up_cols)
    units = gate_up.shape[1] // 2
    gate_part = gate_up[:, :units]
    up_part = gate_up[:, units:]
    sigmoid_gate = jax.nn.sigmoid(gate_part)
    silu_gate = gate_part * sigmoid_gate
    activated = (silu_gate * up_part).astype(LOW)
    act_grad = times_transposed(cot_full, down_rows)
    gate_grad = act_grad * up_part * sigmoid_gate * (1.0 + gate_part * (1.0 - sigmoid_gate))
    up_grad = act_grad * silu_gate
    gate_up_back = jnp.concatenate([gate_grad, up_grad], axis=1).astype(LOW)
    mid_back_terms = times_transposed(gate_up_back, gate_up_cols).astype(LOW)
    mid_back, gate_up_grad, down_grad = call(
        [Scatter(parts, block)],
        [mid_back_terms.reshape((parts,) + block)],
        "mid_back",
        5,
        line,
        Grads([(normed_mid_full, gate_up_back), (activated, cot_full)]),
    )
    gate_up_grad = scatter(gate_up_grad, "fsdp")
    down_grad = scatter(down_grad, "fsdp").astype(jnp.float32)
    residual_back = cotangent.astype(jnp.float32) + norm_back(mid_back, normed_mid, root_mid)
    proj_back = residual_back.astype(LOW)

    down_terms = dot(activated, down_rows).astype(LOW)
    proj_back_full, down_out = call(
        [Gather(parts, block), Scatter(parts, block)],
        [proj_back, down_terms.reshape((parts,) + block)],
        "proj_back",
        6,
        line,
    )
    layer_out = (residual + down_out).astype(LOW)
    proj_back_full = proj_back_full.reshape(length, width)

    back_heads = times_transposed(proj_back_full, out_cols).astype(LOW).reshape(head_shape)
    delta = jnp.einsum("qhd,qhd->hq", back_heads.astype(jnp.float32), attn_heads)
    probs = jnp.where(allowed, jnp.exp(scores - log_total[..., None]), 0.0)
    value_back = jnp.einsum(
        "hqk,qhd->khd", probs.astype(LOW), back_heads, preferred_element_type=jnp.float32
    )
    prob_back = jnp.einsum("qhd,khd->hqk", back_heads, values, preferred_element_type=jnp.float32)
    score_back = (score_scale * probs * (prob_back - delta[..., None])).astype(LOW)
    query_back = jnp.einsum("hqk,khd->qhd", score_back, keys, preferred_element_type=jnp.float32)
    key_back = jnp.einsum("hqk,qhd->khd", score_back, queries, preferred_element_type=jnp.float32)
    qkv_back = jnp.concatenate(
        [
            unrotate(query_back, cosine_table, sine_table).reshape(length, head_width),
            unrotate(key_back, cosine_table, sine_table).reshape(length, head_width),
            value_back.reshape(length, head_width),
        ],
        axis=1,
    ).astype(LOW)
    qkv_grad = scatter(column_product(normed_in_full, qkv_back).astype(LOW), "fsdp")
    in_back_terms = times_transposed(qkv_back, qkv_cols).astype(LOW)
    out_grad = column_product(mix_low, proj_back_full).astype(LOW)
    out_grad = out_grad.reshape(heads, run, shard, width).transpose(1, 0, 2, 3)
    in_back, out_grad, gate_up_grad = call(
        [
            Scatter(parts, block),
            Exchange(run, (heads * shard, width)),
            Exchange(parts, gate_up_pieces.shape[1:]),
        ],
        [
            in_back_terms.reshape((parts,) + block),
            out_grad.reshape(run, heads * shard, width),
            gate_up_grad.reshape(gate_up_pieces.shape),
        ],
        "in_back",
        7,
        line,
    )
    out_grad = scatter(out_grad.reshape(groups * shard, width), "fsdp").astype(jnp.float32)
    tokens_grad = residual_back + norm_back(in_back, normed_in, root_in)
    (qkv_grad,) = call(
        [Exchange(parts, qkv_pieces.shape[1:])],
        [qkv_grad.reshape(qkv_pieces.shape)],
        "last",
        8,
        line,
    )
    return (
        layer_out,
        tokens_grad,
        plan.qkv_rows(qkv_grad),
        out_grad,
        plan.unit_rows(gate_up_grad),
        down_grad,
    )


def solution(mesh):
    both = P(("fsdp", "ctx"), None)
    one = P("fsdp", None)
    return jax.shard_map(
        per_device,
        mesh=mesh,
        in_specs=(both, both, both, both, both, one, one, both),
        out_specs=(both,) * 6,
        check_vma=False,
    )
```

```python
import jax
import jax.numpy as jnp
from jax import lax
from jax.experimental import pallas as pl
from jax.experimental.pallas import tpu as pltpu
from jax.sharding import PartitionSpec as P

HEADS = 16
HEAD_DIM = 128
BLOCK = 128
LOW = jnp.bfloat16


def normalize(values):
    average = jnp.mean(values, axis=-1, keepdims=True)
    centered = values - average
    variance = jnp.mean(centered * centered, axis=-1, keepdims=True)
    inv_root = lax.rsqrt(variance + 1e-05)
    return (centered * inv_root, inv_root)


def norm_back(upstream, normed, inv_root):
    first_mean = jnp.mean(upstream, axis=-1, keepdims=True)
    second_mean = jnp.mean(upstream * normed, axis=-1, keepdims=True)
    return inv_root * (upstream - first_mean - normed * second_mean)


def places(token_index, lengths):
    seq_ends = jnp.cumsum(lengths)
    sequence = jnp.sum((token_index[:, None] >= seq_ends[None, :]).astype(jnp.int32), axis=1)
    before = jnp.arange(lengths.shape[0], dtype=jnp.int32)
    seq_start = jnp.sum(jnp.where(before[None, :] < sequence[:, None], lengths[None, :], 0), axis=1)
    return (sequence, token_index - seq_start)


def initial_index(row_index, order_row):
    slot_index = row_index // BLOCK
    slot_table = jnp.arange(order_row.shape[0], dtype=jnp.int32)
    picked = jnp.sum(
        jnp.where(slot_table[None, :] == slot_index[:, None], order_row[None, :], 0), axis=1
    )
    return picked * BLOCK + row_index % BLOCK


def angle_tables(position):
    half_dim = HEAD_DIM // 2
    frequency = 10000.0 ** (-jnp.arange(half_dim, dtype=jnp.float32) * 2.0 / HEAD_DIM)
    angle_table = position.astype(jnp.float32)[:, None] * frequency[None, :]
    angle_table = jnp.concatenate([angle_table, angle_table], axis=-1)
    return (jnp.cos(angle_table)[:, None, :], jnp.sin(angle_table)[:, None, :])


def rotate(values, cosine_table, sine_table):
    half_dim = values.shape[-1] // 2
    turned = jnp.concatenate([-values[..., half_dim:], values[..., :half_dim]], axis=-1)
    return values * cosine_table + turned * sine_table


def unrotate(values, cosine_table, sine_table):
    half_dim = values.shape[-1] // 2
    scaled = values * sine_table
    turned = jnp.concatenate([scaled[..., half_dim:], -scaled[..., :half_dim]], axis=-1)
    return values * cosine_table + turned


def dot(left, right):
    return jnp.dot(left, right, preferred_element_type=jnp.float32)


def times_transposed(left, right):
    return lax.dot_general(
        left, right, (((1,), (1,)), ((), ())), preferred_element_type=jnp.float32
    )


def column_product(left, right):
    return lax.dot_general(
        left, right, (((0,), (0,)), ((), ())), preferred_element_type=jnp.float32
    )


def gather(values, axes):
    return lax.all_gather(values, axes, axis=0, tiled=True)


def scatter(values, axes):
    return lax.psum_scatter(values, axes, scatter_dimension=0, tiled=True)


def enter(axes):
    barrier = pltpu.get_barrier_semaphore()
    count = 0
    for axis, size in axes:
        me = lax.axis_index(axis)
        for step in range(1, size):
            pl.semaphore_signal(barrier, inc=1, device_id={axis: lax.rem(me + step, size)})
        count += size - 1
    pl.semaphore_wait(barrier, count)


def remote(src, dst, send, recv, axis, peer):
    return pltpu.make_async_remote_copy(
        src_ref=src, dst_ref=dst, send_sem=send, recv_sem=recv, device_id={axis: peer}
    )


class Exchange:
    def __init__(self, parts, shape):
        self.parts = parts
        self.out = jax.ShapeDtypeStruct((parts,) + shape, LOW)
        self.scratch = [
            pltpu.SemaphoreType.DMA((parts - 1,)),
            pltpu.SemaphoreType.DMA((parts - 1,)),
            pltpu.SemaphoreType.DMA,
        ]

    def run(self, src, dst, send, recv, local):
        place = lax.axis_index("ctx")
        me = lax.rem(place, self.parts)
        copies = []
        for step in range(1, self.parts):
            peer = lax.rem(me + step, self.parts)
            copies.append(
                remote(
                    src.at[peer],
                    dst.at[me],
                    send.at[step - 1],
                    recv.at[step - 1],
                    "ctx",
                    place - me + peer,
                )
            )
            copies[-1].start()
        own = pltpu.make_async_copy(src.at[me], dst.at[me], local)
        own.start()
        yield
        for copy in copies:
            copy.wait()
            yield
        own.wait()


class Gather:
    def __init__(self, parts, shape):
        self.parts = parts
        self.out = jax.ShapeDtypeStruct((parts,) + shape, LOW)
        chips = parts // 2
        self.scratch = [
            pltpu.SemaphoreType.DMA((2, chips)),
            pltpu.SemaphoreType.DMA((chips,)),
            pltpu.SemaphoreType.DMA((chips,)),
            pltpu.SemaphoreType.DMA((chips,)),
            pltpu.SemaphoreType.DMA,
        ]

    def run(self, src, dst, send, recv, pair_send, pair_recv, local):
        chips = self.parts // 2
        me = lax.axis_index("ctx")
        chip, core = me // 2, lax.rem(me, 2)
        partner = me + 1 - 2 * core

        def line(block, slot, origin, way):
            return remote(
                block, slot, send.at[way, origin], recv.at[origin], "ctx", me + 2 - 4 * way
            )

        def across(block, slot, origin):
            return remote(block, slot, pair_send.at[origin], pair_recv.at[origin], "ctx", partner)

        mine = dst.at[me]

        @pl.when(chip < chips - 1)
        def _():
            line(src, mine, chip, 0).start()

        @pl.when(chip > 0)
        def _():
            line(src, mine, chip, 1).start()

        across(src, mine, chip).start()
        own = pltpu.make_async_copy(src, mine, local)
        own.start()
        yield
        for step in range(1, chips):
            for way in range(2):
                origin = chip - step if way == 0 else chip + step

                @pl.when((origin >= 0) & (origin < chips))
                def _():
                    slot = dst.at[2 * origin + core]
                    line(slot, slot, origin, way).wait_recv()

                    @pl.when((chip < chips - 1) if way == 0 else (chip > 0))
                    def _():
                        line(slot, slot, origin, way).start()

                    across(slot, slot, origin).start()

            yield
        for step in range(chips):
            for way in range(2):
                origin = chip - step if way == 0 else chip + step
                ahead = (chip < chips - 1) if way == 0 else (chip > 0)

                @pl.when((origin >= 0) & (origin < chips) & ahead)
                def _():
                    slot = dst.at[2 * origin + core]
                    line(slot, slot, origin, way).wait_send()

        for origin in range(chips):
            across(dst.at[2 * origin + core], dst.at[2 * origin + core], origin).wait_send()
            other = dst.at[2 * origin + 1 - core]
            across(other, other, origin).wait_recv()
        own.wait()


class Scatter:
    cuts = 2

    def __init__(self, parts, shape):
        self.parts, self.shape = parts, shape
        self.out = jax.ShapeDtypeStruct(shape, jnp.float32)
        chips = parts // 2
        piece = (self.cuts, shape[0] // self.cuts, shape[1])
        self.scratch = [
            pltpu.VMEM((chips,) + shape, LOW),
            pltpu.VMEM((2, chips) + piece, LOW),
            pltpu.VMEM((chips,) + piece, LOW),
            pltpu.SemaphoreType.DMA((chips,)),
            pltpu.SemaphoreType.DMA((chips,)),
            pltpu.SemaphoreType.DMA((chips, self.cuts)),
            pltpu.SemaphoreType.DMA((2, chips, self.cuts)),
        ]

    def run(self, src, out, pair, come, stage, pair_send, pair_recv, send, recv):
        chips, cuts = self.parts // 2, self.cuts
        me = lax.axis_index("ctx")
        chip, core = me // 2, lax.rem(me, 2)
        partner = me + 1 - 2 * core
        rows = self.shape[0] // cuts
        slab = min(rows, 16)
        last = chips - 1

        def across(goal):
            return remote(
                src.at[2 * goal + 1 - core],
                pair.at[goal],
                pair_send.at[goal],
                pair_recv.at[goal],
                "ctx",
                partner,
            )

        def line(goal, cut, way):
            return remote(
                stage.at[goal, cut],
                come.at[way, goal, cut],
                send.at[goal, cut],
                recv.at[way, goal, cut],
                "ctx",
                me + 2 - 4 * way,
            )

        def wide(ref, *index):
            return ref[index].astype(jnp.float32)

        def slabs(part):
            def one(index, carry):
                part(pl.multiple_of(index * slab, slab))
                return carry

            lax.fori_loop(0, rows // slab, one, 0)

        def both(goal, cut, at):
            at = pl.ds(cut * rows + at, slab)
            return wide(src, 2 * goal + core, at) + wide(pair, goal, at)

        order = []
        for step in range((chips + 1) // 2):
            order += sorted({step, last - step})
        for goal in order:
            across(goal).start()
        yield
        for step in range(last * cuts):
            for way in range(2):
                turn = step - (chip if way == 0 else last - chip)
                goal = (last - turn // cuts) if way == 0 else turn // cuts
                cut = step - (chip if way == 0 else last - chip) - (turn // cuts) * cuts
                first = (chip == 0) if way == 0 else (chip == last)
                ahead = last - chip if way == 0 else chip

                def begin(at):
                    value = both(goal, cut, at)
                    stage[goal, cut, pl.ds(at, slab), :] = value.astype(LOW)

                def middle(at):
                    value = both(goal, cut, at) + wide(come, way, goal, cut, pl.ds(at, slab))
                    stage[goal, cut, pl.ds(at, slab), :] = value.astype(LOW)

                @pl.when((turn >= 0) & (turn < ahead * cuts))
                def _():
                    @pl.when(cut == 0)
                    def _():
                        across(goal).wait_recv()

                    @pl.when(first)
                    def _():
                        slabs(begin)

                    @pl.when(jnp.logical_not(first))
                    def _():
                        line(goal, cut, way).wait_recv()
                        slabs(middle)

                    line(goal, cut, way).start()

            yield
        across(chip).wait_recv()
        for cut in range(cuts):

            def own(at):
                out[pl.ds(cut * rows + at, slab), :] = both(chip, cut, at)

            slabs(own)
        yield
        for cut in range(cuts):
            for way in range(2):

                def final(at):
                    out[pl.ds(cut * rows + at, slab), :] += wide(
                        come, way, chip, cut, pl.ds(at, slab)
                    )

                @pl.when((chip > 0) if way == 0 else (chip < last))
                def _():
                    line(chip, cut, way).wait_recv()
                    slabs(final)

            yield
        for goal in range(chips):
            across(goal).wait_send()

            @pl.when(chip != goal)
            def _():
                for cut in range(cuts):
                    line(goal, cut, 0).wait_send()


class Spread:
    def __init__(self, parts, groups, shape):
        self.parts, self.groups = parts, groups
        self.out = jax.ShapeDtypeStruct((groups, parts) + shape, LOW)
        self.scratch = [
            pltpu.SemaphoreType.DMA((parts - 1,)),
            pltpu.SemaphoreType.DMA((parts - 1,)),
            pltpu.SemaphoreType.DMA((groups - 1, parts)),
            pltpu.SemaphoreType.DMA((groups - 1, parts)),
            pltpu.SemaphoreType.DMA,
        ]

    def run(self, src, dst, send, recv, far_send, far_recv, local):
        parts, groups = self.parts, self.groups
        me, group = lax.axis_index("ctx"), lax.axis_index("fsdp")
        copies = []
        for step in range(1, parts):
            peer = lax.rem(me + step, parts)
            copies.append(
                remote(
                    src.at[peer],
                    dst.at[group, me],
                    send.at[step - 1],
                    recv.at[step - 1],
                    "ctx",
                    peer,
                )
            )
            copies[-1].start()
        own = pltpu.make_async_copy(src.at[me], dst.at[group, me], local)
        own.start()

        def pass_on(block, origin, step):
            out = []
            for hop in range(1, groups):
                copy = remote(
                    block,
                    dst.at[group, origin],
                    far_send.at[hop - 1, step],
                    far_recv.at[hop - 1, step],
                    "fsdp",
                    lax.rem(group + hop, groups),
                )
                copy.start()
                out.append(copy)
            return out

        far = pass_on(src.at[me], me, 0)
        eager = -(-parts // 2)
        yield
        for step in range(1, parts):
            copies[step - 1].wait_recv()
            origin = lax.rem(me - step + parts, parts)
            far += pass_on(dst.at[group, origin], origin, step)
            if step % eager == 0:
                yield
        for at, copy in enumerate(far):
            copy.wait()
            if at % 6 == 5:
                yield
        for copy in copies:
            copy.wait_send()
        own.wait()


class Deliver:
    def __init__(self, parts, shape, offsets):
        self.parts, self.shape, self.offsets = parts, shape, offsets
        self.out = jax.ShapeDtypeStruct((shape[0], parts * shape[1]), jnp.float32)
        self.scratch = [
            pltpu.VMEM((parts - 1,) + shape, LOW),
            pltpu.SemaphoreType.DMA((parts - 1,)),
            pltpu.SemaphoreType.DMA((parts - 1,)),
        ]

    def place(self, out, origin, read):
        starts = self.offsets(origin)
        step = self.shape[1] // len(starts)
        for index, start in enumerate(starts):
            out[:, pl.ds(pl.multiple_of(start, HEAD_DIM), step)] = read(
                index * step, (index + 1) * step
            )

    def send(self, me, step, block, came, send, recv):
        return remote(
            block,
            came.at[step - 1],
            send.at[step - 1],
            recv.at[step - 1],
            "ctx",
            lax.rem(me + step, self.parts),
        )

    def run(self, src, out, came, send, recv):
        me = lax.axis_index("ctx")
        copies = []
        for step in range(1, self.parts):
            block = src.at[lax.rem(me + step, self.parts)]
            copies.append(self.send(me, step, block, came, send, recv))
            copies[-1].start()
        self.place(out, me, lambda lo, hi: src[me, :, lo:hi].astype(jnp.float32))
        yield
        yield from self.finish(me, out, copies, came)

    def finish(self, me, out, copies, came):
        for step in range(1, self.parts):
            copies[step - 1].wait_recv()
            origin = lax.rem(me - step + self.parts, self.parts)
            self.place(out, origin, lambda lo, hi: came[step - 1, :, lo:hi].astype(jnp.float32))
            yield
        for copy in copies:
            copy.wait_send()


class Collect(Deliver):
    def __init__(self, parts, groups, shape, offsets):
        super().__init__(parts, shape, offsets)
        self.groups = groups
        self.scratch = self.scratch + [
            pltpu.VMEM((groups - 1, parts) + shape, LOW),
            pltpu.VMEM((parts,) + shape, LOW),
            pltpu.VMEM(shape, jnp.float32),
            pltpu.SemaphoreType.DMA((groups - 1, parts)),
            pltpu.SemaphoreType.DMA((groups - 1, parts)),
        ]

    def run(self, src, out, came, send, recv, far, stage, mine, far_send, far_recv):
        parts, groups = self.parts, self.groups
        me, group = lax.axis_index("ctx"), lax.axis_index("fsdp")
        goals = [lax.rem(me + step, parts) for step in range(1, parts + 1)]
        hops = []
        for goal in goals:
            for hop in range(1, groups):
                peer = lax.rem(group + hop, groups)
                hops.append(
                    remote(
                        src.at[peer, goal],
                        far.at[hop - 1, goal],
                        far_send.at[hop - 1, goal],
                        far_recv.at[hop - 1, goal],
                        "fsdp",
                        peer,
                    )
                )
                hops[-1].start()
        yield
        copies = []
        for step in range(1, parts + 1):
            goal = goals[step - 1]
            for copy in hops[(step - 1) * (groups - 1) : step * (groups - 1)]:
                copy.wait_recv()
            value = src[group, goal].astype(jnp.float32)
            for hop in range(groups - 1):
                value += far[hop, goal].astype(jnp.float32)
            if step < parts:
                stage[goal] = value.astype(LOW)
                copies.append(self.send(me, step, stage.at[goal], came, send, recv))
                copies[-1].start()
            else:
                mine[...] = value
            yield
        self.place(out, me, lambda lo, hi: mine[:, lo:hi])
        yield from self.finish(me, out, copies, came)
        for copy in hops:
            copy.wait_send()


def call(jobs, operands, name, identity, axes, work=None):
    counts = [len(job.scratch) for job in jobs]
    jobs_n = len(jobs)
    extra = work.operands if work else []
    extra_out = work.outs if work else []
    extra_scratch = work.scratch if work else []

    def kernel(*refs):
        refs = list(refs)

        def take(count):
            taken = refs[:count]
            del refs[:count]
            return taken

        ins, more = take(jobs_n), take(len(extra))
        outs, more_outs = take(jobs_n), take(len(extra_out))
        runs = []
        for job, src, dst, count in zip(jobs, ins, outs, counts):
            runs.append(job.run(src, dst, *take(count)))
        if work:
            runs.append(work.run(*more, *more_outs, *refs))
        enter(axes)
        while runs:
            going = []
            for run in runs:
                try:
                    next(run)
                    going.append(run)
                except StopIteration:
                    pass
            runs = going

    vmem = pl.BlockSpec(memory_space=pltpu.VMEM)
    anywhere = pl.BlockSpec(memory_space=pl.ANY)
    return pl.pallas_call(
        kernel,
        out_shape=tuple(job.out for job in jobs) + tuple(extra_out),
        in_specs=[vmem] * jobs_n + [anywhere] * len(extra),
        out_specs=(vmem,) * jobs_n + (anywhere,) * len(extra_out),
        scratch_shapes=[shape for job in jobs for shape in job.scratch] + list(extra_scratch),
        compiler_params=pltpu.CompilerParams(
            collective_id=identity, has_side_effects=True, vmem_limit_bytes=62 << 20
        ),
        name=name,
    )(*operands, *extra)


class Grads:
    tile = 256

    def __init__(self, pairs):
        self.pairs = pairs
        length, wide = pairs[0][0].shape[0], max(right.shape[1] for _, right in pairs)
        self.operands = [array for pair in pairs for array in pair]
        self.outs = [jax.ShapeDtypeStruct((l.shape[1], r.shape[1]), LOW) for l, r in pairs]
        self.scratch = [pltpu.VMEM(array.shape, LOW) for array in self.operands]
        self.scratch += [
            pltpu.VMEM((self.tile, length), LOW),
            pltpu.VMEM((2, self.tile, wide), LOW),
            pltpu.SemaphoreType.DMA((2 * len(pairs),)),
            pltpu.SemaphoreType.DMA((2,)),
        ]

    def run(self, *refs):
        n, tile = len(self.pairs), self.tile
        sources, outs = refs[: 2 * n], refs[2 * n : 3 * n]
        held = refs[3 * n : 5 * n]
        turned, made, get, put = refs[5 * n :]
        gets = [pltpu.make_async_copy(s, h, get.at[i]) for i, (s, h) in enumerate(zip(sources, held))]
        for copy in gets:
            copy.start()
        yield
        puts = []
        for which in range(n):
            left, right, out = held[2 * which], held[2 * which + 1], outs[which]
            gets[2 * which].wait()
            gets[2 * which + 1].wait()
            columns = right.shape[1]
            step = min(columns, 512)
            for at in range(0, left.shape[1], tile):
                slot = len(puts) % 2
                if len(puts) >= 2:
                    puts[-2].wait()
                turned[...] = left[:, at : at + tile].T

                def one(index, carry):
                    where = pl.ds(pl.multiple_of(index * step, step), step)
                    made[slot, :, where] = jnp.dot(
                        turned[...], right[:, where], preferred_element_type=jnp.float32
                    ).astype(LOW)
                    return carry

                lax.fori_loop(0, columns // step, one, 0)
                part = made.at[slot] if columns == made.shape[2] else made.at[slot, :, :columns]
                puts.append(pltpu.make_async_copy(part, out.at[at : at + tile, :], put.at[slot]))
                puts[-1].start()
                yield
        for copy in puts[-2:]:
            copy.wait()


class Plan:
    def __init__(self, parts, groups, width):
        self.parts, self.groups = parts, groups
        self.shard = width // (parts * groups)
        self.run = HEAD_DIM // self.shard
        self.heads = HEADS // parts
        self.qkv_dims = (3, self.run, self.heads, parts // self.run, HEAD_DIM)

    def qkv_pieces(self, weight):
        rows = weight.shape[0]
        pieces = weight.reshape((rows,) + self.qkv_dims).transpose(4, 2, 0, 1, 3, 5)
        return pieces.reshape(self.parts, rows, 3 * self.heads * HEAD_DIM)

    def qkv_starts(self, part):
        at, index = part // self.run, lax.rem(part, self.run)
        return [
            (kind * HEADS + (index * self.heads + head) * (self.parts // self.run) + at) * HEAD_DIM
            for kind in range(3)
            for head in range(self.heads)
        ]

    def unit_pieces(self, weight):
        rows, columns = weight.shape
        inner = columns // (2 * self.groups * self.parts)
        pieces = weight.reshape(rows, 2 * self.groups, self.parts, inner).transpose(2, 0, 1, 3)
        return pieces.reshape(self.parts, rows, 2 * self.groups * inner)

    def unit_job(self, shape):
        step = shape[1] // (2 * self.groups)
        if step % HEAD_DIM:
            return Exchange(self.parts, shape)
        return Deliver(
            self.parts,
            shape,
            lambda part: [(at * self.parts + part) * step for at in range(2 * self.groups)],
        )

    def unit_rows(self, pieces):
        if pieces.ndim == 2:
            return pieces
        parts, rows, columns = pieces.shape
        outer = 2 * self.groups
        pieces = pieces.reshape(parts, rows, outer, columns // outer).transpose(1, 2, 0, 3)
        return pieces.reshape(rows, parts * columns).astype(jnp.float32)


def per_device(tokens, w_qkv, w_out, w_gate_up, w_down, seq_lengths, block_order, cotangent):
    lengths = seq_lengths[0]
    order_row = block_order[0]
    parts = lax.axis_size("ctx")
    groups = lax.axis_size("fsdp")
    rows, width = tokens.shape
    length = rows * parts
    plan = Plan(parts, groups, width)
    heads, shard, run = plan.heads, plan.shard, plan.run
    head_width = heads * HEAD_DIM
    score_scale = HEAD_DIM ** (-0.5)
    line = (("ctx", parts),)
    plane = (("ctx", parts), ("fsdp", groups))
    block = (rows, width)

    out_rows = gather(w_out, "fsdp")
    down_rows = gather(w_down, "fsdp")
    gate_up_pieces = plan.unit_pieces(w_gate_up)
    inputs = tokens.astype(jnp.float32)
    normed_in, root_in = normalize(inputs)
    qkv_pieces = plan.qkv_pieces(w_qkv)
    qkv_cols, normed_in_full, gate_up_cols = call(
        [
            Spread(parts, groups, qkv_pieces.shape[1:]),
            Gather(parts, block),
            Exchange(parts, gate_up_pieces.shape[1:]),
        ],
        [qkv_pieces, normed_in.astype(LOW), gate_up_pieces],
        "start",
        2,
        plane,
    )
    gate_up_cols, down_rows, out_rows = lax.optimization_barrier(
        (gate_up_cols, down_rows, out_rows)
    )
    gate_up_cols = gather(gate_up_cols.reshape(width // groups, -1), "fsdp")
    (out_cols,) = call(
        [Exchange(run, (heads * shard, width))],
        [out_rows.reshape(run, heads * shard, width)],
        "swap",
        1,
        line,
    )
    qkv_cols = qkv_cols.reshape(width, 3 * head_width)
    normed_in_full = normed_in_full.reshape(length, width)
    out_cols = out_cols.reshape(run, heads, shard, width).transpose(1, 0, 2, 3)
    out_cols = out_cols.reshape(head_width, width)

    row_index = jnp.arange(length, dtype=jnp.int32)
    seq, pos = places(initial_index(row_index, order_row), lengths)
    cosine_table, sine_table = angle_tables(pos)
    allowed = ((seq[:, None] == seq[None, :]) & (pos[None, :] <= pos[:, None]))[None]

    qkv = dot(normed_in_full, qkv_cols)
    head_shape = (length, heads, HEAD_DIM)
    queries = rotate(qkv[:, :head_width].reshape(head_shape), cosine_table, sine_table).astype(LOW)
    keys = rotate(
        qkv[:, head_width : 2 * head_width].reshape(head_shape), cosine_table, sine_table
    ).astype(LOW)
    values = qkv[:, 2 * head_width :].astype(LOW).reshape(head_shape)
    scores = jnp.einsum("qhd,khd->hqk", queries, keys, preferred_element_type=jnp.float32)
    scores = jnp.where(allowed, scores * score_scale, -1e30)
    row_max = jnp.max(scores, axis=-1)
    weights = jnp.where(allowed, jnp.exp(scores - row_max[..., None]), 0.0)
    row_total = jnp.sum(weights, axis=-1)
    mixed = jnp.einsum("hqk,khd->qhd", weights.astype(LOW), values, preferred_element_type=jnp.float32)
    log_total = row_max + jnp.log(row_total)
    attn_heads = mixed / jnp.transpose(row_total)[..., None]
    mix_low = attn_heads.astype(LOW).reshape(length, head_width)

    out_terms = dot(mix_low, out_cols).astype(LOW)
    attn_out, cot_full = call(
        [Scatter(parts, block), Gather(parts, block)],
        [out_terms.reshape((parts,) + block), cotangent],
        "out",
        3,
        line,
    )
    cot_full = cot_full.reshape(length, width)
    residual = inputs + attn_out
    normed_mid, root_mid = normalize(residual)
    (normed_mid_full,) = call([Gather(parts, block)], [normed_mid.astype(LOW)], "mid", 4, line)
    normed_mid_full = normed_mid_full.reshape(length, width)

    gate_up = dot(normed_mid_full, gate_up_cols)
    units = gate_up.shape[1] // 2
    gate_part = gate_up[:, :units]
    up_part = gate_up[:, units:]
    sigmoid_gate = jax.nn.sigmoid(gate_part)
    silu_gate = gate_part * sigmoid_gate
    activated = (silu_gate * up_part).astype(LOW)
    act_grad = times_transposed(cot_full, down_rows)
    gate_grad = act_grad * up_part * sigmoid_gate * (1.0 + gate_part * (1.0 - sigmoid_gate))
    up_grad = act_grad * silu_gate
    gate_up_back = jnp.concatenate([gate_grad, up_grad], axis=1).astype(LOW)
    down_grad = scatter(column_product(activated, cot_full).astype(LOW), "fsdp").astype(jnp.float32)
    mid_back_terms = times_transposed(gate_up_back, gate_up_cols).astype(LOW)
    mid_back, gate_up_grad = call(
        [Scatter(parts, block)],
        [mid_back_terms.reshape((parts,) + block)],
        "mid_back",
        5,
        line,
        Grads([(normed_mid_full, gate_up_back)]),
    )
    gate_up_grad = scatter(gate_up_grad, "fsdp")
    residual_back = cotangent.astype(jnp.float32) + norm_back(mid_back, normed_mid, root_mid)
    proj_back = residual_back.astype(LOW)

    down_terms = dot(activated, down_rows).astype(LOW)
    proj_back_full, down_out = call(
        [Gather(parts, block), Scatter(parts, block)],
        [proj_back, down_terms.reshape((parts,) + block)],
        "proj_back",
        6,
        line,
    )
    layer_out = (residual + down_out).astype(LOW)
    proj_back_full = proj_back_full.reshape(length, width)

    out_grad = column_product(mix_low, proj_back_full).astype(LOW)
    out_grad = out_grad.reshape(heads, run, shard, width).transpose(1, 0, 2, 3)
    (out_grad,) = call(
        [Exchange(run, (heads * shard, width))],
        [out_grad.reshape(run, heads * shard, width)],
        "swap_back",
        8,
        line,
    )
    out_grad = scatter(out_grad.reshape(groups * shard, width), "fsdp").astype(jnp.float32)
    back_heads = times_transposed(proj_back_full, out_cols).astype(LOW).reshape(head_shape)
    delta = jnp.einsum("qhd,qhd->hq", back_heads.astype(jnp.float32), attn_heads)
    probs = jnp.where(allowed, jnp.exp(scores - log_total[..., None]), 0.0)
    value_back = jnp.einsum(
        "hqk,qhd->khd", probs.astype(LOW), back_heads, preferred_element_type=jnp.float32
    )
    prob_back = jnp.einsum("qhd,khd->hqk", back_heads, values, preferred_element_type=jnp.float32)
    score_back = (score_scale * probs * (prob_back - delta[..., None])).astype(LOW)
    query_back = jnp.einsum("hqk,khd->qhd", score_back, keys, preferred_element_type=jnp.float32)
    key_back = jnp.einsum("hqk,qhd->khd", score_back, queries, preferred_element_type=jnp.float32)
    qkv_back = jnp.concatenate(
        [
            unrotate(query_back, cosine_table, sine_table).reshape(length, head_width),
            unrotate(key_back, cosine_table, sine_table).reshape(length, head_width),
            value_back.reshape(length, head_width),
        ],
        axis=1,
    ).astype(LOW)
    qkv_grad = column_product(normed_in_full, qkv_back).astype(LOW)
    in_back_terms = times_transposed(qkv_back, qkv_cols).astype(LOW)
    in_back, qkv_grad, gate_up_grad = call(
        [
            Scatter(parts, block),
            Collect(parts, groups, qkv_pieces.shape[1:], plan.qkv_starts),
            plan.unit_job(gate_up_pieces.shape[1:]),
        ],
        [
            in_back_terms.reshape((parts,) + block),
            qkv_grad.reshape((groups,) + qkv_pieces.shape),
            gate_up_grad.reshape(gate_up_pieces.shape),
        ],
        "in_back",
        7,
        plane,
    )
    tokens_grad = residual_back + norm_back(in_back, normed_in, root_in)
    return (
        layer_out,
        tokens_grad,
        qkv_grad,
        out_grad,
        plan.unit_rows(gate_up_grad),
        down_grad,
    )


def solution(mesh):
    both = P(("fsdp", "ctx"), None)
    one = P("fsdp", None)
    return jax.shard_map(
        per_device,
        mesh=mesh,
        in_specs=(both, both, both, both, both, one, one, both),
        out_specs=(both,) * 6,
        check_vma=False,
    )
```

```python
import jax
import jax.numpy as jnp
from jax import lax
from jax.experimental import pallas as pl
from jax.experimental.pallas import tpu as pltpu
from jax.sharding import PartitionSpec as P

HEADS = 16
HEAD_DIM = 128
BLOCK = 128
LOW = jnp.bfloat16


def normalize(values):
    average = jnp.mean(values, axis=-1, keepdims=True)
    centered = values - average
    variance = jnp.mean(centered * centered, axis=-1, keepdims=True)
    inv_root = lax.rsqrt(variance + 1e-05)
    return (centered * inv_root, inv_root)


def norm_back(upstream, normed, inv_root):
    first_mean = jnp.mean(upstream, axis=-1, keepdims=True)
    second_mean = jnp.mean(upstream * normed, axis=-1, keepdims=True)
    return inv_root * (upstream - first_mean - normed * second_mean)


def places(token_index, lengths):
    seq_ends = jnp.cumsum(lengths)
    sequence = jnp.sum((token_index[:, None] >= seq_ends[None, :]).astype(jnp.int32), axis=1)
    before = jnp.arange(lengths.shape[0], dtype=jnp.int32)
    seq_start = jnp.sum(jnp.where(before[None, :] < sequence[:, None], lengths[None, :], 0), axis=1)
    return (sequence, token_index - seq_start)


def initial_index(row_index, order_row):
    slot_index = row_index // BLOCK
    slot_table = jnp.arange(order_row.shape[0], dtype=jnp.int32)
    picked = jnp.sum(
        jnp.where(slot_table[None, :] == slot_index[:, None], order_row[None, :], 0), axis=1
    )
    return picked * BLOCK + row_index % BLOCK


def angle_tables(position):
    half_dim = HEAD_DIM // 2
    frequency = 10000.0 ** (-jnp.arange(half_dim, dtype=jnp.float32) * 2.0 / HEAD_DIM)
    angle_table = position.astype(jnp.float32)[:, None] * frequency[None, :]
    angle_table = jnp.concatenate([angle_table, angle_table], axis=-1)
    return (jnp.cos(angle_table)[:, None, :], jnp.sin(angle_table)[:, None, :])


def rotate(values, cosine_table, sine_table):
    half_dim = values.shape[-1] // 2
    turned = jnp.concatenate([-values[..., half_dim:], values[..., :half_dim]], axis=-1)
    return values * cosine_table + turned * sine_table


def unrotate(values, cosine_table, sine_table):
    half_dim = values.shape[-1] // 2
    scaled = values * sine_table
    turned = jnp.concatenate([scaled[..., half_dim:], -scaled[..., :half_dim]], axis=-1)
    return values * cosine_table + turned


def dot(left, right):
    return jnp.dot(left, right, preferred_element_type=jnp.float32)


def times_transposed(left, right):
    return lax.dot_general(
        left, right, (((1,), (1,)), ((), ())), preferred_element_type=jnp.float32
    )


def column_product(left, right):
    return lax.dot_general(
        left, right, (((0,), (0,)), ((), ())), preferred_element_type=jnp.float32
    )


def gather(values, axes):
    return lax.all_gather(values, axes, axis=0, tiled=True)


def scatter(values, axes):
    return lax.psum_scatter(values, axes, scatter_dimension=0, tiled=True)


def enter(axes):
    barrier = pltpu.get_barrier_semaphore()
    count = 0
    for axis, size in axes:
        me = lax.axis_index(axis)
        for step in range(1, size):
            pl.semaphore_signal(barrier, inc=1, device_id={axis: lax.rem(me + step, size)})
        count += size - 1
    pl.semaphore_wait(barrier, count)


def remote(src, dst, send, recv, axis, peer):
    return pltpu.make_async_remote_copy(
        src_ref=src, dst_ref=dst, send_sem=send, recv_sem=recv, device_id={axis: peer}
    )


class Exchange:
    def __init__(self, parts, shape):
        self.parts = parts
        self.out = jax.ShapeDtypeStruct((parts,) + shape, LOW)
        self.scratch = [
            pltpu.SemaphoreType.DMA((parts - 1,)),
            pltpu.SemaphoreType.DMA((parts - 1,)),
            pltpu.SemaphoreType.DMA,
        ]

    def run(self, src, dst, send, recv, local):
        place = lax.axis_index("ctx")
        me = lax.rem(place, self.parts)
        copies = []
        for step in range(1, self.parts):
            peer = lax.rem(me + step, self.parts)
            copies.append(
                remote(
                    src.at[peer],
                    dst.at[me],
                    send.at[step - 1],
                    recv.at[step - 1],
                    "ctx",
                    place - me + peer,
                )
            )
            copies[-1].start()
        own = pltpu.make_async_copy(src.at[me], dst.at[me], local)
        own.start()
        yield
        for copy in copies:
            copy.wait()
            yield
        own.wait()


class Gather:
    def __init__(self, parts, shape):
        self.parts = parts
        self.out = jax.ShapeDtypeStruct((parts,) + shape, LOW)
        chips = parts // 2
        self.scratch = [
            pltpu.SemaphoreType.DMA((2, chips)),
            pltpu.SemaphoreType.DMA((chips,)),
            pltpu.SemaphoreType.DMA((chips,)),
            pltpu.SemaphoreType.DMA((chips,)),
            pltpu.SemaphoreType.DMA,
        ]

    def run(self, src, dst, send, recv, pair_send, pair_recv, local):
        chips = self.parts // 2
        me = lax.axis_index("ctx")
        chip, core = me // 2, lax.rem(me, 2)
        partner = me + 1 - 2 * core

        def line(block, slot, origin, way):
            return remote(
                block, slot, send.at[way, origin], recv.at[origin], "ctx", me + 2 - 4 * way
            )

        def across(block, slot, origin):
            return remote(block, slot, pair_send.at[origin], pair_recv.at[origin], "ctx", partner)

        mine = dst.at[me]

        @pl.when(chip < chips - 1)
        def _():
            line(src, mine, chip, 0).start()

        @pl.when(chip > 0)
        def _():
            line(src, mine, chip, 1).start()

        across(src, mine, chip).start()
        own = pltpu.make_async_copy(src, mine, local)
        own.start()
        yield
        for step in range(1, chips):
            for way in range(2):
                origin = chip - step if way == 0 else chip + step

                @pl.when((origin >= 0) & (origin < chips))
                def _():
                    slot = dst.at[2 * origin + core]
                    line(slot, slot, origin, way).wait_recv()

                    @pl.when((chip < chips - 1) if way == 0 else (chip > 0))
                    def _():
                        line(slot, slot, origin, way).start()

                    across(slot, slot, origin).start()

            yield
        for step in range(chips):
            for way in range(2):
                origin = chip - step if way == 0 else chip + step
                ahead = (chip < chips - 1) if way == 0 else (chip > 0)

                @pl.when((origin >= 0) & (origin < chips) & ahead)
                def _():
                    slot = dst.at[2 * origin + core]
                    line(slot, slot, origin, way).wait_send()

        for origin in range(chips):
            across(dst.at[2 * origin + core], dst.at[2 * origin + core], origin).wait_send()
            other = dst.at[2 * origin + 1 - core]
            across(other, other, origin).wait_recv()
        own.wait()


class Scatter:
    cuts = 2

    def __init__(self, parts, shape):
        self.parts, self.shape = parts, shape
        self.out = jax.ShapeDtypeStruct(shape, jnp.float32)
        chips = parts // 2
        piece = (self.cuts, shape[0] // self.cuts, shape[1])
        self.scratch = [
            pltpu.VMEM((chips,) + shape, LOW),
            pltpu.VMEM((2, chips) + piece, LOW),
            pltpu.VMEM((chips,) + piece, LOW),
            pltpu.SemaphoreType.DMA((chips,)),
            pltpu.SemaphoreType.DMA((chips,)),
            pltpu.SemaphoreType.DMA((chips, self.cuts)),
            pltpu.SemaphoreType.DMA((2, chips, self.cuts)),
        ]

    def run(self, src, out, pair, come, stage, pair_send, pair_recv, send, recv):
        chips, cuts = self.parts // 2, self.cuts
        me = lax.axis_index("ctx")
        chip, core = me // 2, lax.rem(me, 2)
        partner = me + 1 - 2 * core
        rows = self.shape[0] // cuts
        slab = min(rows, 16)
        last = chips - 1

        def across(goal):
            return remote(
                src.at[2 * goal + 1 - core],
                pair.at[goal],
                pair_send.at[goal],
                pair_recv.at[goal],
                "ctx",
                partner,
            )

        def line(goal, cut, way):
            return remote(
                stage.at[goal, cut],
                come.at[way, goal, cut],
                send.at[goal, cut],
                recv.at[way, goal, cut],
                "ctx",
                me + 2 - 4 * way,
            )

        def wide(ref, *index):
            return ref[index].astype(jnp.float32)

        def slabs(part):
            def one(index, carry):
                part(pl.multiple_of(index * slab, slab))
                return carry

            lax.fori_loop(0, rows // slab, one, 0)

        def both(goal, cut, at):
            at = pl.ds(cut * rows + at, slab)
            return wide(src, 2 * goal + core, at) + wide(pair, goal, at)

        order = []
        for step in range((chips + 1) // 2):
            order += sorted({step, last - step})
        for goal in order:
            across(goal).start()
        yield
        for step in range(last * cuts):
            for way in range(2):
                turn = step - (chip if way == 0 else last - chip)
                goal = (last - turn // cuts) if way == 0 else turn // cuts
                cut = step - (chip if way == 0 else last - chip) - (turn // cuts) * cuts
                first = (chip == 0) if way == 0 else (chip == last)
                ahead = last - chip if way == 0 else chip

                def begin(at):
                    value = both(goal, cut, at)
                    stage[goal, cut, pl.ds(at, slab), :] = value.astype(LOW)

                def middle(at):
                    value = both(goal, cut, at) + wide(come, way, goal, cut, pl.ds(at, slab))
                    stage[goal, cut, pl.ds(at, slab), :] = value.astype(LOW)

                @pl.when((turn >= 0) & (turn < ahead * cuts))
                def _():
                    @pl.when(cut == 0)
                    def _():
                        across(goal).wait_recv()

                    @pl.when(first)
                    def _():
                        slabs(begin)

                    @pl.when(jnp.logical_not(first))
                    def _():
                        line(goal, cut, way).wait_recv()
                        slabs(middle)

                    line(goal, cut, way).start()

            yield
        across(chip).wait_recv()
        for cut in range(cuts):

            def own(at):
                out[pl.ds(cut * rows + at, slab), :] = both(chip, cut, at)

            slabs(own)
        yield
        for cut in range(cuts):
            for way in range(2):

                def final(at):
                    out[pl.ds(cut * rows + at, slab), :] += wide(
                        come, way, chip, cut, pl.ds(at, slab)
                    )

                @pl.when((chip > 0) if way == 0 else (chip < last))
                def _():
                    line(chip, cut, way).wait_recv()
                    slabs(final)

            yield
        for goal in range(chips):
            across(goal).wait_send()

            @pl.when(chip != goal)
            def _():
                for cut in range(cuts):
                    line(goal, cut, 0).wait_send()


class Spread:
    def __init__(self, parts, groups, shape):
        self.parts, self.groups = parts, groups
        self.out = jax.ShapeDtypeStruct((groups, parts) + shape, LOW)
        self.scratch = [
            pltpu.SemaphoreType.DMA((parts - 1,)),
            pltpu.SemaphoreType.DMA((parts - 1,)),
            pltpu.SemaphoreType.DMA((groups - 1, parts)),
            pltpu.SemaphoreType.DMA((groups - 1, parts)),
            pltpu.SemaphoreType.DMA,
        ]

    def run(self, src, dst, send, recv, far_send, far_recv, local):
        parts, groups = self.parts, self.groups
        me, group = lax.axis_index("ctx"), lax.axis_index("fsdp")
        copies = []
        for step in range(1, parts):
            peer = lax.rem(me + step, parts)
            copies.append(
                remote(
                    src.at[peer],
                    dst.at[group, me],
                    send.at[step - 1],
                    recv.at[step - 1],
                    "ctx",
                    peer,
                )
            )
            copies[-1].start()
        own = pltpu.make_async_copy(src.at[me], dst.at[group, me], local)
        own.start()

        def pass_on(block, origin, step):
            out = []
            for hop in range(1, groups):
                copy = remote(
                    block,
                    dst.at[group, origin],
                    far_send.at[hop - 1, step],
                    far_recv.at[hop - 1, step],
                    "fsdp",
                    lax.rem(group + hop, groups),
                )
                copy.start()
                out.append(copy)
            return out

        far = pass_on(src.at[me], me, 0)
        eager = -(-parts // 2)
        yield
        for step in range(1, parts):
            copies[step - 1].wait_recv()
            origin = lax.rem(me - step + parts, parts)
            far += pass_on(dst.at[group, origin], origin, step)
            if step % eager == 0:
                yield
        for at, copy in enumerate(far):
            copy.wait()
            if at % 6 == 5:
                yield
        for copy in copies:
            copy.wait_send()
        own.wait()


class Deliver:
    def __init__(self, parts, shape, offsets):
        self.parts, self.shape, self.offsets = parts, shape, offsets
        self.out = jax.ShapeDtypeStruct((shape[0], parts * shape[1]), jnp.float32)
        self.scratch = [
            pltpu.VMEM((parts - 1,) + shape, LOW),
            pltpu.SemaphoreType.DMA((parts - 1,)),
            pltpu.SemaphoreType.DMA((parts - 1,)),
        ]

    def place(self, out, origin, read):
        starts = self.offsets(origin)
        step = self.shape[1] // len(starts)
        for index, start in enumerate(starts):
            out[:, pl.ds(pl.multiple_of(start, HEAD_DIM), step)] = read(
                index * step, (index + 1) * step
            )

    def send(self, me, step, block, came, send, recv):
        return remote(
            block,
            came.at[step - 1],
            send.at[step - 1],
            recv.at[step - 1],
            "ctx",
            lax.rem(me + step, self.parts),
        )

    def run(self, src, out, came, send, recv):
        me = lax.axis_index("ctx")
        copies = []
        for step in range(1, self.parts):
            block = src.at[lax.rem(me + step, self.parts)]
            copies.append(self.send(me, step, block, came, send, recv))
            copies[-1].start()
        self.place(out, me, lambda lo, hi: src[me, :, lo:hi].astype(jnp.float32))
        yield
        yield from self.finish(me, out, copies, came)

    def finish(self, me, out, copies, came):
        for step in range(1, self.parts):
            copies[step - 1].wait_recv()
            origin = lax.rem(me - step + self.parts, self.parts)
            self.place(out, origin, lambda lo, hi: came[step - 1, :, lo:hi].astype(jnp.float32))
            yield
        for copy in copies:
            copy.wait_send()


class Collect(Deliver):
    def __init__(self, parts, groups, shape, offsets):
        super().__init__(parts, shape, offsets)
        self.groups = groups
        self.scratch = self.scratch + [
            pltpu.VMEM((groups - 1, parts) + shape, LOW),
            pltpu.VMEM((parts,) + shape, LOW),
            pltpu.VMEM(shape, jnp.float32),
            pltpu.SemaphoreType.DMA((groups - 1, parts)),
            pltpu.SemaphoreType.DMA((groups - 1, parts)),
        ]

    def run(self, src, out, came, send, recv, far, stage, mine, far_send, far_recv):
        parts, groups = self.parts, self.groups
        me, group = lax.axis_index("ctx"), lax.axis_index("fsdp")
        goals = [lax.rem(me + step, parts) for step in range(1, parts + 1)]
        hops = []
        for goal in goals:
            for hop in range(1, groups):
                peer = lax.rem(group + hop, groups)
                hops.append(
                    remote(
                        src.at[peer, goal],
                        far.at[hop - 1, goal],
                        far_send.at[hop - 1, goal],
                        far_recv.at[hop - 1, goal],
                        "fsdp",
                        peer,
                    )
                )
                hops[-1].start()
        yield
        copies = []
        for step in range(1, parts + 1):
            goal = goals[step - 1]
            for copy in hops[(step - 1) * (groups - 1) : step * (groups - 1)]:
                copy.wait_recv()
            value = src[group, goal].astype(jnp.float32)
            for hop in range(groups - 1):
                value += far[hop, goal].astype(jnp.float32)
            if step < parts:
                stage[goal] = value.astype(LOW)
                copies.append(self.send(me, step, stage.at[goal], came, send, recv))
                copies[-1].start()
            else:
                mine[...] = value
            yield
        self.place(out, me, lambda lo, hi: mine[:, lo:hi])
        yield from self.finish(me, out, copies, came)
        for copy in hops:
            copy.wait_send()


def call(jobs, operands, name, identity, axes, work=None, micros=50):
    counts = [len(job.scratch) for job in jobs]
    jobs_n = len(jobs)
    extra = work.operands if work else []
    extra_out = work.outs if work else []
    extra_scratch = work.scratch if work else []

    def kernel(*refs):
        refs = list(refs)

        def take(count):
            taken = refs[:count]
            del refs[:count]
            return taken

        ins, more = take(jobs_n), take(len(extra))
        outs, more_outs = take(jobs_n), take(len(extra_out))
        runs = []
        for job, src, dst, count in zip(jobs, ins, outs, counts):
            runs.append(job.run(src, dst, *take(count)))
        if work:
            runs.append(work.run(*more, *more_outs, *refs))
        enter(axes)
        while runs:
            going = []
            for run in runs:
                try:
                    next(run)
                    going.append(run)
                except StopIteration:
                    pass
            runs = going

    vmem = pl.BlockSpec(memory_space=pltpu.VMEM)
    anywhere = pl.BlockSpec(memory_space=pl.ANY)
    return pl.pallas_call(
        kernel,
        out_shape=tuple(job.out for job in jobs) + tuple(extra_out),
        in_specs=[vmem] * jobs_n + [anywhere] * len(extra),
        out_specs=(vmem,) * jobs_n + (anywhere,) * len(extra_out),
        scratch_shapes=[shape for job in jobs for shape in job.scratch] + list(extra_scratch),
        compiler_params=pltpu.CompilerParams(
            collective_id=identity, has_side_effects=True, vmem_limit_bytes=62 << 20
        ),
        cost_estimate=pl.CostEstimate(
            flops=0, bytes_accessed=micros * 3_000_000, transcendentals=0
        ),
        name=name,
    )(*operands, *extra)


class Grads:
    tile = 256

    def __init__(self, pairs):
        self.pairs = pairs
        length, wide = pairs[0][0].shape[0], max(right.shape[1] for _, right in pairs)
        self.operands = [array for pair in pairs for array in pair]
        self.outs = [jax.ShapeDtypeStruct((l.shape[1], r.shape[1]), LOW) for l, r in pairs]
        self.scratch = [pltpu.VMEM(array.shape, LOW) for array in self.operands]
        self.scratch += [
            pltpu.VMEM((self.tile, length), LOW),
            pltpu.VMEM((2, self.tile, wide), LOW),
            pltpu.SemaphoreType.DMA((2 * len(pairs),)),
            pltpu.SemaphoreType.DMA((2,)),
        ]

    def run(self, *refs):
        n, tile = len(self.pairs), self.tile
        sources, outs = refs[: 2 * n], refs[2 * n : 3 * n]
        held = refs[3 * n : 5 * n]
        turned, made, get, put = refs[5 * n :]
        gets = [pltpu.make_async_copy(s, h, get.at[i]) for i, (s, h) in enumerate(zip(sources, held))]
        for copy in gets:
            copy.start()
        yield
        puts = []
        for which in range(n):
            left, right, out = held[2 * which], held[2 * which + 1], outs[which]
            gets[2 * which].wait()
            gets[2 * which + 1].wait()
            columns = right.shape[1]
            step = min(columns, 512)
            for at in range(0, left.shape[1], tile):
                slot = len(puts) % 2
                if len(puts) >= 2:
                    puts[-2].wait()
                turned[...] = left[:, at : at + tile].T

                def one(index, carry):
                    where = pl.ds(pl.multiple_of(index * step, step), step)
                    made[slot, :, where] = jnp.dot(
                        turned[...], right[:, where], preferred_element_type=jnp.float32
                    ).astype(LOW)
                    return carry

                lax.fori_loop(0, columns // step, one, 0)
                part = made.at[slot] if columns == made.shape[2] else made.at[slot, :, :columns]
                puts.append(pltpu.make_async_copy(part, out.at[at : at + tile, :], put.at[slot]))
                puts[-1].start()
                yield
        for copy in puts[-2:]:
            copy.wait()


class Plan:
    def __init__(self, parts, groups, width):
        self.parts, self.groups = parts, groups
        self.shard = width // (parts * groups)
        self.run = HEAD_DIM // self.shard
        self.heads = HEADS // parts
        self.qkv_dims = (3, self.run, self.heads, parts // self.run, HEAD_DIM)

    def qkv_pieces(self, weight):
        rows = weight.shape[0]
        pieces = weight.reshape((rows,) + self.qkv_dims).transpose(4, 2, 0, 1, 3, 5)
        return pieces.reshape(self.parts, rows, 3 * self.heads * HEAD_DIM)

    def qkv_starts(self, part):
        at, index = part // self.run, lax.rem(part, self.run)
        return [
            (kind * HEADS + (index * self.heads + head) * (self.parts // self.run) + at) * HEAD_DIM
            for kind in range(3)
            for head in range(self.heads)
        ]

    def unit_pieces(self, weight):
        rows, columns = weight.shape
        inner = columns // (2 * self.groups * self.parts)
        pieces = weight.reshape(rows, 2 * self.groups, self.parts, inner).transpose(2, 0, 1, 3)
        return pieces.reshape(self.parts, rows, 2 * self.groups * inner)

    def unit_job(self, shape):
        step = shape[1] // (2 * self.groups)
        if step % HEAD_DIM:
            return Exchange(self.parts, shape)
        return Deliver(
            self.parts,
            shape,
            lambda part: [(at * self.parts + part) * step for at in range(2 * self.groups)],
        )

    def unit_rows(self, pieces):
        if pieces.ndim == 2:
            return pieces
        parts, rows, columns = pieces.shape
        outer = 2 * self.groups
        pieces = pieces.reshape(parts, rows, outer, columns // outer).transpose(1, 2, 0, 3)
        return pieces.reshape(rows, parts * columns).astype(jnp.float32)


def per_device(tokens, w_qkv, w_out, w_gate_up, w_down, seq_lengths, block_order, cotangent):
    lengths = seq_lengths[0]
    order_row = block_order[0]
    parts = lax.axis_size("ctx")
    groups = lax.axis_size("fsdp")
    rows, width = tokens.shape
    length = rows * parts
    plan = Plan(parts, groups, width)
    heads, shard, run = plan.heads, plan.shard, plan.run
    head_width = heads * HEAD_DIM
    score_scale = HEAD_DIM ** (-0.5)
    line = (("ctx", parts),)
    plane = (("ctx", parts), ("fsdp", groups))
    block = (rows, width)

    out_rows = gather(w_out, "fsdp")
    down_rows = gather(w_down, "fsdp")
    gate_up_pieces = plan.unit_pieces(w_gate_up)
    inputs = tokens.astype(jnp.float32)
    normed_in, root_in = normalize(inputs)
    qkv_pieces = plan.qkv_pieces(w_qkv)
    qkv_cols, normed_in_full, gate_up_cols = call(
        [
            Spread(parts, groups, qkv_pieces.shape[1:]),
            Gather(parts, block),
            Exchange(parts, gate_up_pieces.shape[1:]),
        ],
        [qkv_pieces, normed_in.astype(LOW), gate_up_pieces],
        "start",
        2,
        plane,
        micros=110,
    )
    gate_up_cols, down_rows, out_rows = lax.optimization_barrier(
        (gate_up_cols, down_rows, out_rows)
    )
    gate_up_cols = gather(gate_up_cols.reshape(width // groups, -1), "fsdp")
    (out_cols,) = call(
        [Exchange(run, (heads * shard, width))],
        [out_rows.reshape(run, heads * shard, width)],
        "swap",
        1,
        line,
        micros=6,
    )
    qkv_cols = qkv_cols.reshape(width, 3 * head_width)
    normed_in_full = normed_in_full.reshape(length, width)
    out_cols = out_cols.reshape(run, heads, shard, width).transpose(1, 0, 2, 3)
    out_cols = out_cols.reshape(head_width, width)

    row_index = jnp.arange(length, dtype=jnp.int32)
    seq, pos = places(initial_index(row_index, order_row), lengths)
    cosine_table, sine_table = angle_tables(pos)
    allowed = ((seq[:, None] == seq[None, :]) & (pos[None, :] <= pos[:, None]))[None]

    qkv = dot(normed_in_full, qkv_cols)
    head_shape = (length, heads, HEAD_DIM)
    queries = rotate(qkv[:, :head_width].reshape(head_shape), cosine_table, sine_table).astype(LOW)
    keys = rotate(
        qkv[:, head_width : 2 * head_width].reshape(head_shape), cosine_table, sine_table
    ).astype(LOW)
    values = qkv[:, 2 * head_width :].astype(LOW).reshape(head_shape)
    scores = jnp.einsum("qhd,khd->hqk", queries, keys, preferred_element_type=jnp.float32)
    scores = jnp.where(allowed, scores * score_scale, -1e30)
    row_max = jnp.max(scores, axis=-1)
    weights = jnp.where(allowed, jnp.exp(scores - row_max[..., None]), 0.0)
    row_total = jnp.sum(weights, axis=-1)
    mixed = jnp.einsum("hqk,khd->qhd", weights.astype(LOW), values, preferred_element_type=jnp.float32)
    log_total = row_max + jnp.log(row_total)
    attn_heads = mixed / jnp.transpose(row_total)[..., None]
    mix_low = attn_heads.astype(LOW).reshape(length, head_width)

    out_terms = dot(mix_low, out_cols).astype(LOW)
    attn_out, cot_full = call(
        [Scatter(parts, block), Gather(parts, block)],
        [out_terms.reshape((parts,) + block), cotangent],
        "out",
        3,
        line,
        micros=64,
    )
    cot_full = cot_full.reshape(length, width)
    residual = inputs + attn_out
    normed_mid, root_mid = normalize(residual)
    (normed_mid_full,) = call([Gather(parts, block)], [normed_mid.astype(LOW)], "mid", 4, line, micros=45)
    normed_mid_full = normed_mid_full.reshape(length, width)

    gate_up = dot(normed_mid_full, gate_up_cols)
    units = gate_up.shape[1] // 2
    gate_part = gate_up[:, :units]
    up_part = gate_up[:, units:]
    sigmoid_gate = jax.nn.sigmoid(gate_part)
    silu_gate = gate_part * sigmoid_gate
    activated = (silu_gate * up_part).astype(LOW)
    act_grad = times_transposed(cot_full, down_rows)
    gate_grad = act_grad * up_part * sigmoid_gate * (1.0 + gate_part * (1.0 - sigmoid_gate))
    up_grad = act_grad * silu_gate
    gate_up_back = jnp.concatenate([gate_grad, up_grad], axis=1).astype(LOW)
    down_grad = scatter(column_product(activated, cot_full).astype(LOW), "fsdp").astype(jnp.float32)
    mid_back_terms = times_transposed(gate_up_back, gate_up_cols).astype(LOW)
    mid_back, gate_up_grad = call(
        [Scatter(parts, block)],
        [mid_back_terms.reshape((parts,) + block)],
        "mid_back",
        5,
        line,
        Grads([(normed_mid_full, gate_up_back)]),
    )
    gate_up_grad, down_grad = lax.optimization_barrier((gate_up_grad, down_grad))
    gate_up_grad = scatter(gate_up_grad, "fsdp")
    residual_back = cotangent.astype(jnp.float32) + norm_back(mid_back, normed_mid, root_mid)
    proj_back = residual_back.astype(LOW)

    down_terms = dot(activated, down_rows).astype(LOW)
    proj_back_full, down_out = call(
        [Gather(parts, block), Scatter(parts, block)],
        [proj_back, down_terms.reshape((parts,) + block)],
        "proj_back",
        6,
        line,
        micros=70,
    )
    layer_out = (residual + down_out).astype(LOW)
    proj_back_full = proj_back_full.reshape(length, width)

    out_grad = column_product(mix_low, proj_back_full).astype(LOW)
    out_grad = out_grad.reshape(heads, run, shard, width).transpose(1, 0, 2, 3)
    (out_grad,) = call(
        [Exchange(run, (heads * shard, width))],
        [out_grad.reshape(run, heads * shard, width)],
        "swap_back",
        8,
        line,
        micros=6,
    )
    out_grad, gate_up_grad = lax.optimization_barrier((out_grad, gate_up_grad))
    out_grad = scatter(out_grad.reshape(groups * shard, width), "fsdp").astype(jnp.float32)
    back_heads = times_transposed(proj_back_full, out_cols).astype(LOW).reshape(head_shape)
    delta = jnp.einsum("qhd,qhd->hq", back_heads.astype(jnp.float32), attn_heads)
    probs = jnp.where(allowed, jnp.exp(scores - log_total[..., None]), 0.0)
    value_back = jnp.einsum(
        "hqk,qhd->khd", probs.astype(LOW), back_heads, preferred_element_type=jnp.float32
    )
    prob_back = jnp.einsum("qhd,khd->hqk", back_heads, values, preferred_element_type=jnp.float32)
    score_back = (score_scale * probs * (prob_back - delta[..., None])).astype(LOW)
    query_back = jnp.einsum("hqk,khd->qhd", score_back, keys, preferred_element_type=jnp.float32)
    key_back = jnp.einsum("hqk,qhd->khd", score_back, queries, preferred_element_type=jnp.float32)
    qkv_back = jnp.concatenate(
        [
            unrotate(query_back, cosine_table, sine_table).reshape(length, head_width),
            unrotate(key_back, cosine_table, sine_table).reshape(length, head_width),
            value_back.reshape(length, head_width),
        ],
        axis=1,
    ).astype(LOW)
    qkv_grad = column_product(normed_in_full, qkv_back).astype(LOW)
    in_back_terms = times_transposed(qkv_back, qkv_cols).astype(LOW)
    in_back, qkv_grad, gate_up_grad = call(
        [
            Scatter(parts, block),
            Collect(parts, groups, qkv_pieces.shape[1:], plan.qkv_starts),
            plan.unit_job(gate_up_pieces.shape[1:]),
        ],
        [
            in_back_terms.reshape((parts,) + block),
            qkv_grad.reshape((groups,) + qkv_pieces.shape),
            gate_up_grad.reshape(gate_up_pieces.shape),
        ],
        "in_back",
        7,
        plane,
        micros=90,
    )
    tokens_grad = residual_back + norm_back(in_back, normed_in, root_in)
    return (
        layer_out,
        tokens_grad,
        qkv_grad,
        out_grad,
        plan.unit_rows(gate_up_grad),
        down_grad,
    )


def solution(mesh):
    both = P(("fsdp", "ctx"), None)
    one = P("fsdp", None)
    return jax.shard_map(
        per_device,
        mesh=mesh,
        in_specs=(both, both, both, both, both, one, one, both),
        out_specs=(both,) * 6,
        check_vma=False,
    )
```

```python
import jax
import jax.numpy as jnp
from jax import lax
from jax.experimental import pallas as pl
from jax.experimental.pallas import tpu as pltpu
from jax.sharding import PartitionSpec as P

HEADS = 16
HEAD_DIM = 128
BLOCK = 128
LOW = jnp.bfloat16


def normalize(values):
    average = jnp.mean(values, axis=-1, keepdims=True)
    centered = values - average
    variance = jnp.mean(centered * centered, axis=-1, keepdims=True)
    inv_root = lax.rsqrt(variance + 1e-05)
    return (centered * inv_root, inv_root)


def norm_back(upstream, normed, inv_root):
    first_mean = jnp.mean(upstream, axis=-1, keepdims=True)
    second_mean = jnp.mean(upstream * normed, axis=-1, keepdims=True)
    return inv_root * (upstream - first_mean - normed * second_mean)


def places(token_index, lengths):
    seq_ends = jnp.cumsum(lengths)
    sequence = jnp.sum((token_index[:, None] >= seq_ends[None, :]).astype(jnp.int32), axis=1)
    before = jnp.arange(lengths.shape[0], dtype=jnp.int32)
    seq_start = jnp.sum(jnp.where(before[None, :] < sequence[:, None], lengths[None, :], 0), axis=1)
    return (sequence, token_index - seq_start)


def initial_index(row_index, order_row):
    slot_index = row_index // BLOCK
    slot_table = jnp.arange(order_row.shape[0], dtype=jnp.int32)
    picked = jnp.sum(
        jnp.where(slot_table[None, :] == slot_index[:, None], order_row[None, :], 0), axis=1
    )
    return picked * BLOCK + row_index % BLOCK


def angle_tables(position):
    half_dim = HEAD_DIM // 2
    frequency = 10000.0 ** (-jnp.arange(half_dim, dtype=jnp.float32) * 2.0 / HEAD_DIM)
    angle_table = position.astype(jnp.float32)[:, None] * frequency[None, :]
    angle_table = jnp.concatenate([angle_table, angle_table], axis=-1)
    return (jnp.cos(angle_table)[:, None, :], jnp.sin(angle_table)[:, None, :])


def rotate(values, cosine_table, sine_table):
    half_dim = values.shape[-1] // 2
    turned = jnp.concatenate([-values[..., half_dim:], values[..., :half_dim]], axis=-1)
    return values * cosine_table + turned * sine_table


def unrotate(values, cosine_table, sine_table):
    half_dim = values.shape[-1] // 2
    scaled = values * sine_table
    turned = jnp.concatenate([scaled[..., half_dim:], -scaled[..., :half_dim]], axis=-1)
    return values * cosine_table + turned


def dot(left, right):
    return jnp.dot(left, right, preferred_element_type=jnp.float32)


def times_transposed(left, right):
    return lax.dot_general(
        left, right, (((1,), (1,)), ((), ())), preferred_element_type=jnp.float32
    )


def column_product(left, right):
    return lax.dot_general(
        left, right, (((0,), (0,)), ((), ())), preferred_element_type=jnp.float32
    )


def gather(values, axes):
    return lax.all_gather(values, axes, axis=0, tiled=True)


def scatter(values, axes):
    return lax.psum_scatter(values, axes, scatter_dimension=0, tiled=True)


def enter(axes):
    barrier = pltpu.get_barrier_semaphore()
    count = 0
    for axis, size in axes:
        me = lax.axis_index(axis)
        for step in range(1, size):
            pl.semaphore_signal(barrier, inc=1, device_id={axis: lax.rem(me + step, size)})
        count += size - 1
    pl.semaphore_wait(barrier, count)


def remote(src, dst, send, recv, axis, peer):
    return pltpu.make_async_remote_copy(
        src_ref=src, dst_ref=dst, send_sem=send, recv_sem=recv, device_id={axis: peer}
    )


class Exchange:
    def __init__(self, parts, shape):
        self.parts = parts
        self.out = jax.ShapeDtypeStruct((parts,) + shape, LOW)
        self.scratch = [
            pltpu.SemaphoreType.DMA((parts - 1,)),
            pltpu.SemaphoreType.DMA((parts - 1,)),
            pltpu.SemaphoreType.DMA,
        ]

    def run(self, src, dst, send, recv, local):
        place = lax.axis_index("ctx")
        me = lax.rem(place, self.parts)
        copies = []
        for step in range(1, self.parts):
            peer = lax.rem(me + step, self.parts)
            copies.append(
                remote(
                    src.at[peer],
                    dst.at[me],
                    send.at[step - 1],
                    recv.at[step - 1],
                    "ctx",
                    place - me + peer,
                )
            )
            copies[-1].start()
        own = pltpu.make_async_copy(src.at[me], dst.at[me], local)
        own.start()
        yield
        for copy in copies:
            copy.wait()
            yield
        own.wait()


class Gather:
    def __init__(self, parts, shape):
        self.parts = parts
        self.out = jax.ShapeDtypeStruct((parts,) + shape, LOW)
        chips = parts // 2
        self.scratch = [
            pltpu.SemaphoreType.DMA((2, chips)),
            pltpu.SemaphoreType.DMA((chips,)),
            pltpu.SemaphoreType.DMA((chips,)),
            pltpu.SemaphoreType.DMA((chips,)),
            pltpu.SemaphoreType.DMA,
        ]

    def run(self, src, dst, send, recv, pair_send, pair_recv, local):
        chips = self.parts // 2
        me = lax.axis_index("ctx")
        chip, core = me // 2, lax.rem(me, 2)
        partner = me + 1 - 2 * core

        def line(block, slot, origin, way):
            return remote(
                block, slot, send.at[way, origin], recv.at[origin], "ctx", me + 2 - 4 * way
            )

        def across(block, slot, origin):
            return remote(block, slot, pair_send.at[origin], pair_recv.at[origin], "ctx", partner)

        mine = dst.at[me]

        @pl.when(chip < chips - 1)
        def _():
            line(src, mine, chip, 0).start()

        @pl.when(chip > 0)
        def _():
            line(src, mine, chip, 1).start()

        across(src, mine, chip).start()
        own = pltpu.make_async_copy(src, mine, local)
        own.start()
        yield
        for step in range(1, chips):
            for way in range(2):
                origin = chip - step if way == 0 else chip + step

                @pl.when((origin >= 0) & (origin < chips))
                def _():
                    slot = dst.at[2 * origin + core]
                    line(slot, slot, origin, way).wait_recv()

                    @pl.when((chip < chips - 1) if way == 0 else (chip > 0))
                    def _():
                        line(slot, slot, origin, way).start()

                    across(slot, slot, origin).start()

            yield
        for step in range(chips):
            for way in range(2):
                origin = chip - step if way == 0 else chip + step
                ahead = (chip < chips - 1) if way == 0 else (chip > 0)

                @pl.when((origin >= 0) & (origin < chips) & ahead)
                def _():
                    slot = dst.at[2 * origin + core]
                    line(slot, slot, origin, way).wait_send()

        for origin in range(chips):
            across(dst.at[2 * origin + core], dst.at[2 * origin + core], origin).wait_send()
            other = dst.at[2 * origin + 1 - core]
            across(other, other, origin).wait_recv()
        own.wait()


class Scatter:
    cuts = 2

    def __init__(self, parts, shape):
        self.parts, self.shape = parts, shape
        self.out = jax.ShapeDtypeStruct(shape, jnp.float32)
        chips = parts // 2
        piece = (self.cuts, shape[0] // self.cuts, shape[1])
        self.scratch = [
            pltpu.VMEM((chips,) + shape, LOW),
            pltpu.VMEM((2, chips) + piece, LOW),
            pltpu.VMEM((chips,) + piece, LOW),
            pltpu.SemaphoreType.DMA((chips,)),
            pltpu.SemaphoreType.DMA((chips,)),
            pltpu.SemaphoreType.DMA((chips, self.cuts)),
            pltpu.SemaphoreType.DMA((2, chips, self.cuts)),
        ]

    def run(self, src, out, pair, come, stage, pair_send, pair_recv, send, recv):
        chips, cuts = self.parts // 2, self.cuts
        me = lax.axis_index("ctx")
        chip, core = me // 2, lax.rem(me, 2)
        partner = me + 1 - 2 * core
        rows = self.shape[0] // cuts
        slab = min(rows, 16)
        last = chips - 1

        def across(goal):
            return remote(
                src.at[2 * goal + 1 - core],
                pair.at[goal],
                pair_send.at[goal],
                pair_recv.at[goal],
                "ctx",
                partner,
            )

        def line(goal, cut, way):
            return remote(
                stage.at[goal, cut],
                come.at[way, goal, cut],
                send.at[goal, cut],
                recv.at[way, goal, cut],
                "ctx",
                me + 2 - 4 * way,
            )

        def wide(ref, *index):
            return ref[index].astype(jnp.float32)

        def slabs(part):
            def one(index, carry):
                part(pl.multiple_of(index * slab, slab))
                return carry

            lax.fori_loop(0, rows // slab, one, 0)

        def both(goal, cut, at):
            at = pl.ds(cut * rows + at, slab)
            return wide(src, 2 * goal + core, at) + wide(pair, goal, at)

        order = []
        for step in range((chips + 1) // 2):
            order += sorted({step, last - step})
        for goal in order:
            across(goal).start()
        yield
        for step in range(last * cuts):
            for way in range(2):
                turn = step - (chip if way == 0 else last - chip)
                goal = (last - turn // cuts) if way == 0 else turn // cuts
                cut = step - (chip if way == 0 else last - chip) - (turn // cuts) * cuts
                first = (chip == 0) if way == 0 else (chip == last)
                ahead = last - chip if way == 0 else chip

                def begin(at):
                    value = both(goal, cut, at)
                    stage[goal, cut, pl.ds(at, slab), :] = value.astype(LOW)

                def middle(at):
                    value = both(goal, cut, at) + wide(come, way, goal, cut, pl.ds(at, slab))
                    stage[goal, cut, pl.ds(at, slab), :] = value.astype(LOW)

                @pl.when((turn >= 0) & (turn < ahead * cuts))
                def _():
                    @pl.when(cut == 0)
                    def _():
                        across(goal).wait_recv()

                    @pl.when(first)
                    def _():
                        slabs(begin)

                    @pl.when(jnp.logical_not(first))
                    def _():
                        line(goal, cut, way).wait_recv()
                        slabs(middle)

                    line(goal, cut, way).start()

            yield
        across(chip).wait_recv()
        for cut in range(cuts):

            def own(at):
                out[pl.ds(cut * rows + at, slab), :] = both(chip, cut, at)

            slabs(own)
        yield
        for cut in range(cuts):
            for way in range(2):

                def final(at):
                    out[pl.ds(cut * rows + at, slab), :] += wide(
                        come, way, chip, cut, pl.ds(at, slab)
                    )

                @pl.when((chip > 0) if way == 0 else (chip < last))
                def _():
                    line(chip, cut, way).wait_recv()
                    slabs(final)

            yield
        for goal in range(chips):
            across(goal).wait_send()

            @pl.when(chip != goal)
            def _():
                for cut in range(cuts):
                    line(goal, cut, 0).wait_send()


class Spread:
    def __init__(self, parts, groups, shape):
        self.parts, self.groups = parts, groups
        self.out = jax.ShapeDtypeStruct((groups, parts) + shape, LOW)
        self.scratch = [
            pltpu.SemaphoreType.DMA((parts - 1,)),
            pltpu.SemaphoreType.DMA((parts - 1,)),
            pltpu.SemaphoreType.DMA((groups - 1, parts)),
            pltpu.SemaphoreType.DMA((groups - 1, parts)),
            pltpu.SemaphoreType.DMA,
        ]

    def run(self, src, dst, send, recv, far_send, far_recv, local):
        parts, groups = self.parts, self.groups
        me, group = lax.axis_index("ctx"), lax.axis_index("fsdp")
        copies = []
        for step in range(1, parts):
            peer = lax.rem(me + step, parts)
            copies.append(
                remote(
                    src.at[peer],
                    dst.at[group, me],
                    send.at[step - 1],
                    recv.at[step - 1],
                    "ctx",
                    peer,
                )
            )
            copies[-1].start()
        own = pltpu.make_async_copy(src.at[me], dst.at[group, me], local)
        own.start()

        def pass_on(block, origin, step):
            out = []
            for hop in range(1, groups):
                copy = remote(
                    block,
                    dst.at[group, origin],
                    far_send.at[hop - 1, step],
                    far_recv.at[hop - 1, step],
                    "fsdp",
                    lax.rem(group + hop, groups),
                )
                copy.start()
                out.append(copy)
            return out

        far = pass_on(src.at[me], me, 0)
        eager = -(-parts // 2)
        yield
        for step in range(1, parts):
            copies[step - 1].wait_recv()
            origin = lax.rem(me - step + parts, parts)
            far += pass_on(dst.at[group, origin], origin, step)
            if step % eager == 0:
                yield
        for at, copy in enumerate(far):
            copy.wait()
            if at % 6 == 5:
                yield
        for copy in copies:
            copy.wait_send()
        own.wait()


class Deliver:
    def __init__(self, parts, shape, offsets):
        self.parts, self.shape, self.offsets = parts, shape, offsets
        self.out = jax.ShapeDtypeStruct((shape[0], parts * shape[1]), jnp.float32)
        self.scratch = [
            pltpu.VMEM((parts - 1,) + shape, LOW),
            pltpu.SemaphoreType.DMA((parts - 1,)),
            pltpu.SemaphoreType.DMA((parts - 1,)),
        ]

    def place(self, out, origin, read):
        starts = self.offsets(origin)
        step = self.shape[1] // len(starts)
        for index, start in enumerate(starts):
            out[:, pl.ds(pl.multiple_of(start, HEAD_DIM), step)] = read(
                index * step, (index + 1) * step
            )

    def send(self, me, step, block, came, send, recv):
        return remote(
            block,
            came.at[step - 1],
            send.at[step - 1],
            recv.at[step - 1],
            "ctx",
            lax.rem(me + step, self.parts),
        )

    def run(self, src, out, came, send, recv):
        me = lax.axis_index("ctx")
        copies = []
        for step in range(1, self.parts):
            block = src.at[lax.rem(me + step, self.parts)]
            copies.append(self.send(me, step, block, came, send, recv))
            copies[-1].start()
        self.place(out, me, lambda lo, hi: src[me, :, lo:hi].astype(jnp.float32))
        yield
        yield from self.finish(me, out, copies, came)

    def finish(self, me, out, copies, came):
        for step in range(1, self.parts):
            copies[step - 1].wait_recv()
            origin = lax.rem(me - step + self.parts, self.parts)
            self.place(out, origin, lambda lo, hi: came[step - 1, :, lo:hi].astype(jnp.float32))
            yield
        for copy in copies:
            copy.wait_send()


class Collect(Deliver):
    def __init__(self, parts, groups, shape, offsets):
        super().__init__(parts, shape, offsets)
        self.groups = groups
        self.scratch = self.scratch + [
            pltpu.VMEM((groups - 1, parts) + shape, LOW),
            pltpu.VMEM((parts,) + shape, LOW),
            pltpu.VMEM(shape, jnp.float32),
            pltpu.SemaphoreType.DMA((groups - 1, parts)),
            pltpu.SemaphoreType.DMA((groups - 1, parts)),
        ]

    def run(self, src, out, came, send, recv, far, stage, mine, far_send, far_recv):
        parts, groups = self.parts, self.groups
        me, group = lax.axis_index("ctx"), lax.axis_index("fsdp")
        goals = [lax.rem(me + step, parts) for step in range(1, parts + 1)]
        hops = []
        for goal in goals:
            for hop in range(1, groups):
                peer = lax.rem(group + hop, groups)
                hops.append(
                    remote(
                        src.at[peer, goal],
                        far.at[hop - 1, goal],
                        far_send.at[hop - 1, goal],
                        far_recv.at[hop - 1, goal],
                        "fsdp",
                        peer,
                    )
                )
                hops[-1].start()
        yield
        copies = []
        for step in range(1, parts + 1):
            goal = goals[step - 1]
            for copy in hops[(step - 1) * (groups - 1) : step * (groups - 1)]:
                copy.wait_recv()
            value = src[group, goal].astype(jnp.float32)
            for hop in range(groups - 1):
                value += far[hop, goal].astype(jnp.float32)
            if step < parts:
                stage[goal] = value.astype(LOW)
                copies.append(self.send(me, step, stage.at[goal], came, send, recv))
                copies[-1].start()
            else:
                mine[...] = value
            yield
        self.place(out, me, lambda lo, hi: mine[:, lo:hi])
        yield from self.finish(me, out, copies, came)
        for copy in hops:
            copy.wait_send()


def call(jobs, operands, name, identity, axes, work=None, micros=50):
    counts = [len(job.scratch) for job in jobs]
    jobs_n = len(jobs)
    extra = work.operands if work else []
    extra_out = work.outs if work else []
    extra_scratch = work.scratch if work else []

    def kernel(*refs):
        refs = list(refs)

        def take(count):
            taken = refs[:count]
            del refs[:count]
            return taken

        ins, more = take(jobs_n), take(len(extra))
        outs, more_outs = take(jobs_n), take(len(extra_out))
        runs = []
        for job, src, dst, count in zip(jobs, ins, outs, counts):
            runs.append(job.run(src, dst, *take(count)))
        if work:
            runs.append(work.run(*more, *more_outs, *refs))
        enter(axes)
        while runs:
            going = []
            for run in runs:
                try:
                    next(run)
                    going.append(run)
                except StopIteration:
                    pass
            runs = going

    vmem = pl.BlockSpec(memory_space=pltpu.VMEM)
    anywhere = pl.BlockSpec(memory_space=pl.ANY)
    return pl.pallas_call(
        kernel,
        out_shape=tuple(job.out for job in jobs) + tuple(extra_out),
        in_specs=[vmem] * jobs_n + [anywhere] * len(extra),
        out_specs=(vmem,) * jobs_n + (anywhere,) * len(extra_out),
        scratch_shapes=[shape for job in jobs for shape in job.scratch] + list(extra_scratch),
        compiler_params=pltpu.CompilerParams(
            collective_id=identity, has_side_effects=True, vmem_limit_bytes=62 << 20
        ),
        cost_estimate=pl.CostEstimate(
            flops=0, bytes_accessed=micros * 3_000_000, transcendentals=0
        ),
        name=name,
    )(*operands, *extra)


class Grads:
    tile = 256

    def __init__(self, pairs):
        self.pairs = pairs
        length, wide = pairs[0][0].shape[0], max(right.shape[1] for _, right in pairs)
        self.operands = [array for pair in pairs for array in pair]
        self.outs = [jax.ShapeDtypeStruct((l.shape[1], r.shape[1]), LOW) for l, r in pairs]
        self.scratch = [pltpu.VMEM(array.shape, LOW) for array in self.operands]
        self.scratch += [
            pltpu.VMEM((self.tile, length), LOW),
            pltpu.VMEM((2, self.tile, wide), LOW),
            pltpu.SemaphoreType.DMA((2 * len(pairs),)),
            pltpu.SemaphoreType.DMA((2,)),
        ]

    def run(self, *refs):
        n, tile = len(self.pairs), self.tile
        sources, outs = refs[: 2 * n], refs[2 * n : 3 * n]
        held = refs[3 * n : 5 * n]
        turned, made, get, put = refs[5 * n :]
        gets = [pltpu.make_async_copy(s, h, get.at[i]) for i, (s, h) in enumerate(zip(sources, held))]
        for copy in gets:
            copy.start()
        yield
        puts = []
        for which in range(n):
            left, right, out = held[2 * which], held[2 * which + 1], outs[which]
            gets[2 * which].wait()
            gets[2 * which + 1].wait()
            columns = right.shape[1]
            step = min(columns, 512)
            for at in range(0, left.shape[1], tile):
                slot = len(puts) % 2
                if len(puts) >= 2:
                    puts[-2].wait()
                turned[...] = left[:, at : at + tile].T

                def one(index, carry):
                    where = pl.ds(pl.multiple_of(index * step, step), step)
                    made[slot, :, where] = jnp.dot(
                        turned[...], right[:, where], preferred_element_type=jnp.float32
                    ).astype(LOW)
                    return carry

                lax.fori_loop(0, columns // step, one, 0)
                part = made.at[slot] if columns == made.shape[2] else made.at[slot, :, :columns]
                puts.append(pltpu.make_async_copy(part, out.at[at : at + tile, :], put.at[slot]))
                puts[-1].start()
                yield
        for copy in puts[-2:]:
            copy.wait()


def product(left, right):
    return jnp.dot(left, right, preferred_element_type=jnp.float32)


class Puts:
    def __init__(self, made, put):
        self.made, self.put, self.copies = made, put, []

    def buffer(self):
        if len(self.copies) >= 2:
            self.copies[-2].wait()
        return self.made.at[len(self.copies) % 2]

    def send(self, source, target):
        copy = pltpu.make_async_copy(source, target, self.put.at[len(self.copies) % 2])
        copy.start()
        self.copies.append(copy)

    def finish(self):
        for copy in self.copies[-2:]:
            copy.wait()


def softmax_block(query, keys, ok):
    scores = times_transposed(query, keys) * HEAD_DIM ** (-0.5)
    scores = jnp.where(ok, scores, -1e30)
    weights = jnp.exp(scores - jnp.max(scores, axis=-1, keepdims=True))
    weights = jnp.where(ok, weights, 0.0)
    return weights, jnp.sum(weights, axis=-1, keepdims=True)


class Attend:
    tile = 256

    def __init__(self, rows, weight, tables, heads):
        self.heads = heads
        self.operands = [rows, weight] + list(tables)
        length, wide = rows.shape[0], weight.shape[1]
        self.outs = [
            jax.ShapeDtypeStruct((length, wide), LOW),
            jax.ShapeDtypeStruct((length, wide // 3), LOW),
        ]
        self.scratch = [pltpu.VMEM(array.shape, array.dtype) for array in self.operands]
        self.scratch += [pltpu.VMEM(out.shape, out.dtype) for out in self.outs]
        self.scratch += [
            pltpu.SemaphoreType.DMA((len(self.operands),)),
            pltpu.SemaphoreType.DMA((2,)),
        ]

    def run(self, *refs):
        n, tile, heads = len(self.operands), self.tile, self.heads
        sources, results, held = refs[:n], refs[n : n + 2], refs[n + 2 : 2 * n + 2]
        qkv, mix, get, put = refs[2 * n + 2 :]
        rows, weight, cosine, sine, first, last, keys = held
        gets = [pltpu.make_async_copy(s, h, get.at[i]) for i, (s, h) in enumerate(zip(sources, held))]
        for copy in gets:
            copy.start()
        yield
        for copy in gets:
            copy.wait()
        width = heads * HEAD_DIM

        def project(index, carry):
            at = pl.ds(pl.multiple_of(index * tile, tile), tile)
            value = product(rows[at, :], weight[...])
            for head in range(3 * heads):
                block = value[:, head * HEAD_DIM : (head + 1) * HEAD_DIM]
                if head < 2 * heads:
                    turned = pltpu.roll(block, HEAD_DIM // 2, 1)
                    block = block * cosine[at, :] + turned * sine[at, :]
                qkv[at, head * HEAD_DIM : (head + 1) * HEAD_DIM] = block.astype(LOW)
            return carry

        lax.fori_loop(0, rows.shape[0] // tile, project, 0)
        send = pltpu.make_async_copy(qkv, results[0], put.at[0])
        send.start()
        yield

        def attend(index, carry):
            at = pl.ds(pl.multiple_of(index * tile, tile), tile)
            ok = (keys[:1, :] >= first[at, :1]) & (keys[:1, :] <= last[at, :1])
            for head in range(heads):
                lo = head * HEAD_DIM
                weights, total = softmax_block(
                    qkv[at, lo : lo + HEAD_DIM], qkv[:, width + lo : width + lo + HEAD_DIM], ok
                )
                value = qkv[:, 2 * width + lo : 2 * width + lo + HEAD_DIM]
                mixed = product(weights.astype(LOW), value) / total
                mix[at, lo : lo + HEAD_DIM] = mixed.astype(LOW)
            return carry

        lax.fori_loop(0, rows.shape[0] // tile, attend, 0)
        send_mix = pltpu.make_async_copy(mix, results[1], put.at[1])
        send_mix.start()
        yield
        send.wait()
        send_mix.wait()


class AttendBack:
    tile = 256

    def __init__(self, upstream, out_rows, qkv, rows, weight, tables, heads):
        self.heads = heads
        self.operands = [upstream, out_rows, qkv, weight] + list(tables) + [rows]
        length, wide, width = rows.shape[0], weight.shape[1], rows.shape[1]
        self.outs = [
            jax.ShapeDtypeStruct((length, width), LOW),
            jax.ShapeDtypeStruct((width, wide), LOW),
        ]
        self.scratch = [pltpu.VMEM(array.shape, array.dtype) for array in self.operands[:-1]]
        self.scratch += [
            pltpu.VMEM((length, wide // 3), LOW),
            pltpu.VMEM((length, wide), LOW),
            pltpu.VMEM((2, length, HEAD_DIM), jnp.float32),
            pltpu.VMEM((2, self.tile, width), LOW),
            pltpu.SemaphoreType.DMA((len(self.operands),)),
            pltpu.SemaphoreType.DMA((2,)),
        ]

    def run(self, *refs):
        n, tile, heads = len(self.operands), self.tile, self.heads
        sources, results, held = refs[:n], refs[n : n + 2], refs[n + 2 : 2 * n + 1]
        back, grads, sums, made, get, put = refs[2 * n + 1 :]
        upstream, out_rows, qkv, weight, cosine, sine, first, last, keys = held
        length, width = back.shape
        gets = [pltpu.make_async_copy(s, h, get.at[i]) for i, (s, h) in enumerate(zip(sources, held))]
        for copy in gets:
            copy.start()
        yield
        for copy in gets:
            copy.wait()

        def project(index, carry):
            at = pl.ds(pl.multiple_of(index * tile, tile), tile)
            back[at, :] = times_transposed(upstream[at, :], out_rows[...]).astype(LOW)
            return carry

        lax.fori_loop(0, length // tile, project, 0)
        rows = upstream
        fetch = pltpu.make_async_copy(sources[n - 1], rows, get.at[n - 1])
        fetch.start()
        yield

        def unrotated(value, at):
            return value * cosine[at, :] - pltpu.roll(value, HEAD_DIM // 2, 1) * sine[at, :]

        for head in range(heads):
            lo = head * HEAD_DIM
            mine = slice(lo, lo + HEAD_DIM)
            key = slice(width + lo, width + lo + HEAD_DIM)
            val = slice(2 * width + lo, 2 * width + lo + HEAD_DIM)
            sums[...] = jnp.zeros_like(sums)

            def attend(index, carry):
                at = pl.ds(pl.multiple_of(index * tile, tile), tile)
                ok = (keys[:1, :] >= first[at, :1]) & (keys[:1, :] <= last[at, :1])
                weights, total = softmax_block(qkv[at, mine], qkv[:, key], ok)
                probs = weights / total
                upper = back[at, mine]
                prob_back = times_transposed(upper, qkv[:, val])
                delta = jnp.sum(probs * prob_back, axis=-1, keepdims=True)
                score_back = HEAD_DIM ** (-0.5) * probs * (prob_back - delta)
                score_low = score_back.astype(LOW)
                query_back = product(score_low, qkv[:, key])
                grads[at, mine] = unrotated(query_back, at).astype(LOW)
                sums[0] += product(score_low.T, qkv[at, mine])
                sums[1] += product(probs.astype(LOW).T, upper)
                return carry

            half = max(1, length // tile // 2)
            for begin in range(0, length // tile, half):
                lax.fori_loop(begin, begin + half, attend, 0)
                yield

            def settle(index, carry):
                at = pl.ds(pl.multiple_of(index * tile, tile), tile)
                grads[at, key] = unrotated(sums[0, at, :], at).astype(LOW)
                grads[at, val] = sums[1, at, :].astype(LOW)
                return carry

            lax.fori_loop(0, length // tile, settle, 0)
        puts = Puts(made, put)
        for at in range(0, length, tile):
            buffer = puts.buffer()
            buffer[...] = times_transposed(grads[at : at + tile, :], weight[...]).astype(LOW)
            puts.send(buffer, results[0].at[at : at + tile, :])
            yield
        fetch.wait()
        wide = grads.shape[1]
        for at in range(0, rows.shape[1], tile):
            buffer = puts.buffer().at[:, :wide]
            buffer[...] = product(rows[:, at : at + tile].T, grads[...]).astype(LOW)
            puts.send(buffer, results[1].at[at : at + tile, :])
            yield
        puts.finish()


class Plan:
    def __init__(self, parts, groups, width):
        self.parts, self.groups = parts, groups
        self.shard = width // (parts * groups)
        self.run = HEAD_DIM // self.shard
        self.heads = HEADS // parts
        self.qkv_dims = (3, self.run, self.heads, parts // self.run, HEAD_DIM)

    def qkv_pieces(self, weight):
        rows = weight.shape[0]
        pieces = weight.reshape((rows,) + self.qkv_dims).transpose(4, 2, 0, 1, 3, 5)
        return pieces.reshape(self.parts, rows, 3 * self.heads * HEAD_DIM)

    def qkv_starts(self, part):
        at, index = part // self.run, lax.rem(part, self.run)
        return [
            (kind * HEADS + (index * self.heads + head) * (self.parts // self.run) + at) * HEAD_DIM
            for kind in range(3)
            for head in range(self.heads)
        ]

    def unit_pieces(self, weight):
        rows, columns = weight.shape
        inner = columns // (2 * self.groups * self.parts)
        pieces = weight.reshape(rows, 2 * self.groups, self.parts, inner).transpose(2, 0, 1, 3)
        return pieces.reshape(self.parts, rows, 2 * self.groups * inner)

    def unit_job(self, shape):
        step = shape[1] // (2 * self.groups)
        if step % HEAD_DIM:
            return Exchange(self.parts, shape)
        return Deliver(
            self.parts,
            shape,
            lambda part: [(at * self.parts + part) * step for at in range(2 * self.groups)],
        )

    def unit_rows(self, pieces):
        if pieces.ndim == 2:
            return pieces
        parts, rows, columns = pieces.shape
        outer = 2 * self.groups
        pieces = pieces.reshape(parts, rows, outer, columns // outer).transpose(1, 2, 0, 3)
        return pieces.reshape(rows, parts * columns).astype(jnp.float32)


def per_device(tokens, w_qkv, w_out, w_gate_up, w_down, seq_lengths, block_order, cotangent):
    lengths = seq_lengths[0]
    order_row = block_order[0]
    parts = lax.axis_size("ctx")
    groups = lax.axis_size("fsdp")
    rows, width = tokens.shape
    length = rows * parts
    plan = Plan(parts, groups, width)
    heads, shard, run = plan.heads, plan.shard, plan.run
    head_width = heads * HEAD_DIM
    line = (("ctx", parts),)
    plane = (("ctx", parts), ("fsdp", groups))
    block = (rows, width)

    out_rows = gather(w_out, "fsdp")
    down_rows = gather(w_down, "fsdp")
    gate_up_pieces = plan.unit_pieces(w_gate_up)
    inputs = tokens.astype(jnp.float32)
    normed_in, root_in = normalize(inputs)
    qkv_pieces = plan.qkv_pieces(w_qkv)
    qkv_cols, normed_in_full = call(
        [Spread(parts, groups, qkv_pieces.shape[1:]), Gather(parts, block)],
        [qkv_pieces, normed_in.astype(LOW)],
        "start",
        2,
        plane,
        micros=70,
    )
    qkv_cols = qkv_cols.reshape(width, 3 * head_width)
    normed_in_full = normed_in_full.reshape(length, width)

    row_index = jnp.arange(length, dtype=jnp.int32)
    packed = initial_index(row_index, order_row)
    _, pos = places(packed, lengths)
    cosine_table, sine_table = angle_tables(pos)
    half_sign = jnp.where(jnp.arange(HEAD_DIM) < HEAD_DIM // 2, -1.0, 1.0)
    tables = (
        cosine_table[:, 0, :],
        sine_table[:, 0, :] * half_sign,
        jnp.broadcast_to((packed - pos)[:, None], (length, HEAD_DIM)),
        jnp.broadcast_to(packed[:, None], (length, HEAD_DIM)),
        jnp.broadcast_to(packed[None, :], (8, length)),
    )
    gate_up_cols, out_cols, qkv_low, mix_low = call(
        [Exchange(parts, gate_up_pieces.shape[1:]), Exchange(run, (heads * shard, width))],
        [gate_up_pieces, out_rows.reshape(run, heads * shard, width)],
        "attend",
        1,
        line,
        Attend(normed_in_full, qkv_cols, tables, heads),
        micros=55,
    )
    gate_up_cols, down_rows = lax.optimization_barrier((gate_up_cols, down_rows))
    gate_up_cols = gather(gate_up_cols.reshape(width // groups, -1), "fsdp")
    out_cols = out_cols.reshape(run, heads, shard, width).transpose(1, 0, 2, 3)
    out_cols = out_cols.reshape(head_width, width)

    out_terms = dot(mix_low, out_cols).astype(LOW)
    attn_out, cot_full = call(
        [Scatter(parts, block), Gather(parts, block)],
        [out_terms.reshape((parts,) + block), cotangent],
        "out",
        3,
        line,
        micros=64,
    )
    cot_full = cot_full.reshape(length, width)
    residual = inputs + attn_out
    normed_mid, root_mid = normalize(residual)
    (normed_mid_full,) = call([Gather(parts, block)], [normed_mid.astype(LOW)], "mid", 4, line, micros=45)
    normed_mid_full = normed_mid_full.reshape(length, width)

    gate_up = dot(normed_mid_full, gate_up_cols)
    units = gate_up.shape[1] // 2
    gate_part = gate_up[:, :units]
    up_part = gate_up[:, units:]
    sigmoid_gate = jax.nn.sigmoid(gate_part)
    silu_gate = gate_part * sigmoid_gate
    activated = (silu_gate * up_part).astype(LOW)
    act_grad = times_transposed(cot_full, down_rows)
    gate_grad = act_grad * up_part * sigmoid_gate * (1.0 + gate_part * (1.0 - sigmoid_gate))
    up_grad = act_grad * silu_gate
    gate_up_back = jnp.concatenate([gate_grad, up_grad], axis=1).astype(LOW)
    down_grad = scatter(column_product(activated, cot_full).astype(LOW), "fsdp").astype(jnp.float32)
    mid_back_terms = times_transposed(gate_up_back, gate_up_cols).astype(LOW)
    mid_back, gate_up_grad = call(
        [Scatter(parts, block)],
        [mid_back_terms.reshape((parts,) + block)],
        "mid_back",
        5,
        line,
        Grads([(normed_mid_full, gate_up_back)]),
    )
    gate_up_grad, down_grad = lax.optimization_barrier((gate_up_grad, down_grad))
    gate_up_grad = scatter(gate_up_grad, "fsdp")
    residual_back = cotangent.astype(jnp.float32) + norm_back(mid_back, normed_mid, root_mid)
    proj_back = residual_back.astype(LOW)

    down_terms = dot(activated, down_rows).astype(LOW)
    (proj_back_full,) = call([Gather(parts, block)], [proj_back], "proj_back", 6, line, micros=45)
    proj_back_full = proj_back_full.reshape(length, width)
    out_grad = column_product(mix_low, proj_back_full).astype(LOW)
    out_grad = out_grad.reshape(heads, run, shard, width).transpose(1, 0, 2, 3)
    down_out, out_grad, in_back_terms, qkv_grad = call(
        [Scatter(parts, block), Exchange(run, (heads * shard, width))],
        [down_terms.reshape((parts,) + block), out_grad.reshape(run, heads * shard, width)],
        "attend_back",
        8,
        line,
        AttendBack(proj_back_full, out_cols, qkv_low, normed_in_full, qkv_cols, tables, heads),
        micros=60,
    )
    layer_out = (residual + down_out).astype(LOW)
    out_grad, gate_up_grad = lax.optimization_barrier((out_grad, gate_up_grad))
    out_grad = scatter(out_grad.reshape(groups * shard, width), "fsdp").astype(jnp.float32)
    in_back, qkv_grad, gate_up_grad = call(
        [
            Scatter(parts, block),
            Collect(parts, groups, qkv_pieces.shape[1:], plan.qkv_starts),
            plan.unit_job(gate_up_pieces.shape[1:]),
        ],
        [
            in_back_terms.reshape((parts,) + block),
            qkv_grad.reshape((groups,) + qkv_pieces.shape),
            gate_up_grad.reshape(gate_up_pieces.shape),
        ],
        "in_back",
        7,
        plane,
        micros=90,
    )
    tokens_grad = residual_back + norm_back(in_back, normed_in, root_in)
    return (
        layer_out,
        tokens_grad,
        qkv_grad,
        out_grad,
        plan.unit_rows(gate_up_grad),
        down_grad,
    )


def solution(mesh):
    both = P(("fsdp", "ctx"), None)
    one = P("fsdp", None)
    return jax.shard_map(
        per_device,
        mesh=mesh,
        in_specs=(both, both, both, both, both, one, one, both),
        out_specs=(both,) * 6,
        check_vma=False,
    )
```

```python
import jax
import jax.numpy as jnp
from jax import lax
from jax.experimental import pallas as pl
from jax.experimental.pallas import tpu as pltpu
from jax.sharding import PartitionSpec as P

HEADS = 16
HEAD_DIM = 128
BLOCK = 128
LOW = jnp.bfloat16


def normalize(values):
    average = jnp.mean(values, axis=-1, keepdims=True)
    centered = values - average
    variance = jnp.mean(centered * centered, axis=-1, keepdims=True)
    inv_root = lax.rsqrt(variance + 1e-05)
    return (centered * inv_root, inv_root)


def norm_back(upstream, normed, inv_root):
    first_mean = jnp.mean(upstream, axis=-1, keepdims=True)
    second_mean = jnp.mean(upstream * normed, axis=-1, keepdims=True)
    return inv_root * (upstream - first_mean - normed * second_mean)


def places(token_index, lengths):
    seq_ends = jnp.cumsum(lengths)
    sequence = jnp.sum((token_index[:, None] >= seq_ends[None, :]).astype(jnp.int32), axis=1)
    before = jnp.arange(lengths.shape[0], dtype=jnp.int32)
    seq_start = jnp.sum(jnp.where(before[None, :] < sequence[:, None], lengths[None, :], 0), axis=1)
    return (sequence, token_index - seq_start)


def initial_index(row_index, order_row):
    slot_index = row_index // BLOCK
    slot_table = jnp.arange(order_row.shape[0], dtype=jnp.int32)
    picked = jnp.sum(
        jnp.where(slot_table[None, :] == slot_index[:, None], order_row[None, :], 0), axis=1
    )
    return picked * BLOCK + row_index % BLOCK


def angle_tables(position):
    half_dim = HEAD_DIM // 2
    frequency = 10000.0 ** (-jnp.arange(half_dim, dtype=jnp.float32) * 2.0 / HEAD_DIM)
    angle_table = position.astype(jnp.float32)[:, None] * frequency[None, :]
    angle_table = jnp.concatenate([angle_table, angle_table], axis=-1)
    return (jnp.cos(angle_table)[:, None, :], jnp.sin(angle_table)[:, None, :])


def rotate(values, cosine_table, sine_table):
    half_dim = values.shape[-1] // 2
    turned = jnp.concatenate([-values[..., half_dim:], values[..., :half_dim]], axis=-1)
    return values * cosine_table + turned * sine_table


def unrotate(values, cosine_table, sine_table):
    half_dim = values.shape[-1] // 2
    scaled = values * sine_table
    turned = jnp.concatenate([scaled[..., half_dim:], -scaled[..., :half_dim]], axis=-1)
    return values * cosine_table + turned


def dot(left, right):
    return jnp.dot(left, right, preferred_element_type=jnp.float32)


def times_transposed(left, right):
    return lax.dot_general(
        left, right, (((1,), (1,)), ((), ())), preferred_element_type=jnp.float32
    )


def column_product(left, right):
    return lax.dot_general(
        left, right, (((0,), (0,)), ((), ())), preferred_element_type=jnp.float32
    )


def gather(values, axes):
    return lax.all_gather(values, axes, axis=0, tiled=True)


def scatter(values, axes):
    return lax.psum_scatter(values, axes, scatter_dimension=0, tiled=True)


def enter(axes):
    barrier = pltpu.get_barrier_semaphore()
    count = 0
    for axis, size in axes:
        me = lax.axis_index(axis)
        for step in range(1, size):
            pl.semaphore_signal(barrier, inc=1, device_id={axis: lax.rem(me + step, size)})
        count += size - 1
    pl.semaphore_wait(barrier, count)


def remote(src, dst, send, recv, axis, peer):
    return pltpu.make_async_remote_copy(
        src_ref=src, dst_ref=dst, send_sem=send, recv_sem=recv, device_id={axis: peer}
    )


class Exchange:
    def __init__(self, parts, shape):
        self.parts = parts
        self.out = jax.ShapeDtypeStruct((parts,) + shape, LOW)
        self.scratch = [
            pltpu.SemaphoreType.DMA((parts - 1,)),
            pltpu.SemaphoreType.DMA((parts - 1,)),
            pltpu.SemaphoreType.DMA,
        ]

    def run(self, src, dst, send, recv, local):
        place = lax.axis_index("ctx")
        me = lax.rem(place, self.parts)
        copies = []
        for step in range(1, self.parts):
            peer = lax.rem(me + step, self.parts)
            copies.append(
                remote(
                    src.at[peer],
                    dst.at[me],
                    send.at[step - 1],
                    recv.at[step - 1],
                    "ctx",
                    place - me + peer,
                )
            )
            copies[-1].start()
        own = pltpu.make_async_copy(src.at[me], dst.at[me], local)
        own.start()
        yield
        for copy in copies:
            copy.wait()
            yield
        own.wait()


class Gather:
    def __init__(self, parts, shape, watched=False):
        self.parts, self.watched = parts, watched
        self.out = jax.ShapeDtypeStruct((parts,) + shape, LOW)
        chips = parts // 2
        self.scratch = [
            pltpu.SemaphoreType.DMA((2, chips)),
            pltpu.SemaphoreType.DMA((chips,)),
            pltpu.SemaphoreType.DMA((chips,)),
            pltpu.SemaphoreType.DMA((chips,)),
            pltpu.SemaphoreType.DMA,
        ]

    def run(self, src, dst, send, recv, pair_send, pair_recv, local):
        chips = self.parts // 2
        me = lax.axis_index("ctx")
        chip, core = me // 2, lax.rem(me, 2)
        partner = me + 1 - 2 * core

        def line(block, slot, origin, way):
            return remote(
                block, slot, send.at[way, origin], recv.at[origin], "ctx", me + 2 - 4 * way
            )

        def across(block, slot, origin):
            return remote(block, slot, pair_send.at[origin], pair_recv.at[origin], "ctx", partner)

        mine = dst.at[me]
        own = pltpu.make_async_copy(src, mine, local)

        def arrived(origin):
            other = dst.at[2 * origin + 1 - core]
            across(other, other, origin).wait_recv()

            @pl.when(origin == chip)
            def _():
                own.wait()

        self.dst, self.arrived = dst, arrived

        @pl.when(chip < chips - 1)
        def _():
            line(src, mine, chip, 0).start()

        @pl.when(chip > 0)
        def _():
            line(src, mine, chip, 1).start()

        across(src, mine, chip).start()
        own.start()
        yield
        if self.watched:
            yield
        for step in range(1, chips):
            for way in range(2):
                origin = chip - step if way == 0 else chip + step

                @pl.when((origin >= 0) & (origin < chips))
                def _():
                    slot = dst.at[2 * origin + core]
                    line(slot, slot, origin, way).wait_recv()

                    @pl.when((chip < chips - 1) if way == 0 else (chip > 0))
                    def _():
                        line(slot, slot, origin, way).start()

                    across(slot, slot, origin).start()

            yield
        for step in range(chips):
            for way in range(2):
                origin = chip - step if way == 0 else chip + step
                ahead = (chip < chips - 1) if way == 0 else (chip > 0)

                @pl.when((origin >= 0) & (origin < chips) & ahead)
                def _():
                    slot = dst.at[2 * origin + core]
                    line(slot, slot, origin, way).wait_send()

        for origin in range(chips):
            across(dst.at[2 * origin + core], dst.at[2 * origin + core], origin).wait_send()
            if not self.watched:
                arrived(origin)


class Scatter:
    cuts = 2

    def __init__(self, parts, shape):
        self.parts, self.shape = parts, shape
        self.out = jax.ShapeDtypeStruct(shape, jnp.float32)
        chips = parts // 2
        piece = (self.cuts, shape[0] // self.cuts, shape[1])
        self.scratch = [
            pltpu.VMEM((chips,) + shape, LOW),
            pltpu.VMEM((2, chips) + piece, LOW),
            pltpu.VMEM((chips,) + piece, LOW),
            pltpu.SemaphoreType.DMA((chips,)),
            pltpu.SemaphoreType.DMA((chips,)),
            pltpu.SemaphoreType.DMA((chips, self.cuts)),
            pltpu.SemaphoreType.DMA((2, chips, self.cuts)),
        ]

    def run(self, src, out, pair, come, stage, pair_send, pair_recv, send, recv):
        chips, cuts = self.parts // 2, self.cuts
        me = lax.axis_index("ctx")
        chip, core = me // 2, lax.rem(me, 2)
        partner = me + 1 - 2 * core
        rows = self.shape[0] // cuts
        slab = min(rows, 16)
        last = chips - 1

        def across(goal):
            return remote(
                src.at[2 * goal + 1 - core],
                pair.at[goal],
                pair_send.at[goal],
                pair_recv.at[goal],
                "ctx",
                partner,
            )

        def line(goal, cut, way):
            return remote(
                stage.at[goal, cut],
                come.at[way, goal, cut],
                send.at[goal, cut],
                recv.at[way, goal, cut],
                "ctx",
                me + 2 - 4 * way,
            )

        def wide(ref, *index):
            return ref[index].astype(jnp.float32)

        def slabs(part):
            def one(index, carry):
                part(pl.multiple_of(index * slab, slab))
                return carry

            lax.fori_loop(0, rows // slab, one, 0)

        def both(goal, cut, at):
            at = pl.ds(cut * rows + at, slab)
            return wide(src, 2 * goal + core, at) + wide(pair, goal, at)

        order = []
        for step in range((chips + 1) // 2):
            order += sorted({step, last - step})
        for goal in order:
            across(goal).start()
        yield
        for step in range(last * cuts):
            for way in range(2):
                turn = step - (chip if way == 0 else last - chip)
                goal = (last - turn // cuts) if way == 0 else turn // cuts
                cut = step - (chip if way == 0 else last - chip) - (turn // cuts) * cuts
                first = (chip == 0) if way == 0 else (chip == last)
                ahead = last - chip if way == 0 else chip

                def begin(at):
                    value = both(goal, cut, at)
                    stage[goal, cut, pl.ds(at, slab), :] = value.astype(LOW)

                def middle(at):
                    value = both(goal, cut, at) + wide(come, way, goal, cut, pl.ds(at, slab))
                    stage[goal, cut, pl.ds(at, slab), :] = value.astype(LOW)

                @pl.when((turn >= 0) & (turn < ahead * cuts))
                def _():
                    @pl.when(cut == 0)
                    def _():
                        across(goal).wait_recv()

                    @pl.when(first)
                    def _():
                        slabs(begin)

                    @pl.when(jnp.logical_not(first))
                    def _():
                        line(goal, cut, way).wait_recv()
                        slabs(middle)

                    line(goal, cut, way).start()

            yield
        across(chip).wait_recv()
        for cut in range(cuts):

            def own(at):
                out[pl.ds(cut * rows + at, slab), :] = both(chip, cut, at)

            slabs(own)
        yield
        for cut in range(cuts):
            for way in range(2):

                def final(at):
                    out[pl.ds(cut * rows + at, slab), :] += wide(
                        come, way, chip, cut, pl.ds(at, slab)
                    )

                @pl.when((chip > 0) if way == 0 else (chip < last))
                def _():
                    line(chip, cut, way).wait_recv()
                    slabs(final)

            yield
        for goal in range(chips):
            across(goal).wait_send()

            @pl.when(chip != goal)
            def _():
                for cut in range(cuts):
                    line(goal, cut, 0).wait_send()


class Spread:
    def __init__(self, parts, groups, shape):
        self.parts, self.groups = parts, groups
        self.out = jax.ShapeDtypeStruct((groups, parts) + shape, LOW)
        self.scratch = [
            pltpu.SemaphoreType.DMA((parts - 1,)),
            pltpu.SemaphoreType.DMA((parts - 1,)),
            pltpu.SemaphoreType.DMA((groups - 1, parts)),
            pltpu.SemaphoreType.DMA((groups - 1, parts)),
            pltpu.SemaphoreType.DMA,
        ]

    def run(self, src, dst, send, recv, far_send, far_recv, local):
        parts, groups = self.parts, self.groups
        me, group = lax.axis_index("ctx"), lax.axis_index("fsdp")
        copies = []
        for step in range(1, parts):
            peer = lax.rem(me + step, parts)
            copies.append(
                remote(
                    src.at[peer],
                    dst.at[group, me],
                    send.at[step - 1],
                    recv.at[step - 1],
                    "ctx",
                    peer,
                )
            )
            copies[-1].start()
        own = pltpu.make_async_copy(src.at[me], dst.at[group, me], local)
        own.start()

        def pass_on(block, origin, step):
            out = []
            for hop in range(1, groups):
                copy = remote(
                    block,
                    dst.at[group, origin],
                    far_send.at[hop - 1, step],
                    far_recv.at[hop - 1, step],
                    "fsdp",
                    lax.rem(group + hop, groups),
                )
                copy.start()
                out.append(copy)
            return out

        far = pass_on(src.at[me], me, 0)
        eager = -(-parts // 2)
        yield
        for step in range(1, parts):
            copies[step - 1].wait_recv()
            origin = lax.rem(me - step + parts, parts)
            far += pass_on(dst.at[group, origin], origin, step)
            if step % eager == 0:
                yield
        for at, copy in enumerate(far):
            copy.wait()
            if at % 6 == 5:
                yield
        for copy in copies:
            copy.wait_send()
        own.wait()


class Deliver:
    def __init__(self, parts, shape, offsets):
        self.parts, self.shape, self.offsets = parts, shape, offsets
        self.out = jax.ShapeDtypeStruct((shape[0], parts * shape[1]), jnp.float32)
        self.scratch = [
            pltpu.VMEM((parts - 1,) + shape, LOW),
            pltpu.SemaphoreType.DMA((parts - 1,)),
            pltpu.SemaphoreType.DMA((parts - 1,)),
        ]

    def place(self, out, origin, read):
        starts = self.offsets(origin)
        step = self.shape[1] // len(starts)
        for index, start in enumerate(starts):
            out[:, pl.ds(pl.multiple_of(start, HEAD_DIM), step)] = read(
                index * step, (index + 1) * step
            )

    def send(self, me, step, block, came, send, recv):
        return remote(
            block,
            came.at[step - 1],
            send.at[step - 1],
            recv.at[step - 1],
            "ctx",
            lax.rem(me + step, self.parts),
        )

    def run(self, src, out, came, send, recv):
        me = lax.axis_index("ctx")
        copies = []
        for step in range(1, self.parts):
            block = src.at[lax.rem(me + step, self.parts)]
            copies.append(self.send(me, step, block, came, send, recv))
            copies[-1].start()
        self.place(out, me, lambda lo, hi: src[me, :, lo:hi].astype(jnp.float32))
        yield
        yield from self.finish(me, out, copies, came)

    def finish(self, me, out, copies, came):
        for step in range(1, self.parts):
            copies[step - 1].wait_recv()
            origin = lax.rem(me - step + self.parts, self.parts)
            self.place(out, origin, lambda lo, hi: came[step - 1, :, lo:hi].astype(jnp.float32))
            yield
        for copy in copies:
            copy.wait_send()


class Collect(Deliver):
    def __init__(self, parts, groups, shape, offsets):
        super().__init__(parts, shape, offsets)
        self.groups = groups
        self.scratch = self.scratch + [
            pltpu.VMEM((groups - 1, parts) + shape, LOW),
            pltpu.VMEM((parts,) + shape, LOW),
            pltpu.VMEM(shape, jnp.float32),
            pltpu.SemaphoreType.DMA((groups - 1, parts)),
            pltpu.SemaphoreType.DMA((groups - 1, parts)),
        ]

    def run(self, src, out, came, send, recv, far, stage, mine, far_send, far_recv):
        parts, groups = self.parts, self.groups
        me, group = lax.axis_index("ctx"), lax.axis_index("fsdp")
        goals = [lax.rem(me + step, parts) for step in range(1, parts + 1)]
        hops = []
        for goal in goals:
            for hop in range(1, groups):
                peer = lax.rem(group + hop, groups)
                hops.append(
                    remote(
                        src.at[peer, goal],
                        far.at[hop - 1, goal],
                        far_send.at[hop - 1, goal],
                        far_recv.at[hop - 1, goal],
                        "fsdp",
                        peer,
                    )
                )
                hops[-1].start()
        yield
        copies = []
        for step in range(1, parts + 1):
            goal = goals[step - 1]
            for copy in hops[(step - 1) * (groups - 1) : step * (groups - 1)]:
                copy.wait_recv()
            value = src[group, goal].astype(jnp.float32)
            for hop in range(groups - 1):
                value += far[hop, goal].astype(jnp.float32)
            if step < parts:
                stage[goal] = value.astype(LOW)
                copies.append(self.send(me, step, stage.at[goal], came, send, recv))
                copies[-1].start()
            else:
                mine[...] = value
            yield
        self.place(out, me, lambda lo, hi: mine[:, lo:hi])
        yield from self.finish(me, out, copies, came)
        for copy in hops:
            copy.wait_send()


def call(jobs, operands, name, identity, axes, work=None, micros=50):
    counts = [len(job.scratch) for job in jobs]
    jobs_n = len(jobs)
    extra = work.operands if work else []
    extra_out = work.outs if work else []
    extra_scratch = work.scratch if work else []

    def kernel(*refs):
        refs = list(refs)

        def take(count):
            taken = refs[:count]
            del refs[:count]
            return taken

        ins, more = take(jobs_n), take(len(extra))
        outs, more_outs = take(jobs_n), take(len(extra_out))
        runs = []
        for job, src, dst, count in zip(jobs, ins, outs, counts):
            runs.append(job.run(src, dst, *take(count)))
        if work:
            runs.append(work.run(*more, *more_outs, *refs))
        enter(axes)
        while runs:
            going = []
            for run in runs:
                try:
                    next(run)
                    going.append(run)
                except StopIteration:
                    pass
            runs = going

    vmem = pl.BlockSpec(memory_space=pltpu.VMEM)
    anywhere = pl.BlockSpec(memory_space=pl.ANY)
    return pl.pallas_call(
        kernel,
        out_shape=tuple(job.out for job in jobs) + tuple(extra_out),
        in_specs=[vmem] * jobs_n + [anywhere] * len(extra),
        out_specs=(vmem,) * jobs_n + (anywhere,) * len(extra_out),
        scratch_shapes=[shape for job in jobs for shape in job.scratch] + list(extra_scratch),
        compiler_params=pltpu.CompilerParams(
            collective_id=identity, has_side_effects=True, vmem_limit_bytes=62 << 20
        ),
        cost_estimate=pl.CostEstimate(
            flops=0, bytes_accessed=micros * 3_000_000, transcendentals=0
        ),
        name=name,
    )(*operands, *extra)


class Grads:
    tile = 256

    def __init__(self, pairs):
        self.pairs = pairs
        length, wide = pairs[0][0].shape[0], max(right.shape[1] for _, right in pairs)
        self.operands = [array for pair in pairs for array in pair]
        self.outs = [jax.ShapeDtypeStruct((l.shape[1], r.shape[1]), LOW) for l, r in pairs]
        self.scratch = [pltpu.VMEM(array.shape, LOW) for array in self.operands]
        self.scratch += [
            pltpu.VMEM((self.tile, length), LOW),
            pltpu.VMEM((2, self.tile, wide), LOW),
            pltpu.SemaphoreType.DMA((2 * len(pairs),)),
            pltpu.SemaphoreType.DMA((2,)),
        ]

    def run(self, *refs):
        n, tile = len(self.pairs), self.tile
        sources, outs = refs[: 2 * n], refs[2 * n : 3 * n]
        held = refs[3 * n : 5 * n]
        turned, made, get, put = refs[5 * n :]
        gets = [pltpu.make_async_copy(s, h, get.at[i]) for i, (s, h) in enumerate(zip(sources, held))]
        for copy in gets:
            copy.start()
        yield
        puts = []
        for which in range(n):
            left, right, out = held[2 * which], held[2 * which + 1], outs[which]
            gets[2 * which].wait()
            gets[2 * which + 1].wait()
            columns = right.shape[1]
            step = min(columns, 512)
            for at in range(0, left.shape[1], tile):
                slot = len(puts) % 2
                if len(puts) >= 2:
                    puts[-2].wait()
                turned[...] = left[:, at : at + tile].T

                def one(index, carry):
                    where = pl.ds(pl.multiple_of(index * step, step), step)
                    made[slot, :, where] = jnp.dot(
                        turned[...], right[:, where], preferred_element_type=jnp.float32
                    ).astype(LOW)
                    return carry

                lax.fori_loop(0, columns // step, one, 0)
                part = made.at[slot] if columns == made.shape[2] else made.at[slot, :, :columns]
                puts.append(pltpu.make_async_copy(part, out.at[at : at + tile, :], put.at[slot]))
                puts[-1].start()
                yield
        for copy in puts[-2:]:
            copy.wait()


def product(left, right):
    return jnp.dot(left, right, preferred_element_type=jnp.float32)


class Puts:
    def __init__(self, made, put):
        self.made, self.put, self.copies = made, put, []

    def buffer(self):
        if len(self.copies) >= 2:
            self.copies[-2].wait()
        return self.made.at[len(self.copies) % 2]

    def send(self, source, target):
        copy = pltpu.make_async_copy(source, target, self.put.at[len(self.copies) % 2])
        copy.start()
        self.copies.append(copy)

    def finish(self):
        for copy in self.copies[-2:]:
            copy.wait()


def softmax_block(query, keys, ok):
    scores = times_transposed(query, keys) * HEAD_DIM ** (-0.5)
    scores = jnp.where(ok, scores, -1e30)
    weights = jnp.exp(scores - jnp.max(scores, axis=-1, keepdims=True))
    weights = jnp.where(ok, weights, 0.0)
    return weights, jnp.sum(weights, axis=-1, keepdims=True)


class Attend:
    tile = 256

    def __init__(self, rows, weight, tables, heads):
        self.heads = heads
        self.operands = [rows, weight] + list(tables)
        length, wide = rows.shape[0], weight.shape[1]
        self.outs = [
            jax.ShapeDtypeStruct((length, wide), LOW),
            jax.ShapeDtypeStruct((length, wide // 3), LOW),
        ]
        self.scratch = [pltpu.VMEM(array.shape, array.dtype) for array in self.operands]
        self.scratch += [pltpu.VMEM(out.shape, out.dtype) for out in self.outs]
        self.scratch += [
            pltpu.SemaphoreType.DMA((len(self.operands),)),
            pltpu.SemaphoreType.DMA((2,)),
        ]

    def run(self, *refs):
        n, tile, heads = len(self.operands), self.tile, self.heads
        sources, results, held = refs[:n], refs[n : n + 2], refs[n + 2 : 2 * n + 2]
        qkv, mix, get, put = refs[2 * n + 2 :]
        rows, weight, cosine, sine, first, last, keys = held
        gets = [pltpu.make_async_copy(s, h, get.at[i]) for i, (s, h) in enumerate(zip(sources, held))]
        for copy in gets:
            copy.start()
        yield
        for copy in gets:
            copy.wait()
        width = heads * HEAD_DIM

        def project(index, carry):
            at = pl.ds(pl.multiple_of(index * tile, tile), tile)
            value = product(rows[at, :], weight[...])
            for head in range(3 * heads):
                block = value[:, head * HEAD_DIM : (head + 1) * HEAD_DIM]
                if head < 2 * heads:
                    turned = pltpu.roll(block, HEAD_DIM // 2, 1)
                    block = block * cosine[at, :] + turned * sine[at, :]
                qkv[at, head * HEAD_DIM : (head + 1) * HEAD_DIM] = block.astype(LOW)
            return carry

        lax.fori_loop(0, rows.shape[0] // tile, project, 0)
        send = pltpu.make_async_copy(qkv, results[0], put.at[0])
        send.start()
        yield

        def attend(index, carry):
            at = pl.ds(pl.multiple_of(index * tile, tile), tile)
            ok = (keys[:1, :] >= first[at, :1]) & (keys[:1, :] <= last[at, :1])
            for head in range(heads):
                lo = head * HEAD_DIM
                weights, total = softmax_block(
                    qkv[at, lo : lo + HEAD_DIM], qkv[:, width + lo : width + lo + HEAD_DIM], ok
                )
                value = qkv[:, 2 * width + lo : 2 * width + lo + HEAD_DIM]
                mixed = product(weights.astype(LOW), value) / total
                mix[at, lo : lo + HEAD_DIM] = mixed.astype(LOW)
            return carry

        lax.fori_loop(0, rows.shape[0] // tile, attend, 0)
        send_mix = pltpu.make_async_copy(mix, results[1], put.at[1])
        send_mix.start()
        yield
        send.wait()
        send_mix.wait()


class AttendBack:
    tile = 256

    def __init__(self, upstream, out_rows, qkv, rows, weight, tables, heads):
        self.heads = heads
        self.operands = [upstream, out_rows, qkv, weight] + list(tables) + [rows]
        length, wide, width = rows.shape[0], weight.shape[1], rows.shape[1]
        self.outs = [
            jax.ShapeDtypeStruct((length, width), LOW),
            jax.ShapeDtypeStruct((width, wide), LOW),
        ]
        self.scratch = [pltpu.VMEM(array.shape, array.dtype) for array in self.operands[:-1]]
        self.scratch += [
            pltpu.VMEM((length, wide // 3), LOW),
            pltpu.VMEM((length, wide), LOW),
            pltpu.VMEM((2, length, HEAD_DIM), jnp.float32),
            pltpu.VMEM((2, self.tile, width), LOW),
            pltpu.SemaphoreType.DMA((len(self.operands),)),
            pltpu.SemaphoreType.DMA((2,)),
        ]

    def run(self, *refs):
        n, tile, heads = len(self.operands), self.tile, self.heads
        sources, results, held = refs[:n], refs[n : n + 2], refs[n + 2 : 2 * n + 1]
        back, grads, sums, made, get, put = refs[2 * n + 1 :]
        upstream, out_rows, qkv, weight, cosine, sine, first, last, keys = held
        length, width = back.shape
        gets = [pltpu.make_async_copy(s, h, get.at[i]) for i, (s, h) in enumerate(zip(sources, held))]
        for copy in gets:
            copy.start()
        yield
        for copy in gets:
            copy.wait()

        def project(index, carry):
            at = pl.ds(pl.multiple_of(index * tile, tile), tile)
            back[at, :] = times_transposed(upstream[at, :], out_rows[...]).astype(LOW)
            return carry

        lax.fori_loop(0, length // tile, project, 0)
        rows = upstream
        fetch = pltpu.make_async_copy(sources[n - 1], rows, get.at[n - 1])
        fetch.start()
        yield

        def unrotated(value, at):
            return value * cosine[at, :] - pltpu.roll(value, HEAD_DIM // 2, 1) * sine[at, :]

        for head in range(heads):
            lo = head * HEAD_DIM
            mine = slice(lo, lo + HEAD_DIM)
            key = slice(width + lo, width + lo + HEAD_DIM)
            val = slice(2 * width + lo, 2 * width + lo + HEAD_DIM)
            sums[...] = jnp.zeros_like(sums)

            def attend(index, carry):
                at = pl.ds(pl.multiple_of(index * tile, tile), tile)
                ok = (keys[:1, :] >= first[at, :1]) & (keys[:1, :] <= last[at, :1])
                weights, total = softmax_block(qkv[at, mine], qkv[:, key], ok)
                probs = weights / total
                upper = back[at, mine]
                prob_back = times_transposed(upper, qkv[:, val])
                delta = jnp.sum(probs * prob_back, axis=-1, keepdims=True)
                score_back = HEAD_DIM ** (-0.5) * probs * (prob_back - delta)
                score_low = score_back.astype(LOW)
                query_back = product(score_low, qkv[:, key])
                grads[at, mine] = unrotated(query_back, at).astype(LOW)
                sums[0] += product(score_low.T, qkv[at, mine])
                sums[1] += product(probs.astype(LOW).T, upper)
                return carry

            half = max(1, length // tile // 2)
            for begin in range(0, length // tile, half):
                lax.fori_loop(begin, begin + half, attend, 0)
                yield

            def settle(index, carry):
                at = pl.ds(pl.multiple_of(index * tile, tile), tile)
                grads[at, key] = unrotated(sums[0, at, :], at).astype(LOW)
                grads[at, val] = sums[1, at, :].astype(LOW)
                return carry

            lax.fori_loop(0, length // tile, settle, 0)
        puts = Puts(made, put)
        for at in range(0, length, tile):
            buffer = puts.buffer()
            buffer[...] = times_transposed(grads[at : at + tile, :], weight[...]).astype(LOW)
            puts.send(buffer, results[0].at[at : at + tile, :])
            yield
        fetch.wait()
        wide = grads.shape[1]
        for at in range(0, rows.shape[1], tile):
            buffer = puts.buffer().at[:, :wide]
            buffer[...] = product(rows[:, at : at + tile].T, grads[...]).astype(LOW)
            puts.send(buffer, results[1].at[at : at + tile, :])
            yield
        puts.finish()


def near_first(chips):
    table = []
    for chip in range(chips):
        order = [chip]
        for step in range(1, chips):
            order += [at for at in (chip + step, chip - step) if 0 <= at < chips]
        table.append(order)
    return table


class FeedForward:
    def __init__(self, job, upstream, gate_up, down):
        self.job = job
        self.operands = [upstream, gate_up, down]
        length, width = upstream.shape
        wide = gate_up.shape[1]
        self.outs = [
            jax.ShapeDtypeStruct((length, wide // 2), LOW),
            jax.ShapeDtypeStruct((length, wide), LOW),
            jax.ShapeDtypeStruct((length, width), LOW),
        ]
        self.tile = length // (job.parts // 2)
        self.scratch = [pltpu.VMEM(array.shape, array.dtype) for array in self.operands]
        self.scratch += [pltpu.VMEM((2, self.tile) + out.shape[1:], LOW) for out in self.outs]
        self.scratch += [pltpu.SemaphoreType.DMA((3,)), pltpu.SemaphoreType.DMA((3, 2))]

    def run(self, *refs):
        job, tile = self.job, self.tile
        sources, results, held, made = refs[:3], refs[3:6], refs[6:9], refs[9:12]
        get, put = refs[12:]
        upstream, gate_up, down = held
        acts, backs, terms = made
        rows = tile // 2
        width, wide = gate_up.shape
        units = wide // 2
        step = min(units, 256)
        span = min(width, 512)
        chip = lax.axis_index("ctx") // 2
        gets = [pltpu.make_async_copy(sources[i], held[i], get.at[i]) for i in (1, 2, 0)]
        for copy in gets:
            copy.start()
        yield
        for copy in gets:
            copy.wait()
        table = near_first(job.parts // 2)
        puts = []
        for turn in range(len(table)):
            origin = sum(jnp.where(chip == at, order[turn], 0) for at, order in enumerate(table))
            slot = turn % 2
            if turn >= 2:
                for copy in puts[turn - 2]:
                    copy.wait()
            job.arrived(origin)
            at = pl.ds(pl.multiple_of(origin * tile, tile), tile)
            normed = job.dst.at[pl.ds(2 * origin, 2)]

            def forward(index, carry):
                left = pl.ds(pl.multiple_of(index * step, step), step)
                right = pl.ds(pl.multiple_of(units + index * step, step), step)
                value = normed[...].reshape(tile, width)
                gate = product(value, gate_up[:, left])
                up = product(value, gate_up[:, right])
                act_grad = times_transposed(upstream[at, :], down[left, :])
                sigmoid = jax.nn.sigmoid(gate)
                silu = gate * sigmoid
                acts[slot, :, left] = (silu * up).astype(LOW)
                gate_grad = act_grad * up * sigmoid * (1.0 + gate * (1.0 - sigmoid))
                backs[slot, :, left] = gate_grad.astype(LOW)
                backs[slot, :, right] = (act_grad * silu).astype(LOW)
                return carry

            lax.fori_loop(0, units // step, forward, 0)

            def backward(index, carry):
                where = pl.ds(pl.multiple_of(index * span, span), span)
                value = times_transposed(backs[slot], gate_up[where, :])
                terms[slot, :, where] = value.astype(LOW)
                return carry

            lax.fori_loop(0, width // span, backward, 0)
            puts.append(
                [
                    pltpu.make_async_copy(made[i].at[slot], results[i].at[at, :], put.at[i, slot])
                    for i in range(3)
                ]
            )
            for copy in puts[-1]:
                copy.start()
            yield
        for copies in puts[-2:]:
            for copy in copies:
                copy.wait()


class Plan:
    def __init__(self, parts, groups, width):
        self.parts, self.groups = parts, groups
        self.shard = width // (parts * groups)
        self.run = HEAD_DIM // self.shard
        self.heads = HEADS // parts
        self.qkv_dims = (3, self.run, self.heads, parts // self.run, HEAD_DIM)

    def qkv_pieces(self, weight):
        rows = weight.shape[0]
        pieces = weight.reshape((rows,) + self.qkv_dims).transpose(4, 2, 0, 1, 3, 5)
        return pieces.reshape(self.parts, rows, 3 * self.heads * HEAD_DIM)

    def qkv_starts(self, part):
        at, index = part // self.run, lax.rem(part, self.run)
        return [
            (kind * HEADS + (index * self.heads + head) * (self.parts // self.run) + at) * HEAD_DIM
            for kind in range(3)
            for head in range(self.heads)
        ]

    def unit_pieces(self, weight):
        rows, columns = weight.shape
        inner = columns // (2 * self.groups * self.parts)
        pieces = weight.reshape(rows, 2 * self.groups, self.parts, inner).transpose(2, 0, 1, 3)
        return pieces.reshape(self.parts, rows, 2 * self.groups * inner)

    def unit_job(self, shape):
        step = shape[1] // (2 * self.groups)
        if step % HEAD_DIM:
            return Exchange(self.parts, shape)
        return Deliver(
            self.parts,
            shape,
            lambda part: [(at * self.parts + part) * step for at in range(2 * self.groups)],
        )

    def unit_rows(self, pieces):
        if pieces.ndim == 2:
            return pieces
        parts, rows, columns = pieces.shape
        outer = 2 * self.groups
        pieces = pieces.reshape(parts, rows, outer, columns // outer).transpose(1, 2, 0, 3)
        return pieces.reshape(rows, parts * columns).astype(jnp.float32)


def per_device(tokens, w_qkv, w_out, w_gate_up, w_down, seq_lengths, block_order, cotangent):
    lengths = seq_lengths[0]
    order_row = block_order[0]
    parts = lax.axis_size("ctx")
    groups = lax.axis_size("fsdp")
    rows, width = tokens.shape
    length = rows * parts
    plan = Plan(parts, groups, width)
    heads, shard, run = plan.heads, plan.shard, plan.run
    head_width = heads * HEAD_DIM
    line = (("ctx", parts),)
    plane = (("ctx", parts), ("fsdp", groups))
    block = (rows, width)

    out_rows = gather(w_out, "fsdp")
    down_rows = gather(w_down, "fsdp")
    gate_up_pieces = plan.unit_pieces(w_gate_up)
    inputs = tokens.astype(jnp.float32)
    normed_in, root_in = normalize(inputs)
    qkv_pieces = plan.qkv_pieces(w_qkv)
    qkv_cols, normed_in_full = call(
        [Spread(parts, groups, qkv_pieces.shape[1:]), Gather(parts, block)],
        [qkv_pieces, normed_in.astype(LOW)],
        "start",
        2,
        plane,
        micros=70,
    )
    qkv_cols = qkv_cols.reshape(width, 3 * head_width)
    normed_in_full = normed_in_full.reshape(length, width)

    row_index = jnp.arange(length, dtype=jnp.int32)
    packed = initial_index(row_index, order_row)
    _, pos = places(packed, lengths)
    cosine_table, sine_table = angle_tables(pos)
    half_sign = jnp.where(jnp.arange(HEAD_DIM) < HEAD_DIM // 2, -1.0, 1.0)
    tables = (
        cosine_table[:, 0, :],
        sine_table[:, 0, :] * half_sign,
        jnp.broadcast_to((packed - pos)[:, None], (length, HEAD_DIM)),
        jnp.broadcast_to(packed[:, None], (length, HEAD_DIM)),
        jnp.broadcast_to(packed[None, :], (8, length)),
    )
    gate_up_cols, out_cols, qkv_low, mix_low = call(
        [Exchange(parts, gate_up_pieces.shape[1:]), Exchange(run, (heads * shard, width))],
        [gate_up_pieces, out_rows.reshape(run, heads * shard, width)],
        "attend",
        1,
        line,
        Attend(normed_in_full, qkv_cols, tables, heads),
        micros=55,
    )
    gate_up_cols, down_rows = lax.optimization_barrier((gate_up_cols, down_rows))
    gate_up_cols = gather(gate_up_cols.reshape(width // groups, -1), "fsdp")
    out_cols = out_cols.reshape(run, heads, shard, width).transpose(1, 0, 2, 3)
    out_cols = out_cols.reshape(head_width, width)

    out_terms = dot(mix_low, out_cols).astype(LOW)
    attn_out, cot_full = call(
        [Scatter(parts, block), Gather(parts, block)],
        [out_terms.reshape((parts,) + block), cotangent],
        "out",
        3,
        line,
        micros=64,
    )
    cot_full = cot_full.reshape(length, width)
    residual = inputs + attn_out
    normed_mid, root_mid = normalize(residual)
    mid_job = Gather(parts, block, watched=True)
    normed_mid_full, activated, gate_up_back, mid_back_terms = call(
        [mid_job],
        [normed_mid.astype(LOW)],
        "mid",
        4,
        line,
        FeedForward(mid_job, cot_full, gate_up_cols, down_rows),
        micros=60,
    )
    normed_mid_full = normed_mid_full.reshape(length, width)
    down_grad = scatter(column_product(activated, cot_full).astype(LOW), "fsdp").astype(jnp.float32)
    mid_back, gate_up_grad = call(
        [Scatter(parts, block)],
        [mid_back_terms.reshape((parts,) + block)],
        "mid_back",
        5,
        line,
        Grads([(normed_mid_full, gate_up_back)]),
    )
    gate_up_grad, down_grad = lax.optimization_barrier((gate_up_grad, down_grad))
    gate_up_grad = scatter(gate_up_grad, "fsdp")
    residual_back = cotangent.astype(jnp.float32) + norm_back(mid_back, normed_mid, root_mid)
    proj_back = residual_back.astype(LOW)

    down_terms = dot(activated, down_rows).astype(LOW)
    (proj_back_full,) = call([Gather(parts, block)], [proj_back], "proj_back", 6, line, micros=45)
    proj_back_full = proj_back_full.reshape(length, width)
    out_grad = column_product(mix_low, proj_back_full).astype(LOW)
    out_grad = out_grad.reshape(heads, run, shard, width).transpose(1, 0, 2, 3)
    down_out, out_grad, in_back_terms, qkv_grad = call(
        [Scatter(parts, block), Exchange(run, (heads * shard, width))],
        [down_terms.reshape((parts,) + block), out_grad.reshape(run, heads * shard, width)],
        "attend_back",
        8,
        line,
        AttendBack(proj_back_full, out_cols, qkv_low, normed_in_full, qkv_cols, tables, heads),
        micros=60,
    )
    layer_out = (residual + down_out).astype(LOW)
    out_grad, gate_up_grad = lax.optimization_barrier((out_grad, gate_up_grad))
    out_grad = scatter(out_grad.reshape(groups * shard, width), "fsdp").astype(jnp.float32)
    in_back, qkv_grad, gate_up_grad = call(
        [
            Scatter(parts, block),
            Collect(parts, groups, qkv_pieces.shape[1:], plan.qkv_starts),
            plan.unit_job(gate_up_pieces.shape[1:]),
        ],
        [
            in_back_terms.reshape((parts,) + block),
            qkv_grad.reshape((groups,) + qkv_pieces.shape),
            gate_up_grad.reshape(gate_up_pieces.shape),
        ],
        "in_back",
        7,
        plane,
        micros=90,
    )
    tokens_grad = residual_back + norm_back(in_back, normed_in, root_in)
    return (
        layer_out,
        tokens_grad,
        qkv_grad,
        out_grad,
        plan.unit_rows(gate_up_grad),
        down_grad,
    )


def solution(mesh):
    both = P(("fsdp", "ctx"), None)
    one = P("fsdp", None)
    return jax.shard_map(
        per_device,
        mesh=mesh,
        in_specs=(both, both, both, both, both, one, one, both),
        out_specs=(both,) * 6,
        check_vma=False,
    )
```

```python
import jax
import jax.numpy as jnp
from jax import lax
from jax.experimental import pallas as pl
from jax.experimental.pallas import tpu as pltpu
from jax.sharding import PartitionSpec as P

HEADS = 16
HEAD_DIM = 128
BLOCK = 128
LOW = jnp.bfloat16


def normalize(values):
    average = jnp.mean(values, axis=-1, keepdims=True)
    centered = values - average
    variance = jnp.mean(centered * centered, axis=-1, keepdims=True)
    inv_root = lax.rsqrt(variance + 1e-05)
    return (centered * inv_root, inv_root)


def norm_back(upstream, normed, inv_root):
    first_mean = jnp.mean(upstream, axis=-1, keepdims=True)
    second_mean = jnp.mean(upstream * normed, axis=-1, keepdims=True)
    return inv_root * (upstream - first_mean - normed * second_mean)


def places(token_index, lengths):
    seq_ends = jnp.cumsum(lengths)
    sequence = jnp.sum((token_index[:, None] >= seq_ends[None, :]).astype(jnp.int32), axis=1)
    before = jnp.arange(lengths.shape[0], dtype=jnp.int32)
    seq_start = jnp.sum(jnp.where(before[None, :] < sequence[:, None], lengths[None, :], 0), axis=1)
    return (sequence, token_index - seq_start)


def initial_index(row_index, order_row):
    slot_index = row_index // BLOCK
    slot_table = jnp.arange(order_row.shape[0], dtype=jnp.int32)
    picked = jnp.sum(
        jnp.where(slot_table[None, :] == slot_index[:, None], order_row[None, :], 0), axis=1
    )
    return picked * BLOCK + row_index % BLOCK


def angle_tables(position):
    half_dim = HEAD_DIM // 2
    frequency = 10000.0 ** (-jnp.arange(half_dim, dtype=jnp.float32) * 2.0 / HEAD_DIM)
    angle_table = position.astype(jnp.float32)[:, None] * frequency[None, :]
    angle_table = jnp.concatenate([angle_table, angle_table], axis=-1)
    return (jnp.cos(angle_table)[:, None, :], jnp.sin(angle_table)[:, None, :])


def rotate(values, cosine_table, sine_table):
    half_dim = values.shape[-1] // 2
    turned = jnp.concatenate([-values[..., half_dim:], values[..., :half_dim]], axis=-1)
    return values * cosine_table + turned * sine_table


def unrotate(values, cosine_table, sine_table):
    half_dim = values.shape[-1] // 2
    scaled = values * sine_table
    turned = jnp.concatenate([scaled[..., half_dim:], -scaled[..., :half_dim]], axis=-1)
    return values * cosine_table + turned


def dot(left, right):
    return jnp.dot(left, right, preferred_element_type=jnp.float32)


def times_transposed(left, right):
    return lax.dot_general(
        left, right, (((1,), (1,)), ((), ())), preferred_element_type=jnp.float32
    )


def column_product(left, right):
    return lax.dot_general(
        left, right, (((0,), (0,)), ((), ())), preferred_element_type=jnp.float32
    )


def gather(values, axes):
    return lax.all_gather(values, axes, axis=0, tiled=True)


def scatter(values, axes):
    return lax.psum_scatter(values, axes, scatter_dimension=0, tiled=True)


def enter(axes):
    barrier = pltpu.get_barrier_semaphore()
    count = 0
    for axis, size in axes:
        me = lax.axis_index(axis)
        for step in range(1, size):
            pl.semaphore_signal(barrier, inc=1, device_id={axis: lax.rem(me + step, size)})
        count += size - 1
    pl.semaphore_wait(barrier, count)


def remote(src, dst, send, recv, axis, peer):
    return pltpu.make_async_remote_copy(
        src_ref=src, dst_ref=dst, send_sem=send, recv_sem=recv, device_id={axis: peer}
    )


class Exchange:
    def __init__(self, parts, shape):
        self.parts = parts
        self.out = jax.ShapeDtypeStruct((parts,) + shape, LOW)
        self.scratch = [
            pltpu.SemaphoreType.DMA((parts - 1,)),
            pltpu.SemaphoreType.DMA((parts - 1,)),
            pltpu.SemaphoreType.DMA,
        ]

    def run(self, src, dst, send, recv, local):
        place = lax.axis_index("ctx")
        me = lax.rem(place, self.parts)
        copies = []
        for step in range(1, self.parts):
            peer = lax.rem(me + step, self.parts)
            copies.append(
                remote(
                    src.at[peer],
                    dst.at[me],
                    send.at[step - 1],
                    recv.at[step - 1],
                    "ctx",
                    place - me + peer,
                )
            )
            copies[-1].start()
        own = pltpu.make_async_copy(src.at[me], dst.at[me], local)
        own.start()
        yield
        for copy in copies:
            copy.wait()
            yield
        own.wait()


class Gather:
    def __init__(self, parts, shape, watched=False, cuts=2):
        self.parts, self.watched, self.shape, self.cuts = parts, watched, shape, cuts
        self.out = jax.ShapeDtypeStruct((parts,) + shape, LOW)
        chips = parts // 2
        self.scratch = [
            pltpu.SemaphoreType.DMA((2, chips, self.cuts)),
            pltpu.SemaphoreType.DMA((chips, self.cuts)),
            pltpu.SemaphoreType.DMA((chips, self.cuts)),
            pltpu.SemaphoreType.DMA((chips, self.cuts)),
            pltpu.SemaphoreType.DMA,
        ]

    def run(self, src, dst, send, recv, pair_send, pair_recv, local):
        chips, cuts = self.parts // 2, self.cuts
        rows = self.shape[0] // cuts
        me = lax.axis_index("ctx")
        chip, core = me // 2, lax.rem(me, 2)
        partner = me + 1 - 2 * core

        def piece(block, cut):
            return block.at[pl.ds(cut * rows, rows)]

        def line(block, slot, origin, way, cut):
            return remote(
                piece(block, cut),
                piece(slot, cut),
                send.at[way, origin, cut],
                recv.at[origin, cut],
                "ctx",
                me + 2 - 4 * way,
            )

        def across(block, slot, origin, cut):
            return remote(
                piece(block, cut),
                piece(slot, cut),
                pair_send.at[origin, cut],
                pair_recv.at[origin, cut],
                "ctx",
                partner,
            )

        mine = dst.at[me]
        own = pltpu.make_async_copy(src, mine, local)

        def arrived(origin):
            other = dst.at[2 * origin + 1 - core]
            for cut in range(cuts):
                across(other, other, origin, cut).wait_recv()

            @pl.when(origin == chip)
            def _():
                own.wait()

        def relay(step):
            for cut in range(cuts):
                for way in range(2):
                    origin = chip - step if way == 0 else chip + step

                    @pl.when((origin >= 0) & (origin < chips))
                    def _():
                        slot = dst.at[2 * origin + core]
                        line(slot, slot, origin, way, cut).wait_recv()

                        @pl.when((chip < chips - 1) if way == 0 else (chip > 0))
                        def _():
                            line(slot, slot, origin, way, cut).start()

                        across(slot, slot, origin, cut).start()

        self.dst, self.arrived, self.relay = dst, arrived, relay
        for cut in range(cuts):

            @pl.when(chip < chips - 1)
            def _():
                line(src, mine, chip, 0, cut).start()

            @pl.when(chip > 0)
            def _():
                line(src, mine, chip, 1, cut).start()

        for cut in range(cuts):
            across(src, mine, chip, cut).start()
        own.start()
        yield
        if self.watched:
            yield
        for step in range(1, chips):
            if not self.watched:
                relay(step)
                yield
        for step in range(chips):
            for way in range(2):
                origin = chip - step if way == 0 else chip + step
                ahead = (chip < chips - 1) if way == 0 else (chip > 0)

                @pl.when((origin >= 0) & (origin < chips) & ahead)
                def _():
                    slot = dst.at[2 * origin + core]
                    for cut in range(cuts):
                        line(slot, slot, origin, way, cut).wait_send()

        for origin in range(chips):
            slot = dst.at[2 * origin + core]
            for cut in range(cuts):
                across(slot, slot, origin, cut).wait_send()
            if not self.watched:
                arrived(origin)


class Scatter:
    def __init__(self, parts, shape, cuts=2):
        self.parts, self.shape, self.cuts = parts, shape, cuts
        self.out = jax.ShapeDtypeStruct(shape, jnp.float32)
        chips = parts // 2
        piece = (self.cuts, shape[0] // self.cuts, shape[1])
        self.scratch = [
            pltpu.VMEM((chips,) + shape, LOW),
            pltpu.VMEM((2, chips) + piece, LOW),
            pltpu.VMEM((chips,) + piece, LOW),
            pltpu.SemaphoreType.DMA((chips,)),
            pltpu.SemaphoreType.DMA((chips,)),
            pltpu.SemaphoreType.DMA((chips, self.cuts)),
            pltpu.SemaphoreType.DMA((2, chips, self.cuts)),
        ]

    def run(self, src, out, pair, come, stage, pair_send, pair_recv, send, recv):
        chips, cuts = self.parts // 2, self.cuts
        me = lax.axis_index("ctx")
        chip, core = me // 2, lax.rem(me, 2)
        partner = me + 1 - 2 * core
        rows = self.shape[0] // cuts
        slab = min(rows, 16)
        last = chips - 1

        def across(goal):
            return remote(
                src.at[2 * goal + 1 - core],
                pair.at[goal],
                pair_send.at[goal],
                pair_recv.at[goal],
                "ctx",
                partner,
            )

        def line(goal, cut, way):
            return remote(
                stage.at[goal, cut],
                come.at[way, goal, cut],
                send.at[goal, cut],
                recv.at[way, goal, cut],
                "ctx",
                me + 2 - 4 * way,
            )

        def wide(ref, *index):
            return ref[index].astype(jnp.float32)

        def slabs(part):
            def one(index, carry):
                part(pl.multiple_of(index * slab, slab))
                return carry

            lax.fori_loop(0, rows // slab, one, 0)

        def both(goal, cut, at):
            at = pl.ds(cut * rows + at, slab)
            return wide(src, 2 * goal + core, at) + wide(pair, goal, at)

        order = []
        for step in range((chips + 1) // 2):
            order += sorted({step, last - step})
        for goal in order:
            across(goal).start()
        yield
        for step in range(last * cuts):
            for way in range(2):
                turn = step - (chip if way == 0 else last - chip)
                goal = (last - turn // cuts) if way == 0 else turn // cuts
                cut = step - (chip if way == 0 else last - chip) - (turn // cuts) * cuts
                first = (chip == 0) if way == 0 else (chip == last)
                ahead = last - chip if way == 0 else chip

                def begin(at):
                    value = both(goal, cut, at)
                    stage[goal, cut, pl.ds(at, slab), :] = value.astype(LOW)

                def middle(at):
                    value = both(goal, cut, at) + wide(come, way, goal, cut, pl.ds(at, slab))
                    stage[goal, cut, pl.ds(at, slab), :] = value.astype(LOW)

                @pl.when((turn >= 0) & (turn < ahead * cuts))
                def _():
                    @pl.when(cut == 0)
                    def _():
                        across(goal).wait_recv()

                    @pl.when(first)
                    def _():
                        slabs(begin)

                    @pl.when(jnp.logical_not(first))
                    def _():
                        line(goal, cut, way).wait_recv()
                        slabs(middle)

                    line(goal, cut, way).start()

            yield
        across(chip).wait_recv()
        for cut in range(cuts):

            def own(at):
                out[pl.ds(cut * rows + at, slab), :] = both(chip, cut, at)

            slabs(own)
        yield
        for cut in range(cuts):
            for way in range(2):

                def final(at):
                    out[pl.ds(cut * rows + at, slab), :] += wide(
                        come, way, chip, cut, pl.ds(at, slab)
                    )

                @pl.when((chip > 0) if way == 0 else (chip < last))
                def _():
                    line(chip, cut, way).wait_recv()
                    slabs(final)

            yield
        for goal in range(chips):
            across(goal).wait_send()

            @pl.when(chip != goal)
            def _():
                for cut in range(cuts):
                    line(goal, cut, 0).wait_send()


class Spread:
    def __init__(self, parts, groups, shape):
        self.parts, self.groups = parts, groups
        self.out = jax.ShapeDtypeStruct((groups, parts) + shape, LOW)
        self.scratch = [
            pltpu.SemaphoreType.DMA((parts - 1,)),
            pltpu.SemaphoreType.DMA((parts - 1,)),
            pltpu.SemaphoreType.DMA((groups - 1, parts)),
            pltpu.SemaphoreType.DMA((groups - 1, parts)),
            pltpu.SemaphoreType.DMA,
        ]

    def run(self, src, dst, send, recv, far_send, far_recv, local):
        parts, groups = self.parts, self.groups
        me, group = lax.axis_index("ctx"), lax.axis_index("fsdp")
        copies = []
        for step in range(1, parts):
            peer = lax.rem(me + step, parts)
            copies.append(
                remote(
                    src.at[peer],
                    dst.at[group, me],
                    send.at[step - 1],
                    recv.at[step - 1],
                    "ctx",
                    peer,
                )
            )
            copies[-1].start()
        own = pltpu.make_async_copy(src.at[me], dst.at[group, me], local)
        own.start()

        def pass_on(block, origin, step):
            out = []
            for hop in range(1, groups):
                copy = remote(
                    block,
                    dst.at[group, origin],
                    far_send.at[hop - 1, step],
                    far_recv.at[hop - 1, step],
                    "fsdp",
                    lax.rem(group + hop, groups),
                )
                copy.start()
                out.append(copy)
            return out

        far = pass_on(src.at[me], me, 0)
        eager = -(-parts // 2)
        yield
        for step in range(1, parts):
            copies[step - 1].wait_recv()
            origin = lax.rem(me - step + parts, parts)
            far += pass_on(dst.at[group, origin], origin, step)
            if step % eager == 0:
                yield
        for at, copy in enumerate(far):
            copy.wait()
            if at % 6 == 5:
                yield
        for copy in copies:
            copy.wait_send()
        own.wait()


class Deliver:
    def __init__(self, parts, shape, offsets):
        self.parts, self.shape, self.offsets = parts, shape, offsets
        self.out = jax.ShapeDtypeStruct((shape[0], parts * shape[1]), jnp.float32)
        self.scratch = [
            pltpu.VMEM((parts - 1,) + shape, LOW),
            pltpu.SemaphoreType.DMA((parts - 1,)),
            pltpu.SemaphoreType.DMA((parts - 1,)),
        ]

    def place(self, out, origin, read):
        starts = self.offsets(origin)
        step = self.shape[1] // len(starts)
        for index, start in enumerate(starts):
            out[:, pl.ds(pl.multiple_of(start, HEAD_DIM), step)] = read(
                index * step, (index + 1) * step
            )

    def send(self, me, step, block, came, send, recv):
        return remote(
            block,
            came.at[step - 1],
            send.at[step - 1],
            recv.at[step - 1],
            "ctx",
            lax.rem(me + step, self.parts),
        )

    def run(self, src, out, came, send, recv):
        me = lax.axis_index("ctx")
        copies = []
        for step in range(1, self.parts):
            block = src.at[lax.rem(me + step, self.parts)]
            copies.append(self.send(me, step, block, came, send, recv))
            copies[-1].start()
        self.place(out, me, lambda lo, hi: src[me, :, lo:hi].astype(jnp.float32))
        yield
        yield from self.finish(me, out, copies, came)

    def finish(self, me, out, copies, came):
        for step in range(1, self.parts):
            copies[step - 1].wait_recv()
            origin = lax.rem(me - step + self.parts, self.parts)
            self.place(out, origin, lambda lo, hi: came[step - 1, :, lo:hi].astype(jnp.float32))
            yield
        for copy in copies:
            copy.wait_send()


class Collect(Deliver):
    def __init__(self, parts, groups, shape, offsets):
        super().__init__(parts, shape, offsets)
        self.groups = groups
        self.scratch = self.scratch + [
            pltpu.VMEM((groups - 1, parts) + shape, LOW),
            pltpu.VMEM((parts,) + shape, LOW),
            pltpu.VMEM(shape, jnp.float32),
            pltpu.SemaphoreType.DMA((groups - 1, parts)),
            pltpu.SemaphoreType.DMA((groups - 1, parts)),
        ]

    def run(self, src, out, came, send, recv, far, stage, mine, far_send, far_recv):
        parts, groups = self.parts, self.groups
        me, group = lax.axis_index("ctx"), lax.axis_index("fsdp")
        goals = [lax.rem(me + step, parts) for step in range(1, parts + 1)]
        hops = []
        for goal in goals:
            for hop in range(1, groups):
                peer = lax.rem(group + hop, groups)
                hops.append(
                    remote(
                        src.at[peer, goal],
                        far.at[hop - 1, goal],
                        far_send.at[hop - 1, goal],
                        far_recv.at[hop - 1, goal],
                        "fsdp",
                        peer,
                    )
                )
                hops[-1].start()
        yield
        copies = []
        for step in range(1, parts + 1):
            goal = goals[step - 1]
            for copy in hops[(step - 1) * (groups - 1) : step * (groups - 1)]:
                copy.wait_recv()
            value = src[group, goal].astype(jnp.float32)
            for hop in range(groups - 1):
                value += far[hop, goal].astype(jnp.float32)
            if step < parts:
                stage[goal] = value.astype(LOW)
                copies.append(self.send(me, step, stage.at[goal], came, send, recv))
                copies[-1].start()
            else:
                mine[...] = value
            yield
        self.place(out, me, lambda lo, hi: mine[:, lo:hi])
        yield from self.finish(me, out, copies, came)
        for copy in hops:
            copy.wait_send()


def call(jobs, operands, name, identity, axes, work=None, micros=50):
    counts = [len(job.scratch) for job in jobs]
    jobs_n = len(jobs)
    extra = work.operands if work else []
    extra_out = work.outs if work else []
    extra_scratch = work.scratch if work else []

    def kernel(*refs):
        refs = list(refs)

        def take(count):
            taken = refs[:count]
            del refs[:count]
            return taken

        ins, more = take(jobs_n), take(len(extra))
        outs, more_outs = take(jobs_n), take(len(extra_out))
        runs = []
        for job, src, dst, count in zip(jobs, ins, outs, counts):
            runs.append(job.run(src, dst, *take(count)))
        if work:
            runs.append(work.run(*more, *more_outs, *refs))
        enter(axes)
        while runs:
            going = []
            for run in runs:
                try:
                    next(run)
                    going.append(run)
                except StopIteration:
                    pass
            runs = going

    vmem = pl.BlockSpec(memory_space=pltpu.VMEM)
    anywhere = pl.BlockSpec(memory_space=pl.ANY)
    return pl.pallas_call(
        kernel,
        out_shape=tuple(job.out for job in jobs) + tuple(extra_out),
        in_specs=[vmem] * jobs_n + [anywhere] * len(extra),
        out_specs=(vmem,) * jobs_n + (anywhere,) * len(extra_out),
        scratch_shapes=[shape for job in jobs for shape in job.scratch] + list(extra_scratch),
        compiler_params=pltpu.CompilerParams(
            collective_id=identity, has_side_effects=True, vmem_limit_bytes=62 << 20
        ),
        cost_estimate=pl.CostEstimate(
            flops=0, bytes_accessed=micros * 3_000_000, transcendentals=0
        ),
        name=name,
    )(*operands, *extra)


def product(left, right):
    return jnp.dot(left, right, preferred_element_type=jnp.float32)


class Puts:
    def __init__(self, made, put):
        self.made, self.put, self.copies = made, put, []

    def pair(self, fill, columns, out, at, tile):
        for copy in self.copies:
            copy.wait()
        lax.fori_loop(0, 2, fill, 0)
        self.copies = []
        for half in range(2):
            begin = at + half * tile
            copy = pltpu.make_async_copy(
                self.made.at[half, :, pl.ds(0, columns)],
                out.at[begin : begin + tile, :],
                self.put.at[half],
            )
            copy.start()
            self.copies.append(copy)

    def finish(self):
        for copy in self.copies:
            copy.wait()


class Grads:
    tile = 256

    def __init__(self, pairs):
        self.pairs = pairs
        length, wide = pairs[0][0].shape[0], max(right.shape[1] for _, right in pairs)
        self.operands = [array for pair in pairs for array in pair]
        self.outs = [jax.ShapeDtypeStruct((l.shape[1], r.shape[1]), LOW) for l, r in pairs]
        self.scratch = [pltpu.VMEM(array.shape, LOW) for array in self.operands]
        self.scratch += [
            pltpu.VMEM((self.tile, length), LOW),
            pltpu.VMEM((2, self.tile, wide), LOW),
            pltpu.SemaphoreType.DMA((2 * len(pairs),)),
            pltpu.SemaphoreType.DMA((2,)),
        ]

    def run(self, *refs):
        n, tile = len(self.pairs), self.tile
        sources, outs = refs[: 2 * n], refs[2 * n : 3 * n]
        held = refs[3 * n : 5 * n]
        turned, made, get, put = refs[5 * n :]
        gets = [pltpu.make_async_copy(s, h, get.at[i]) for i, (s, h) in enumerate(zip(sources, held))]
        for copy in gets:
            copy.start()
        yield
        puts = Puts(made, put)
        for which in range(n):
            left, right, out = held[2 * which], held[2 * which + 1], outs[which]
            gets[2 * which].wait()
            gets[2 * which + 1].wait()
            columns = right.shape[1]
            step = min(columns, 256)
            for at in range(0, left.shape[1], 2 * tile):
                def pair(half, carry):
                    begin = pl.multiple_of(at + half * tile, tile)
                    turned[...] = left[:, pl.ds(begin, tile)].T

                    def one(index, carry):
                        where = pl.ds(pl.multiple_of(index * step, step), step)
                        made[half, :, where] = product(turned[...], right[:, where]).astype(LOW)
                        return carry

                    return lax.fori_loop(0, columns // step, one, carry)

                puts.pair(pair, columns, out, at, tile)
                yield
        puts.finish()


class Deliver:
    def __init__(self, parts, shape, offsets):
        self.parts, self.shape, self.offsets = parts, shape, offsets
        self.out = jax.ShapeDtypeStruct((shape[0], parts * shape[1]), jnp.float32)
        self.scratch = [
            pltpu.VMEM((parts - 1,) + shape, LOW),
            pltpu.SemaphoreType.DMA((parts - 1,)),
            pltpu.SemaphoreType.DMA((parts - 1,)),
        ]

    def place(self, out, origin, read):
        starts = self.offsets(origin)
        step = self.shape[1] // len(starts)
        for index, start in enumerate(starts):
            out[:, pl.ds(pl.multiple_of(start, HEAD_DIM), step)] = read(
                index * step, (index + 1) * step
            )

    def send(self, me, step, block, came, send, recv):
        return remote(
            block,
            came.at[step - 1],
            send.at[step - 1],
            recv.at[step - 1],
            "ctx",
            lax.rem(me + step, self.parts),
        )

    def run(self, src, out, came, send, recv):
        me = lax.axis_index("ctx")
        copies = []
        for step in range(1, self.parts):
            block = src.at[lax.rem(me + step, self.parts)]
            copies.append(self.send(me, step, block, came, send, recv))
            copies[-1].start()
        self.place(out, me, lambda lo, hi: src[me, :, lo:hi].astype(jnp.float32))
        yield
        yield from self.finish(me, out, copies, came)

    def finish(self, me, out, copies, came):
        for step in range(1, self.parts):
            copies[step - 1].wait_recv()
            origin = lax.rem(me - step + self.parts, self.parts)
            self.place(out, origin, lambda lo, hi: came[step - 1, :, lo:hi].astype(jnp.float32))
            yield
        for copy in copies:
            copy.wait_send()


class Collect(Deliver):
    def __init__(self, parts, groups, shape, offsets):
        super().__init__(parts, shape, offsets)
        self.groups = groups
        self.scratch = self.scratch + [
            pltpu.VMEM((groups - 1, parts) + shape, LOW),
            pltpu.VMEM((parts,) + shape, LOW),
            pltpu.VMEM(shape, jnp.float32),
            pltpu.SemaphoreType.DMA((groups - 1, parts)),
            pltpu.SemaphoreType.DMA((groups - 1, parts)),
        ]

    def run(self, src, out, came, send, recv, far, stage, mine, far_send, far_recv):
        parts, groups = self.parts, self.groups
        me, group = lax.axis_index("ctx"), lax.axis_index("fsdp")
        goals = [lax.rem(me + step, parts) for step in range(1, parts + 1)]
        hops = []
        for goal in goals:
            for hop in range(1, groups):
                peer = lax.rem(group + hop, groups)
                hops.append(
                    remote(
                        src.at[peer, goal],
                        far.at[hop - 1, goal],
                        far_send.at[hop - 1, goal],
                        far_recv.at[hop - 1, goal],
                        "fsdp",
                        peer,
                    )
                )
                hops[-1].start()
        yield
        copies = []
        for step in range(1, parts + 1):
            goal = goals[step - 1]
            for copy in hops[(step - 1) * (groups - 1) : step * (groups - 1)]:
                copy.wait_recv()
            value = src[group, goal].astype(jnp.float32)
            for hop in range(groups - 1):
                value += far[hop, goal].astype(jnp.float32)
            if step < parts:
                stage[goal] = value.astype(LOW)
                copies.append(self.send(me, step, stage.at[goal], came, send, recv))
                copies[-1].start()
            else:
                mine[...] = value
            yield
        self.place(out, me, lambda lo, hi: mine[:, lo:hi])
        yield from self.finish(me, out, copies, came)
        for copy in hops:
            copy.wait_send()


def call(jobs, operands, name, identity, axes, work=None, micros=50):
    counts = [len(job.scratch) for job in jobs]
    jobs_n = len(jobs)
    extra = work.operands if work else []
    extra_out = work.outs if work else []
    extra_scratch = work.scratch if work else []

    def kernel(*refs):
        refs = list(refs)

        def take(count):
            taken = refs[:count]
            del refs[:count]
            return taken

        ins, more = take(jobs_n), take(len(extra))
        outs, more_outs = take(jobs_n), take(len(extra_out))
        runs = []
        for job, src, dst, count in zip(jobs, ins, outs, counts):
            runs.append(job.run(src, dst, *take(count)))
        if work:
            runs.append(work.run(*more, *more_outs, *refs))
        enter(axes)
        while runs:
            going = []
            for run in runs:
                try:
                    next(run)
                    going.append(run)
                except StopIteration:
                    pass
            runs = going

    vmem = pl.BlockSpec(memory_space=pltpu.VMEM)
    anywhere = pl.BlockSpec(memory_space=pl.ANY)
    return pl.pallas_call(
        kernel,
        out_shape=tuple(job.out for job in jobs) + tuple(extra_out),
        in_specs=[vmem] * jobs_n + [anywhere] * len(extra),
        out_specs=(vmem,) * jobs_n + (anywhere,) * len(extra_out),
        scratch_shapes=[shape for job in jobs for shape in job.scratch] + list(extra_scratch),
        compiler_params=pltpu.CompilerParams(
            collective_id=identity, has_side_effects=True, vmem_limit_bytes=62 << 20
        ),
        cost_estimate=pl.CostEstimate(
            flops=0, bytes_accessed=micros * 3_000_000, transcendentals=0
        ),
        name=name,
    )(*operands, *extra)


class Grads:
    tile = 256

    def __init__(self, pairs):
        self.pairs = pairs
        length, wide = pairs[0][0].shape[0], max(right.shape[1] for _, right in pairs)
        self.operands = [array for pair in pairs for array in pair]
        self.outs = [jax.ShapeDtypeStruct((l.shape[1], r.shape[1]), LOW) for l, r in pairs]
        self.scratch = [pltpu.VMEM(array.shape, LOW) for array in self.operands]
        self.scratch += [
            pltpu.VMEM((self.tile, length), LOW),
            pltpu.VMEM((2, self.tile, wide), LOW),
            pltpu.SemaphoreType.DMA((2 * len(pairs),)),
            pltpu.SemaphoreType.DMA((2,)),
        ]

    def run(self, *refs):
        n, tile = len(self.pairs), self.tile
        sources, outs = refs[: 2 * n], refs[2 * n : 3 * n]
        held = refs[3 * n : 5 * n]
        turned, made, get, put = refs[5 * n :]
        gets = [pltpu.make_async_copy(s, h, get.at[i]) for i, (s, h) in enumerate(zip(sources, held))]
        for copy in gets:
            copy.start()
        yield
        puts = []
        for which in range(n):
            left, right, out = held[2 * which], held[2 * which + 1], outs[which]
            gets[2 * which].wait()
            gets[2 * which + 1].wait()
            columns = right.shape[1]
            step = min(columns, 512)
            for at in range(0, left.shape[1], tile):
                slot = len(puts) % 2
                if len(puts) >= 2:
                    puts[-2].wait()
                turned[...] = left[:, at : at + tile].T

                def one(index, carry):
                    where = pl.ds(pl.multiple_of(index * step, step), step)
                    made[slot, :, where] = jnp.dot(
                        turned[...], right[:, where], preferred_element_type=jnp.float32
                    ).astype(LOW)
                    return carry

                lax.fori_loop(0, columns // step, one, 0)
                part = made.at[slot] if columns == made.shape[2] else made.at[slot, :, :columns]
                puts.append(pltpu.make_async_copy(part, out.at[at : at + tile, :], put.at[slot]))
                puts[-1].start()
                yield
        for copy in puts[-2:]:
            copy.wait()


def softmax_block(query, keys, ok):
    scores = times_transposed(query, keys) * HEAD_DIM ** (-0.5)
    scores = jnp.where(ok, scores, -1e30)
    weights = jnp.exp(scores - jnp.max(scores, axis=-1, keepdims=True))
    weights = jnp.where(ok, weights, 0.0)
    return weights, jnp.sum(weights, axis=-1, keepdims=True)


class Attend:
    tile = 256

    def __init__(self, rows, weight, tables, heads):
        self.heads = heads
        self.operands = [rows, weight] + list(tables)
        length, wide = rows.shape[0], weight.shape[1]
        self.outs = [
            jax.ShapeDtypeStruct((length, wide), LOW),
            jax.ShapeDtypeStruct((length, wide // 3), LOW),
        ]
        self.scratch = [pltpu.VMEM(array.shape, array.dtype) for array in self.operands]
        self.scratch += [pltpu.VMEM(out.shape, out.dtype) for out in self.outs]
        self.scratch += [
            pltpu.SemaphoreType.DMA((len(self.operands),)),
            pltpu.SemaphoreType.DMA((2,)),
        ]

    def run(self, *refs):
        n, tile, heads = len(self.operands), self.tile, self.heads
        sources, results, held = refs[:n], refs[n : n + 2], refs[n + 2 : 2 * n + 2]
        qkv, mix, get, put = refs[2 * n + 2 :]
        rows, weight, cosine, sine, first, last, keys = held
        gets = [pltpu.make_async_copy(s, h, get.at[i]) for i, (s, h) in enumerate(zip(sources, held))]
        for copy in gets:
            copy.start()
        yield
        for copy in gets:
            copy.wait()
        width = heads * HEAD_DIM

        def project(index, carry):
            at = pl.ds(pl.multiple_of(index * tile, tile), tile)
            value = product(rows[at, :], weight[...])
            for head in range(3 * heads):
                block = value[:, head * HEAD_DIM : (head + 1) * HEAD_DIM]
                if head < 2 * heads:
                    turned = pltpu.roll(block, HEAD_DIM // 2, 1)
                    block = block * cosine[at, :] + turned * sine[at, :]
                qkv[at, head * HEAD_DIM : (head + 1) * HEAD_DIM] = block.astype(LOW)
            return carry

        lax.fori_loop(0, rows.shape[0] // tile, project, 0)
        send = pltpu.make_async_copy(qkv, results[0], put.at[0])
        send.start()
        yield

        def attend(index, carry):
            at = pl.ds(pl.multiple_of(index * tile, tile), tile)
            ok = (keys[:1, :] >= first[at, :1]) & (keys[:1, :] <= last[at, :1])
            for head in range(heads):
                lo = head * HEAD_DIM
                weights, total = softmax_block(
                    qkv[at, lo : lo + HEAD_DIM], qkv[:, width + lo : width + lo + HEAD_DIM], ok
                )
                value = qkv[:, 2 * width + lo : 2 * width + lo + HEAD_DIM]
                mixed = product(weights.astype(LOW), value) / total
                mix[at, lo : lo + HEAD_DIM] = mixed.astype(LOW)
            return carry

        lax.fori_loop(0, rows.shape[0] // tile, attend, 0)
        send_mix = pltpu.make_async_copy(mix, results[1], put.at[1])
        send_mix.start()
        yield
        send.wait()
        send_mix.wait()


class AttendBack:
    tile = 256

    def __init__(self, upstream, out_rows, qkv, rows, weight, tables, heads):
        self.heads = heads
        self.operands = [upstream, out_rows, qkv, weight] + list(tables) + [rows]
        length, wide, width = rows.shape[0], weight.shape[1], rows.shape[1]
        self.outs = [
            jax.ShapeDtypeStruct((length, width), LOW),
            jax.ShapeDtypeStruct((width, wide), LOW),
        ]
        self.scratch = [pltpu.VMEM(array.shape, array.dtype) for array in self.operands[:-1]]
        self.scratch += [
            pltpu.VMEM((length, wide // 3), LOW),
            pltpu.VMEM((length, wide), LOW),
            pltpu.VMEM((2, length, HEAD_DIM), jnp.float32),
            pltpu.VMEM((self.tile, length), LOW),
            pltpu.VMEM((2, self.tile, width), LOW),
            pltpu.SemaphoreType.DMA((len(self.operands),)),
            pltpu.SemaphoreType.DMA((2,)),
        ]

    def run(self, *refs):
        n, tile, heads = len(self.operands), self.tile, self.heads
        sources, results, held = refs[:n], refs[n : n + 2], refs[n + 2 : 2 * n + 1]
        back, grads, sums, turned, made, get, put = refs[2 * n + 1 :]
        upstream, out_rows, qkv, weight, cosine, sine, first, last, keys = held
        length, width = back.shape
        gets = [pltpu.make_async_copy(s, h, get.at[i]) for i, (s, h) in enumerate(zip(sources, held))]
        for copy in gets:
            copy.start()
        yield
        for copy in gets:
            copy.wait()

        def project(index, carry):
            at = pl.ds(pl.multiple_of(index * tile, tile), tile)
            back[at, :] = times_transposed(upstream[at, :], out_rows[...]).astype(LOW)
            return carry

        lax.fori_loop(0, length // tile, project, 0)
        rows = upstream
        fetch = pltpu.make_async_copy(sources[n - 1], rows, get.at[n - 1])
        fetch.start()
        yield

        def unrotated(value, at):
            return value * cosine[at, :] - pltpu.roll(value, HEAD_DIM // 2, 1) * sine[at, :]

        for head in range(heads):
            lo = head * HEAD_DIM
            mine = slice(lo, lo + HEAD_DIM)
            key = slice(width + lo, width + lo + HEAD_DIM)
            val = slice(2 * width + lo, 2 * width + lo + HEAD_DIM)
            sums[...] = jnp.zeros_like(sums)

            def attend(index, carry):
                at = pl.ds(pl.multiple_of(index * tile, tile), tile)
                ok = (keys[:1, :] >= first[at, :1]) & (keys[:1, :] <= last[at, :1])
                weights, total = softmax_block(qkv[at, mine], qkv[:, key], ok)
                probs = weights / total
                upper = back[at, mine]
                prob_back = times_transposed(upper, qkv[:, val])
                delta = jnp.sum(probs * prob_back, axis=-1, keepdims=True)
                score_back = HEAD_DIM ** (-0.5) * probs * (prob_back - delta)
                score_low = score_back.astype(LOW)
                query_back = product(score_low, qkv[:, key])
                grads[at, mine] = unrotated(query_back, at).astype(LOW)
                sums[0] += product(score_low.T, qkv[at, mine])
                sums[1] += product(probs.astype(LOW).T, upper)
                return carry

            lax.fori_loop(0, length // tile, attend, 0)
            yield

            def settle(index, carry):
                at = pl.ds(pl.multiple_of(index * tile, tile), tile)
                grads[at, key] = unrotated(sums[0, at, :], at).astype(LOW)
                grads[at, val] = sums[1, at, :].astype(LOW)
                return carry

            lax.fori_loop(0, length // tile, settle, 0)
        puts = Puts(made, put)
        wide = grads.shape[1]
        part = tile if wide % tile == 0 else HEAD_DIM
        for at in range(0, length, 2 * tile):

            def terms(half, carry):
                where = pl.ds(pl.multiple_of(at + half * tile, tile), tile)

                def one(index, carry):
                    span = pl.ds(pl.multiple_of(index * tile, tile), tile)
                    value = times_transposed(grads[where, :], weight[span, :])
                    made[half, :, span] = value.astype(LOW)
                    return carry

                return lax.fori_loop(0, made.shape[2] // tile, one, carry)

            puts.pair(terms, made.shape[2], results[0], at, tile)
            yield
        fetch.wait()
        for at in range(0, rows.shape[1], 2 * tile):

            def weights(half, carry):
                where = pl.ds(pl.multiple_of(at + half * tile, tile), tile)
                turned[...] = rows[:, where].T

                def one(index, carry):
                    span = pl.ds(pl.multiple_of(index * part, part), part)
                    made[half, :, span] = product(turned[...], grads[:, span]).astype(LOW)
                    return carry

                return lax.fori_loop(0, wide // part, one, carry)

            puts.pair(weights, wide, results[1], at, tile)
            yield
        puts.finish()


def near_first(chips):
    table = []
    for chip in range(chips):
        order = [chip]
        for step in range(1, chips):
            order += [at for at in (chip + step, chip - step) if 0 <= at < chips]
        table.append(order)
    return table


class FeedForward:
    def __init__(self, job, upstream, gate, up, down):
        self.job = job
        self.operands = [upstream, gate, up, down]
        length, width = upstream.shape
        units = gate.shape[1]
        self.outs = [
            jax.ShapeDtypeStruct((length, units), LOW),
            jax.ShapeDtypeStruct((length, 2 * units), LOW),
            jax.ShapeDtypeStruct((length, width), LOW),
        ]
        self.tile = length // (job.parts // 2)
        self.scratch = [pltpu.VMEM(array.shape, array.dtype) for array in self.operands]
        self.scratch += [pltpu.VMEM((2, self.tile) + out.shape[1:], LOW) for out in self.outs]
        self.scratch += [pltpu.SemaphoreType.DMA((4,)), pltpu.SemaphoreType.DMA((3, 2))]

    def run(self, *refs):
        job, tile = self.job, self.tile
        sources, results, held, made = refs[:4], refs[4:7], refs[7:11], refs[11:14]
        get, put = refs[14:]
        upstream, gate_w, up_w, down = held
        acts, backs, terms = made
        width, units = gate_w.shape
        step = min(units, 256)
        span = min(width, 512)
        chip = lax.axis_index("ctx") // 2
        gets = [pltpu.make_async_copy(sources[i], held[i], get.at[i]) for i in (1, 2, 3, 0)]
        for copy in gets:
            copy.start()
        yield
        for copy in gets:
            copy.wait()
        table = near_first(job.parts // 2)
        chips = len(table)

        def leave(slot, origin):
            at = pl.ds(pl.multiple_of(origin * tile, tile), tile)
            return [
                pltpu.make_async_copy(made[i].at[slot], results[i].at[at, :], put.at[i, slot])
                for i in range(3)
            ]

        def one_chip(turn, carry):
            origin = sum(
                jnp.where((chip == at) & (turn == when), order[when], 0)
                for at, order in enumerate(table)
                for when in range(chips)
            )
            slot = lax.rem(turn, 2)

            @pl.when(turn > 0)
            def _():
                job.relay(turn)

            @pl.when(turn >= 2)
            def _():
                for copy in leave(slot, 0):
                    copy.wait()

            job.arrived(origin)
            at = pl.ds(pl.multiple_of(origin * tile, tile), tile)
            normed = job.dst.at[pl.ds(2 * origin, 2)]

            def forward(index, carry):
                left = pl.ds(pl.multiple_of(index * step, step), step)
                right = pl.ds(pl.multiple_of(units + index * step, step), step)
                value = normed[...].reshape(tile, width)
                gate = product(value, gate_w[:, left])
                up = product(value, up_w[:, left])
                act_grad = times_transposed(upstream[at, :], down[left, :])
                sigmoid = jax.nn.sigmoid(gate)
                silu = gate * sigmoid
                acts[slot, :, left] = (silu * up).astype(LOW)
                gate_grad = act_grad * up * sigmoid * (1.0 + gate * (1.0 - sigmoid))
                backs[slot, :, left] = gate_grad.astype(LOW)
                backs[slot, :, right] = (act_grad * silu).astype(LOW)
                return carry

            lax.fori_loop(0, units // step, forward, 0)

            def backward(index, carry):
                where = pl.ds(pl.multiple_of(index * span, span), span)
                value = times_transposed(backs[slot, :, :units], gate_w[where, :])
                value += times_transposed(backs[slot, :, units:], up_w[where, :])
                terms[slot, :, where] = value.astype(LOW)
                return carry

            lax.fori_loop(0, width // span, backward, 0)
            for copy in leave(slot, origin):
                copy.start()
            return carry

        lax.fori_loop(0, chips, one_chip, 0)
        for slot in range(min(2, chips)):
            for copy in leave(slot, 0):
                copy.wait()


class Plan:
    def __init__(self, parts, groups, width):
        self.parts, self.groups = parts, groups
        self.shard = width // (parts * groups)
        self.run = HEAD_DIM // self.shard
        self.heads = HEADS // parts
        self.qkv_dims = (3, self.run, self.heads, parts // self.run, HEAD_DIM)

    def qkv_pieces(self, weight):
        rows = weight.shape[0]
        pieces = weight.reshape((rows,) + self.qkv_dims).transpose(4, 2, 0, 1, 3, 5)
        return pieces.reshape(self.parts, rows, 3 * self.heads * HEAD_DIM)

    def qkv_starts(self, part):
        at, index = part // self.run, lax.rem(part, self.run)
        return [
            (kind * HEADS + (index * self.heads + head) * (self.parts // self.run) + at) * HEAD_DIM
            for kind in range(3)
            for head in range(self.heads)
        ]

    def unit_pieces(self, weight):
        rows, columns = weight.shape
        inner = columns // (2 * self.groups * self.parts)
        pieces = weight.reshape(rows, 2 * self.groups, self.parts, inner).transpose(2, 0, 1, 3)
        return pieces.reshape(self.parts, rows, 2 * self.groups * inner)

    def unit_job(self, shape):
        step = shape[1] // (2 * self.groups)
        if step % HEAD_DIM:
            return Exchange(self.parts, shape)
        return Deliver(
            self.parts,
            shape,
            lambda part: [(at * self.parts + part) * step for at in range(2 * self.groups)],
        )

    def unit_rows(self, pieces):
        if pieces.ndim == 2:
            return pieces
        parts, rows, columns = pieces.shape
        outer = 2 * self.groups
        pieces = pieces.reshape(parts, rows, outer, columns // outer).transpose(1, 2, 0, 3)
        return pieces.reshape(rows, parts * columns).astype(jnp.float32)


def per_device(tokens, w_qkv, w_out, w_gate_up, w_down, seq_lengths, block_order, cotangent):
    lengths = seq_lengths[0]
    order_row = block_order[0]
    parts = lax.axis_size("ctx")
    groups = lax.axis_size("fsdp")
    rows, width = tokens.shape
    length = rows * parts
    plan = Plan(parts, groups, width)
    heads, shard, run = plan.heads, plan.shard, plan.run
    head_width = heads * HEAD_DIM
    line = (("ctx", parts),)
    plane = (("ctx", parts), ("fsdp", groups))
    block = (rows, width)

    out_rows = gather(w_out, "fsdp")
    down_rows = gather(w_down, "fsdp")
    gate_up_pieces = plan.unit_pieces(w_gate_up)
    unit_columns = gate_up_pieces.shape[2] // 2
    unit_shape = (w_gate_up.shape[0], unit_columns)
    inputs = tokens.astype(jnp.float32)
    normed_in, root_in = normalize(inputs)
    qkv_pieces = plan.qkv_pieces(w_qkv)
    qkv_cols, normed_in_full, gate_cols = call(
        [
            Spread(parts, groups, qkv_pieces.shape[1:]),
            Gather(parts, block, cuts=1),
            Exchange(parts, unit_shape),
        ],
        [qkv_pieces, normed_in.astype(LOW), gate_up_pieces[:, :, :unit_columns]],
        "start",
        2,
        plane,
        micros=90,
    )
    gate_cols = gather(gate_cols.reshape(width // groups, -1), "fsdp")
    qkv_cols = qkv_cols.reshape(width, 3 * head_width)
    normed_in_full = normed_in_full.reshape(length, width)

    row_index = jnp.arange(length, dtype=jnp.int32)
    packed = initial_index(row_index, order_row)
    _, pos = places(packed, lengths)
    cosine_table, sine_table = angle_tables(pos)
    half_sign = jnp.where(jnp.arange(HEAD_DIM) < HEAD_DIM // 2, -1.0, 1.0)
    tables = (
        cosine_table[:, 0, :],
        sine_table[:, 0, :] * half_sign,
        jnp.broadcast_to((packed - pos)[:, None], (length, HEAD_DIM)),
        jnp.broadcast_to(packed[:, None], (length, HEAD_DIM)),
        jnp.broadcast_to(packed[None, :], (8, length)),
    )
    up_cols, out_cols, qkv_low, mix_low = call(
        [Exchange(parts, unit_shape), Exchange(run, (heads * shard, width))],
        [gate_up_pieces[:, :, unit_columns:], out_rows.reshape(run, heads * shard, width)],
        "attend",
        1,
        line,
        Attend(normed_in_full, qkv_cols, tables, heads),
        micros=40,
    )
    up_cols = gather(up_cols.reshape(width // groups, -1), "fsdp")
    out_cols = out_cols.reshape(run, heads, shard, width).transpose(1, 0, 2, 3)
    out_cols = out_cols.reshape(head_width, width)

    out_terms = dot(mix_low, out_cols).astype(LOW)
    attn_out, cot_full = call(
        [Scatter(parts, block, cuts=1), Gather(parts, block, cuts=1)],
        [out_terms.reshape((parts,) + block), cotangent],
        "out",
        3,
        line,
        micros=64,
    )
    cot_full = cot_full.reshape(length, width)
    residual = inputs + attn_out
    normed_mid, root_mid = normalize(residual)
    mid_job = Gather(parts, block, watched=True)
    normed_mid_full, activated, gate_up_back, mid_back_terms = call(
        [mid_job],
        [normed_mid.astype(LOW)],
        "mid",
        4,
        line,
        FeedForward(mid_job, cot_full, gate_cols, up_cols, down_rows),
        micros=60,
    )
    normed_mid_full = normed_mid_full.reshape(length, width)
    mid_back, gate_up_grad, down_grad = call(
        [Scatter(parts, block)],
        [mid_back_terms.reshape((parts,) + block)],
        "mid_back",
        5,
        line,
        Grads([(normed_mid_full, gate_up_back), (activated, cot_full)]),
    )
    gate_up_grad = scatter(gate_up_grad, "fsdp")
    down_grad = scatter(down_grad, "fsdp")
    residual_back = cotangent.astype(jnp.float32) + norm_back(mid_back, normed_mid, root_mid)
    proj_back = residual_back.astype(LOW)

    down_terms = dot(activated, down_rows).astype(LOW)
    (proj_back_full,) = call([Gather(parts, block)], [proj_back], "proj_back", 6, line, micros=45)
    proj_back_full = proj_back_full.reshape(length, width)
    out_grad = column_product(mix_low, proj_back_full).astype(LOW)
    out_grad = out_grad.reshape(heads, run, shard, width).transpose(1, 0, 2, 3)
    down_out, out_grad, in_back_terms, qkv_grad = call(
        [Scatter(parts, block), Exchange(run, (heads * shard, width))],
        [down_terms.reshape((parts,) + block), out_grad.reshape(run, heads * shard, width)],
        "attend_back",
        8,
        line,
        AttendBack(proj_back_full, out_cols, qkv_low, normed_in_full, qkv_cols, tables, heads),
        micros=60,
    )
    layer_out = (residual + down_out).astype(LOW)
    out_grad, gate_up_grad = lax.optimization_barrier((out_grad, gate_up_grad))
    out_grad = scatter(out_grad.reshape(groups * shard, width), "fsdp")
    in_back, qkv_grad, gate_up_grad = call(
        [
            Scatter(parts, block),
            Collect(parts, groups, qkv_pieces.shape[1:], plan.qkv_starts),
            plan.unit_job(gate_up_pieces.shape[1:]),
        ],
        [
            in_back_terms.reshape((parts,) + block),
            qkv_grad.reshape((groups,) + qkv_pieces.shape),
            gate_up_grad.reshape(gate_up_pieces.shape),
        ],
        "in_back",
        7,
        plane,
        micros=90,
    )
    in_back, down_grad, out_grad = lax.optimization_barrier((in_back, down_grad, out_grad))
    tokens_grad = residual_back + norm_back(in_back, normed_in, root_in)
    return (
        layer_out,
        tokens_grad,
        qkv_grad,
        out_grad.astype(jnp.float32),
        plan.unit_rows(gate_up_grad),
        down_grad.astype(jnp.float32),
    )


def solution(mesh):
    both = P(("fsdp", "ctx"), None)
    one = P("fsdp", None)
    return jax.shard_map(
        per_device,
        mesh=mesh,
        in_specs=(both, both, both, both, both, one, one, both),
        out_specs=(both,) * 6,
        check_vma=False,
    )
```

```python
import jax
import jax.numpy as jnp
from jax import lax
from jax.experimental import pallas as pl
from jax.experimental.pallas import tpu as pltpu
from jax.sharding import PartitionSpec as P

HEADS = 16
HEAD_DIM = 128
BLOCK = 128
LOW = jnp.bfloat16


def normalize(values):
    average = jnp.mean(values, axis=-1, keepdims=True)
    centered = values - average
    variance = jnp.mean(centered * centered, axis=-1, keepdims=True)
    inv_root = lax.rsqrt(variance + 1e-05)
    return (centered * inv_root, inv_root)


def norm_back(upstream, normed, inv_root):
    first_mean = jnp.mean(upstream, axis=-1, keepdims=True)
    second_mean = jnp.mean(upstream * normed, axis=-1, keepdims=True)
    return inv_root * (upstream - first_mean - normed * second_mean)


def places(token_index, lengths):
    seq_ends = jnp.cumsum(lengths)
    sequence = jnp.sum((token_index[:, None] >= seq_ends[None, :]).astype(jnp.int32), axis=1)
    before = jnp.arange(lengths.shape[0], dtype=jnp.int32)
    seq_start = jnp.sum(jnp.where(before[None, :] < sequence[:, None], lengths[None, :], 0), axis=1)
    return (sequence, token_index - seq_start)


def initial_index(row_index, order_row):
    slot_index = row_index // BLOCK
    slot_table = jnp.arange(order_row.shape[0], dtype=jnp.int32)
    picked = jnp.sum(
        jnp.where(slot_table[None, :] == slot_index[:, None], order_row[None, :], 0), axis=1
    )
    return picked * BLOCK + row_index % BLOCK


def angle_tables(position):
    half_dim = HEAD_DIM // 2
    frequency = 10000.0 ** (-jnp.arange(half_dim, dtype=jnp.float32) * 2.0 / HEAD_DIM)
    angle_table = position.astype(jnp.float32)[:, None] * frequency[None, :]
    angle_table = jnp.concatenate([angle_table, angle_table], axis=-1)
    return (jnp.cos(angle_table)[:, None, :], jnp.sin(angle_table)[:, None, :])


def rotate(values, cosine_table, sine_table):
    half_dim = values.shape[-1] // 2
    turned = jnp.concatenate([-values[..., half_dim:], values[..., :half_dim]], axis=-1)
    return values * cosine_table + turned * sine_table


def unrotate(values, cosine_table, sine_table):
    half_dim = values.shape[-1] // 2
    scaled = values * sine_table
    turned = jnp.concatenate([scaled[..., half_dim:], -scaled[..., :half_dim]], axis=-1)
    return values * cosine_table + turned


def dot(left, right):
    return jnp.dot(left, right, preferred_element_type=jnp.float32)


def times_transposed(left, right):
    return lax.dot_general(
        left, right, (((1,), (1,)), ((), ())), preferred_element_type=jnp.float32
    )


def column_product(left, right):
    return lax.dot_general(
        left, right, (((0,), (0,)), ((), ())), preferred_element_type=jnp.float32
    )


def gather(values, axes):
    return lax.all_gather(values, axes, axis=0, tiled=True)


def scatter(values, axes):
    return lax.psum_scatter(values, axes, scatter_dimension=0, tiled=True)


def enter(axes):
    barrier = pltpu.get_barrier_semaphore()
    count = 0
    for axis, size in axes:
        me = lax.axis_index(axis)
        for step in range(1, size):
            pl.semaphore_signal(barrier, inc=1, device_id={axis: lax.rem(me + step, size)})
        count += size - 1
    pl.semaphore_wait(barrier, count)


def remote(src, dst, send, recv, axis, peer):
    return pltpu.make_async_remote_copy(
        src_ref=src, dst_ref=dst, send_sem=send, recv_sem=recv, device_id={axis: peer}
    )


class Exchange:
    def __init__(self, parts, shape, delay=0):
        self.parts, self.delay = parts, delay
        self.out = jax.ShapeDtypeStruct((parts,) + shape, LOW)
        self.scratch = [
            pltpu.SemaphoreType.DMA((parts - 1,)),
            pltpu.SemaphoreType.DMA((parts - 1,)),
            pltpu.SemaphoreType.DMA,
        ]

    def run(self, src, dst, send, recv, local):
        for _ in range(self.delay):
            yield
        place = lax.axis_index("ctx")
        me = lax.rem(place, self.parts)
        copies = []
        for step in range(1, self.parts):
            peer = lax.rem(me + step, self.parts)
            copies.append(
                remote(
                    src.at[peer],
                    dst.at[me],
                    send.at[step - 1],
                    recv.at[step - 1],
                    "ctx",
                    place - me + peer,
                )
            )
            copies[-1].start()
        own = pltpu.make_async_copy(src.at[me], dst.at[me], local)
        own.start()
        yield
        for copy in copies:
            copy.wait()
            yield
        own.wait()


class Gather:
    def __init__(self, parts, shape, watched=False, cuts=2):
        self.parts, self.watched, self.shape, self.cuts = parts, watched, shape, cuts
        self.out = jax.ShapeDtypeStruct((parts,) + shape, LOW)
        chips = parts // 2
        self.scratch = [
            pltpu.SemaphoreType.DMA((2, chips, self.cuts)),
            pltpu.SemaphoreType.DMA((chips, self.cuts)),
            pltpu.SemaphoreType.DMA((chips, self.cuts)),
            pltpu.SemaphoreType.DMA((chips, self.cuts)),
            pltpu.SemaphoreType.DMA,
        ]

    def run(self, src, dst, send, recv, pair_send, pair_recv, local):
        chips, cuts = self.parts // 2, self.cuts
        rows = self.shape[0] // cuts
        me = lax.axis_index("ctx")
        chip, core = me // 2, lax.rem(me, 2)
        partner = me + 1 - 2 * core

        def piece(block, cut):
            return block.at[pl.ds(cut * rows, rows)]

        def line(block, slot, origin, way, cut):
            return remote(
                piece(block, cut),
                piece(slot, cut),
                send.at[way, origin, cut],
                recv.at[origin, cut],
                "ctx",
                me + 2 - 4 * way,
            )

        def across(block, slot, origin, cut):
            return remote(
                piece(block, cut),
                piece(slot, cut),
                pair_send.at[origin, cut],
                pair_recv.at[origin, cut],
                "ctx",
                partner,
            )

        mine = dst.at[me]
        own = pltpu.make_async_copy(src, mine, local)

        def arrived(origin):
            other = dst.at[2 * origin + 1 - core]
            for cut in range(cuts):
                across(other, other, origin, cut).wait_recv()

            @pl.when(origin == chip)
            def _():
                own.wait()

        def relay(step):
            for cut in range(cuts):
                for way in range(2):
                    origin = chip - step if way == 0 else chip + step

                    @pl.when((origin >= 0) & (origin < chips))
                    def _():
                        slot = dst.at[2 * origin + core]
                        line(slot, slot, origin, way, cut).wait_recv()

                        @pl.when((chip < chips - 1) if way == 0 else (chip > 0))
                        def _():
                            line(slot, slot, origin, way, cut).start()

                        across(slot, slot, origin, cut).start()

        self.dst, self.arrived, self.relay = dst, arrived, relay
        for cut in range(cuts):

            @pl.when(chip < chips - 1)
            def _():
                line(src, mine, chip, 0, cut).start()

            @pl.when(chip > 0)
            def _():
                line(src, mine, chip, 1, cut).start()

        for cut in range(cuts):
            across(src, mine, chip, cut).start()
        own.start()
        yield
        if self.watched:
            yield
        for step in range(1, chips):
            if not self.watched:
                relay(step)
                yield
        for step in range(chips):
            for way in range(2):
                origin = chip - step if way == 0 else chip + step
                ahead = (chip < chips - 1) if way == 0 else (chip > 0)

                @pl.when((origin >= 0) & (origin < chips) & ahead)
                def _():
                    slot = dst.at[2 * origin + core]
                    for cut in range(cuts):
                        line(slot, slot, origin, way, cut).wait_send()

        for origin in range(chips):
            slot = dst.at[2 * origin + core]
            for cut in range(cuts):
                across(slot, slot, origin, cut).wait_send()
            if not self.watched:
                arrived(origin)


class Scatter:
    def __init__(self, parts, shape, cuts=2):
        self.parts, self.shape, self.cuts = parts, shape, cuts
        self.out = jax.ShapeDtypeStruct(shape, jnp.float32)
        chips = parts // 2
        piece = (self.cuts, shape[0] // self.cuts, shape[1])
        self.scratch = [
            pltpu.VMEM((chips,) + shape, LOW),
            pltpu.VMEM((2, chips) + piece, LOW),
            pltpu.VMEM((chips,) + piece, LOW),
            pltpu.SemaphoreType.DMA((chips,)),
            pltpu.SemaphoreType.DMA((chips,)),
            pltpu.SemaphoreType.DMA((chips, self.cuts)),
            pltpu.SemaphoreType.DMA((2, chips, self.cuts)),
        ]

    def run(self, src, out, pair, come, stage, pair_send, pair_recv, send, recv):
        chips, cuts = self.parts // 2, self.cuts
        me = lax.axis_index("ctx")
        chip, core = me // 2, lax.rem(me, 2)
        partner = me + 1 - 2 * core
        rows = self.shape[0] // cuts
        slab = min(rows, 16)
        last = chips - 1

        def across(goal):
            return remote(
                src.at[2 * goal + 1 - core],
                pair.at[goal],
                pair_send.at[goal],
                pair_recv.at[goal],
                "ctx",
                partner,
            )

        def line(goal, cut, way):
            return remote(
                stage.at[goal, cut],
                come.at[way, goal, cut],
                send.at[goal, cut],
                recv.at[way, goal, cut],
                "ctx",
                me + 2 - 4 * way,
            )

        def wide(ref, *index):
            return ref[index].astype(jnp.float32)

        def slabs(part):
            def one(index, carry):
                part(pl.multiple_of(index * slab, slab))
                return carry

            lax.fori_loop(0, rows // slab, one, 0)

        def both(goal, cut, at):
            at = pl.ds(cut * rows + at, slab)
            return wide(src, 2 * goal + core, at) + wide(pair, goal, at)

        order = []
        for step in range((chips + 1) // 2):
            order += sorted({step, last - step})
        for goal in order:
            across(goal).start()
        yield
        for step in range(last * cuts):
            for way in range(2):
                turn = step - (chip if way == 0 else last - chip)
                goal = (last - turn // cuts) if way == 0 else turn // cuts
                cut = step - (chip if way == 0 else last - chip) - (turn // cuts) * cuts
                first = (chip == 0) if way == 0 else (chip == last)
                ahead = last - chip if way == 0 else chip

                def begin(at):
                    value = both(goal, cut, at)
                    stage[goal, cut, pl.ds(at, slab), :] = value.astype(LOW)

                def middle(at):
                    value = both(goal, cut, at) + wide(come, way, goal, cut, pl.ds(at, slab))
                    stage[goal, cut, pl.ds(at, slab), :] = value.astype(LOW)

                @pl.when((turn >= 0) & (turn < ahead * cuts))
                def _():
                    @pl.when(cut == 0)
                    def _():
                        across(goal).wait_recv()

                    @pl.when(first)
                    def _():
                        slabs(begin)

                    @pl.when(jnp.logical_not(first))
                    def _():
                        line(goal, cut, way).wait_recv()
                        slabs(middle)

                    line(goal, cut, way).start()

            yield
        across(chip).wait_recv()
        for cut in range(cuts):

            def own(at):
                out[pl.ds(cut * rows + at, slab), :] = both(chip, cut, at)

            slabs(own)
        yield
        for cut in range(cuts):
            for way in range(2):

                def final(at):
                    out[pl.ds(cut * rows + at, slab), :] += wide(
                        come, way, chip, cut, pl.ds(at, slab)
                    )

                @pl.when((chip > 0) if way == 0 else (chip < last))
                def _():
                    line(chip, cut, way).wait_recv()
                    slabs(final)

            yield
        for goal in range(chips):
            across(goal).wait_send()

            @pl.when(chip != goal)
            def _():
                for cut in range(cuts):
                    line(goal, cut, 0).wait_send()


class Fan:
    def __init__(self, groups, shape):
        self.groups = groups
        self.out = jax.ShapeDtypeStruct((groups,) + shape, LOW)
        self.scratch = [
            pltpu.SemaphoreType.DMA((groups - 1,)),
            pltpu.SemaphoreType.DMA((groups - 1,)),
            pltpu.SemaphoreType.DMA,
        ]

    def run(self, src, dst, send, recv, local):
        groups = self.groups
        group = lax.axis_index("fsdp")
        copies = []
        for hop in range(1, groups):
            peer = lax.rem(group + hop, groups)
            copies.append(
                remote(src, dst.at[group], send.at[hop - 1], recv.at[hop - 1], "fsdp", peer)
            )
            copies[-1].start()
        own = pltpu.make_async_copy(src, dst.at[group], local)
        own.start()
        yield
        yield
        yield
        for copy in copies:
            copy.wait()
        own.wait()


class Spread:
    def __init__(self, parts, groups, shape):
        self.parts, self.groups = parts, groups
        self.out = jax.ShapeDtypeStruct((groups, parts) + shape, LOW)
        self.scratch = [
            pltpu.SemaphoreType.DMA((parts - 1,)),
            pltpu.SemaphoreType.DMA((parts - 1,)),
            pltpu.SemaphoreType.DMA((groups - 1, parts)),
            pltpu.SemaphoreType.DMA((groups - 1, parts)),
            pltpu.SemaphoreType.DMA,
        ]

    def run(self, src, dst, send, recv, far_send, far_recv, local):
        parts, groups = self.parts, self.groups
        me, group = lax.axis_index("ctx"), lax.axis_index("fsdp")
        copies = []
        for step in range(1, parts):
            peer = lax.rem(me + step, parts)
            copies.append(
                remote(
                    src.at[peer],
                    dst.at[group, me],
                    send.at[step - 1],
                    recv.at[step - 1],
                    "ctx",
                    peer,
                )
            )
            copies[-1].start()
        own = pltpu.make_async_copy(src.at[me], dst.at[group, me], local)
        own.start()

        def pass_on(block, origin, step):
            out = []
            for hop in range(1, groups):
                copy = remote(
                    block,
                    dst.at[group, origin],
                    far_send.at[hop - 1, step],
                    far_recv.at[hop - 1, step],
                    "fsdp",
                    lax.rem(group + hop, groups),
                )
                copy.start()
                out.append(copy)
            return out

        far = pass_on(src.at[me], me, 0)
        eager = -(-parts // 2)
        yield
        for step in range(1, parts):
            copies[step - 1].wait_recv()
            origin = lax.rem(me - step + parts, parts)
            far += pass_on(dst.at[group, origin], origin, step)
            if step % eager == 0:
                yield
        for at, copy in enumerate(far):
            copy.wait()
            if at % 6 == 5:
                yield
        for copy in copies:
            copy.wait_send()
        own.wait()


class Deliver:
    def __init__(self, parts, shape, offsets, delay=0, eager=1):
        self.parts, self.shape, self.offsets = parts, shape, offsets
        self.delay, self.eager = delay, eager
        self.out = jax.ShapeDtypeStruct((shape[0], parts * shape[1]), jnp.float32)
        self.scratch = [
            pltpu.VMEM((parts - 1,) + shape, LOW),
            pltpu.SemaphoreType.DMA((parts - 1,)),
            pltpu.SemaphoreType.DMA((parts - 1,)),
        ]

    def place(self, out, origin, read):
        starts = self.offsets(origin)
        step = self.shape[1] // len(starts)
        for index, start in enumerate(starts):
            out[:, pl.ds(pl.multiple_of(start, HEAD_DIM), step)] = read(
                index * step, (index + 1) * step
            )

    def send(self, me, step, block, came, send, recv):
        return remote(
            block,
            came.at[step - 1],
            send.at[step - 1],
            recv.at[step - 1],
            "ctx",
            lax.rem(me + step, self.parts),
        )

    def run(self, src, out, came, send, recv):
        for _ in range(self.delay):
            yield
        me = lax.axis_index("ctx")
        copies = []
        for step in range(1, self.parts):
            block = src.at[lax.rem(me + step, self.parts)]
            copies.append(self.send(me, step, block, came, send, recv))
            copies[-1].start()
        self.place(out, me, lambda lo, hi: src[me, :, lo:hi].astype(jnp.float32))
        yield
        yield from self.finish(me, out, copies, came)

    def finish(self, me, out, copies, came):
        for step in range(1, self.parts):
            copies[step - 1].wait_recv()
            origin = lax.rem(me - step + self.parts, self.parts)
            self.place(out, origin, lambda lo, hi: came[step - 1, :, lo:hi].astype(jnp.float32))
            if step % self.eager == 0:
                yield
        for copy in copies:
            copy.wait_send()


class Collect(Deliver):
    def __init__(self, parts, groups, shape, offsets, delay=0, eager=1):
        super().__init__(parts, shape, offsets, delay, eager)
        self.groups = groups
        self.scratch = self.scratch + [
            pltpu.VMEM((groups - 1, parts) + shape, LOW),
            pltpu.VMEM((parts,) + shape, LOW),
            pltpu.VMEM(shape, jnp.float32),
            pltpu.SemaphoreType.DMA((groups - 1, parts)),
            pltpu.SemaphoreType.DMA((groups - 1, parts)),
        ]

    def run(self, src, out, came, send, recv, far, stage, mine, far_send, far_recv):
        parts, groups = self.parts, self.groups
        me, group = lax.axis_index("ctx"), lax.axis_index("fsdp")
        goals = [lax.rem(me + step, parts) for step in range(1, parts + 1)]
        hops = []
        for goal in goals:
            for hop in range(1, groups):
                peer = lax.rem(group + hop, groups)
                hops.append(
                    remote(
                        src.at[peer, goal],
                        far.at[hop - 1, goal],
                        far_send.at[hop - 1, goal],
                        far_recv.at[hop - 1, goal],
                        "fsdp",
                        peer,
                    )
                )
                hops[-1].start()
        yield
        copies = []
        for step in range(1, parts + 1):
            goal = goals[step - 1]
            for copy in hops[(step - 1) * (groups - 1) : step * (groups - 1)]:
                copy.wait_recv()
            value = src[group, goal].astype(jnp.float32)
            for hop in range(groups - 1):
                value += far[hop, goal].astype(jnp.float32)
            if step < parts:
                stage[goal] = value.astype(LOW)
                copies.append(self.send(me, step, stage.at[goal], came, send, recv))
                copies[-1].start()
            else:
                mine[...] = value
            if step % self.eager == 0:
                yield
        self.place(out, me, lambda lo, hi: mine[:, lo:hi])
        yield from self.finish(me, out, copies, came)
        for copy in hops:
            copy.wait_send()


def call(jobs, operands, name, identity, axes, work=None, micros=50):
    counts = [len(job.scratch) for job in jobs]
    jobs_n = len(jobs)
    extra = work.operands if work else []
    extra_out = work.outs if work else []
    extra_scratch = work.scratch if work else []

    def kernel(*refs):
        refs = list(refs)

        def take(count):
            taken = refs[:count]
            del refs[:count]
            return taken

        ins, more = take(jobs_n), take(len(extra))
        outs, more_outs = take(jobs_n), take(len(extra_out))
        runs = []
        for job, src, dst, count in zip(jobs, ins, outs, counts):
            runs.append(job.run(src, dst, *take(count)))
        if work:
            runs.append(work.run(*more, *more_outs, *refs))
        enter(axes)
        while runs:
            going = []
            for run in runs:
                try:
                    next(run)
                    going.append(run)
                except StopIteration:
                    pass
            runs = going

    vmem = pl.BlockSpec(memory_space=pltpu.VMEM)
    anywhere = pl.BlockSpec(memory_space=pl.ANY)
    return pl.pallas_call(
        kernel,
        out_shape=tuple(job.out for job in jobs) + tuple(extra_out),
        in_specs=[vmem] * jobs_n + [anywhere] * len(extra),
        out_specs=(vmem,) * jobs_n + (anywhere,) * len(extra_out),
        scratch_shapes=[shape for job in jobs for shape in job.scratch] + list(extra_scratch),
        compiler_params=pltpu.CompilerParams(
            collective_id=identity, has_side_effects=True, vmem_limit_bytes=62 << 20
        ),
        cost_estimate=pl.CostEstimate(
            flops=0, bytes_accessed=micros * 3_000_000, transcendentals=0
        ),
        name=name,
    )(*operands, *extra)


def product(left, right):
    return jnp.dot(left, right, preferred_element_type=jnp.float32)


class Puts:
    def __init__(self, made, put):
        self.made, self.put, self.copies = made, put, []

    def pair(self, fill, columns, out, at, tile):
        for copy in self.copies:
            copy.wait()
        lax.fori_loop(0, 2, fill, 0)
        self.copies = []
        for half in range(2):
            begin = at + half * tile
            copy = pltpu.make_async_copy(
                self.made.at[half, :, pl.ds(0, columns)],
                out.at[begin : begin + tile, :],
                self.put.at[half],
            )
            copy.start()
            self.copies.append(copy)

    def finish(self):
        for copy in self.copies:
            copy.wait()


class Grads:
    tile = 256

    def __init__(self, pairs):
        self.pairs = pairs
        length, wide = pairs[0][0].shape[0], max(right.shape[1] for _, right in pairs)
        self.operands = [array for pair in pairs for array in pair]
        self.outs = [jax.ShapeDtypeStruct((l.shape[1], r.shape[1]), LOW) for l, r in pairs]
        self.slots = [[id(array) for array in self.operands].index(id(a)) for a in self.operands]
        self.operands = [a for i, a in enumerate(self.operands) if self.slots[i] == i]
        self.slots = [sorted(set(self.slots)).index(slot) for slot in self.slots]
        self.scratch = [pltpu.VMEM(array.shape, LOW) for array in self.operands]
        self.scratch += [
            pltpu.VMEM((self.tile, length), LOW),
            pltpu.VMEM((2, self.tile, wide), LOW),
            pltpu.SemaphoreType.DMA((len(self.operands),)),
            pltpu.SemaphoreType.DMA((2,)),
        ]

    def run(self, *refs):
        n, tile, count = len(self.pairs), self.tile, len(self.operands)
        sources, outs = refs[:count], refs[count : count + n]
        held = refs[count + n : 2 * count + n]
        turned, made, get, put = refs[2 * count + n :]
        gets = [pltpu.make_async_copy(s, h, get.at[i]) for i, (s, h) in enumerate(zip(sources, held))]
        for copy in gets:
            copy.start()
        yield
        puts = Puts(made, put)
        for which in range(n):
            first, second = self.slots[2 * which : 2 * which + 2]
            left, right, out = held[first], held[second], outs[which]
            for slot in (first, second):
                if slot not in self.slots[: 2 * which]:
                    gets[slot].wait()
            columns = right.shape[1]
            step = min(columns, 256)
            for at in range(0, left.shape[1], 2 * tile):
                def pair(half, carry):
                    begin = pl.multiple_of(at + half * tile, tile)
                    turned[...] = left[:, pl.ds(begin, tile)].T

                    def one(index, carry):
                        where = pl.ds(pl.multiple_of(index * step, step), step)
                        made[half, :, where] = product(turned[...], right[:, where]).astype(LOW)
                        return carry

                    return lax.fori_loop(0, columns // step, one, carry)

                puts.pair(pair, columns, out, at, tile)
                yield
        puts.finish()


class Deliver:
    def __init__(self, parts, shape, offsets, delay=0, eager=1):
        self.parts, self.shape, self.offsets = parts, shape, offsets
        self.delay, self.eager = delay, eager
        self.out = jax.ShapeDtypeStruct((shape[0], parts * shape[1]), jnp.float32)
        self.scratch = [
            pltpu.VMEM((parts - 1,) + shape, LOW),
            pltpu.SemaphoreType.DMA((parts - 1,)),
            pltpu.SemaphoreType.DMA((parts - 1,)),
        ]

    def place(self, out, origin, read):
        starts = self.offsets(origin)
        step = self.shape[1] // len(starts)
        for index, start in enumerate(starts):
            out[:, pl.ds(pl.multiple_of(start, HEAD_DIM), step)] = read(
                index * step, (index + 1) * step
            )

    def send(self, me, step, block, came, send, recv):
        return remote(
            block,
            came.at[step - 1],
            send.at[step - 1],
            recv.at[step - 1],
            "ctx",
            lax.rem(me + step, self.parts),
        )

    def run(self, src, out, came, send, recv):
        for _ in range(self.delay):
            yield
        me = lax.axis_index("ctx")
        copies = []
        for step in range(1, self.parts):
            block = src.at[lax.rem(me + step, self.parts)]
            copies.append(self.send(me, step, block, came, send, recv))
            copies[-1].start()
        self.place(out, me, lambda lo, hi: src[me, :, lo:hi].astype(jnp.float32))
        yield
        yield from self.finish(me, out, copies, came)

    def finish(self, me, out, copies, came):
        for step in range(1, self.parts):
            copies[step - 1].wait_recv()
            origin = lax.rem(me - step + self.parts, self.parts)
            self.place(out, origin, lambda lo, hi: came[step - 1, :, lo:hi].astype(jnp.float32))
            if step % self.eager == 0:
                yield
        for copy in copies:
            copy.wait_send()


class Collect(Deliver):
    def __init__(self, parts, groups, shape, offsets, delay=0, eager=1):
        super().__init__(parts, shape, offsets, delay, eager)
        self.groups = groups
        self.scratch = self.scratch + [
            pltpu.VMEM((groups - 1, parts) + shape, LOW),
            pltpu.VMEM((parts,) + shape, LOW),
            pltpu.VMEM(shape, jnp.float32),
            pltpu.SemaphoreType.DMA((groups - 1, parts)),
            pltpu.SemaphoreType.DMA((groups - 1, parts)),
        ]

    def run(self, src, out, came, send, recv, far, stage, mine, far_send, far_recv):
        parts, groups = self.parts, self.groups
        me, group = lax.axis_index("ctx"), lax.axis_index("fsdp")
        goals = [lax.rem(me + step, parts) for step in range(1, parts + 1)]
        hops = []
        for goal in goals:
            for hop in range(1, groups):
                peer = lax.rem(group + hop, groups)
                hops.append(
                    remote(
                        src.at[peer, goal],
                        far.at[hop - 1, goal],
                        far_send.at[hop - 1, goal],
                        far_recv.at[hop - 1, goal],
                        "fsdp",
                        peer,
                    )
                )
                hops[-1].start()
        yield
        copies = []
        for step in range(1, parts + 1):
            goal = goals[step - 1]
            for copy in hops[(step - 1) * (groups - 1) : step * (groups - 1)]:
                copy.wait_recv()
            value = src[group, goal].astype(jnp.float32)
            for hop in range(groups - 1):
                value += far[hop, goal].astype(jnp.float32)
            if step < parts:
                stage[goal] = value.astype(LOW)
                copies.append(self.send(me, step, stage.at[goal], came, send, recv))
                copies[-1].start()
            else:
                mine[...] = value
            if step % self.eager == 0:
                yield
        self.place(out, me, lambda lo, hi: mine[:, lo:hi])
        yield from self.finish(me, out, copies, came)
        for copy in hops:
            copy.wait_send()


def call(jobs, operands, name, identity, axes, work=None, micros=50):
    counts = [len(job.scratch) for job in jobs]
    jobs_n = len(jobs)
    extra = work.operands if work else []
    extra_out = work.outs if work else []
    extra_scratch = work.scratch if work else []

    def kernel(*refs):
        refs = list(refs)

        def take(count):
            taken = refs[:count]
            del refs[:count]
            return taken

        ins, more = take(jobs_n), take(len(extra))
        outs, more_outs = take(jobs_n), take(len(extra_out))
        runs = []
        for job, src, dst, count in zip(jobs, ins, outs, counts):
            runs.append(job.run(src, dst, *take(count)))
        if work:
            runs.append(work.run(*more, *more_outs, *refs))
        enter(axes)
        while runs:
            going = []
            for run in runs:
                try:
                    next(run)
                    going.append(run)
                except StopIteration:
                    pass
            runs = going

    vmem = pl.BlockSpec(memory_space=pltpu.VMEM)
    anywhere = pl.BlockSpec(memory_space=pl.ANY)
    return pl.pallas_call(
        kernel,
        out_shape=tuple(job.out for job in jobs) + tuple(extra_out),
        in_specs=[vmem] * jobs_n + [anywhere] * len(extra),
        out_specs=(vmem,) * jobs_n + (anywhere,) * len(extra_out),
        scratch_shapes=[shape for job in jobs for shape in job.scratch] + list(extra_scratch),
        compiler_params=pltpu.CompilerParams(
            collective_id=identity, has_side_effects=True, vmem_limit_bytes=62 << 20
        ),
        cost_estimate=pl.CostEstimate(
            flops=0, bytes_accessed=micros * 3_000_000, transcendentals=0
        ),
        name=name,
    )(*operands, *extra)


class Grads:
    tile = 256

    def __init__(self, pairs):
        self.pairs = pairs
        length, wide = pairs[0][0].shape[0], max(right.shape[1] for _, right in pairs)
        self.operands = [array for pair in pairs for array in pair]
        self.outs = [jax.ShapeDtypeStruct((l.shape[1], r.shape[1]), LOW) for l, r in pairs]
        self.slots = [[id(array) for array in self.operands].index(id(a)) for a in self.operands]
        self.operands = [a for i, a in enumerate(self.operands) if self.slots[i] == i]
        self.slots = [sorted(set(self.slots)).index(slot) for slot in self.slots]
        self.scratch = [pltpu.VMEM(array.shape, LOW) for array in self.operands]
        self.scratch += [
            pltpu.VMEM((self.tile, length), LOW),
            pltpu.VMEM((2, self.tile, wide), LOW),
            pltpu.SemaphoreType.DMA((len(self.operands),)),
            pltpu.SemaphoreType.DMA((2,)),
        ]

    def run(self, *refs):
        n, tile, count = len(self.pairs), self.tile, len(self.operands)
        sources, outs = refs[:count], refs[count : count + n]
        held = refs[count + n : 2 * count + n]
        turned, made, get, put = refs[2 * count + n :]
        gets = [pltpu.make_async_copy(s, h, get.at[i]) for i, (s, h) in enumerate(zip(sources, held))]
        for copy in gets:
            copy.start()
        yield
        puts = []
        for which in range(n):
            first, second = self.slots[2 * which : 2 * which + 2]
            left, right, out = held[first], held[second], outs[which]
            for slot in (first, second):
                if slot not in self.slots[: 2 * which]:
                    gets[slot].wait()
            columns = right.shape[1]
            step = min(columns, 512)
            for at in range(0, left.shape[1], tile):
                slot = len(puts) % 2
                if len(puts) >= 2:
                    puts[-2].wait()
                turned[...] = left[:, at : at + tile].T

                def one(index, carry):
                    where = pl.ds(pl.multiple_of(index * step, step), step)
                    made[slot, :, where] = jnp.dot(
                        turned[...], right[:, where], preferred_element_type=jnp.float32
                    ).astype(LOW)
                    return carry

                lax.fori_loop(0, columns // step, one, 0)
                part = made.at[slot] if columns == made.shape[2] else made.at[slot, :, :columns]
                puts.append(pltpu.make_async_copy(part, out.at[at : at + tile, :], put.at[slot]))
                puts[-1].start()
                yield
        for copy in puts[-2:]:
            copy.wait()


def softmax_block(query, keys, ok):
    scores = times_transposed(query, keys) * HEAD_DIM ** (-0.5)
    scores = jnp.where(ok, scores, -1e30)
    weights = jnp.exp(scores - jnp.max(scores, axis=-1, keepdims=True))
    weights = jnp.where(ok, weights, 0.0)
    return weights, jnp.sum(weights, axis=-1, keepdims=True)


class Attend:
    tile = 256

    def __init__(self, rows, weight, tables, heads):
        self.heads = heads
        self.operands = [rows, weight] + list(tables)
        length, wide = rows.shape[0], weight.shape[1]
        self.outs = [
            jax.ShapeDtypeStruct((length, wide), LOW),
            jax.ShapeDtypeStruct((length, wide // 3), LOW),
        ]
        self.scratch = [pltpu.VMEM(array.shape, array.dtype) for array in self.operands]
        self.scratch += [pltpu.VMEM(out.shape, out.dtype) for out in self.outs]
        self.scratch += [
            pltpu.SemaphoreType.DMA((len(self.operands),)),
            pltpu.SemaphoreType.DMA((2,)),
        ]

    def run(self, *refs):
        n, tile, heads = len(self.operands), self.tile, self.heads
        sources, results, held = refs[:n], refs[n : n + 2], refs[n + 2 : 2 * n + 2]
        qkv, mix, get, put = refs[2 * n + 2 :]
        rows, weight, cosine, sine, first, last, keys = held
        gets = [pltpu.make_async_copy(s, h, get.at[i]) for i, (s, h) in enumerate(zip(sources, held))]
        for copy in gets:
            copy.start()
        yield
        for copy in gets:
            copy.wait()
        width = heads * HEAD_DIM

        def project(index, carry):
            at = pl.ds(pl.multiple_of(index * tile, tile), tile)
            value = product(rows[at, :], weight[...])
            for head in range(3 * heads):
                block = value[:, head * HEAD_DIM : (head + 1) * HEAD_DIM]
                if head < 2 * heads:
                    turned = pltpu.roll(block, HEAD_DIM // 2, 1)
                    block = block * cosine[at, :] + turned * sine[at, :]
                qkv[at, head * HEAD_DIM : (head + 1) * HEAD_DIM] = block.astype(LOW)
            return carry

        lax.fori_loop(0, rows.shape[0] // tile, project, 0)
        send = pltpu.make_async_copy(qkv, results[0], put.at[0])
        send.start()
        yield

        def attend(index, carry):
            at = pl.ds(pl.multiple_of(index * tile, tile), tile)
            ok = (keys[:1, :] >= first[at, :1]) & (keys[:1, :] <= last[at, :1])
            for head in range(heads):
                lo = head * HEAD_DIM
                weights, total = softmax_block(
                    qkv[at, lo : lo + HEAD_DIM], qkv[:, width + lo : width + lo + HEAD_DIM], ok
                )
                value = qkv[:, 2 * width + lo : 2 * width + lo + HEAD_DIM]
                mixed = product(weights.astype(LOW), value) / total
                mix[at, lo : lo + HEAD_DIM] = mixed.astype(LOW)
            return carry

        lax.fori_loop(0, rows.shape[0] // tile, attend, 0)
        send_mix = pltpu.make_async_copy(mix, results[1], put.at[1])
        send_mix.start()
        yield
        send.wait()
        send_mix.wait()


class AttendBack:
    tile = 256

    def __init__(self, back, qkv, rows, weight, tables, heads):
        self.heads = heads
        self.operands = [back, qkv] + list(tables) + [weight, rows]
        length, wide, width = rows.shape[0], weight.shape[1], rows.shape[1]
        self.outs = [
            jax.ShapeDtypeStruct((length, width), LOW),
            jax.ShapeDtypeStruct((width, wide), LOW),
        ]
        self.scratch = [pltpu.VMEM(array.shape, array.dtype) for array in self.operands]
        self.scratch += [
            pltpu.VMEM((length, wide), LOW),
            pltpu.VMEM((2, length, HEAD_DIM), jnp.float32),
            pltpu.VMEM((self.tile, length), LOW),
            pltpu.VMEM((2, self.tile, width), LOW),
            pltpu.SemaphoreType.DMA((len(self.operands),)),
            pltpu.SemaphoreType.DMA((2,)),
        ]

    def run(self, *refs):
        n, tile, heads = len(self.operands), self.tile, self.heads
        sources, results, held = refs[:n], refs[n : n + 2], refs[n + 2 : 2 * n + 2]
        grads, sums, turned, made, get, put = refs[2 * n + 2 :]
        back, qkv, cosine, sine, first, last, keys, weight, rows = held
        length, width = back.shape
        gets = [pltpu.make_async_copy(s, h, get.at[i]) for i, (s, h) in enumerate(zip(sources, held))]
        for copy in gets:
            copy.start()
        yield
        for copy in gets[:-2]:
            copy.wait()

        def unrotated(value, at):
            return value * cosine[at, :] - pltpu.roll(value, HEAD_DIM // 2, 1) * sine[at, :]

        for head in range(heads):
            lo = head * HEAD_DIM
            mine = slice(lo, lo + HEAD_DIM)
            key = slice(width + lo, width + lo + HEAD_DIM)
            val = slice(2 * width + lo, 2 * width + lo + HEAD_DIM)
            sums[...] = jnp.zeros_like(sums)

            def attend(index, carry):
                at = pl.ds(pl.multiple_of(index * tile, tile), tile)
                ok = (keys[:1, :] >= first[at, :1]) & (keys[:1, :] <= last[at, :1])
                weights, total = softmax_block(qkv[at, mine], qkv[:, key], ok)
                probs = weights / total
                upper = back[at, mine]
                prob_back = times_transposed(upper, qkv[:, val])
                delta = jnp.sum(probs * prob_back, axis=-1, keepdims=True)
                score_back = HEAD_DIM ** (-0.5) * probs * (prob_back - delta)
                score_low = score_back.astype(LOW)
                query_back = product(score_low, qkv[:, key])
                grads[at, mine] = unrotated(query_back, at).astype(LOW)
                sums[0] += product(score_low.T, qkv[at, mine])
                sums[1] += product(probs.astype(LOW).T, upper)
                return carry

            lax.fori_loop(0, length // tile, attend, 0)
            yield

            def settle(index, carry):
                at = pl.ds(pl.multiple_of(index * tile, tile), tile)
                grads[at, key] = unrotated(sums[0, at, :], at).astype(LOW)
                grads[at, val] = sums[1, at, :].astype(LOW)
                return carry

            lax.fori_loop(0, length // tile, settle, 0)
        puts = Puts(made, put)
        wide = grads.shape[1]
        part = tile if wide % tile == 0 else HEAD_DIM
        gets[-2].wait()
        for at in range(0, length, 2 * tile):

            def terms(half, carry):
                where = pl.ds(pl.multiple_of(at + half * tile, tile), tile)

                def one(index, carry):
                    span = pl.ds(pl.multiple_of(index * tile, tile), tile)
                    value = times_transposed(grads[where, :], weight[span, :])
                    made[half, :, span] = value.astype(LOW)
                    return carry

                return lax.fori_loop(0, made.shape[2] // tile, one, carry)

            puts.pair(terms, made.shape[2], results[0], at, tile)
            yield
        gets[-1].wait()
        for at in range(0, rows.shape[1], 2 * tile):

            def weights(half, carry):
                where = pl.ds(pl.multiple_of(at + half * tile, tile), tile)
                turned[...] = rows[:, where].T

                def one(index, carry):
                    span = pl.ds(pl.multiple_of(index * part, part), part)
                    made[half, :, span] = product(turned[...], grads[:, span]).astype(LOW)
                    return carry

                return lax.fori_loop(0, wide // part, one, carry)

            puts.pair(weights, wide, results[1], at, tile)
            yield
        puts.finish()


def near_first(chips):
    table = []
    for chip in range(chips):
        order = [chip]
        for step in range(1, chips):
            order += [at for at in (chip + step, chip - step) if 0 <= at < chips]
        table.append(order)
    return table


def next_chip(chips, turn):
    chip = lax.axis_index("ctx") // 2
    return sum(
        jnp.where((chip == at) & (turn == when), order[when], 0)
        for at, order in enumerate(near_first(chips))
        for when in range(chips)
    )


class ProjectBack:
    tile = 256

    def __init__(self, job, activated, down, out_rows, mix):
        self.job = job
        self.operands = [activated, down, out_rows, mix]
        length, heads_width = mix.shape
        width = down.shape[1]
        self.outs = [
            jax.ShapeDtypeStruct((length, width), LOW),
            jax.ShapeDtypeStruct((length, heads_width), LOW),
            jax.ShapeDtypeStruct((heads_width, width), LOW),
        ]
        self.scratch = [pltpu.VMEM(array.shape, array.dtype) for array in self.operands]
        self.scratch += [
            pltpu.VMEM((2, self.tile, width), LOW),
            pltpu.VMEM((length, heads_width), LOW),
            pltpu.VMEM((heads_width, width), jnp.float32),
            pltpu.VMEM((heads_width, width), LOW),
            pltpu.SemaphoreType.DMA((4,)),
            pltpu.SemaphoreType.DMA((2,)),
            pltpu.SemaphoreType.DMA((2,)),
        ]

    def run(self, *refs):
        job, tile = self.job, self.tile
        sources, results, held = refs[:4], refs[4:7], refs[7:11]
        made, back, total, total_low, get, put, leave = refs[11:]
        activated, down, out_rows, mix = held
        length, width = mix.shape[0], down.shape[1]
        gets = [pltpu.make_async_copy(s, h, get.at[i]) for i, (s, h) in enumerate(zip(sources, held))]
        for copy in gets:
            copy.start()
        yield
        for copy in gets:
            copy.wait()
        total[...] = jnp.zeros_like(total)
        puts = Puts(made, put)
        for at in range(0, length, 2 * tile):

            def terms(half, carry):
                where = pl.ds(pl.multiple_of(at + half * tile, tile), tile)

                def one(index, carry):
                    span = pl.ds(pl.multiple_of(index * tile, tile), tile)
                    value = product(activated[where, :], down[:, span])
                    made[half, :, span] = value.astype(LOW)
                    return carry

                return lax.fori_loop(0, width // tile, one, carry)

            puts.pair(terms, width, results[0], at, tile)
        chips = job.parts // 2
        rows = length // chips

        def one_chip(turn, carry):
            origin = next_chip(chips, turn)

            @pl.when(turn > 0)
            def _():
                job.relay(turn)

            job.arrived(origin)
            at = pl.ds(pl.multiple_of(origin * rows, rows), rows)
            block = job.dst.at[pl.ds(2 * origin, 2)]
            value = block[...].reshape(rows, width)
            back[at, :] = times_transposed(value, out_rows[...]).astype(LOW)
            total[...] += product(mix[at, :].T, value)
            return carry

        lax.fori_loop(0, chips, one_chip, 0)
        total_low[...] = total[...].astype(LOW)
        out = [
            pltpu.make_async_copy(back, results[1], leave.at[0]),
            pltpu.make_async_copy(total_low, results[2], leave.at[1]),
        ]
        for copy in out:
            copy.start()
        puts.finish()
        for copy in out:
            copy.wait()


class FeedForward:
    def __init__(self, job, upstream, gate, up, down):
        self.job = job
        self.operands = [upstream, gate, up, down]
        length, width = upstream.shape
        units = gate.shape[1]
        self.outs = [
            jax.ShapeDtypeStruct((length, units), LOW),
            jax.ShapeDtypeStruct((length, units), LOW),
            jax.ShapeDtypeStruct((length, units), LOW),
            jax.ShapeDtypeStruct((length, width), LOW),
        ]
        self.tile = length // (job.parts // 2)
        self.scratch = [pltpu.VMEM(array.shape, array.dtype) for array in self.operands]
        self.scratch += [pltpu.VMEM((2, self.tile) + out.shape[1:], LOW) for out in self.outs]
        self.scratch += [pltpu.SemaphoreType.DMA((4,)), pltpu.SemaphoreType.DMA((4, 2))]

    def run(self, *refs):
        job, tile = self.job, self.tile
        sources, results, held, made = refs[:4], refs[4:8], refs[8:12], refs[12:16]
        get, put = refs[16:]
        upstream, gate_w, up_w, down = held
        acts, gate_backs, up_backs, terms = made
        width, units = gate_w.shape
        step = min(units, 256)
        span = min(width, 512)
        gets = [pltpu.make_async_copy(sources[i], held[i], get.at[i]) for i in (1, 2, 3, 0)]
        for copy in gets:
            copy.start()
        yield
        for copy in gets:
            copy.wait()
        chips = job.parts // 2

        def leave(slot, origin):
            at = pl.ds(pl.multiple_of(origin * tile, tile), tile)
            return [
                pltpu.make_async_copy(made[i].at[slot], results[i].at[at, :], put.at[i, slot])
                for i in range(4)
            ]

        def one_chip(turn, carry):
            origin = next_chip(chips, turn)
            slot = lax.rem(turn, 2)

            @pl.when(turn > 0)
            def _():
                job.relay(turn)

            @pl.when(turn >= 2)
            def _():
                for copy in leave(slot, 0):
                    copy.wait()

            job.arrived(origin)
            at = pl.ds(pl.multiple_of(origin * tile, tile), tile)
            normed = job.dst.at[pl.ds(2 * origin, 2)]

            def forward(index, carry):
                left = pl.ds(pl.multiple_of(index * step, step), step)
                value = normed[...].reshape(tile, width)
                gate = product(value, gate_w[:, left])
                up = product(value, up_w[:, left])
                act_grad = times_transposed(upstream[at, :], down[left, :])
                sigmoid = jax.nn.sigmoid(gate)
                silu = gate * sigmoid
                acts[slot, :, left] = (silu * up).astype(LOW)
                gate_grad = act_grad * up * sigmoid * (1.0 + gate * (1.0 - sigmoid))
                gate_backs[slot, :, left] = gate_grad.astype(LOW)
                up_backs[slot, :, left] = (act_grad * silu).astype(LOW)
                return carry

            lax.fori_loop(0, units // step, forward, 0)

            def backward(index, carry):
                where = pl.ds(pl.multiple_of(index * span, span), span)
                value = times_transposed(gate_backs[slot], gate_w[where, :])
                value += times_transposed(up_backs[slot], up_w[where, :])
                terms[slot, :, where] = value.astype(LOW)
                return carry

            lax.fori_loop(0, width // span, backward, 0)
            for copy in leave(slot, origin):
                copy.start()
            return carry

        lax.fori_loop(0, chips, one_chip, 0)
        for slot in range(min(2, chips)):
            for copy in leave(slot, 0):
                copy.wait()


class Plan:
    def __init__(self, parts, groups, width):
        self.parts, self.groups = parts, groups
        self.shard = width // (parts * groups)
        self.run = HEAD_DIM // self.shard
        self.heads = HEADS // parts
        self.qkv_dims = (3, self.run, self.heads, parts // self.run, HEAD_DIM)

    def qkv_pieces(self, weight):
        rows = weight.shape[0]
        pieces = weight.reshape((rows,) + self.qkv_dims).transpose(4, 2, 0, 1, 3, 5)
        return pieces.reshape(self.parts, rows, 3 * self.heads * HEAD_DIM)

    def qkv_starts(self, part):
        at, index = part // self.run, lax.rem(part, self.run)
        return [
            (kind * HEADS + (index * self.heads + head) * (self.parts // self.run) + at) * HEAD_DIM
            for kind in range(3)
            for head in range(self.heads)
        ]

    def unit_pieces(self, weight):
        rows, columns = weight.shape
        inner = columns // (2 * self.groups * self.parts)
        pieces = weight.reshape(rows, 2 * self.groups, self.parts, inner).transpose(2, 0, 1, 3)
        return pieces.reshape(self.parts, rows, 2 * self.groups * inner)

    def unit_job(self, shape):
        step = shape[1] // self.groups
        if step % HEAD_DIM:
            return Exchange(self.parts, shape)
        return Deliver(
            self.parts,
            shape,
            lambda part: [(at * self.parts + part) * step for at in range(self.groups)],
        )

    def unit_rows(self, pieces):
        if pieces.ndim == 2:
            return pieces
        parts, rows, columns = pieces.shape
        outer = self.groups
        pieces = pieces.reshape(parts, rows, outer, columns // outer).transpose(1, 2, 0, 3)
        return pieces.reshape(rows, parts * columns).astype(jnp.float32)


def per_device(tokens, w_qkv, w_out, w_gate_up, w_down, seq_lengths, block_order, cotangent):
    lengths = seq_lengths[0]
    order_row = block_order[0]
    parts = lax.axis_size("ctx")
    groups = lax.axis_size("fsdp")
    rows, width = tokens.shape
    length = rows * parts
    plan = Plan(parts, groups, width)
    heads, shard, run = plan.heads, plan.shard, plan.run
    head_width = heads * HEAD_DIM
    line = (("ctx", parts),)
    plane = (("ctx", parts), ("fsdp", groups))
    block = (rows, width)

    down_rows = gather(w_down, "fsdp")
    gate_up_pieces = plan.unit_pieces(w_gate_up)
    unit_columns = gate_up_pieces.shape[2] // 2
    unit_shape = (w_gate_up.shape[0], unit_columns)
    inputs = tokens.astype(jnp.float32)
    normed_in, root_in = normalize(inputs)
    qkv_pieces = plan.qkv_pieces(w_qkv)
    qkv_cols, normed_in_full, gate_cols, out_rows = call(
        [
            Spread(parts, groups, qkv_pieces.shape[1:]),
            Gather(parts, block, cuts=1),
            Exchange(parts, unit_shape, delay=2),
            Fan(groups, w_out.shape),
        ],
        [qkv_pieces, normed_in.astype(LOW), gate_up_pieces[:, :, :unit_columns], w_out],
        "start",
        2,
        plane,
        micros=90,
    )
    gate_cols = gather(gate_cols.reshape(width // groups, -1), "fsdp")
    qkv_cols = qkv_cols.reshape(width, 3 * head_width)
    normed_in_full = normed_in_full.reshape(length, width)

    row_index = jnp.arange(length, dtype=jnp.int32)
    packed = initial_index(row_index, order_row)
    _, pos = places(packed, lengths)
    cosine_table, sine_table = angle_tables(pos)
    half_sign = jnp.where(jnp.arange(HEAD_DIM) < HEAD_DIM // 2, -1.0, 1.0)
    tables = (
        cosine_table[:, 0, :],
        sine_table[:, 0, :] * half_sign,
        jnp.broadcast_to((packed - pos)[:, None], (length, HEAD_DIM)),
        jnp.broadcast_to(packed[:, None], (length, HEAD_DIM)),
        jnp.broadcast_to(packed[None, :], (8, length)),
    )
    up_cols, out_cols, qkv_low, mix_low = call(
        [Exchange(parts, unit_shape), Exchange(run, (heads * shard, width))],
        [gate_up_pieces[:, :, unit_columns:], out_rows.reshape(run, heads * shard, width)],
        "attend",
        1,
        line,
        Attend(normed_in_full, qkv_cols, tables, heads),
        micros=40,
    )
    up_cols = gather(up_cols.reshape(width // groups, -1), "fsdp")
    out_cols = out_cols.reshape(run, heads, shard, width).transpose(1, 0, 2, 3)
    out_cols = out_cols.reshape(head_width, width)

    out_terms = dot(mix_low, out_cols).astype(LOW)
    attn_out, cot_full = call(
        [Scatter(parts, block, cuts=1), Gather(parts, block, cuts=1)],
        [out_terms.reshape((parts,) + block), cotangent],
        "out",
        3,
        line,
        micros=64,
    )
    cot_full = cot_full.reshape(length, width)
    residual = inputs + attn_out
    normed_mid, root_mid = normalize(residual)
    mid_job = Gather(parts, block, watched=True)
    normed_mid_full, activated, gate_back, up_back, mid_back_terms = call(
        [mid_job],
        [normed_mid.astype(LOW)],
        "mid",
        4,
        line,
        FeedForward(mid_job, cot_full, gate_cols, up_cols, down_rows),
        micros=60,
    )
    normed_mid_full = normed_mid_full.reshape(length, width)
    mid_back, gate_grad, up_grad, down_grad = call(
        [Scatter(parts, block)],
        [mid_back_terms.reshape((parts,) + block)],
        "mid_back",
        5,
        line,
        Grads([(normed_mid_full, gate_back), (normed_mid_full, up_back), (activated, cot_full)]),
    )
    gate_grad = scatter(gate_grad, "fsdp")
    up_grad = scatter(up_grad, "fsdp")
    down_grad = scatter(down_grad, "fsdp")
    residual_back = cotangent.astype(jnp.float32) + norm_back(mid_back, normed_mid, root_mid)
    proj_back = residual_back.astype(LOW)

    proj_job = Gather(parts, block, watched=True)
    _, down_terms, back_heads, out_grad = call(
        [proj_job],
        [proj_back],
        "proj_back",
        6,
        line,
        ProjectBack(proj_job, activated, down_rows, out_cols, mix_low),
        micros=45,
    )
    out_grad = out_grad.reshape(heads, run, shard, width).transpose(1, 0, 2, 3)
    down_out, out_grad, gate_grad, in_back_terms, qkv_grad = call(
        [
            Scatter(parts, block, cuts=1),
            Exchange(run, (heads * shard, width)),
            plan.unit_job(unit_shape),
        ],
        [
            down_terms.reshape((parts,) + block),
            out_grad.reshape(run, heads * shard, width),
            gate_grad.reshape((parts,) + unit_shape),
        ],
        "attend_back",
        8,
        line,
        AttendBack(back_heads, qkv_low, normed_in_full, qkv_cols, tables, heads),
        micros=60,
    )
    layer_out = (residual + down_out).astype(LOW)
    out_grad, up_grad = lax.optimization_barrier((out_grad, up_grad))
    out_grad = scatter(out_grad.reshape(groups * shard, width), "fsdp")
    in_back, qkv_grad, up_grad = call(
        [
            Scatter(parts, block),
            Collect(parts, groups, qkv_pieces.shape[1:], plan.qkv_starts),
            plan.unit_job(unit_shape),
        ],
        [
            in_back_terms.reshape((parts,) + block),
            qkv_grad.reshape((groups,) + qkv_pieces.shape),
            up_grad.reshape((parts,) + unit_shape),
        ],
        "in_back",
        7,
        plane,
        micros=90,
    )
    in_back, down_grad, out_grad = lax.optimization_barrier((in_back, down_grad, out_grad))
    tokens_grad = residual_back + norm_back(in_back, normed_in, root_in)
    return (
        layer_out,
        tokens_grad,
        qkv_grad,
        out_grad.astype(jnp.float32),
        jnp.concatenate([plan.unit_rows(gate_grad), plan.unit_rows(up_grad)], axis=1),
        down_grad.astype(jnp.float32),
    )


def solution(mesh):
    both = P(("fsdp", "ctx"), None)
    one = P("fsdp", None)
    return jax.shard_map(
        per_device,
        mesh=mesh,
        in_specs=(both, both, both, both, both, one, one, both),
        out_specs=(both,) * 6,
        check_vma=False,
    )
```

```python
import jax
import jax.numpy as jnp
from jax import lax
from jax.experimental import pallas as pl
from jax.experimental.pallas import tpu as pltpu
from jax.sharding import PartitionSpec as P

HEADS = 16
HEAD_DIM = 128
BLOCK = 128
LOW = jnp.bfloat16


def normalize(values):
    average = jnp.mean(values, axis=-1, keepdims=True)
    centered = values - average
    variance = jnp.mean(centered * centered, axis=-1, keepdims=True)
    inv_root = lax.rsqrt(variance + 1e-05)
    return (centered * inv_root, inv_root)


def norm_back(upstream, normed, inv_root):
    first_mean = jnp.mean(upstream, axis=-1, keepdims=True)
    second_mean = jnp.mean(upstream * normed, axis=-1, keepdims=True)
    return inv_root * (upstream - first_mean - normed * second_mean)


def places(token_index, lengths):
    seq_ends = jnp.cumsum(lengths)
    sequence = jnp.sum((token_index[:, None] >= seq_ends[None, :]).astype(jnp.int32), axis=1)
    before = jnp.arange(lengths.shape[0], dtype=jnp.int32)
    seq_start = jnp.sum(jnp.where(before[None, :] < sequence[:, None], lengths[None, :], 0), axis=1)
    return (sequence, token_index - seq_start)


def initial_index(row_index, order_row):
    slot_index = row_index // BLOCK
    slot_table = jnp.arange(order_row.shape[0], dtype=jnp.int32)
    picked = jnp.sum(
        jnp.where(slot_table[None, :] == slot_index[:, None], order_row[None, :], 0), axis=1
    )
    return picked * BLOCK + row_index % BLOCK


def angle_tables(position):
    half_dim = HEAD_DIM // 2
    frequency = 10000.0 ** (-jnp.arange(half_dim, dtype=jnp.float32) * 2.0 / HEAD_DIM)
    angle_table = position.astype(jnp.float32)[:, None] * frequency[None, :]
    angle_table = jnp.concatenate([angle_table, angle_table], axis=-1)
    return (jnp.cos(angle_table)[:, None, :], jnp.sin(angle_table)[:, None, :])


def rotate(values, cosine_table, sine_table):
    half_dim = values.shape[-1] // 2
    turned = jnp.concatenate([-values[..., half_dim:], values[..., :half_dim]], axis=-1)
    return values * cosine_table + turned * sine_table


def unrotate(values, cosine_table, sine_table):
    half_dim = values.shape[-1] // 2
    scaled = values * sine_table
    turned = jnp.concatenate([scaled[..., half_dim:], -scaled[..., :half_dim]], axis=-1)
    return values * cosine_table + turned


def dot(left, right):
    return jnp.dot(left, right, preferred_element_type=jnp.float32)


def times_transposed(left, right):
    return lax.dot_general(
        left, right, (((1,), (1,)), ((), ())), preferred_element_type=jnp.float32
    )


def column_product(left, right):
    return lax.dot_general(
        left, right, (((0,), (0,)), ((), ())), preferred_element_type=jnp.float32
    )


def gather(values, axes):
    return lax.all_gather(values, axes, axis=0, tiled=True)


def scatter(values, axes):
    return lax.psum_scatter(values, axes, scatter_dimension=0, tiled=True)


def enter(axes):
    barrier = pltpu.get_barrier_semaphore()
    count = 0
    for axis, size in axes:
        me = lax.axis_index(axis)
        for step in range(1, size):
            pl.semaphore_signal(barrier, inc=1, device_id={axis: lax.rem(me + step, size)})
        count += size - 1
    pl.semaphore_wait(barrier, count)


def remote(src, dst, send, recv, axis, peer):
    return pltpu.make_async_remote_copy(
        src_ref=src, dst_ref=dst, send_sem=send, recv_sem=recv, device_id={axis: peer}
    )


class Exchange:
    def __init__(self, parts, shape, delay=0, columns=None):
        self.parts, self.delay, self.columns = parts, delay, columns
        self.out = jax.ShapeDtypeStruct((parts,) + shape, LOW)
        self.scratch = [
            pltpu.SemaphoreType.DMA((parts - 1,)),
            pltpu.SemaphoreType.DMA((parts - 1,)),
            pltpu.SemaphoreType.DMA,
        ]

    def run(self, src, dst, send, recv, local):
        for _ in range(self.delay):
            yield
        place = lax.axis_index("ctx")
        me = lax.rem(place, self.parts)
        slot = dst.at[me]
        copies = []
        for step in range(1, self.parts):
            peer = lax.rem(me + step, self.parts)
            whole = (send.at[step - 1], recv.at[step - 1], "ctx", place - me + peer)
            for block, target in blocks_of(src, peer, slot, self.columns):
                copies.append(remote(block, target, *whole))
                copies[-1].start()
            if self.columns:
                del copies[step - 1 :]
                copies.append(remote(slot, slot, *whole))
        for block, target in blocks_of(src, me, slot, self.columns):
            pltpu.make_async_copy(block, target, local).start()
        yield
        for copy in copies:
            copy.wait()
            yield
        pltpu.make_async_copy(slot, slot, local).wait()


def blocks_of(src, part, slot, columns):
    if columns is None:
        return [(src.at[part], slot)]
    starts = columns(part)
    wide = slot.shape[1] // len(starts)
    return [
        (
            src.at[:, pl.ds(pl.multiple_of(start, HEAD_DIM), wide)],
            slot.at[:, pl.ds(index * wide, wide)],
        )
        for index, start in enumerate(starts)
    ]


class Gather:
    def __init__(self, parts, shape, watched=False, cuts=2):
        self.parts, self.watched, self.shape, self.cuts = parts, watched, shape, cuts
        self.out = jax.ShapeDtypeStruct((parts,) + shape, LOW)
        chips = parts // 2
        self.scratch = [
            pltpu.SemaphoreType.DMA((2, chips, self.cuts)),
            pltpu.SemaphoreType.DMA((chips, self.cuts)),
            pltpu.SemaphoreType.DMA((chips, self.cuts)),
            pltpu.SemaphoreType.DMA((chips, self.cuts)),
            pltpu.SemaphoreType.DMA,
        ]

    def run(self, src, dst, send, recv, pair_send, pair_recv, local):
        chips, cuts = self.parts // 2, self.cuts
        rows = self.shape[0] // cuts
        me = lax.axis_index("ctx")
        chip, core = me // 2, lax.rem(me, 2)
        partner = me + 1 - 2 * core

        def piece(block, cut):
            return block.at[pl.ds(cut * rows, rows)]

        def line(block, slot, origin, way, cut):
            return remote(
                piece(block, cut),
                piece(slot, cut),
                send.at[way, origin, cut],
                recv.at[origin, cut],
                "ctx",
                me + 2 - 4 * way,
            )

        def across(block, slot, origin, cut):
            return remote(
                piece(block, cut),
                piece(slot, cut),
                pair_send.at[origin, cut],
                pair_recv.at[origin, cut],
                "ctx",
                partner,
            )

        mine = dst.at[me]
        own = pltpu.make_async_copy(src, mine, local)

        def arrived(origin):
            other = dst.at[2 * origin + 1 - core]
            for cut in range(cuts):
                across(other, other, origin, cut).wait_recv()

            @pl.when(origin == chip)
            def _():
                own.wait()

        def relay(step):
            for cut in range(cuts):
                for way in range(2):
                    origin = chip - step if way == 0 else chip + step

                    @pl.when((origin >= 0) & (origin < chips))
                    def _():
                        slot = dst.at[2 * origin + core]
                        line(slot, slot, origin, way, cut).wait_recv()

                        @pl.when((chip < chips - 1) if way == 0 else (chip > 0))
                        def _():
                            line(slot, slot, origin, way, cut).start()

                        across(slot, slot, origin, cut).start()

        self.dst, self.arrived, self.relay = dst, arrived, relay
        for cut in range(cuts):

            @pl.when(chip < chips - 1)
            def _():
                line(src, mine, chip, 0, cut).start()

            @pl.when(chip > 0)
            def _():
                line(src, mine, chip, 1, cut).start()

        for cut in range(cuts):
            across(src, mine, chip, cut).start()
        own.start()
        yield
        if self.watched:
            yield
        for step in range(1, chips):
            if not self.watched:
                relay(step)
                yield
        for step in range(chips):
            for way in range(2):
                origin = chip - step if way == 0 else chip + step
                ahead = (chip < chips - 1) if way == 0 else (chip > 0)

                @pl.when((origin >= 0) & (origin < chips) & ahead)
                def _():
                    slot = dst.at[2 * origin + core]
                    for cut in range(cuts):
                        line(slot, slot, origin, way, cut).wait_send()

        for origin in range(chips):
            slot = dst.at[2 * origin + core]
            for cut in range(cuts):
                across(slot, slot, origin, cut).wait_send()
            if not self.watched:
                arrived(origin)


class Scatter:
    def __init__(self, parts, shape, cuts=2):
        self.parts, self.shape, self.cuts = parts, shape, cuts
        self.out = jax.ShapeDtypeStruct(shape, jnp.float32)
        chips = parts // 2
        piece = (self.cuts, shape[0] // self.cuts, shape[1])
        self.scratch = [
            pltpu.VMEM((chips,) + shape, LOW),
            pltpu.VMEM((2, chips) + piece, LOW),
            pltpu.VMEM((chips,) + piece, LOW),
            pltpu.SemaphoreType.DMA((chips,)),
            pltpu.SemaphoreType.DMA((chips,)),
            pltpu.SemaphoreType.DMA((chips, self.cuts)),
            pltpu.SemaphoreType.DMA((2, chips, self.cuts)),
        ]

    def run(self, src, out, pair, come, stage, pair_send, pair_recv, send, recv):
        chips, cuts = self.parts // 2, self.cuts
        me = lax.axis_index("ctx")
        chip, core = me // 2, lax.rem(me, 2)
        partner = me + 1 - 2 * core
        rows = self.shape[0] // cuts
        slab = min(rows, 16)
        last = chips - 1

        def across(goal):
            return remote(
                src.at[2 * goal + 1 - core],
                pair.at[goal],
                pair_send.at[goal],
                pair_recv.at[goal],
                "ctx",
                partner,
            )

        def line(goal, cut, way):
            return remote(
                stage.at[goal, cut],
                come.at[way, goal, cut],
                send.at[goal, cut],
                recv.at[way, goal, cut],
                "ctx",
                me + 2 - 4 * way,
            )

        def wide(ref, *index):
            return ref[index].astype(jnp.float32)

        def slabs(part):
            def one(index, carry):
                part(pl.multiple_of(index * slab, slab))
                return carry

            lax.fori_loop(0, rows // slab, one, 0)

        def both(goal, cut, at):
            at = pl.ds(cut * rows + at, slab)
            return wide(src, 2 * goal + core, at) + wide(pair, goal, at)

        order = []
        for step in range((chips + 1) // 2):
            order += sorted({step, last - step})
        for goal in order:
            across(goal).start()
        yield
        for step in range(last * cuts):
            for way in range(2):
                turn = step - (chip if way == 0 else last - chip)
                goal = (last - turn // cuts) if way == 0 else turn // cuts
                cut = step - (chip if way == 0 else last - chip) - (turn // cuts) * cuts
                first = (chip == 0) if way == 0 else (chip == last)
                ahead = last - chip if way == 0 else chip

                def begin(at):
                    value = both(goal, cut, at)
                    stage[goal, cut, pl.ds(at, slab), :] = value.astype(LOW)

                def middle(at):
                    value = both(goal, cut, at) + wide(come, way, goal, cut, pl.ds(at, slab))
                    stage[goal, cut, pl.ds(at, slab), :] = value.astype(LOW)

                @pl.when((turn >= 0) & (turn < ahead * cuts))
                def _():
                    @pl.when(cut == 0)
                    def _():
                        across(goal).wait_recv()

                    @pl.when(first)
                    def _():
                        slabs(begin)

                    @pl.when(jnp.logical_not(first))
                    def _():
                        line(goal, cut, way).wait_recv()
                        slabs(middle)

                    line(goal, cut, way).start()

            yield
        across(chip).wait_recv()
        for cut in range(cuts):

            def own(at):
                out[pl.ds(cut * rows + at, slab), :] = both(chip, cut, at)

            slabs(own)
        yield
        for cut in range(cuts):
            for way in range(2):

                def final(at):
                    out[pl.ds(cut * rows + at, slab), :] += wide(
                        come, way, chip, cut, pl.ds(at, slab)
                    )

                @pl.when((chip > 0) if way == 0 else (chip < last))
                def _():
                    line(chip, cut, way).wait_recv()
                    slabs(final)

            yield
        for goal in range(chips):
            across(goal).wait_send()

            @pl.when(chip != goal)
            def _():
                for cut in range(cuts):
                    line(goal, cut, 0).wait_send()


class Fan:
    def __init__(self, groups, shape):
        self.groups = groups
        self.out = jax.ShapeDtypeStruct((groups,) + shape, LOW)
        self.scratch = [
            pltpu.SemaphoreType.DMA((groups - 1,)),
            pltpu.SemaphoreType.DMA((groups - 1,)),
            pltpu.SemaphoreType.DMA,
        ]

    def run(self, src, dst, send, recv, local):
        groups = self.groups
        group = lax.axis_index("fsdp")
        copies = []
        for hop in range(1, groups):
            peer = lax.rem(group + hop, groups)
            copies.append(
                remote(src, dst.at[group], send.at[hop - 1], recv.at[hop - 1], "fsdp", peer)
            )
            copies[-1].start()
        own = pltpu.make_async_copy(src, dst.at[group], local)
        own.start()
        yield
        yield
        yield
        for copy in copies:
            copy.wait()
        own.wait()


class Spread:
    def __init__(self, parts, groups, shape, columns=None):
        self.parts, self.groups, self.columns = parts, groups, columns
        self.out = jax.ShapeDtypeStruct((groups, parts) + shape, LOW)
        self.scratch = [
            pltpu.SemaphoreType.DMA((parts - 1,)),
            pltpu.SemaphoreType.DMA((parts - 1,)),
            pltpu.SemaphoreType.DMA((groups - 1, parts)),
            pltpu.SemaphoreType.DMA((groups - 1, parts)),
            pltpu.SemaphoreType.DMA,
        ]

    def run(self, src, dst, send, recv, far_send, far_recv, local):
        parts, groups = self.parts, self.groups
        me, group = lax.axis_index("ctx"), lax.axis_index("fsdp")
        slot = dst.at[group, me]
        for block, target in blocks_of(src, me, slot, self.columns):
            pltpu.make_async_copy(block, target, local).start()
        copies = []
        for step in range(1, parts):
            peer = lax.rem(me + step, parts)
            whole = (send.at[step - 1], recv.at[step - 1], "ctx", peer)
            for block, target in blocks_of(src, peer, slot, self.columns):
                remote(block, target, *whole).start()
            copies.append(remote(slot, slot, *whole))
        pltpu.make_async_copy(slot, slot, local).wait()

        def pass_on(block, origin, step):
            out = []
            for hop in range(1, groups):
                copy = remote(
                    block,
                    dst.at[group, origin],
                    far_send.at[hop - 1, step],
                    far_recv.at[hop - 1, step],
                    "fsdp",
                    lax.rem(group + hop, groups),
                )
                copy.start()
                out.append(copy)
            return out

        far = pass_on(slot, me, 0)
        eager = -(-parts // 2)
        yield
        for step in range(1, parts):
            copies[step - 1].wait_recv()
            origin = lax.rem(me - step + parts, parts)
            far += pass_on(dst.at[group, origin], origin, step)
            if step % eager == 0:
                yield
        for at, copy in enumerate(far):
            copy.wait()
            if at % 6 == 5:
                yield
        for copy in copies:
            copy.wait_send()


class Deliver:
    def __init__(self, parts, shape, offsets, delay=0, eager=1):
        self.parts, self.shape, self.offsets = parts, shape, offsets
        self.delay, self.eager = delay, eager
        self.out = jax.ShapeDtypeStruct((shape[0], parts * shape[1]), jnp.float32)
        self.scratch = [
            pltpu.VMEM((parts - 1,) + shape, LOW),
            pltpu.SemaphoreType.DMA((parts - 1,)),
            pltpu.SemaphoreType.DMA((parts - 1,)),
        ]

    def place(self, out, origin, read):
        starts = self.offsets(origin)
        step = self.shape[1] // len(starts)
        for index, start in enumerate(starts):
            out[:, pl.ds(pl.multiple_of(start, HEAD_DIM), step)] = read(
                index * step, (index + 1) * step
            )

    def send(self, me, step, block, came, send, recv):
        return remote(
            block,
            came.at[step - 1],
            send.at[step - 1],
            recv.at[step - 1],
            "ctx",
            lax.rem(me + step, self.parts),
        )

    def run(self, src, out, came, send, recv):
        for _ in range(self.delay):
            yield
        me = lax.axis_index("ctx")
        copies = []
        for step in range(1, self.parts):
            block = src.at[lax.rem(me + step, self.parts)]
            copies.append(self.send(me, step, block, came, send, recv))
            copies[-1].start()
        self.place(out, me, lambda lo, hi: src[me, :, lo:hi].astype(jnp.float32))
        yield
        yield from self.finish(me, out, copies, came)

    def finish(self, me, out, copies, came):
        for step in range(1, self.parts):
            copies[step - 1].wait_recv()
            origin = lax.rem(me - step + self.parts, self.parts)
            self.place(out, origin, lambda lo, hi: came[step - 1, :, lo:hi].astype(jnp.float32))
            if step % self.eager == 0:
                yield
        for copy in copies:
            copy.wait_send()


class Collect(Deliver):
    def __init__(self, parts, groups, shape, offsets, delay=0, eager=1):
        super().__init__(parts, shape, offsets, delay, eager)
        self.groups = groups
        self.scratch = self.scratch + [
            pltpu.VMEM((groups - 1, parts) + shape, LOW),
            pltpu.VMEM((parts,) + shape, LOW),
            pltpu.VMEM(shape, jnp.float32),
            pltpu.SemaphoreType.DMA((groups - 1, parts)),
            pltpu.SemaphoreType.DMA((groups - 1, parts)),
        ]

    def run(self, src, out, came, send, recv, far, stage, mine, far_send, far_recv):
        parts, groups = self.parts, self.groups
        me, group = lax.axis_index("ctx"), lax.axis_index("fsdp")
        goals = [lax.rem(me + step, parts) for step in range(1, parts + 1)]
        hops = []
        for goal in goals:
            for hop in range(1, groups):
                peer = lax.rem(group + hop, groups)
                hops.append(
                    remote(
                        src.at[peer, goal],
                        far.at[hop - 1, goal],
                        far_send.at[hop - 1, goal],
                        far_recv.at[hop - 1, goal],
                        "fsdp",
                        peer,
                    )
                )
                hops[-1].start()
        yield
        copies = []
        for step in range(1, parts + 1):
            goal = goals[step - 1]
            for copy in hops[(step - 1) * (groups - 1) : step * (groups - 1)]:
                copy.wait_recv()
            value = src[group, goal].astype(jnp.float32)
            for hop in range(groups - 1):
                value += far[hop, goal].astype(jnp.float32)
            if step < parts:
                stage[goal] = value.astype(LOW)
                copies.append(self.send(me, step, stage.at[goal], came, send, recv))
                copies[-1].start()
            else:
                mine[...] = value
            if step % self.eager == 0:
                yield
        self.place(out, me, lambda lo, hi: mine[:, lo:hi])
        yield from self.finish(me, out, copies, came)
        for copy in hops:
            copy.wait_send()


def call(jobs, operands, name, identity, axes, work=None, micros=50):
    counts = [len(job.scratch) for job in jobs]
    jobs_n = len(jobs)
    extra = work.operands if work else []
    extra_out = work.outs if work else []
    extra_scratch = work.scratch if work else []

    def kernel(*refs):
        refs = list(refs)

        def take(count):
            taken = refs[:count]
            del refs[:count]
            return taken

        ins, more = take(jobs_n), take(len(extra))
        outs, more_outs = take(jobs_n), take(len(extra_out))
        runs = []
        for job, src, dst, count in zip(jobs, ins, outs, counts):
            runs.append(job.run(src, dst, *take(count)))
        if work:
            runs.append(work.run(*more, *more_outs, *refs))
        enter(axes)
        while runs:
            going = []
            for run in runs:
                try:
                    next(run)
                    going.append(run)
                except StopIteration:
                    pass
            runs = going

    vmem = pl.BlockSpec(memory_space=pltpu.VMEM)
    anywhere = pl.BlockSpec(memory_space=pl.ANY)
    return pl.pallas_call(
        kernel,
        out_shape=tuple(job.out for job in jobs) + tuple(extra_out),
        in_specs=[vmem] * jobs_n + [anywhere] * len(extra),
        out_specs=(vmem,) * jobs_n + (anywhere,) * len(extra_out),
        scratch_shapes=[shape for job in jobs for shape in job.scratch] + list(extra_scratch),
        compiler_params=pltpu.CompilerParams(
            collective_id=identity, has_side_effects=True, vmem_limit_bytes=62 << 20
        ),
        cost_estimate=pl.CostEstimate(
            flops=0, bytes_accessed=micros * 3_000_000, transcendentals=0
        ),
        name=name,
    )(*operands, *extra)


def product(left, right):
    return jnp.dot(left, right, preferred_element_type=jnp.float32)


class Puts:
    def __init__(self, made, put):
        self.made, self.put, self.copies = made, put, []

    def pair(self, fill, columns, out, at, tile):
        for copy in self.copies:
            copy.wait()
        lax.fori_loop(0, 2, fill, 0)
        self.copies = []
        for half in range(2):
            begin = at + half * tile
            copy = pltpu.make_async_copy(
                self.made.at[half, :, pl.ds(0, columns)],
                out.at[begin : begin + tile, :],
                self.put.at[half],
            )
            copy.start()
            self.copies.append(copy)

    def finish(self):
        for copy in self.copies:
            copy.wait()


class Grads:
    tile = 256

    def __init__(self, pairs):
        self.pairs = pairs
        length, wide = pairs[0][0].shape[0], max(right.shape[1] for _, right in pairs)
        self.operands = [array for pair in pairs for array in pair]
        self.outs = [jax.ShapeDtypeStruct((l.shape[1], r.shape[1]), LOW) for l, r in pairs]
        self.slots = [[id(array) for array in self.operands].index(id(a)) for a in self.operands]
        self.operands = [a for i, a in enumerate(self.operands) if self.slots[i] == i]
        self.slots = [sorted(set(self.slots)).index(slot) for slot in self.slots]
        self.scratch = [pltpu.VMEM(array.shape, LOW) for array in self.operands]
        self.scratch += [
            pltpu.VMEM((self.tile, length), LOW),
            pltpu.VMEM((2, self.tile, wide), LOW),
            pltpu.SemaphoreType.DMA((len(self.operands),)),
            pltpu.SemaphoreType.DMA((2,)),
        ]

    def run(self, *refs):
        n, tile, count = len(self.pairs), self.tile, len(self.operands)
        sources, outs = refs[:count], refs[count : count + n]
        held = refs[count + n : 2 * count + n]
        turned, made, get, put = refs[2 * count + n :]
        gets = [pltpu.make_async_copy(s, h, get.at[i]) for i, (s, h) in enumerate(zip(sources, held))]
        for copy in gets:
            copy.start()
        yield
        puts = Puts(made, put)
        for which in range(n):
            first, second = self.slots[2 * which : 2 * which + 2]
            left, right, out = held[first], held[second], outs[which]
            for slot in (first, second):
                if slot not in self.slots[: 2 * which]:
                    gets[slot].wait()
            columns = right.shape[1]
            step = min(columns, 256)
            for at in range(0, left.shape[1], 2 * tile):
                def pair(half, carry):
                    begin = pl.multiple_of(at + half * tile, tile)
                    turned[...] = left[:, pl.ds(begin, tile)].T

                    def one(index, carry):
                        where = pl.ds(pl.multiple_of(index * step, step), step)
                        made[half, :, where] = product(turned[...], right[:, where]).astype(LOW)
                        return carry

                    return lax.fori_loop(0, columns // step, one, carry)

                puts.pair(pair, columns, out, at, tile)
                yield
        puts.finish()


class Deliver:
    def __init__(self, parts, shape, offsets, delay=0, eager=1):
        self.parts, self.shape, self.offsets = parts, shape, offsets
        self.delay, self.eager = delay, eager
        self.out = jax.ShapeDtypeStruct((shape[0], parts * shape[1]), jnp.float32)
        self.scratch = [
            pltpu.VMEM((parts - 1,) + shape, LOW),
            pltpu.SemaphoreType.DMA((parts - 1,)),
            pltpu.SemaphoreType.DMA((parts - 1,)),
        ]

    def place(self, out, origin, read):
        starts = self.offsets(origin)
        step = self.shape[1] // len(starts)
        for index, start in enumerate(starts):
            out[:, pl.ds(pl.multiple_of(start, HEAD_DIM), step)] = read(
                index * step, (index + 1) * step
            )

    def send(self, me, step, block, came, send, recv):
        return remote(
            block,
            came.at[step - 1],
            send.at[step - 1],
            recv.at[step - 1],
            "ctx",
            lax.rem(me + step, self.parts),
        )

    def run(self, src, out, came, send, recv):
        for _ in range(self.delay):
            yield
        me = lax.axis_index("ctx")
        copies = []
        for step in range(1, self.parts):
            block = src.at[lax.rem(me + step, self.parts)]
            copies.append(self.send(me, step, block, came, send, recv))
            copies[-1].start()
        self.place(out, me, lambda lo, hi: src[me, :, lo:hi].astype(jnp.float32))
        yield
        yield from self.finish(me, out, copies, came)

    def finish(self, me, out, copies, came):
        for step in range(1, self.parts):
            copies[step - 1].wait_recv()
            origin = lax.rem(me - step + self.parts, self.parts)
            self.place(out, origin, lambda lo, hi: came[step - 1, :, lo:hi].astype(jnp.float32))
            if step % self.eager == 0:
                yield
        for copy in copies:
            copy.wait_send()


class Collect(Deliver):
    def __init__(self, parts, groups, shape, offsets, delay=0, eager=1):
        super().__init__(parts, shape, offsets, delay, eager)
        self.groups = groups
        self.scratch = self.scratch + [
            pltpu.VMEM((groups - 1, parts) + shape, LOW),
            pltpu.VMEM((parts,) + shape, LOW),
            pltpu.VMEM(shape, jnp.float32),
            pltpu.SemaphoreType.DMA((groups - 1, parts)),
            pltpu.SemaphoreType.DMA((groups - 1, parts)),
        ]

    def run(self, src, out, came, send, recv, far, stage, mine, far_send, far_recv):
        parts, groups = self.parts, self.groups
        me, group = lax.axis_index("ctx"), lax.axis_index("fsdp")
        goals = [lax.rem(me + step, parts) for step in range(1, parts + 1)]
        hops = []
        for goal in goals:
            for hop in range(1, groups):
                peer = lax.rem(group + hop, groups)
                hops.append(
                    remote(
                        src.at[peer, goal],
                        far.at[hop - 1, goal],
                        far_send.at[hop - 1, goal],
                        far_recv.at[hop - 1, goal],
                        "fsdp",
                        peer,
                    )
                )
                hops[-1].start()
        yield
        copies = []
        for step in range(1, parts + 1):
            goal = goals[step - 1]
            for copy in hops[(step - 1) * (groups - 1) : step * (groups - 1)]:
                copy.wait_recv()
            value = src[group, goal].astype(jnp.float32)
            for hop in range(groups - 1):
                value += far[hop, goal].astype(jnp.float32)
            if step < parts:
                stage[goal] = value.astype(LOW)
                copies.append(self.send(me, step, stage.at[goal], came, send, recv))
                copies[-1].start()
            else:
                mine[...] = value
            if step % self.eager == 0:
                yield
        self.place(out, me, lambda lo, hi: mine[:, lo:hi])
        yield from self.finish(me, out, copies, came)
        for copy in hops:
            copy.wait_send()


def call(jobs, operands, name, identity, axes, work=None, micros=50):
    counts = [len(job.scratch) for job in jobs]
    jobs_n = len(jobs)
    extra = work.operands if work else []
    extra_out = work.outs if work else []
    extra_scratch = work.scratch if work else []

    def kernel(*refs):
        refs = list(refs)

        def take(count):
            taken = refs[:count]
            del refs[:count]
            return taken

        ins, more = take(jobs_n), take(len(extra))
        outs, more_outs = take(jobs_n), take(len(extra_out))
        runs = []
        for job, src, dst, count in zip(jobs, ins, outs, counts):
            runs.append(job.run(src, dst, *take(count)))
        if work:
            runs.append(work.run(*more, *more_outs, *refs))
        enter(axes)
        while runs:
            going = []
            for run in runs:
                try:
                    next(run)
                    going.append(run)
                except StopIteration:
                    pass
            runs = going

    vmem = pl.BlockSpec(memory_space=pltpu.VMEM)
    anywhere = pl.BlockSpec(memory_space=pl.ANY)
    return pl.pallas_call(
        kernel,
        out_shape=tuple(job.out for job in jobs) + tuple(extra_out),
        in_specs=[vmem] * jobs_n + [anywhere] * len(extra),
        out_specs=(vmem,) * jobs_n + (anywhere,) * len(extra_out),
        scratch_shapes=[shape for job in jobs for shape in job.scratch] + list(extra_scratch),
        compiler_params=pltpu.CompilerParams(
            collective_id=identity, has_side_effects=True, vmem_limit_bytes=62 << 20
        ),
        cost_estimate=pl.CostEstimate(
            flops=0, bytes_accessed=micros * 3_000_000, transcendentals=0
        ),
        name=name,
    )(*operands, *extra)


class Grads:
    tile = 256

    def __init__(self, pairs):
        self.pairs = pairs
        length, wide = pairs[0][0].shape[0], max(right.shape[1] for _, right in pairs)
        self.operands = [array for pair in pairs for array in pair]
        self.outs = [jax.ShapeDtypeStruct((l.shape[1], r.shape[1]), LOW) for l, r in pairs]
        self.slots = [[id(array) for array in self.operands].index(id(a)) for a in self.operands]
        self.operands = [a for i, a in enumerate(self.operands) if self.slots[i] == i]
        self.slots = [sorted(set(self.slots)).index(slot) for slot in self.slots]
        self.scratch = [pltpu.VMEM(array.shape, LOW) for array in self.operands]
        self.scratch += [
            pltpu.VMEM((self.tile, length), LOW),
            pltpu.VMEM((2, self.tile, wide), LOW),
            pltpu.SemaphoreType.DMA((len(self.operands),)),
            pltpu.SemaphoreType.DMA((2,)),
        ]

    def run(self, *refs):
        n, tile, count = len(self.pairs), self.tile, len(self.operands)
        sources, outs = refs[:count], refs[count : count + n]
        held = refs[count + n : 2 * count + n]
        turned, made, get, put = refs[2 * count + n :]
        gets = [pltpu.make_async_copy(s, h, get.at[i]) for i, (s, h) in enumerate(zip(sources, held))]
        for copy in gets:
            copy.start()
        yield
        puts = []
        for which in range(n):
            first, second = self.slots[2 * which : 2 * which + 2]
            left, right, out = held[first], held[second], outs[which]
            for slot in (first, second):
                if slot not in self.slots[: 2 * which]:
                    gets[slot].wait()
            columns = right.shape[1]
            step = min(columns, 512)
            for at in range(0, left.shape[1], tile):
                slot = len(puts) % 2
                if len(puts) >= 2:
                    puts[-2].wait()
                turned[...] = left[:, at : at + tile].T

                def one(index, carry):
                    where = pl.ds(pl.multiple_of(index * step, step), step)
                    made[slot, :, where] = jnp.dot(
                        turned[...], right[:, where], preferred_element_type=jnp.float32
                    ).astype(LOW)
                    return carry

                lax.fori_loop(0, columns // step, one, 0)
                part = made.at[slot] if columns == made.shape[2] else made.at[slot, :, :columns]
                puts.append(pltpu.make_async_copy(part, out.at[at : at + tile, :], put.at[slot]))
                puts[-1].start()
                yield
        for copy in puts[-2:]:
            copy.wait()


def softmax_block(query, keys, ok):
    scores = times_transposed(query, keys) * HEAD_DIM ** (-0.5)
    scores = jnp.where(ok, scores, -1e30)
    weights = jnp.exp(scores - jnp.max(scores, axis=-1, keepdims=True))
    weights = jnp.where(ok, weights, 0.0)
    return weights, jnp.sum(weights, axis=-1, keepdims=True)


class Attend:
    tile = 256

    def __init__(self, rows, weight, tables, heads):
        self.heads = heads
        self.operands = [rows, weight] + list(tables)
        length, wide = rows.shape[0], weight.shape[1]
        self.outs = [
            jax.ShapeDtypeStruct((length, wide), LOW),
            jax.ShapeDtypeStruct((length, wide // 3), LOW),
        ]
        self.scratch = [pltpu.VMEM(array.shape, array.dtype) for array in self.operands]
        self.scratch += [pltpu.VMEM(out.shape, out.dtype) for out in self.outs]
        self.scratch += [
            pltpu.SemaphoreType.DMA((len(self.operands),)),
            pltpu.SemaphoreType.DMA((2,)),
        ]

    def run(self, *refs):
        n, tile, heads = len(self.operands), self.tile, self.heads
        sources, results, held = refs[:n], refs[n : n + 2], refs[n + 2 : 2 * n + 2]
        qkv, mix, get, put = refs[2 * n + 2 :]
        rows, weight, cosine, sine, first, last, keys = held
        gets = [pltpu.make_async_copy(s, h, get.at[i]) for i, (s, h) in enumerate(zip(sources, held))]
        for copy in gets:
            copy.start()
        yield
        for copy in gets:
            copy.wait()
        width = heads * HEAD_DIM

        def project(index, carry):
            at = pl.ds(pl.multiple_of(index * tile, tile), tile)
            value = product(rows[at, :], weight[...])
            for head in range(3 * heads):
                block = value[:, head * HEAD_DIM : (head + 1) * HEAD_DIM]
                if head < 2 * heads:
                    turned = pltpu.roll(block, HEAD_DIM // 2, 1)
                    block = block * cosine[at, :] + turned * sine[at, :]
                qkv[at, head * HEAD_DIM : (head + 1) * HEAD_DIM] = block.astype(LOW)
            return carry

        lax.fori_loop(0, rows.shape[0] // tile, project, 0)
        send = pltpu.make_async_copy(qkv, results[0], put.at[0])
        send.start()
        yield

        def attend(index, carry):
            at = pl.ds(pl.multiple_of(index * tile, tile), tile)
            ok = (keys[:1, :] >= first[at, :1]) & (keys[:1, :] <= last[at, :1])
            for head in range(heads):
                lo = head * HEAD_DIM
                weights, total = softmax_block(
                    qkv[at, lo : lo + HEAD_DIM], qkv[:, width + lo : width + lo + HEAD_DIM], ok
                )
                value = qkv[:, 2 * width + lo : 2 * width + lo + HEAD_DIM]
                mixed = product(weights.astype(LOW), value) / total
                mix[at, lo : lo + HEAD_DIM] = mixed.astype(LOW)
            return carry

        lax.fori_loop(0, rows.shape[0] // tile, attend, 0)
        send_mix = pltpu.make_async_copy(mix, results[1], put.at[1])
        send_mix.start()
        yield
        send.wait()
        send_mix.wait()


class AttendBack:
    tile = 256

    def __init__(self, back, qkv, rows, weight, tables, heads):
        self.heads = heads
        self.operands = [back, qkv] + list(tables) + [weight, rows]
        length, wide, width = rows.shape[0], weight.shape[1], rows.shape[1]
        self.outs = [
            jax.ShapeDtypeStruct((length, width), LOW),
            jax.ShapeDtypeStruct((width, wide), LOW),
        ]
        self.scratch = [pltpu.VMEM(array.shape, array.dtype) for array in self.operands]
        self.scratch += [
            pltpu.VMEM((length, wide), LOW),
            pltpu.VMEM((2, length, HEAD_DIM), jnp.float32),
            pltpu.VMEM((self.tile, length), LOW),
            pltpu.VMEM((2, self.tile, width), LOW),
            pltpu.SemaphoreType.DMA((len(self.operands),)),
            pltpu.SemaphoreType.DMA((2,)),
        ]

    def run(self, *refs):
        n, tile, heads = len(self.operands), self.tile, self.heads
        sources, results, held = refs[:n], refs[n : n + 2], refs[n + 2 : 2 * n + 2]
        grads, sums, turned, made, get, put = refs[2 * n + 2 :]
        back, qkv, cosine, sine, first, last, keys, weight, rows = held
        length, width = back.shape
        gets = [pltpu.make_async_copy(s, h, get.at[i]) for i, (s, h) in enumerate(zip(sources, held))]
        for copy in gets:
            copy.start()
        yield
        for copy in gets[:-2]:
            copy.wait()

        def unrotated(value, at):
            return value * cosine[at, :] - pltpu.roll(value, HEAD_DIM // 2, 1) * sine[at, :]

        for head in range(heads):
            lo = head * HEAD_DIM
            mine = slice(lo, lo + HEAD_DIM)
            key = slice(width + lo, width + lo + HEAD_DIM)
            val = slice(2 * width + lo, 2 * width + lo + HEAD_DIM)
            sums[...] = jnp.zeros_like(sums)

            def attend(index, carry):
                at = pl.ds(pl.multiple_of(index * tile, tile), tile)
                ok = (keys[:1, :] >= first[at, :1]) & (keys[:1, :] <= last[at, :1])
                weights, total = softmax_block(qkv[at, mine], qkv[:, key], ok)
                probs = weights / total
                upper = back[at, mine]
                prob_back = times_transposed(upper, qkv[:, val])
                delta = jnp.sum(probs * prob_back, axis=-1, keepdims=True)
                score_back = HEAD_DIM ** (-0.5) * probs * (prob_back - delta)
                score_low = score_back.astype(LOW)
                query_back = product(score_low, qkv[:, key])
                grads[at, mine] = unrotated(query_back, at).astype(LOW)
                sums[0] += product(score_low.T, qkv[at, mine])
                sums[1] += product(probs.astype(LOW).T, upper)
                return carry

            lax.fori_loop(0, length // tile, attend, 0)
            yield

            def settle(index, carry):
                at = pl.ds(pl.multiple_of(index * tile, tile), tile)
                grads[at, key] = unrotated(sums[0, at, :], at).astype(LOW)
                grads[at, val] = sums[1, at, :].astype(LOW)
                return carry

            lax.fori_loop(0, length // tile, settle, 0)
        puts = Puts(made, put)
        wide = grads.shape[1]
        part = tile if wide % tile == 0 else HEAD_DIM
        gets[-2].wait()
        for at in range(0, length, 2 * tile):

            def terms(half, carry):
                where = pl.ds(pl.multiple_of(at + half * tile, tile), tile)

                def one(index, carry):
                    span = pl.ds(pl.multiple_of(index * tile, tile), tile)
                    value = times_transposed(grads[where, :], weight[span, :])
                    made[half, :, span] = value.astype(LOW)
                    return carry

                return lax.fori_loop(0, made.shape[2] // tile, one, carry)

            puts.pair(terms, made.shape[2], results[0], at, tile)
            yield
        gets[-1].wait()
        for at in range(0, rows.shape[1], 2 * tile):

            def weights(half, carry):
                where = pl.ds(pl.multiple_of(at + half * tile, tile), tile)
                turned[...] = rows[:, where].T

                def one(index, carry):
                    span = pl.ds(pl.multiple_of(index * part, part), part)
                    made[half, :, span] = product(turned[...], grads[:, span]).astype(LOW)
                    return carry

                return lax.fori_loop(0, wide // part, one, carry)

            puts.pair(weights, wide, results[1], at, tile)
            yield
        puts.finish()


def near_first(chips):
    table = []
    for chip in range(chips):
        order = [chip]
        for step in range(1, chips):
            order += [at for at in (chip + step, chip - step) if 0 <= at < chips]
        table.append(order)
    return table


def next_chip(chips, turn):
    chip = lax.axis_index("ctx") // 2
    return sum(
        jnp.where((chip == at) & (turn == when), order[when], 0)
        for at, order in enumerate(near_first(chips))
        for when in range(chips)
    )


class ProjectBack:
    tile = 256

    def __init__(self, job, activated, down, out_rows, mix):
        self.job = job
        self.operands = [activated, down, out_rows, mix]
        length, heads_width = mix.shape
        width = down.shape[1]
        self.outs = [
            jax.ShapeDtypeStruct((length, width), LOW),
            jax.ShapeDtypeStruct((length, heads_width), LOW),
            jax.ShapeDtypeStruct((heads_width, width), LOW),
        ]
        self.scratch = [pltpu.VMEM(array.shape, array.dtype) for array in self.operands]
        self.scratch += [
            pltpu.VMEM((2, self.tile, width), LOW),
            pltpu.VMEM((length, heads_width), LOW),
            pltpu.VMEM((heads_width, width), jnp.float32),
            pltpu.VMEM((heads_width, width), LOW),
            pltpu.SemaphoreType.DMA((4,)),
            pltpu.SemaphoreType.DMA((2,)),
            pltpu.SemaphoreType.DMA((2,)),
        ]

    def run(self, *refs):
        job, tile = self.job, self.tile
        sources, results, held = refs[:4], refs[4:7], refs[7:11]
        made, back, total, total_low, get, put, leave = refs[11:]
        activated, down, out_rows, mix = held
        length, width = mix.shape[0], down.shape[1]
        gets = [pltpu.make_async_copy(s, h, get.at[i]) for i, (s, h) in enumerate(zip(sources, held))]
        for copy in gets:
            copy.start()
        yield
        for copy in gets:
            copy.wait()
        total[...] = jnp.zeros_like(total)
        puts = Puts(made, put)
        for at in range(0, length, 2 * tile):

            def terms(half, carry):
                where = pl.ds(pl.multiple_of(at + half * tile, tile), tile)

                def one(index, carry):
                    span = pl.ds(pl.multiple_of(index * tile, tile), tile)
                    value = product(activated[where, :], down[:, span])
                    made[half, :, span] = value.astype(LOW)
                    return carry

                return lax.fori_loop(0, width // tile, one, carry)

            puts.pair(terms, width, results[0], at, tile)
        chips = job.parts // 2
        rows = length // chips

        def one_chip(turn, carry):
            origin = next_chip(chips, turn)

            @pl.when(turn > 0)
            def _():
                job.relay(turn)

            job.arrived(origin)
            at = pl.ds(pl.multiple_of(origin * rows, rows), rows)
            block = job.dst.at[pl.ds(2 * origin, 2)]
            value = block[...].reshape(rows, width)
            back[at, :] = times_transposed(value, out_rows[...]).astype(LOW)
            total[...] += product(mix[at, :].T, value)
            return carry

        lax.fori_loop(0, chips, one_chip, 0)
        total_low[...] = total[...].astype(LOW)
        out = [
            pltpu.make_async_copy(back, results[1], leave.at[0]),
            pltpu.make_async_copy(total_low, results[2], leave.at[1]),
        ]
        for copy in out:
            copy.start()
        puts.finish()
        for copy in out:
            copy.wait()


class FeedForward:
    def __init__(self, job, upstream, gate, up, down):
        self.job = job
        self.operands = [upstream, gate, up, down]
        length, width = upstream.shape
        units = gate.shape[1]
        self.outs = [
            jax.ShapeDtypeStruct((length, units), LOW),
            jax.ShapeDtypeStruct((length, 2 * units), LOW),
            jax.ShapeDtypeStruct((length, width), LOW),
        ]
        self.tile = length // (job.parts // 2)
        self.scratch = [pltpu.VMEM(array.shape, array.dtype) for array in self.operands]
        self.scratch += [pltpu.VMEM((2, self.tile) + out.shape[1:], LOW) for out in self.outs]
        self.scratch += [pltpu.SemaphoreType.DMA((4,)), pltpu.SemaphoreType.DMA((3, 2))]

    def run(self, *refs):
        job, tile = self.job, self.tile
        sources, results, held, made = refs[:4], refs[4:7], refs[7:11], refs[11:14]
        get, put = refs[14:]
        upstream, gate_w, up_w, down = held
        acts, backs, terms = made
        width, units = gate_w.shape
        step = min(units, 256)
        span = min(width, 512)
        gets = [pltpu.make_async_copy(sources[i], held[i], get.at[i]) for i in (1, 2, 3, 0)]
        for copy in gets:
            copy.start()
        yield
        for copy in gets:
            copy.wait()
        chips = job.parts // 2

        def leave(slot, origin):
            at = pl.ds(pl.multiple_of(origin * tile, tile), tile)
            return [
                pltpu.make_async_copy(made[i].at[slot], results[i].at[at, :], put.at[i, slot])
                for i in range(3)
            ]

        def one_chip(turn, carry):
            origin = next_chip(chips, turn)
            slot = lax.rem(turn, 2)

            @pl.when(turn > 0)
            def _():
                job.relay(turn)

            @pl.when(turn >= 2)
            def _():
                for copy in leave(slot, 0):
                    copy.wait()

            job.arrived(origin)
            at = pl.ds(pl.multiple_of(origin * tile, tile), tile)
            normed = job.dst.at[pl.ds(2 * origin, 2)]

            def forward(index, carry):
                left = pl.ds(pl.multiple_of(index * step, step), step)
                right = pl.ds(pl.multiple_of(units + index * step, step), step)
                value = normed[...].reshape(tile, width)
                gate = product(value, gate_w[:, left])
                up = product(value, up_w[:, left])
                act_grad = times_transposed(upstream[at, :], down[left, :])
                sigmoid = jax.nn.sigmoid(gate)
                silu = gate * sigmoid
                acts[slot, :, left] = (silu * up).astype(LOW)
                gate_grad = act_grad * up * sigmoid * (1.0 + gate * (1.0 - sigmoid))
                backs[slot, :, left] = gate_grad.astype(LOW)
                backs[slot, :, right] = (act_grad * silu).astype(LOW)
                return carry

            lax.fori_loop(0, units // step, forward, 0)

            def backward(index, carry):
                where = pl.ds(pl.multiple_of(index * span, span), span)
                value = times_transposed(backs[slot, :, :units], gate_w[where, :])
                value += times_transposed(backs[slot, :, units:], up_w[where, :])
                terms[slot, :, where] = value.astype(LOW)
                return carry

            lax.fori_loop(0, width // span, backward, 0)
            for copy in leave(slot, origin):
                copy.start()
            return carry

        lax.fori_loop(0, chips, one_chip, 0)
        for slot in range(min(2, chips)):
            for copy in leave(slot, 0):
                copy.wait()


class Plan:
    def __init__(self, parts, groups, width):
        self.parts, self.groups = parts, groups
        self.shard = width // (parts * groups)
        self.run = HEAD_DIM // self.shard
        self.heads = HEADS // parts

    def qkv_starts(self, part):
        at, index = part // self.run, lax.rem(part, self.run)
        return [
            (kind * HEADS + (index * self.heads + head) * (self.parts // self.run) + at) * HEAD_DIM
            for kind in range(3)
            for head in range(self.heads)
        ]

    def unit_source(self, weight, kind):
        rows, columns = weight.shape
        half = columns // 2
        step = half // (self.groups * self.parts)
        if step % HEAD_DIM == 0:
            return weight, lambda part: [
                kind * half + (at * self.parts + part) * step for at in range(self.groups)
            ]
        pieces = weight[:, kind * half : (kind + 1) * half]
        pieces = pieces.reshape(rows, self.groups, self.parts, step).transpose(2, 0, 1, 3)
        return pieces.reshape(self.parts, rows, self.groups * step), None

    def unit_job(self, shape):
        step = shape[1] // (2 * self.groups)
        if step % HEAD_DIM:
            return Exchange(self.parts, shape)
        return Deliver(
            self.parts,
            shape,
            lambda part: [(at * self.parts + part) * step for at in range(2 * self.groups)],
        )

    def unit_rows(self, pieces):
        if pieces.ndim == 2:
            return pieces
        parts, rows, columns = pieces.shape
        outer = 2 * self.groups
        pieces = pieces.reshape(parts, rows, outer, columns // outer).transpose(1, 2, 0, 3)
        return pieces.reshape(rows, parts * columns).astype(jnp.float32)


def per_device(tokens, w_qkv, w_out, w_gate_up, w_down, seq_lengths, block_order, cotangent):
    lengths = seq_lengths[0]
    order_row = block_order[0]
    parts = lax.axis_size("ctx")
    groups = lax.axis_size("fsdp")
    rows, width = tokens.shape
    length = rows * parts
    plan = Plan(parts, groups, width)
    heads, shard, run = plan.heads, plan.shard, plan.run
    head_width = heads * HEAD_DIM
    line = (("ctx", parts),)
    plane = (("ctx", parts), ("fsdp", groups))
    block = (rows, width)

    down_rows = gather(w_down, "fsdp")
    unit_columns = w_gate_up.shape[1] // (2 * parts)
    unit_shape = (w_gate_up.shape[0], unit_columns)
    both_shape = (w_gate_up.shape[0], 2 * unit_columns)
    qkv_shape = (w_qkv.shape[0], 3 * head_width)
    gate_source, gate_starts = plan.unit_source(w_gate_up, 0)
    up_source, up_starts = plan.unit_source(w_gate_up, 1)
    inputs = tokens.astype(jnp.float32)
    normed_in, root_in = normalize(inputs)
    qkv_cols, normed_in_full, gate_cols, out_rows = call(
        [
            Spread(parts, groups, qkv_shape, plan.qkv_starts),
            Gather(parts, block, cuts=1),
            Exchange(parts, unit_shape, 2, gate_starts),
            Fan(groups, w_out.shape),
        ],
        [w_qkv, normed_in.astype(LOW), gate_source, w_out],
        "start",
        2,
        plane,
        micros=90,
    )
    gate_cols = gather(gate_cols.reshape(width // groups, -1), "fsdp")
    qkv_cols = qkv_cols.reshape(width, 3 * head_width)
    normed_in_full = normed_in_full.reshape(length, width)

    row_index = jnp.arange(length, dtype=jnp.int32)
    packed = initial_index(row_index, order_row)
    _, pos = places(packed, lengths)
    cosine_table, sine_table = angle_tables(pos)
    half_sign = jnp.where(jnp.arange(HEAD_DIM) < HEAD_DIM // 2, -1.0, 1.0)
    tables = (
        cosine_table[:, 0, :],
        sine_table[:, 0, :] * half_sign,
        jnp.broadcast_to((packed - pos)[:, None], (length, HEAD_DIM)),
        jnp.broadcast_to(packed[:, None], (length, HEAD_DIM)),
        jnp.broadcast_to(packed[None, :], (8, length)),
    )
    up_cols, out_cols, qkv_low, mix_low = call(
        [
            Exchange(parts, unit_shape, 0, up_starts),
            Exchange(run, (heads * shard, width)),
        ],
        [up_source, out_rows.reshape(run, heads * shard, width)],
        "attend",
        1,
        line,
        Attend(normed_in_full, qkv_cols, tables, heads),
        micros=40,
    )
    up_cols = gather(up_cols.reshape(width // groups, -1), "fsdp")
    out_cols = out_cols.reshape(run, heads, shard, width).transpose(1, 0, 2, 3)
    out_cols = out_cols.reshape(head_width, width)

    out_terms = dot(mix_low, out_cols).astype(LOW)
    attn_out, cot_full = call(
        [Scatter(parts, block, cuts=1), Gather(parts, block, cuts=1)],
        [out_terms.reshape((parts,) + block), cotangent],
        "out",
        3,
        line,
        micros=64,
    )
    cot_full = cot_full.reshape(length, width)
    residual = inputs + attn_out
    normed_mid, root_mid = normalize(residual)
    mid_job = Gather(parts, block, watched=True)
    normed_mid_full, activated, gate_up_back, mid_back_terms = call(
        [mid_job],
        [normed_mid.astype(LOW)],
        "mid",
        4,
        line,
        FeedForward(mid_job, cot_full, gate_cols, up_cols, down_rows),
        micros=60,
    )
    normed_mid_full = normed_mid_full.reshape(length, width)
    mid_back, gate_up_grad, down_grad = call(
        [Scatter(parts, block)],
        [mid_back_terms.reshape((parts,) + block)],
        "mid_back",
        5,
        line,
        Grads([(normed_mid_full, gate_up_back), (activated, cot_full)]),
    )
    gate_up_grad = scatter(gate_up_grad, "fsdp")
    down_grad = scatter(down_grad, "fsdp")
    residual_back = cotangent.astype(jnp.float32) + norm_back(mid_back, normed_mid, root_mid)
    proj_back = residual_back.astype(LOW)

    proj_job = Gather(parts, block, watched=True)
    _, down_terms, back_heads, out_grad = call(
        [proj_job],
        [proj_back],
        "proj_back",
        6,
        line,
        ProjectBack(proj_job, activated, down_rows, out_cols, mix_low),
        micros=45,
    )
    out_grad = out_grad.reshape(heads, run, shard, width).transpose(1, 0, 2, 3)
    down_out, out_grad, in_back_terms, qkv_grad = call(
        [
            Scatter(parts, block),
            Exchange(run, (heads * shard, width)),
        ],
        [
            down_terms.reshape((parts,) + block),
            out_grad.reshape(run, heads * shard, width),
        ],
        "attend_back",
        8,
        line,
        AttendBack(back_heads, qkv_low, normed_in_full, qkv_cols, tables, heads),
        micros=60,
    )
    layer_out = (residual + down_out).astype(LOW)
    out_grad, gate_up_grad = lax.optimization_barrier((out_grad, gate_up_grad))
    out_grad = scatter(out_grad.reshape(groups * shard, width), "fsdp")
    in_back, qkv_grad, gate_up_grad = call(
        [
            Scatter(parts, block),
            Collect(parts, groups, qkv_shape, plan.qkv_starts),
            plan.unit_job(both_shape),
        ],
        [
            in_back_terms.reshape((parts,) + block),
            qkv_grad.reshape((groups, parts) + qkv_shape),
            gate_up_grad.reshape((parts,) + both_shape),
        ],
        "in_back",
        7,
        plane,
        micros=90,
    )
    in_back, down_grad, out_grad = lax.optimization_barrier((in_back, down_grad, out_grad))
    tokens_grad = residual_back + norm_back(in_back, normed_in, root_in)
    return (
        layer_out,
        tokens_grad,
        qkv_grad,
        out_grad.astype(jnp.float32),
        plan.unit_rows(gate_up_grad),
        down_grad.astype(jnp.float32),
    )


def solution(mesh):
    both = P(("fsdp", "ctx"), None)
    one = P("fsdp", None)
    return jax.shard_map(
        per_device,
        mesh=mesh,
        in_specs=(both, both, both, both, both, one, one, both),
        out_specs=(both,) * 6,
        check_vma=False,
    )
```

```python
import jax
import jax.numpy as jnp
from jax import lax
from jax.experimental import pallas as pl
from jax.experimental.pallas import tpu as pltpu
from jax.sharding import PartitionSpec as P

HEADS = 16
HEAD_DIM = 128
BLOCK = 128
LOW = jnp.bfloat16


def normalize(values):
    average = jnp.mean(values, axis=-1, keepdims=True)
    centered = values - average
    variance = jnp.mean(centered * centered, axis=-1, keepdims=True)
    inv_root = lax.rsqrt(variance + 1e-05)
    return (centered * inv_root, inv_root)


def norm_back(upstream, normed, inv_root):
    first_mean = jnp.mean(upstream, axis=-1, keepdims=True)
    second_mean = jnp.mean(upstream * normed, axis=-1, keepdims=True)
    return inv_root * (upstream - first_mean - normed * second_mean)


def places(token_index, lengths):
    seq_ends = jnp.cumsum(lengths)
    sequence = jnp.sum((token_index[:, None] >= seq_ends[None, :]).astype(jnp.int32), axis=1)
    before = jnp.arange(lengths.shape[0], dtype=jnp.int32)
    seq_start = jnp.sum(jnp.where(before[None, :] < sequence[:, None], lengths[None, :], 0), axis=1)
    return (sequence, token_index - seq_start)


def initial_index(row_index, order_row):
    slot_index = row_index // BLOCK
    slot_table = jnp.arange(order_row.shape[0], dtype=jnp.int32)
    picked = jnp.sum(
        jnp.where(slot_table[None, :] == slot_index[:, None], order_row[None, :], 0), axis=1
    )
    return picked * BLOCK + row_index % BLOCK


def angle_tables(position):
    half_dim = HEAD_DIM // 2
    frequency = 10000.0 ** (-jnp.arange(half_dim, dtype=jnp.float32) * 2.0 / HEAD_DIM)
    angle_table = position.astype(jnp.float32)[:, None] * frequency[None, :]
    angle_table = jnp.concatenate([angle_table, angle_table], axis=-1)
    return (jnp.cos(angle_table)[:, None, :], jnp.sin(angle_table)[:, None, :])


def rotate(values, cosine_table, sine_table):
    half_dim = values.shape[-1] // 2
    turned = jnp.concatenate([-values[..., half_dim:], values[..., :half_dim]], axis=-1)
    return values * cosine_table + turned * sine_table


def unrotate(values, cosine_table, sine_table):
    half_dim = values.shape[-1] // 2
    scaled = values * sine_table
    turned = jnp.concatenate([scaled[..., half_dim:], -scaled[..., :half_dim]], axis=-1)
    return values * cosine_table + turned


def dot(left, right):
    return jnp.dot(left, right, preferred_element_type=jnp.float32)


def times_transposed(left, right):
    return lax.dot_general(
        left, right, (((1,), (1,)), ((), ())), preferred_element_type=jnp.float32
    )


def column_product(left, right):
    return lax.dot_general(
        left, right, (((0,), (0,)), ((), ())), preferred_element_type=jnp.float32
    )


def gather(values, axes):
    return lax.all_gather(values, axes, axis=0, tiled=True)


def scatter(values, axes):
    return lax.psum_scatter(values, axes, scatter_dimension=0, tiled=True)


def enter(axes):
    barrier = pltpu.get_barrier_semaphore()
    count = 0
    for axis, size in axes:
        me = lax.axis_index(axis)
        for step in range(1, size):
            pl.semaphore_signal(barrier, inc=1, device_id={axis: lax.rem(me + step, size)})
        count += size - 1
    pl.semaphore_wait(barrier, count)


def remote(src, dst, send, recv, axis, peer):
    return pltpu.make_async_remote_copy(
        src_ref=src, dst_ref=dst, send_sem=send, recv_sem=recv, device_id={axis: peer}
    )


class Exchange:
    outside = ("in", "out")

    def __init__(self, parts, shape, delay=0, columns=None, second=""):
        self.parts, self.delay, self.columns, self.second = parts, delay, columns, second
        placed = shape[:1] + (parts,) + shape[1:] if second == "out" else (parts,) + shape
        self.out = jax.ShapeDtypeStruct(placed, LOW)
        self.scratch = [
            pltpu.SemaphoreType.DMA((parts - 1,)),
            pltpu.SemaphoreType.DMA((parts - 1,)),
            pltpu.SemaphoreType.DMA,
        ]

    def run(self, src, dst, send, recv, local):
        for _ in range(self.delay):
            yield
        place = lax.axis_index("ctx")
        me = lax.rem(place, self.parts)
        slot = dst.at[:, me] if self.second == "out" else dst.at[me]

        def blocks(part):
            if self.second == "in":
                return [(src.at[:, part], slot)]
            return blocks_of(src, part, slot, self.columns)

        copies = []
        for step in range(1, self.parts):
            peer = lax.rem(me + step, self.parts)
            whole = (send.at[step - 1], recv.at[step - 1], "ctx", place - me + peer)
            for block, target in blocks(peer):
                copies.append(remote(block, target, *whole))
                copies[-1].start()
            if self.columns:
                del copies[step - 1 :]
                copies.append(remote(slot, slot, *whole))
        for block, target in blocks(me):
            pltpu.make_async_copy(block, target, local).start()
        yield
        for copy in copies:
            copy.wait()
            yield
        pltpu.make_async_copy(slot, slot, local).wait()


def blocks_of(src, part, slot, columns):
    if columns is None:
        return [(src.at[part], slot)]
    starts = columns(part)
    wide = slot.shape[1] // len(starts)
    return [
        (
            src.at[:, pl.ds(pl.multiple_of(start, HEAD_DIM), wide)],
            slot.at[:, pl.ds(index * wide, wide)],
        )
        for index, start in enumerate(starts)
    ]


class Gather:
    def __init__(self, parts, shape, watched=False, cuts=2):
        self.outside = ("in", "out")
        self.parts, self.watched, self.shape, self.cuts = parts, watched, shape, cuts
        self.out = jax.ShapeDtypeStruct((parts,) + shape, LOW)
        chips = parts // 2
        self.scratch = [
            pltpu.SemaphoreType.DMA((2, chips, self.cuts)),
            pltpu.SemaphoreType.DMA((chips, self.cuts)),
            pltpu.SemaphoreType.DMA((chips, self.cuts)),
            pltpu.SemaphoreType.DMA((chips, self.cuts)),
            pltpu.SemaphoreType.DMA,
        ]
        if watched:
            self.scratch += [pltpu.VMEM(self.out.shape, LOW), pltpu.SemaphoreType.DMA((chips,))]

    def run(self, src, out, send, recv, pair_send, pair_recv, local, *watch):
        dst = watch[0] if self.watched else out
        chips, cuts = self.parts // 2, self.cuts
        rows = self.shape[0] // cuts
        me = lax.axis_index("ctx")
        chip, core = me // 2, lax.rem(me, 2)
        partner = me + 1 - 2 * core

        def piece(block, cut):
            return block.at[pl.ds(cut * rows, rows)]

        def line(block, slot, origin, way, cut):
            return remote(
                piece(block, cut),
                piece(slot, cut),
                send.at[way, origin, cut],
                recv.at[origin, cut],
                "ctx",
                me + 2 - 4 * way,
            )

        def across(block, slot, origin, cut):
            return remote(
                piece(block, cut),
                piece(slot, cut),
                pair_send.at[origin, cut],
                pair_recv.at[origin, cut],
                "ctx",
                partner,
            )

        mine = dst.at[me]
        own = pltpu.make_async_copy(src, mine, local)

        def arrived(origin):
            other = dst.at[2 * origin + 1 - core]
            for cut in range(cuts):
                across(other, other, origin, cut).wait_recv()

            @pl.when(origin == chip)
            def _():
                own.wait()

            if self.watched:
                kept(origin).start()

        def kept(origin):
            rows = pl.ds(2 * origin, 2)
            return pltpu.make_async_copy(dst.at[rows], out.at[rows], watch[1].at[origin])

        def relay(step):
            for cut in range(cuts):
                for way in range(2):
                    origin = chip - step if way == 0 else chip + step

                    @pl.when((origin >= 0) & (origin < chips))
                    def _():
                        slot = dst.at[2 * origin + core]
                        line(slot, slot, origin, way, cut).wait_recv()

                        @pl.when((chip < chips - 1) if way == 0 else (chip > 0))
                        def _():
                            line(slot, slot, origin, way, cut).start()

                        across(slot, slot, origin, cut).start()

        self.dst, self.arrived, self.relay = dst, arrived, relay
        for cut in range(cuts):

            @pl.when(chip < chips - 1)
            def _():
                line(src, mine, chip, 0, cut).start()

            @pl.when(chip > 0)
            def _():
                line(src, mine, chip, 1, cut).start()

        for cut in range(cuts):
            across(src, mine, chip, cut).start()
        own.start()
        yield
        if self.watched:
            yield
        for step in range(1, chips):
            if not self.watched:
                relay(step)
                yield
        for step in range(chips):
            for way in range(2):
                origin = chip - step if way == 0 else chip + step
                ahead = (chip < chips - 1) if way == 0 else (chip > 0)

                @pl.when((origin >= 0) & (origin < chips) & ahead)
                def _():
                    slot = dst.at[2 * origin + core]
                    for cut in range(cuts):
                        line(slot, slot, origin, way, cut).wait_send()

        for origin in range(chips):
            slot = dst.at[2 * origin + core]
            for cut in range(cuts):
                across(slot, slot, origin, cut).wait_send()
            if self.watched:
                kept(origin).wait()
            else:
                arrived(origin)


class Scatter:
    outside = ()

    def __init__(self, parts, shape, cuts=2):
        self.parts, self.shape, self.cuts = parts, shape, cuts
        self.out = jax.ShapeDtypeStruct(shape, jnp.float32)
        chips = parts // 2
        piece = (self.cuts, shape[0] // self.cuts, shape[1])
        self.scratch = [
            pltpu.VMEM((chips,) + shape, LOW),
            pltpu.VMEM((2, chips) + piece, LOW),
            pltpu.VMEM((chips,) + piece, LOW),
            pltpu.SemaphoreType.DMA((chips,)),
            pltpu.SemaphoreType.DMA((chips,)),
            pltpu.SemaphoreType.DMA((chips, self.cuts)),
            pltpu.SemaphoreType.DMA((2, chips, self.cuts)),
        ]

    def run(self, src, out, pair, come, stage, pair_send, pair_recv, send, recv):
        chips, cuts = self.parts // 2, self.cuts
        me = lax.axis_index("ctx")
        chip, core = me // 2, lax.rem(me, 2)
        partner = me + 1 - 2 * core
        rows = self.shape[0] // cuts
        slab = min(rows, 16)
        last = chips - 1

        def across(goal):
            return remote(
                src.at[2 * goal + 1 - core],
                pair.at[goal],
                pair_send.at[goal],
                pair_recv.at[goal],
                "ctx",
                partner,
            )

        def line(goal, cut, way):
            return remote(
                stage.at[goal, cut],
                come.at[way, goal, cut],
                send.at[goal, cut],
                recv.at[way, goal, cut],
                "ctx",
                me + 2 - 4 * way,
            )

        def wide(ref, *index):
            return ref[index].astype(jnp.float32)

        def slabs(part):
            def one(index, carry):
                part(pl.multiple_of(index * slab, slab))
                return carry

            lax.fori_loop(0, rows // slab, one, 0)

        def both(goal, cut, at):
            at = pl.ds(cut * rows + at, slab)
            return wide(src, 2 * goal + core, at) + wide(pair, goal, at)

        order = []
        for step in range((chips + 1) // 2):
            order += sorted({step, last - step})
        for goal in order:
            across(goal).start()
        yield
        for step in range(last * cuts):
            for way in range(2):
                turn = step - (chip if way == 0 else last - chip)
                goal = (last - turn // cuts) if way == 0 else turn // cuts
                cut = step - (chip if way == 0 else last - chip) - (turn // cuts) * cuts
                first = (chip == 0) if way == 0 else (chip == last)
                ahead = last - chip if way == 0 else chip

                def begin(at):
                    value = both(goal, cut, at)
                    stage[goal, cut, pl.ds(at, slab), :] = value.astype(LOW)

                def middle(at):
                    value = both(goal, cut, at) + wide(come, way, goal, cut, pl.ds(at, slab))
                    stage[goal, cut, pl.ds(at, slab), :] = value.astype(LOW)

                @pl.when((turn >= 0) & (turn < ahead * cuts))
                def _():
                    @pl.when(cut == 0)
                    def _():
                        across(goal).wait_recv()

                    @pl.when(first)
                    def _():
                        slabs(begin)

                    @pl.when(jnp.logical_not(first))
                    def _():
                        line(goal, cut, way).wait_recv()
                        slabs(middle)

                    line(goal, cut, way).start()

            yield
        across(chip).wait_recv()
        for cut in range(cuts):

            def own(at):
                out[pl.ds(cut * rows + at, slab), :] = both(chip, cut, at)

            slabs(own)
        yield
        for cut in range(cuts):
            for way in range(2):

                def final(at):
                    out[pl.ds(cut * rows + at, slab), :] += wide(
                        come, way, chip, cut, pl.ds(at, slab)
                    )

                @pl.when((chip > 0) if way == 0 else (chip < last))
                def _():
                    line(chip, cut, way).wait_recv()
                    slabs(final)

            yield
        for goal in range(chips):
            across(goal).wait_send()

            @pl.when(chip != goal)
            def _():
                for cut in range(cuts):
                    line(goal, cut, 0).wait_send()


class Fan:
    outside = ("in", "out")

    def __init__(self, groups, shape):
        self.groups = groups
        self.out = jax.ShapeDtypeStruct((groups,) + shape, LOW)
        self.scratch = [
            pltpu.SemaphoreType.DMA((groups - 1,)),
            pltpu.SemaphoreType.DMA((groups - 1,)),
            pltpu.SemaphoreType.DMA,
        ]

    def run(self, src, dst, send, recv, local):
        groups = self.groups
        group = lax.axis_index("fsdp")
        copies = []
        for hop in range(1, groups):
            peer = lax.rem(group + hop, groups)
            copies.append(
                remote(src, dst.at[group], send.at[hop - 1], recv.at[hop - 1], "fsdp", peer)
            )
            copies[-1].start()
        own = pltpu.make_async_copy(src, dst.at[group], local)
        own.start()
        yield
        yield
        yield
        for copy in copies:
            copy.wait()
        own.wait()


class Spread:
    outside = ("in", "out")

    def __init__(self, parts, groups, shape, columns=None):
        self.parts, self.groups, self.columns = parts, groups, columns
        self.out = jax.ShapeDtypeStruct((groups, parts) + shape, LOW)
        self.scratch = [
            pltpu.SemaphoreType.DMA((parts - 1,)),
            pltpu.SemaphoreType.DMA((parts - 1,)),
            pltpu.SemaphoreType.DMA((groups - 1, parts)),
            pltpu.SemaphoreType.DMA((groups - 1, parts)),
            pltpu.SemaphoreType.DMA,
        ]

    def run(self, src, dst, send, recv, far_send, far_recv, local):
        parts, groups = self.parts, self.groups
        me, group = lax.axis_index("ctx"), lax.axis_index("fsdp")
        slot = dst.at[group, me]
        for block, target in blocks_of(src, me, slot, self.columns):
            pltpu.make_async_copy(block, target, local).start()
        copies = []
        for step in range(1, parts):
            peer = lax.rem(me + step, parts)
            whole = (send.at[step - 1], recv.at[step - 1], "ctx", peer)
            for block, target in blocks_of(src, peer, slot, self.columns):
                remote(block, target, *whole).start()
            copies.append(remote(slot, slot, *whole))
        pltpu.make_async_copy(slot, slot, local).wait()

        def pass_on(block, origin, step):
            out = []
            for hop in range(1, groups):
                copy = remote(
                    block,
                    dst.at[group, origin],
                    far_send.at[hop - 1, step],
                    far_recv.at[hop - 1, step],
                    "fsdp",
                    lax.rem(group + hop, groups),
                )
                copy.start()
                out.append(copy)
            return out

        far = pass_on(slot, me, 0)
        eager = -(-parts // 2)
        yield
        for step in range(1, parts):
            copies[step - 1].wait_recv()
            origin = lax.rem(me - step + parts, parts)
            far += pass_on(dst.at[group, origin], origin, step)
            if step % eager == 0:
                yield
        for at, copy in enumerate(far):
            copy.wait()
            if at % 6 == 5:
                yield
        for copy in copies:
            copy.wait_send()


class Deliver:
    outside = ("in",)

    def __init__(self, parts, shape, offsets, delay=0, eager=1):
        self.parts, self.shape, self.offsets = parts, shape, offsets
        self.delay, self.eager = delay, eager
        self.out = jax.ShapeDtypeStruct((shape[0], parts * shape[1]), jnp.float32)
        self.scratch = [
            pltpu.VMEM((parts,) + shape, LOW),
            pltpu.SemaphoreType.DMA((parts - 1,)),
            pltpu.SemaphoreType.DMA((parts,)),
        ]

    def place(self, out, origin, read):
        starts = self.offsets(origin)
        step = self.shape[1] // len(starts)
        for index, start in enumerate(starts):
            out[:, pl.ds(pl.multiple_of(start, HEAD_DIM), step)] = read(
                index * step, (index + 1) * step
            )

    def send(self, me, step, block, came, send, recv):
        return remote(
            block,
            came.at[step - 1],
            send.at[step - 1],
            recv.at[step - 1],
            "ctx",
            lax.rem(me + step, self.parts),
        )

    def run(self, src, out, came, send, recv):
        for _ in range(self.delay):
            yield
        me = lax.axis_index("ctx")
        copies = []
        for step in range(1, self.parts):
            block = src.at[lax.rem(me + step, self.parts)]
            copies.append(self.send(me, step, block, came, send, recv))
            copies[-1].start()
        last = self.parts - 1
        own = pltpu.make_async_copy(src.at[me], came.at[last], recv.at[last])
        own.start()
        yield
        own.wait()
        self.place(out, me, lambda lo, hi: came[last, :, lo:hi].astype(jnp.float32))
        yield from self.finish(me, out, copies, came)

    def finish(self, me, out, copies, came):
        for step in range(1, self.parts):
            copies[step - 1].wait_recv()
            origin = lax.rem(me - step + self.parts, self.parts)
            self.place(out, origin, lambda lo, hi: came[step - 1, :, lo:hi].astype(jnp.float32))
            if step % self.eager == 0:
                yield
        for copy in copies:
            copy.wait_send()


class Collect(Deliver):
    outside = ()

    def __init__(self, parts, groups, shape, offsets, delay=0, eager=1):
        super().__init__(parts, shape, offsets, delay, eager)
        self.groups = groups
        self.scratch = self.scratch + [
            pltpu.VMEM((groups - 1, parts) + shape, LOW),
            pltpu.VMEM((parts,) + shape, LOW),
            pltpu.VMEM(shape, jnp.float32),
            pltpu.SemaphoreType.DMA((groups - 1, parts)),
            pltpu.SemaphoreType.DMA((groups - 1, parts)),
        ]

    def run(self, src, out, came, send, recv, far, stage, mine, far_send, far_recv):
        parts, groups = self.parts, self.groups
        me, group = lax.axis_index("ctx"), lax.axis_index("fsdp")
        goals = [lax.rem(me + step, parts) for step in range(1, parts + 1)]
        hops = []
        for goal in goals:
            for hop in range(1, groups):
                peer = lax.rem(group + hop, groups)
                hops.append(
                    remote(
                        src.at[peer, goal],
                        far.at[hop - 1, goal],
                        far_send.at[hop - 1, goal],
                        far_recv.at[hop - 1, goal],
                        "fsdp",
                        peer,
                    )
                )
                hops[-1].start()
        yield
        copies = []
        for step in range(1, parts + 1):
            goal = goals[step - 1]
            for copy in hops[(step - 1) * (groups - 1) : step * (groups - 1)]:
                copy.wait_recv()
            value = src[group, goal].astype(jnp.float32)
            for hop in range(groups - 1):
                value += far[hop, goal].astype(jnp.float32)
            if step < parts:
                stage[goal] = value.astype(LOW)
                copies.append(self.send(me, step, stage.at[goal], came, send, recv))
                copies[-1].start()
            else:
                mine[...] = value
            if step % self.eager == 0:
                yield
        self.place(out, me, lambda lo, hi: mine[:, lo:hi])
        yield from self.finish(me, out, copies, came)
        for copy in hops:
            copy.wait_send()


def product(left, right):
    return jnp.dot(left, right, preferred_element_type=jnp.float32)


class Puts:
    def __init__(self, made, put):
        self.made, self.put, self.copies = made, put, []

    def pair(self, fill, columns, out, at, tile):
        for copy in self.copies:
            copy.wait()
        lax.fori_loop(0, 2, fill, 0)
        self.copies = []
        for half in range(2):
            begin = at + half * tile
            copy = pltpu.make_async_copy(
                self.made.at[half, :, pl.ds(0, columns)],
                out.at[begin : begin + tile, :],
                self.put.at[half],
            )
            copy.start()
            self.copies.append(copy)

    def finish(self):
        for copy in self.copies:
            copy.wait()


def call(jobs, operands, name, identity, axes, work=None, micros=50):
    counts = [len(job.scratch) for job in jobs]
    jobs_n = len(jobs)
    extra = work.operands if work else []
    extra_out = work.outs if work else []
    extra_scratch = work.scratch if work else []

    def kernel(*refs):
        refs = list(refs)

        def take(count):
            taken = refs[:count]
            del refs[:count]
            return taken

        ins, more = take(jobs_n), take(len(extra))
        outs, more_outs = take(jobs_n), take(len(extra_out))
        runs = []
        for job, src, dst, count in zip(jobs, ins, outs, counts):
            runs.append(job.run(src, dst, *take(count)))
        if work:
            runs.append(work.run(*more, *more_outs, *refs))
        enter(axes)
        while runs:
            going = []
            for run in runs:
                try:
                    next(run)
                    going.append(run)
                except StopIteration:
                    pass
            runs = going

    vmem = pl.BlockSpec(memory_space=pltpu.VMEM)
    anywhere = pl.BlockSpec(memory_space=pl.ANY)
    in_specs = [anywhere if "in" in job.outside else vmem for job in jobs]
    out_specs = [anywhere if "out" in job.outside else vmem for job in jobs]
    return pl.pallas_call(
        kernel,
        out_shape=tuple(job.out for job in jobs) + tuple(extra_out),
        in_specs=in_specs + [anywhere] * len(extra),
        out_specs=tuple(out_specs) + (anywhere,) * len(extra_out),
        scratch_shapes=[shape for job in jobs for shape in job.scratch] + list(extra_scratch),
        compiler_params=pltpu.CompilerParams(
            collective_id=identity, has_side_effects=True, vmem_limit_bytes=62 << 20
        ),
        cost_estimate=pl.CostEstimate(
            flops=0, bytes_accessed=micros * 3_000_000, transcendentals=0
        ),
        name=name,
    )(*operands, *extra)


class Grads:
    tile = 256

    def __init__(self, pairs):
        self.pairs = pairs
        length, wide = pairs[0][0].shape[0], max(right.shape[1] for _, right in pairs)
        self.operands = [array for pair in pairs for array in pair]
        self.outs = [jax.ShapeDtypeStruct((l.shape[1], r.shape[1]), LOW) for l, r in pairs]
        self.slots = [[id(array) for array in self.operands].index(id(a)) for a in self.operands]
        self.operands = [a for i, a in enumerate(self.operands) if self.slots[i] == i]
        self.slots = [sorted(set(self.slots)).index(slot) for slot in self.slots]
        self.scratch = [pltpu.VMEM(array.shape, LOW) for array in self.operands]
        self.scratch += [
            pltpu.VMEM((self.tile, length), LOW),
            pltpu.VMEM((2, self.tile, wide), LOW),
            pltpu.SemaphoreType.DMA((len(self.operands),)),
            pltpu.SemaphoreType.DMA((2,)),
        ]

    def run(self, *refs):
        n, tile, count = len(self.pairs), self.tile, len(self.operands)
        sources, outs = refs[:count], refs[count : count + n]
        held = refs[count + n : 2 * count + n]
        turned, made, get, put = refs[2 * count + n :]
        gets = [pltpu.make_async_copy(s, h, get.at[i]) for i, (s, h) in enumerate(zip(sources, held))]
        for copy in gets:
            copy.start()
        yield
        puts = []
        for which in range(n):
            first, second = self.slots[2 * which : 2 * which + 2]
            left, right, out = held[first], held[second], outs[which]
            for slot in (first, second):
                if slot not in self.slots[: 2 * which]:
                    gets[slot].wait()
            columns = right.shape[1]
            step = min(columns, 512)
            for at in range(0, left.shape[1], tile):
                slot = len(puts) % 2
                if len(puts) >= 2:
                    puts[-2].wait()
                turned[...] = left[:, at : at + tile].T

                def one(index, carry):
                    where = pl.ds(pl.multiple_of(index * step, step), step)
                    made[slot, :, where] = jnp.dot(
                        turned[...], right[:, where], preferred_element_type=jnp.float32
                    ).astype(LOW)
                    return carry

                lax.fori_loop(0, columns // step, one, 0)
                part = made.at[slot] if columns == made.shape[2] else made.at[slot, :, :columns]
                puts.append(pltpu.make_async_copy(part, out.at[at : at + tile, :], put.at[slot]))
                puts[-1].start()
                yield
        for copy in puts[-2:]:
            copy.wait()


def softmax_block(query, keys, ok):
    scores = times_transposed(query, keys) * HEAD_DIM ** (-0.5)
    scores = jnp.where(ok, scores, -1e30)
    weights = jnp.exp(scores - jnp.max(scores, axis=-1, keepdims=True))
    weights = jnp.where(ok, weights, 0.0)
    return weights, jnp.sum(weights, axis=-1, keepdims=True)


class Attend:
    tile = 256

    def __init__(self, rows, weight, tables, heads):
        self.heads = heads
        self.operands = [rows, weight] + list(tables)
        length, wide = rows.shape[0], weight.shape[1]
        self.outs = [
            jax.ShapeDtypeStruct((length, wide), LOW),
            jax.ShapeDtypeStruct((length, wide // 3), LOW),
        ]
        self.scratch = [pltpu.VMEM(array.shape, array.dtype) for array in self.operands]
        self.scratch += [pltpu.VMEM(out.shape, out.dtype) for out in self.outs]
        self.scratch += [
            pltpu.SemaphoreType.DMA((len(self.operands),)),
            pltpu.SemaphoreType.DMA((2,)),
        ]

    def run(self, *refs):
        n, tile, heads = len(self.operands), self.tile, self.heads
        sources, results, held = refs[:n], refs[n : n + 2], refs[n + 2 : 2 * n + 2]
        qkv, mix, get, put = refs[2 * n + 2 :]
        rows, weight, cosine, sine, first, last, keys = held
        gets = [pltpu.make_async_copy(s, h, get.at[i]) for i, (s, h) in enumerate(zip(sources, held))]
        for copy in gets:
            copy.start()
        yield
        for copy in gets:
            copy.wait()
        width = heads * HEAD_DIM

        def project(index, carry):
            at = pl.ds(pl.multiple_of(index * tile, tile), tile)
            value = product(rows[at, :], weight[...])
            for head in range(3 * heads):
                block = value[:, head * HEAD_DIM : (head + 1) * HEAD_DIM]
                if head < 2 * heads:
                    turned = pltpu.roll(block, HEAD_DIM // 2, 1)
                    block = block * cosine[at, :] + turned * sine[at, :]
                qkv[at, head * HEAD_DIM : (head + 1) * HEAD_DIM] = block.astype(LOW)
            return carry

        lax.fori_loop(0, rows.shape[0] // tile, project, 0)
        send = pltpu.make_async_copy(qkv, results[0], put.at[0])
        send.start()
        yield

        def attend(index, carry):
            at = pl.ds(pl.multiple_of(index * tile, tile), tile)
            ok = (keys[:1, :] >= first[at, :1]) & (keys[:1, :] <= last[at, :1])
            for head in range(heads):
                lo = head * HEAD_DIM
                weights, total = softmax_block(
                    qkv[at, lo : lo + HEAD_DIM], qkv[:, width + lo : width + lo + HEAD_DIM], ok
                )
                value = qkv[:, 2 * width + lo : 2 * width + lo + HEAD_DIM]
                mixed = product(weights.astype(LOW), value) / total
                mix[at, lo : lo + HEAD_DIM] = mixed.astype(LOW)
            return carry

        lax.fori_loop(0, rows.shape[0] // tile, attend, 0)
        send_mix = pltpu.make_async_copy(mix, results[1], put.at[1])
        send_mix.start()
        yield
        send.wait()
        send_mix.wait()


class AttendBack:
    tile = 256

    def __init__(self, back, qkv, rows, weight, tables, heads):
        self.heads = heads
        self.operands = [back, qkv] + list(tables) + [weight, rows]
        length, wide, width = rows.shape[0], weight.shape[1], rows.shape[1]
        self.outs = [
            jax.ShapeDtypeStruct((length, width), LOW),
            jax.ShapeDtypeStruct((width, wide), LOW),
        ]
        self.scratch = [pltpu.VMEM(array.shape, array.dtype) for array in self.operands]
        self.scratch += [
            pltpu.VMEM((length, wide), LOW),
            pltpu.VMEM((2, length, HEAD_DIM), jnp.float32),
            pltpu.VMEM((self.tile, length), LOW),
            pltpu.VMEM((2, self.tile, width), LOW),
            pltpu.SemaphoreType.DMA((len(self.operands),)),
            pltpu.SemaphoreType.DMA((2,)),
        ]

    def run(self, *refs):
        n, tile, heads = len(self.operands), self.tile, self.heads
        sources, results, held = refs[:n], refs[n : n + 2], refs[n + 2 : 2 * n + 2]
        grads, sums, turned, made, get, put = refs[2 * n + 2 :]
        back, qkv, cosine, sine, first, last, keys, weight, rows = held
        length, width = back.shape
        gets = [pltpu.make_async_copy(s, h, get.at[i]) for i, (s, h) in enumerate(zip(sources, held))]
        for copy in gets:
            copy.start()
        yield
        for copy in gets[:-2]:
            copy.wait()

        def unrotated(value, at):
            return value * cosine[at, :] - pltpu.roll(value, HEAD_DIM // 2, 1) * sine[at, :]

        for head in range(heads):
            lo = head * HEAD_DIM
            mine = slice(lo, lo + HEAD_DIM)
            key = slice(width + lo, width + lo + HEAD_DIM)
            val = slice(2 * width + lo, 2 * width + lo + HEAD_DIM)
            sums[...] = jnp.zeros_like(sums)

            def attend(index, carry):
                at = pl.ds(pl.multiple_of(index * tile, tile), tile)
                ok = (keys[:1, :] >= first[at, :1]) & (keys[:1, :] <= last[at, :1])
                weights, total = softmax_block(qkv[at, mine], qkv[:, key], ok)
                probs = weights / total
                upper = back[at, mine]
                prob_back = times_transposed(upper, qkv[:, val])
                delta = jnp.sum(probs * prob_back, axis=-1, keepdims=True)
                score_back = HEAD_DIM ** (-0.5) * probs * (prob_back - delta)
                score_low = score_back.astype(LOW)
                query_back = product(score_low, qkv[:, key])
                grads[at, mine] = unrotated(query_back, at).astype(LOW)
                sums[0] += product(score_low.T, qkv[at, mine])
                sums[1] += product(probs.astype(LOW).T, upper)
                return carry

            lax.fori_loop(0, length // tile, attend, 0)
            yield

            def settle(index, carry):
                at = pl.ds(pl.multiple_of(index * tile, tile), tile)
                grads[at, key] = unrotated(sums[0, at, :], at).astype(LOW)
                grads[at, val] = sums[1, at, :].astype(LOW)
                return carry

            lax.fori_loop(0, length // tile, settle, 0)
        puts = Puts(made, put)
        wide = grads.shape[1]
        part = tile if wide % tile == 0 else HEAD_DIM
        gets[-2].wait()
        for at in range(0, length, 2 * tile):

            def terms(half, carry):
                where = pl.ds(pl.multiple_of(at + half * tile, tile), tile)

                def one(index, carry):
                    span = pl.ds(pl.multiple_of(index * tile, tile), tile)
                    value = times_transposed(grads[where, :], weight[span, :])
                    made[half, :, span] = value.astype(LOW)
                    return carry

                return lax.fori_loop(0, made.shape[2] // tile, one, carry)

            puts.pair(terms, made.shape[2], results[0], at, tile)
            yield
        gets[-1].wait()
        for at in range(0, rows.shape[1], 2 * tile):

            def weights(half, carry):
                where = pl.ds(pl.multiple_of(at + half * tile, tile), tile)
                turned[...] = rows[:, where].T

                def one(index, carry):
                    span = pl.ds(pl.multiple_of(index * part, part), part)
                    made[half, :, span] = product(turned[...], grads[:, span]).astype(LOW)
                    return carry

                return lax.fori_loop(0, wide // part, one, carry)

            puts.pair(weights, wide, results[1], at, tile)
            yield
        puts.finish()


def near_first(chips):
    table = []
    for chip in range(chips):
        order = [chip]
        for step in range(1, chips):
            order += [at for at in (chip + step, chip - step) if 0 <= at < chips]
        table.append(order)
    return table


def next_chip(chips, turn):
    chip = lax.axis_index("ctx") // 2
    return sum(
        jnp.where((chip == at) & (turn == when), order[when], 0)
        for at, order in enumerate(near_first(chips))
        for when in range(chips)
    )


class ProjectBack:
    tile = 256

    def __init__(self, job, activated, down, out_rows, mix):
        self.job = job
        self.operands = [activated, down, out_rows, mix]
        length, heads_width = mix.shape
        width = down.shape[1]
        self.outs = [
            jax.ShapeDtypeStruct((length, width), LOW),
            jax.ShapeDtypeStruct((length, heads_width), LOW),
            jax.ShapeDtypeStruct((heads_width, width), LOW),
        ]
        self.scratch = [pltpu.VMEM(array.shape, array.dtype) for array in self.operands]
        self.scratch += [
            pltpu.VMEM((2, self.tile, width), LOW),
            pltpu.VMEM((length, heads_width), LOW),
            pltpu.VMEM((heads_width, width), jnp.float32),
            pltpu.VMEM((heads_width, width), LOW),
            pltpu.SemaphoreType.DMA((4,)),
            pltpu.SemaphoreType.DMA((2,)),
            pltpu.SemaphoreType.DMA((2,)),
        ]

    def run(self, *refs):
        job, tile = self.job, self.tile
        sources, results, held = refs[:4], refs[4:7], refs[7:11]
        made, back, total, total_low, get, put, leave = refs[11:]
        activated, down, out_rows, mix = held
        length, width = mix.shape[0], down.shape[1]
        gets = [pltpu.make_async_copy(s, h, get.at[i]) for i, (s, h) in enumerate(zip(sources, held))]
        for copy in gets:
            copy.start()
        yield
        for copy in gets:
            copy.wait()
        total[...] = jnp.zeros_like(total)
        puts = Puts(made, put)
        for at in range(0, length, 2 * tile):

            def terms(half, carry):
                where = pl.ds(pl.multiple_of(at + half * tile, tile), tile)

                def one(index, carry):
                    span = pl.ds(pl.multiple_of(index * tile, tile), tile)
                    value = product(activated[where, :], down[:, span])
                    made[half, :, span] = value.astype(LOW)
                    return carry

                return lax.fori_loop(0, width // tile, one, carry)

            puts.pair(terms, width, results[0], at, tile)
        chips = job.parts // 2
        rows = length // chips

        def one_chip(turn, carry):
            origin = next_chip(chips, turn)

            @pl.when(turn > 0)
            def _():
                job.relay(turn)

            job.arrived(origin)
            at = pl.ds(pl.multiple_of(origin * rows, rows), rows)
            block = job.dst.at[pl.ds(2 * origin, 2)]
            value = block[...].reshape(rows, width)
            back[at, :] = times_transposed(value, out_rows[...]).astype(LOW)
            total[...] += product(mix[at, :].T, value)
            return carry

        lax.fori_loop(0, chips, one_chip, 0)
        total_low[...] = total[...].astype(LOW)
        out = [
            pltpu.make_async_copy(back, results[1], leave.at[0]),
            pltpu.make_async_copy(total_low, results[2], leave.at[1]),
        ]
        for copy in out:
            copy.start()
        puts.finish()
        for copy in out:
            copy.wait()


class FeedForward:
    def __init__(self, job, upstream, gate, up, down):
        self.job = job
        self.operands = [upstream, gate, up, down]
        length, width = upstream.shape
        units = gate.shape[1]
        self.outs = [
            jax.ShapeDtypeStruct((length, units), LOW),
            jax.ShapeDtypeStruct((length, 2 * units), LOW),
            jax.ShapeDtypeStruct((length, width), LOW),
        ]
        self.tile = length // (job.parts // 2)
        self.scratch = [pltpu.VMEM(array.shape, array.dtype) for array in self.operands]
        self.scratch += [pltpu.VMEM((2, self.tile) + out.shape[1:], LOW) for out in self.outs]
        self.scratch += [pltpu.SemaphoreType.DMA((4,)), pltpu.SemaphoreType.DMA((3, 2))]

    def run(self, *refs):
        job, tile = self.job, self.tile
        sources, results, held, made = refs[:4], refs[4:7], refs[7:11], refs[11:14]
        get, put = refs[14:]
        upstream, gate_w, up_w, down = held
        acts, backs, terms = made
        width, units = gate_w.shape
        step = min(units, 256)
        span = min(width, 512)
        gets = [pltpu.make_async_copy(sources[i], held[i], get.at[i]) for i in (1, 2, 3, 0)]
        for copy in gets:
            copy.start()
        yield
        for copy in gets:
            copy.wait()
        chips = job.parts // 2

        def leave(slot, origin):
            at = pl.ds(pl.multiple_of(origin * tile, tile), tile)
            return [
                pltpu.make_async_copy(made[i].at[slot], results[i].at[at, :], put.at[i, slot])
                for i in range(3)
            ]

        def one_chip(turn, carry):
            origin = next_chip(chips, turn)
            slot = lax.rem(turn, 2)

            @pl.when(turn > 0)
            def _():
                job.relay(turn)

            @pl.when(turn >= 2)
            def _():
                for copy in leave(slot, 0):
                    copy.wait()

            job.arrived(origin)
            at = pl.ds(pl.multiple_of(origin * tile, tile), tile)
            normed = job.dst.at[pl.ds(2 * origin, 2)]

            def forward(index, carry):
                left = pl.ds(pl.multiple_of(index * step, step), step)
                right = pl.ds(pl.multiple_of(units + index * step, step), step)
                value = normed[...].reshape(tile, width)
                gate = product(value, gate_w[:, left])
                up = product(value, up_w[:, left])
                act_grad = times_transposed(upstream[at, :], down[left, :])
                sigmoid = jax.nn.sigmoid(gate)
                silu = gate * sigmoid
                acts[slot, :, left] = (silu * up).astype(LOW)
                gate_grad = act_grad * up * sigmoid * (1.0 + gate * (1.0 - sigmoid))
                backs[slot, :, left] = gate_grad.astype(LOW)
                backs[slot, :, right] = (act_grad * silu).astype(LOW)
                return carry

            lax.fori_loop(0, units // step, forward, 0)

            def backward(index, carry):
                where = pl.ds(pl.multiple_of(index * span, span), span)
                value = times_transposed(backs[slot, :, :units], gate_w[where, :])
                value += times_transposed(backs[slot, :, units:], up_w[where, :])
                terms[slot, :, where] = value.astype(LOW)
                return carry

            lax.fori_loop(0, width // span, backward, 0)
            for copy in leave(slot, origin):
                copy.start()
            return carry

        lax.fori_loop(0, chips, one_chip, 0)
        for slot in range(min(2, chips)):
            for copy in leave(slot, 0):
                copy.wait()


class Plan:
    def __init__(self, parts, groups, width):
        self.parts, self.groups = parts, groups
        self.shard = width // (parts * groups)
        self.run = HEAD_DIM // self.shard
        self.heads = HEADS // parts

    def qkv_starts(self, part):
        at, index = part // self.run, lax.rem(part, self.run)
        return [
            (kind * HEADS + (index * self.heads + head) * (self.parts // self.run) + at) * HEAD_DIM
            for kind in range(3)
            for head in range(self.heads)
        ]

    def unit_source(self, weight, kind):
        rows, columns = weight.shape
        half = columns // 2
        step = half // (self.groups * self.parts)
        if step % HEAD_DIM == 0:
            return weight, lambda part: [
                kind * half + (at * self.parts + part) * step for at in range(self.groups)
            ]
        pieces = weight[:, kind * half : (kind + 1) * half]
        pieces = pieces.reshape(rows, self.groups, self.parts, step).transpose(2, 0, 1, 3)
        return pieces.reshape(self.parts, rows, self.groups * step), None

    def unit_job(self, shape):
        step = shape[1] // (2 * self.groups)
        if step % HEAD_DIM:
            return Exchange(self.parts, shape)
        return Deliver(
            self.parts,
            shape,
            lambda part: [(at * self.parts + part) * step for at in range(2 * self.groups)],
        )

    def unit_rows(self, pieces):
        if pieces.ndim == 2:
            return pieces
        parts, rows, columns = pieces.shape
        outer = 2 * self.groups
        pieces = pieces.reshape(parts, rows, outer, columns // outer).transpose(1, 2, 0, 3)
        return pieces.reshape(rows, parts * columns).astype(jnp.float32)


def per_device(tokens, w_qkv, w_out, w_gate_up, w_down, seq_lengths, block_order, cotangent):
    lengths = seq_lengths[0]
    order_row = block_order[0]
    parts = lax.axis_size("ctx")
    groups = lax.axis_size("fsdp")
    rows, width = tokens.shape
    length = rows * parts
    plan = Plan(parts, groups, width)
    heads, shard, run = plan.heads, plan.shard, plan.run
    head_width = heads * HEAD_DIM
    line = (("ctx", parts),)
    plane = (("ctx", parts), ("fsdp", groups))
    block = (rows, width)

    down_rows = gather(w_down, "fsdp")
    unit_columns = w_gate_up.shape[1] // (2 * parts)
    unit_shape = (w_gate_up.shape[0], unit_columns)
    both_shape = (w_gate_up.shape[0], 2 * unit_columns)
    qkv_shape = (w_qkv.shape[0], 3 * head_width)
    gate_source, gate_starts = plan.unit_source(w_gate_up, 0)
    up_source, up_starts = plan.unit_source(w_gate_up, 1)
    inputs = tokens.astype(jnp.float32)
    normed_in, root_in = normalize(inputs)
    qkv_cols, normed_in_full, gate_cols, out_rows = call(
        [
            Spread(parts, groups, qkv_shape, plan.qkv_starts),
            Gather(parts, block, cuts=1),
            Exchange(parts, unit_shape, 2, gate_starts),
            Fan(groups, w_out.shape),
        ],
        [w_qkv, normed_in.astype(LOW), gate_source, w_out],
        "start",
        2,
        plane,
        micros=90,
    )
    gate_cols = gather(gate_cols.reshape(width // groups, -1), "fsdp")
    qkv_cols = qkv_cols.reshape(width, 3 * head_width)
    normed_in_full = normed_in_full.reshape(length, width)

    row_index = jnp.arange(length, dtype=jnp.int32)
    packed = initial_index(row_index, order_row)
    _, pos = places(packed, lengths)
    cosine_table, sine_table = angle_tables(pos)
    half_sign = jnp.where(jnp.arange(HEAD_DIM) < HEAD_DIM // 2, -1.0, 1.0)
    tables = (
        cosine_table[:, 0, :],
        sine_table[:, 0, :] * half_sign,
        jnp.broadcast_to((packed - pos)[:, None], (length, HEAD_DIM)),
        jnp.broadcast_to(packed[:, None], (length, HEAD_DIM)),
        jnp.broadcast_to(packed[None, :], (8, length)),
    )
    up_cols, out_cols, qkv_low, mix_low = call(
        [
            Exchange(parts, unit_shape, 0, up_starts),
            Exchange(run, (heads, shard, width), second="out"),
        ],
        [up_source, out_rows.reshape(run, heads, shard, width)],
        "attend",
        1,
        line,
        Attend(normed_in_full, qkv_cols, tables, heads),
        micros=40,
    )
    up_cols = gather(up_cols.reshape(width // groups, -1), "fsdp")
    out_cols = out_cols.reshape(head_width, width)

    out_terms = dot(mix_low, out_cols).astype(LOW)
    attn_out, cot_full = call(
        [Scatter(parts, block, cuts=1), Gather(parts, block, cuts=1)],
        [out_terms.reshape((parts,) + block), cotangent],
        "out",
        3,
        line,
        micros=64,
    )
    cot_full = cot_full.reshape(length, width)
    residual = inputs + attn_out
    normed_mid, root_mid = normalize(residual)
    mid_job = Gather(parts, block, watched=True)
    normed_mid_full, activated, gate_up_back, mid_back_terms = call(
        [mid_job],
        [normed_mid.astype(LOW)],
        "mid",
        4,
        line,
        FeedForward(mid_job, cot_full, gate_cols, up_cols, down_rows),
        micros=60,
    )
    normed_mid_full = normed_mid_full.reshape(length, width)
    mid_back, gate_up_grad, down_grad = call(
        [Scatter(parts, block)],
        [mid_back_terms.reshape((parts,) + block)],
        "mid_back",
        5,
        line,
        Grads([(normed_mid_full, gate_up_back), (activated, cot_full)]),
    )
    gate_up_grad = scatter(gate_up_grad, "fsdp")
    down_grad = scatter(down_grad, "fsdp")
    residual_back = cotangent.astype(jnp.float32) + norm_back(mid_back, normed_mid, root_mid)
    proj_back = residual_back.astype(LOW)

    proj_job = Gather(parts, block, watched=True)
    _, down_terms, back_heads, out_grad = call(
        [proj_job],
        [proj_back],
        "proj_back",
        6,
        line,
        ProjectBack(proj_job, activated, down_rows, out_cols, mix_low),
        micros=45,
    )
    down_out, out_grad, in_back_terms, qkv_grad = call(
        [
            Scatter(parts, block),
            Exchange(run, (heads, shard, width), second="in"),
        ],
        [
            down_terms.reshape((parts,) + block),
            out_grad.reshape(heads, run, shard, width),
        ],
        "attend_back",
        8,
        line,
        AttendBack(back_heads, qkv_low, normed_in_full, qkv_cols, tables, heads),
        micros=60,
    )
    layer_out = (residual + down_out).astype(LOW)
    out_grad, gate_up_grad = lax.optimization_barrier((out_grad, gate_up_grad))
    out_grad = scatter(out_grad.reshape(groups * shard, width), "fsdp")
    in_back, qkv_grad, gate_up_grad = call(
        [
            Scatter(parts, block),
            Collect(parts, groups, qkv_shape, plan.qkv_starts),
            plan.unit_job(both_shape),
        ],
        [
            in_back_terms.reshape((parts,) + block),
            qkv_grad.reshape((groups, parts) + qkv_shape),
            gate_up_grad.reshape((parts,) + both_shape),
        ],
        "in_back",
        7,
        plane,
        micros=90,
    )
    in_back, down_grad, out_grad = lax.optimization_barrier((in_back, down_grad, out_grad))
    tokens_grad = residual_back + norm_back(in_back, normed_in, root_in)
    return (
        layer_out,
        tokens_grad,
        qkv_grad,
        out_grad.astype(jnp.float32),
        plan.unit_rows(gate_up_grad),
        down_grad.astype(jnp.float32),
    )


def solution(mesh):
    both = P(("fsdp", "ctx"), None)
    one = P("fsdp", None)
    return jax.shard_map(
        per_device,
        mesh=mesh,
        in_specs=(both, both, both, both, both, one, one, both),
        out_specs=(both,) * 6,
        check_vma=False,
    )
```

```python
import jax
import jax.numpy as jnp
from jax import lax
from jax.experimental import pallas as pl
from jax.experimental.pallas import tpu as pltpu
from jax.sharding import PartitionSpec as P

HEADS = 16
HEAD_DIM = 128
BLOCK = 128
LOW = jnp.bfloat16


def normalize(values):
    average = jnp.mean(values, axis=-1, keepdims=True)
    centered = values - average
    variance = jnp.mean(centered * centered, axis=-1, keepdims=True)
    inv_root = lax.rsqrt(variance + 1e-05)
    return (centered * inv_root, inv_root)


def norm_back(upstream, normed, inv_root):
    first_mean = jnp.mean(upstream, axis=-1, keepdims=True)
    second_mean = jnp.mean(upstream * normed, axis=-1, keepdims=True)
    return inv_root * (upstream - first_mean - normed * second_mean)


def places(token_index, lengths):
    seq_ends = jnp.cumsum(lengths)
    sequence = jnp.sum((token_index[:, None] >= seq_ends[None, :]).astype(jnp.int32), axis=1)
    before = jnp.arange(lengths.shape[0], dtype=jnp.int32)
    seq_start = jnp.sum(jnp.where(before[None, :] < sequence[:, None], lengths[None, :], 0), axis=1)
    return (sequence, token_index - seq_start)


def initial_index(row_index, order_row):
    slot_index = row_index // BLOCK
    slot_table = jnp.arange(order_row.shape[0], dtype=jnp.int32)
    picked = jnp.sum(
        jnp.where(slot_table[None, :] == slot_index[:, None], order_row[None, :], 0), axis=1
    )
    return picked * BLOCK + row_index % BLOCK


def angle_tables(position):
    half_dim = HEAD_DIM // 2
    frequency = 10000.0 ** (-jnp.arange(half_dim, dtype=jnp.float32) * 2.0 / HEAD_DIM)
    angle_table = position.astype(jnp.float32)[:, None] * frequency[None, :]
    angle_table = jnp.concatenate([angle_table, angle_table], axis=-1)
    return (jnp.cos(angle_table)[:, None, :], jnp.sin(angle_table)[:, None, :])


def rotate(values, cosine_table, sine_table):
    half_dim = values.shape[-1] // 2
    turned = jnp.concatenate([-values[..., half_dim:], values[..., :half_dim]], axis=-1)
    return values * cosine_table + turned * sine_table


def unrotate(values, cosine_table, sine_table):
    half_dim = values.shape[-1] // 2
    scaled = values * sine_table
    turned = jnp.concatenate([scaled[..., half_dim:], -scaled[..., :half_dim]], axis=-1)
    return values * cosine_table + turned


def dot(left, right):
    return jnp.dot(left, right, preferred_element_type=jnp.float32)


def times_transposed(left, right):
    return lax.dot_general(
        left, right, (((1,), (1,)), ((), ())), preferred_element_type=jnp.float32
    )


def column_product(left, right):
    return lax.dot_general(
        left, right, (((0,), (0,)), ((), ())), preferred_element_type=jnp.float32
    )


def gather(values, axes):
    return lax.all_gather(values, axes, axis=0, tiled=True)


def scatter(values, axes):
    return lax.psum_scatter(values, axes, scatter_dimension=0, tiled=True)


def enter(axes):
    barrier = pltpu.get_barrier_semaphore()
    count = 0
    for axis, size in axes:
        me = lax.axis_index(axis)
        for step in range(1, size):
            pl.semaphore_signal(barrier, inc=1, device_id={axis: lax.rem(me + step, size)})
        count += size - 1
    pl.semaphore_wait(barrier, count)


def remote(src, dst, send, recv, axis, peer):
    return pltpu.make_async_remote_copy(
        src_ref=src, dst_ref=dst, send_sem=send, recv_sem=recv, device_id={axis: peer}
    )


class Exchange:
    def __init__(self, parts, shape, delay=0, columns=None, second=""):
        self.parts, self.delay, self.columns, self.second = parts, delay, columns, second
        self.outside = () if second else ("in", "out")
        placed = shape[:1] + (parts,) + shape[1:] if second == "out" else (parts,) + shape
        self.out = jax.ShapeDtypeStruct(placed, LOW)
        self.scratch = [
            pltpu.SemaphoreType.DMA((parts - 1,)),
            pltpu.SemaphoreType.DMA((parts - 1,)),
            pltpu.SemaphoreType.DMA,
        ]

    def run(self, src, dst, send, recv, local):
        for _ in range(self.delay):
            yield
        place = lax.axis_index("ctx")
        me = lax.rem(place, self.parts)
        slot = dst.at[:, me] if self.second == "out" else dst.at[me]

        def blocks(part):
            if self.second == "in":
                return [(src.at[:, part], slot)]
            return blocks_of(src, part, slot, self.columns)

        copies = []
        for step in range(1, self.parts):
            peer = lax.rem(me + step, self.parts)
            whole = (send.at[step - 1], recv.at[step - 1], "ctx", place - me + peer)
            for block, target in blocks(peer):
                copies.append(remote(block, target, *whole))
                copies[-1].start()
            if self.columns:
                del copies[step - 1 :]
                copies.append(remote(slot, slot, *whole))
        for block, target in blocks(me):
            pltpu.make_async_copy(block, target, local).start()
        yield
        for copy in copies:
            copy.wait()
            yield
        pltpu.make_async_copy(slot, slot, local).wait()


def blocks_of(src, part, slot, columns):
    if columns is None:
        return [(src.at[part], slot)]
    starts = columns(part)
    wide = slot.shape[1] // len(starts)
    return [
        (
            src.at[:, pl.ds(pl.multiple_of(start, HEAD_DIM), wide)],
            slot.at[:, pl.ds(index * wide, wide)],
        )
        for index, start in enumerate(starts)
    ]


class Gather:
    def __init__(self, parts, shape, watched=False, cuts=2):
        self.outside = ("in", "out")
        self.parts, self.watched, self.shape, self.cuts = parts, watched, shape, cuts
        self.out = jax.ShapeDtypeStruct((parts,) + shape, LOW)
        chips = parts // 2
        self.scratch = [
            pltpu.SemaphoreType.DMA((2, chips, self.cuts)),
            pltpu.SemaphoreType.DMA((chips, self.cuts)),
            pltpu.SemaphoreType.DMA((chips, self.cuts)),
            pltpu.SemaphoreType.DMA((chips, self.cuts)),
            pltpu.SemaphoreType.DMA,
        ]
        if watched:
            self.scratch += [pltpu.VMEM(self.out.shape, LOW), pltpu.SemaphoreType.DMA((chips,))]

    def run(self, src, out, send, recv, pair_send, pair_recv, local, *watch):
        dst = watch[0] if self.watched else out
        chips, cuts = self.parts // 2, self.cuts
        rows = self.shape[0] // cuts
        me = lax.axis_index("ctx")
        chip, core = me // 2, lax.rem(me, 2)
        partner = me + 1 - 2 * core

        def piece(block, cut):
            return block.at[pl.ds(cut * rows, rows)]

        def line(block, slot, origin, way, cut):
            return remote(
                piece(block, cut),
                piece(slot, cut),
                send.at[way, origin, cut],
                recv.at[origin, cut],
                "ctx",
                me + 2 - 4 * way,
            )

        def across(block, slot, origin, cut):
            return remote(
                piece(block, cut),
                piece(slot, cut),
                pair_send.at[origin, cut],
                pair_recv.at[origin, cut],
                "ctx",
                partner,
            )

        mine = dst.at[me]
        own = pltpu.make_async_copy(src, mine, local)

        def arrived(origin):
            other = dst.at[2 * origin + 1 - core]
            for cut in range(cuts):
                across(other, other, origin, cut).wait_recv()

            @pl.when(origin == chip)
            def _():
                own.wait()

            if self.watched:
                kept(origin).start()

        def kept(origin):
            rows = pl.ds(2 * origin, 2)
            return pltpu.make_async_copy(dst.at[rows], out.at[rows], watch[1].at[origin])

        def relay(step):
            for cut in range(cuts):
                for way in range(2):
                    origin = chip - step if way == 0 else chip + step

                    @pl.when((origin >= 0) & (origin < chips))
                    def _():
                        slot = dst.at[2 * origin + core]
                        line(slot, slot, origin, way, cut).wait_recv()

                        @pl.when((chip < chips - 1) if way == 0 else (chip > 0))
                        def _():
                            line(slot, slot, origin, way, cut).start()

                        across(slot, slot, origin, cut).start()

        self.dst, self.arrived, self.relay = dst, arrived, relay
        for cut in range(cuts):

            @pl.when(chip < chips - 1)
            def _():
                line(src, mine, chip, 0, cut).start()

            @pl.when(chip > 0)
            def _():
                line(src, mine, chip, 1, cut).start()

        for cut in range(cuts):
            across(src, mine, chip, cut).start()
        own.start()
        yield
        if self.watched:
            yield
        for step in range(1, chips):
            if not self.watched:
                relay(step)
                yield
        for step in range(chips):
            for way in range(2):
                origin = chip - step if way == 0 else chip + step
                ahead = (chip < chips - 1) if way == 0 else (chip > 0)

                @pl.when((origin >= 0) & (origin < chips) & ahead)
                def _():
                    slot = dst.at[2 * origin + core]
                    for cut in range(cuts):
                        line(slot, slot, origin, way, cut).wait_send()

        for origin in range(chips):
            slot = dst.at[2 * origin + core]
            for cut in range(cuts):
                across(slot, slot, origin, cut).wait_send()
            if self.watched:
                kept(origin).wait()
            else:
                arrived(origin)


class Scatter:
    outside = ()

    def __init__(self, parts, shape, cuts=2):
        self.parts, self.shape, self.cuts = parts, shape, cuts
        self.out = jax.ShapeDtypeStruct(shape, jnp.float32)
        chips = parts // 2
        piece = (self.cuts, shape[0] // self.cuts, shape[1])
        self.scratch = [
            pltpu.VMEM((chips,) + shape, LOW),
            pltpu.VMEM((2, chips) + piece, LOW),
            pltpu.VMEM((chips,) + piece, LOW),
            pltpu.SemaphoreType.DMA((chips,)),
            pltpu.SemaphoreType.DMA((chips,)),
            pltpu.SemaphoreType.DMA((chips, self.cuts)),
            pltpu.SemaphoreType.DMA((2, chips, self.cuts)),
        ]

    def run(self, src, out, pair, come, stage, pair_send, pair_recv, send, recv):
        chips, cuts = self.parts // 2, self.cuts
        me = lax.axis_index("ctx")
        chip, core = me // 2, lax.rem(me, 2)
        partner = me + 1 - 2 * core
        rows = self.shape[0] // cuts
        slab = min(rows, 16)
        last = chips - 1

        def across(goal):
            return remote(
                src.at[2 * goal + 1 - core],
                pair.at[goal],
                pair_send.at[goal],
                pair_recv.at[goal],
                "ctx",
                partner,
            )

        def line(goal, cut, way):
            return remote(
                stage.at[goal, cut],
                come.at[way, goal, cut],
                send.at[goal, cut],
                recv.at[way, goal, cut],
                "ctx",
                me + 2 - 4 * way,
            )

        def wide(ref, *index):
            return ref[index].astype(jnp.float32)

        def slabs(part):
            def one(index, carry):
                part(pl.multiple_of(index * slab, slab))
                return carry

            lax.fori_loop(0, rows // slab, one, 0)

        def both(goal, cut, at):
            at = pl.ds(cut * rows + at, slab)
            return wide(src, 2 * goal + core, at) + wide(pair, goal, at)

        order = []
        for step in range((chips + 1) // 2):
            order += sorted({step, last - step})
        for goal in order:
            across(goal).start()
        yield
        for step in range(last * cuts):
            for way in range(2):
                turn = step - (chip if way == 0 else last - chip)
                goal = (last - turn // cuts) if way == 0 else turn // cuts
                cut = step - (chip if way == 0 else last - chip) - (turn // cuts) * cuts
                first = (chip == 0) if way == 0 else (chip == last)
                ahead = last - chip if way == 0 else chip

                def begin(at):
                    value = both(goal, cut, at)
                    stage[goal, cut, pl.ds(at, slab), :] = value.astype(LOW)

                def middle(at):
                    value = both(goal, cut, at) + wide(come, way, goal, cut, pl.ds(at, slab))
                    stage[goal, cut, pl.ds(at, slab), :] = value.astype(LOW)

                @pl.when((turn >= 0) & (turn < ahead * cuts))
                def _():
                    @pl.when(cut == 0)
                    def _():
                        across(goal).wait_recv()

                    @pl.when(first)
                    def _():
                        slabs(begin)

                    @pl.when(jnp.logical_not(first))
                    def _():
                        line(goal, cut, way).wait_recv()
                        slabs(middle)

                    line(goal, cut, way).start()

            yield
        across(chip).wait_recv()
        for cut in range(cuts):

            def own(at):
                out[pl.ds(cut * rows + at, slab), :] = both(chip, cut, at)

            slabs(own)
        yield
        for cut in range(cuts):
            for way in range(2):

                def final(at):
                    out[pl.ds(cut * rows + at, slab), :] += wide(
                        come, way, chip, cut, pl.ds(at, slab)
                    )

                @pl.when((chip > 0) if way == 0 else (chip < last))
                def _():
                    line(chip, cut, way).wait_recv()
                    slabs(final)

            yield
        for goal in range(chips):
            across(goal).wait_send()

            @pl.when(chip != goal)
            def _():
                for cut in range(cuts):
                    line(goal, cut, 0).wait_send()


class Fan:
    outside = ("in", "out")

    def __init__(self, groups, shape):
        self.groups = groups
        self.out = jax.ShapeDtypeStruct((groups,) + shape, LOW)
        self.scratch = [
            pltpu.SemaphoreType.DMA((groups - 1,)),
            pltpu.SemaphoreType.DMA((groups - 1,)),
            pltpu.SemaphoreType.DMA,
        ]

    def run(self, src, dst, send, recv, local):
        groups = self.groups
        group = lax.axis_index("fsdp")
        copies = []
        for hop in range(1, groups):
            peer = lax.rem(group + hop, groups)
            copies.append(
                remote(src, dst.at[group], send.at[hop - 1], recv.at[hop - 1], "fsdp", peer)
            )
            copies[-1].start()
        own = pltpu.make_async_copy(src, dst.at[group], local)
        own.start()
        yield
        yield
        yield
        for copy in copies:
            copy.wait()
        own.wait()


class Spread:
    outside = ("in", "out")

    def __init__(self, parts, groups, shape, columns=None):
        self.parts, self.groups, self.columns = parts, groups, columns
        self.out = jax.ShapeDtypeStruct((groups, parts) + shape, LOW)
        self.scratch = [
            pltpu.SemaphoreType.DMA((parts - 1,)),
            pltpu.SemaphoreType.DMA((parts - 1,)),
            pltpu.SemaphoreType.DMA((groups - 1, parts)),
            pltpu.SemaphoreType.DMA((groups - 1, parts)),
            pltpu.SemaphoreType.DMA,
        ]

    def run(self, src, dst, send, recv, far_send, far_recv, local):
        parts, groups = self.parts, self.groups
        me, group = lax.axis_index("ctx"), lax.axis_index("fsdp")
        slot = dst.at[group, me]
        for block, target in blocks_of(src, me, slot, self.columns):
            pltpu.make_async_copy(block, target, local).start()
        copies = []
        for step in range(1, parts):
            peer = lax.rem(me + step, parts)
            whole = (send.at[step - 1], recv.at[step - 1], "ctx", peer)
            for block, target in blocks_of(src, peer, slot, self.columns):
                remote(block, target, *whole).start()
            copies.append(remote(slot, slot, *whole))
        pltpu.make_async_copy(slot, slot, local).wait()

        def pass_on(block, origin, step):
            out = []
            for hop in range(1, groups):
                copy = remote(
                    block,
                    dst.at[group, origin],
                    far_send.at[hop - 1, step],
                    far_recv.at[hop - 1, step],
                    "fsdp",
                    lax.rem(group + hop, groups),
                )
                copy.start()
                out.append(copy)
            return out

        far = pass_on(slot, me, 0)
        eager = -(-parts // 2)
        yield
        for step in range(1, parts):
            copies[step - 1].wait_recv()
            origin = lax.rem(me - step + parts, parts)
            far += pass_on(dst.at[group, origin], origin, step)
            if step % eager == 0:
                yield
        for at, copy in enumerate(far):
            copy.wait()
            if at % 6 == 5:
                yield
        for copy in copies:
            copy.wait_send()


class Deliver:
    outside = ("in",)

    def __init__(self, parts, shape, offsets, delay=0, eager=1):
        self.parts, self.shape, self.offsets = parts, shape, offsets
        self.delay, self.eager = delay, eager
        self.out = jax.ShapeDtypeStruct((shape[0], parts * shape[1]), jnp.float32)
        self.scratch = [
            pltpu.VMEM((parts,) + shape, LOW),
            pltpu.SemaphoreType.DMA((parts - 1,)),
            pltpu.SemaphoreType.DMA((parts,)),
        ]

    def place(self, out, origin, read):
        starts = self.offsets(origin)
        step = self.shape[1] // len(starts)
        for index, start in enumerate(starts):
            out[:, pl.ds(pl.multiple_of(start, HEAD_DIM), step)] = read(
                index * step, (index + 1) * step
            )

    def send(self, me, step, block, came, send, recv):
        return remote(
            block,
            came.at[step - 1],
            send.at[step - 1],
            recv.at[step - 1],
            "ctx",
            lax.rem(me + step, self.parts),
        )

    def run(self, src, out, came, send, recv):
        for _ in range(self.delay):
            yield
        me = lax.axis_index("ctx")
        copies = []
        for step in range(1, self.parts):
            block = src.at[lax.rem(me + step, self.parts)]
            copies.append(self.send(me, step, block, came, send, recv))
            copies[-1].start()
        last = self.parts - 1
        own = pltpu.make_async_copy(src.at[me], came.at[last], recv.at[last])
        own.start()
        yield
        own.wait()
        self.place(out, me, lambda lo, hi: came[last, :, lo:hi].astype(jnp.float32))
        yield from self.finish(me, out, copies, came)

    def finish(self, me, out, copies, came):
        for step in range(1, self.parts):
            copies[step - 1].wait_recv()
            origin = lax.rem(me - step + self.parts, self.parts)
            self.place(out, origin, lambda lo, hi: came[step - 1, :, lo:hi].astype(jnp.float32))
            if step % self.eager == 0:
                yield
        for copy in copies:
            copy.wait_send()


class Collect(Deliver):
    outside = ()

    def __init__(self, parts, groups, shape, offsets, delay=0, eager=1):
        super().__init__(parts, shape, offsets, delay, eager)
        self.groups = groups
        self.scratch = self.scratch + [
            pltpu.VMEM((groups - 1, parts) + shape, LOW),
            pltpu.VMEM((parts,) + shape, LOW),
            pltpu.VMEM(shape, jnp.float32),
            pltpu.SemaphoreType.DMA((groups - 1, parts)),
            pltpu.SemaphoreType.DMA((groups - 1, parts)),
        ]

    def run(self, src, out, came, send, recv, far, stage, mine, far_send, far_recv):
        parts, groups = self.parts, self.groups
        me, group = lax.axis_index("ctx"), lax.axis_index("fsdp")
        goals = [lax.rem(me + step, parts) for step in range(1, parts + 1)]
        hops = []
        for goal in goals:
            for hop in range(1, groups):
                peer = lax.rem(group + hop, groups)
                hops.append(
                    remote(
                        src.at[peer, goal],
                        far.at[hop - 1, goal],
                        far_send.at[hop - 1, goal],
                        far_recv.at[hop - 1, goal],
                        "fsdp",
                        peer,
                    )
                )
                hops[-1].start()
        yield
        copies = []
        for step in range(1, parts + 1):
            goal = goals[step - 1]
            for copy in hops[(step - 1) * (groups - 1) : step * (groups - 1)]:
                copy.wait_recv()
            value = src[group, goal].astype(jnp.float32)
            for hop in range(groups - 1):
                value += far[hop, goal].astype(jnp.float32)
            if step < parts:
                stage[goal] = value.astype(LOW)
                copies.append(self.send(me, step, stage.at[goal], came, send, recv))
                copies[-1].start()
            else:
                mine[...] = value
            if step % self.eager == 0:
                yield
        self.place(out, me, lambda lo, hi: mine[:, lo:hi])
        yield from self.finish(me, out, copies, came)
        for copy in hops:
            copy.wait_send()


def product(left, right):
    return jnp.dot(left, right, preferred_element_type=jnp.float32)


class Puts:
    def __init__(self, made, put):
        self.made, self.put, self.copies = made, put, []

    def pair(self, fill, columns, out, at, tile):
        for copy in self.copies:
            copy.wait()
        lax.fori_loop(0, 2, fill, 0)
        self.copies = []
        for half in range(2):
            begin = at + half * tile
            copy = pltpu.make_async_copy(
                self.made.at[half, :, pl.ds(0, columns)],
                out.at[begin : begin + tile, :],
                self.put.at[half],
            )
            copy.start()
            self.copies.append(copy)

    def finish(self):
        for copy in self.copies:
            copy.wait()


def call(jobs, operands, name, identity, axes, work=None, micros=50):
    counts = [len(job.scratch) for job in jobs]
    jobs_n = len(jobs)
    extra = work.operands if work else []
    extra_out = work.outs if work else []
    extra_scratch = work.scratch if work else []

    def kernel(*refs):
        refs = list(refs)

        def take(count):
            taken = refs[:count]
            del refs[:count]
            return taken

        ins, more = take(jobs_n), take(len(extra))
        outs, more_outs = take(jobs_n), take(len(extra_out))
        runs = []
        for job, src, dst, count in zip(jobs, ins, outs, counts):
            runs.append(job.run(src, dst, *take(count)))
        if work:
            runs.append(work.run(*more, *more_outs, *refs))
        enter(axes)
        while runs:
            going = []
            for run in runs:
                try:
                    next(run)
                    going.append(run)
                except StopIteration:
                    pass
            runs = going

    vmem = pl.BlockSpec(memory_space=pltpu.VMEM)
    anywhere = pl.BlockSpec(memory_space=pl.ANY)
    in_specs = [anywhere if "in" in job.outside else vmem for job in jobs]
    out_specs = [anywhere if "out" in job.outside else vmem for job in jobs]
    return pl.pallas_call(
        kernel,
        out_shape=tuple(job.out for job in jobs) + tuple(extra_out),
        in_specs=in_specs + [anywhere] * len(extra),
        out_specs=tuple(out_specs) + (anywhere,) * len(extra_out),
        scratch_shapes=[shape for job in jobs for shape in job.scratch] + list(extra_scratch),
        compiler_params=pltpu.CompilerParams(
            collective_id=identity, has_side_effects=True, vmem_limit_bytes=62 << 20
        ),
        cost_estimate=pl.CostEstimate(
            flops=0, bytes_accessed=micros * 3_000_000, transcendentals=0
        ),
        name=name,
    )(*operands, *extra)


class Grads:
    tile = 256

    def __init__(self, pairs):
        self.pairs = pairs
        length, wide = pairs[0][0].shape[0], max(right.shape[1] for _, right in pairs)
        self.operands = [array for pair in pairs for array in pair]
        self.outs = [jax.ShapeDtypeStruct((l.shape[1], r.shape[1]), LOW) for l, r in pairs]
        self.slots = [[id(array) for array in self.operands].index(id(a)) for a in self.operands]
        self.operands = [a for i, a in enumerate(self.operands) if self.slots[i] == i]
        self.slots = [sorted(set(self.slots)).index(slot) for slot in self.slots]
        self.scratch = [pltpu.VMEM(array.shape, LOW) for array in self.operands]
        self.scratch += [
            pltpu.VMEM((self.tile, length), LOW),
            pltpu.VMEM((2, self.tile, wide), LOW),
            pltpu.SemaphoreType.DMA((len(self.operands),)),
            pltpu.SemaphoreType.DMA((2,)),
        ]

    def run(self, *refs):
        n, tile, count = len(self.pairs), self.tile, len(self.operands)
        sources, outs = refs[:count], refs[count : count + n]
        held = refs[count + n : 2 * count + n]
        turned, made, get, put = refs[2 * count + n :]
        gets = [pltpu.make_async_copy(s, h, get.at[i]) for i, (s, h) in enumerate(zip(sources, held))]
        for copy in gets:
            copy.start()
        yield
        puts = Puts(made, put)
        for which in range(n):
            first, second = self.slots[2 * which : 2 * which + 2]
            left, right, out = held[first], held[second], outs[which]
            for slot in (first, second):
                if slot not in self.slots[: 2 * which]:
                    gets[slot].wait()
            columns = right.shape[1]
            step = min(columns, 512)
            for at in range(0, left.shape[1], 2 * tile):

                def pair(half, carry):
                    begin = pl.multiple_of(at + half * tile, tile)
                    turned[...] = left[:, pl.ds(begin, tile)].T

                    def one(index, carry):
                        where = pl.ds(pl.multiple_of(index * step, step), step)
                        made[half, :, where] = product(turned[...], right[:, where]).astype(LOW)
                        return carry

                    return lax.fori_loop(0, columns // step, one, carry)

                puts.pair(pair, columns, out, at, tile)
                yield
        puts.finish()


def softmax_block(query, keys, ok):
    scores = times_transposed(query, keys) * HEAD_DIM ** (-0.5)
    scores = jnp.where(ok, scores, -1e30)
    weights = jnp.exp(scores - jnp.max(scores, axis=-1, keepdims=True))
    weights = jnp.where(ok, weights, 0.0)
    return weights, jnp.sum(weights, axis=-1, keepdims=True)


class Attend:
    tile = 256

    def __init__(self, rows, weight, tables, heads):
        self.heads = heads
        self.operands = [rows, weight] + list(tables)
        length, wide = rows.shape[0], weight.shape[1]
        self.outs = [
            jax.ShapeDtypeStruct((length, wide), LOW),
            jax.ShapeDtypeStruct((length, wide // 3), LOW),
        ]
        self.scratch = [pltpu.VMEM(array.shape, array.dtype) for array in self.operands]
        self.scratch += [pltpu.VMEM(out.shape, out.dtype) for out in self.outs]
        self.scratch += [
            pltpu.SemaphoreType.DMA((len(self.operands),)),
            pltpu.SemaphoreType.DMA((2,)),
        ]

    def run(self, *refs):
        n, tile, heads = len(self.operands), self.tile, self.heads
        sources, results, held = refs[:n], refs[n : n + 2], refs[n + 2 : 2 * n + 2]
        qkv, mix, get, put = refs[2 * n + 2 :]
        rows, weight, cosine, sine, ends, keys = held
        gets = [pltpu.make_async_copy(s, h, get.at[i]) for i, (s, h) in enumerate(zip(sources, held))]
        for copy in gets:
            copy.start()
        yield
        for copy in gets:
            copy.wait()
        width = heads * HEAD_DIM

        def project(index, carry):
            at = pl.ds(pl.multiple_of(index * tile, tile), tile)
            value = product(rows[at, :], weight[...])
            for head in range(3 * heads):
                block = value[:, head * HEAD_DIM : (head + 1) * HEAD_DIM]
                if head < 2 * heads:
                    turned = pltpu.roll(block, HEAD_DIM // 2, 1)
                    block = block * cosine[at, :] + turned * sine[at, :]
                qkv[at, head * HEAD_DIM : (head + 1) * HEAD_DIM] = block.astype(LOW)
            return carry

        lax.fori_loop(0, rows.shape[0] // tile, project, 0)
        send = pltpu.make_async_copy(qkv, results[0], put.at[0])
        send.start()
        yield

        half = HEAD_DIM // 2

        def attend(index, carry):
            at = pl.ds(pl.multiple_of(index * tile, tile), tile)
            ok = (keys[:1, :] >= ends[at, :1]) & (keys[:1, :] <= ends[at, half : half + 1])
            for head in range(heads):
                lo = head * HEAD_DIM
                weights, total = softmax_block(
                    qkv[at, lo : lo + HEAD_DIM], qkv[:, width + lo : width + lo + HEAD_DIM], ok
                )
                value = qkv[:, 2 * width + lo : 2 * width + lo + HEAD_DIM]
                mixed = product(weights.astype(LOW), value) / total
                mix[at, lo : lo + HEAD_DIM] = mixed.astype(LOW)
            return carry

        lax.fori_loop(0, rows.shape[0] // tile, attend, 0)
        send_mix = pltpu.make_async_copy(mix, results[1], put.at[1])
        send_mix.start()
        yield
        send.wait()
        send_mix.wait()


class AttendBack:
    tile = 256

    def __init__(self, back, qkv, rows, weight, tables, heads):
        self.heads = heads
        self.operands = [back, qkv] + list(tables) + [weight, rows]
        length, wide, width = rows.shape[0], weight.shape[1], rows.shape[1]
        self.outs = [
            jax.ShapeDtypeStruct((length, width), LOW),
            jax.ShapeDtypeStruct((width, wide), LOW),
        ]
        self.scratch = [pltpu.VMEM(array.shape, array.dtype) for array in self.operands]
        self.scratch += [
            pltpu.VMEM((length, wide), LOW),
            pltpu.VMEM((2, length, HEAD_DIM), jnp.float32),
            pltpu.VMEM((self.tile, length), LOW),
            pltpu.VMEM((2, self.tile, width), LOW),
            pltpu.SemaphoreType.DMA((len(self.operands),)),
            pltpu.SemaphoreType.DMA((2,)),
        ]

    def run(self, *refs):
        n, tile, heads = len(self.operands), self.tile, self.heads
        sources, results, held = refs[:n], refs[n : n + 2], refs[n + 2 : 2 * n + 2]
        grads, sums, turned, made, get, put = refs[2 * n + 2 :]
        back, qkv, cosine, sine, ends, keys, weight, rows = held
        length, width = back.shape
        gets = [pltpu.make_async_copy(s, h, get.at[i]) for i, (s, h) in enumerate(zip(sources, held))]
        for copy in gets:
            copy.start()
        yield
        for copy in gets[:-2]:
            copy.wait()

        def unrotated(value, at):
            return value * cosine[at, :] - pltpu.roll(value, HEAD_DIM // 2, 1) * sine[at, :]

        half = HEAD_DIM // 2
        for head in range(heads):
            lo = head * HEAD_DIM
            mine = slice(lo, lo + HEAD_DIM)
            key = slice(width + lo, width + lo + HEAD_DIM)
            val = slice(2 * width + lo, 2 * width + lo + HEAD_DIM)
            sums[...] = jnp.zeros_like(sums)

            def attend(index, carry):
                at = pl.ds(pl.multiple_of(index * tile, tile), tile)
                ok = (keys[:1, :] >= ends[at, :1]) & (keys[:1, :] <= ends[at, half : half + 1])
                weights, total = softmax_block(qkv[at, mine], qkv[:, key], ok)
                probs = weights / total
                upper = back[at, mine]
                prob_back = times_transposed(upper, qkv[:, val])
                delta = jnp.sum(probs * prob_back, axis=-1, keepdims=True)
                score_back = HEAD_DIM ** (-0.5) * probs * (prob_back - delta)
                score_low = score_back.astype(LOW)
                query_back = product(score_low, qkv[:, key])
                grads[at, mine] = unrotated(query_back, at).astype(LOW)
                sums[0] += product(score_low.T, qkv[at, mine])
                sums[1] += product(probs.astype(LOW).T, upper)
                return carry

            lax.fori_loop(0, length // tile, attend, 0)
            yield

            def settle(index, carry):
                at = pl.ds(pl.multiple_of(index * tile, tile), tile)
                grads[at, key] = unrotated(sums[0, at, :], at).astype(LOW)
                grads[at, val] = sums[1, at, :].astype(LOW)
                return carry

            lax.fori_loop(0, length // tile, settle, 0)
        puts = Puts(made, put)
        wide = grads.shape[1]
        part = tile if wide % tile == 0 else HEAD_DIM
        gets[-2].wait()
        for at in range(0, length, 2 * tile):

            def terms(half, carry):
                where = pl.ds(pl.multiple_of(at + half * tile, tile), tile)

                def one(index, carry):
                    span = pl.ds(pl.multiple_of(index * tile, tile), tile)
                    value = times_transposed(grads[where, :], weight[span, :])
                    made[half, :, span] = value.astype(LOW)
                    return carry

                return lax.fori_loop(0, made.shape[2] // tile, one, carry)

            puts.pair(terms, made.shape[2], results[0], at, tile)
            yield
        gets[-1].wait()
        for at in range(0, rows.shape[1], 2 * tile):

            def weights(half, carry):
                where = pl.ds(pl.multiple_of(at + half * tile, tile), tile)
                turned[...] = rows[:, where].T

                def one(index, carry):
                    span = pl.ds(pl.multiple_of(index * part, part), part)
                    made[half, :, span] = product(turned[...], grads[:, span]).astype(LOW)
                    return carry

                return lax.fori_loop(0, wide // part, one, carry)

            puts.pair(weights, wide, results[1], at, tile)
            yield
        puts.finish()


def near_first(chips):
    table = []
    for chip in range(chips):
        order = [chip]
        for step in range(1, chips):
            order += [at for at in (chip + step, chip - step) if 0 <= at < chips]
        table.append(order)
    return table


def next_chip(chips, turn):
    chip = lax.axis_index("ctx") // 2
    return sum(
        jnp.where((chip == at) & (turn == when), order[when], 0)
        for at, order in enumerate(near_first(chips))
        for when in range(chips)
    )


class ProjectBack:
    tile = 256

    def __init__(self, job, activated, down, out_rows, mix):
        self.job = job
        self.operands = [activated, down, out_rows, mix]
        length, heads_width = mix.shape
        width = down.shape[1]
        self.outs = [
            jax.ShapeDtypeStruct((length, width), LOW),
            jax.ShapeDtypeStruct((length, heads_width), LOW),
            jax.ShapeDtypeStruct((heads_width, width), LOW),
        ]
        self.scratch = [pltpu.VMEM(array.shape, array.dtype) for array in self.operands]
        self.scratch += [
            pltpu.VMEM((2, self.tile, width), LOW),
            pltpu.VMEM((length, heads_width), LOW),
            pltpu.VMEM((heads_width, width), jnp.float32),
            pltpu.VMEM((heads_width, width), LOW),
            pltpu.SemaphoreType.DMA((4,)),
            pltpu.SemaphoreType.DMA((2,)),
            pltpu.SemaphoreType.DMA((2,)),
        ]

    def run(self, *refs):
        job, tile = self.job, self.tile
        sources, results, held = refs[:4], refs[4:7], refs[7:11]
        made, back, total, total_low, get, put, leave = refs[11:]
        activated, down, out_rows, mix = held
        length, width = mix.shape[0], down.shape[1]
        gets = [pltpu.make_async_copy(s, h, get.at[i]) for i, (s, h) in enumerate(zip(sources, held))]
        for copy in gets:
            copy.start()
        yield
        for copy in gets:
            copy.wait()
        total[...] = jnp.zeros_like(total)
        puts = Puts(made, put)
        for at in range(0, length, 2 * tile):

            def terms(half, carry):
                where = pl.ds(pl.multiple_of(at + half * tile, tile), tile)

                def one(index, carry):
                    span = pl.ds(pl.multiple_of(index * tile, tile), tile)
                    value = product(activated[where, :], down[:, span])
                    made[half, :, span] = value.astype(LOW)
                    return carry

                return lax.fori_loop(0, width // tile, one, carry)

            puts.pair(terms, width, results[0], at, tile)
        chips = job.parts // 2
        rows = length // chips

        def one_chip(turn, carry):
            origin = next_chip(chips, turn)

            @pl.when(turn > 0)
            def _():
                job.relay(turn)

            job.arrived(origin)
            at = pl.ds(pl.multiple_of(origin * rows, rows), rows)
            block = job.dst.at[pl.ds(2 * origin, 2)]
            value = block[...].reshape(rows, width)
            back[at, :] = times_transposed(value, out_rows[...]).astype(LOW)
            total[...] += product(mix[at, :].T, value)
            return carry

        lax.fori_loop(0, chips, one_chip, 0)
        total_low[...] = total[...].astype(LOW)
        out = [
            pltpu.make_async_copy(back, results[1], leave.at[0]),
            pltpu.make_async_copy(total_low, results[2], leave.at[1]),
        ]
        for copy in out:
            copy.start()
        puts.finish()
        for copy in out:
            copy.wait()


class FeedForward:
    def __init__(self, job, act_grad, gate, up):
        self.job = job
        self.operands = [act_grad, gate, up]
        length = act_grad.shape[0]
        width, units = gate.shape
        self.outs = [
            jax.ShapeDtypeStruct((length, units), LOW),
            jax.ShapeDtypeStruct((length, 2 * units), LOW),
            jax.ShapeDtypeStruct((length, width), LOW),
        ]
        self.tile = length // (job.parts // 2)
        self.scratch = [pltpu.VMEM(array.shape, array.dtype) for array in self.operands]
        self.scratch += [pltpu.VMEM((2, self.tile) + out.shape[1:], LOW) for out in self.outs]
        self.scratch += [pltpu.SemaphoreType.DMA((3,)), pltpu.SemaphoreType.DMA((3, 2))]

    def run(self, *refs):
        job, tile = self.job, self.tile
        sources, results, held, made = refs[:3], refs[3:6], refs[6:9], refs[9:12]
        get, put = refs[12:]
        act_grads, gate_w, up_w = held
        acts, backs, terms = made
        width, units = gate_w.shape
        step = min(units, 256)
        span = min(width, 512)
        gets = [pltpu.make_async_copy(sources[i], held[i], get.at[i]) for i in (1, 2, 0)]
        for copy in gets:
            copy.start()
        yield
        for copy in gets:
            copy.wait()
        chips = job.parts // 2

        def leave(slot, origin):
            at = pl.ds(pl.multiple_of(origin * tile, tile), tile)
            return [
                pltpu.make_async_copy(made[i].at[slot], results[i].at[at, :], put.at[i, slot])
                for i in range(3)
            ]

        def one_chip(turn, carry):
            origin = next_chip(chips, turn)
            slot = lax.rem(turn, 2)

            @pl.when(turn > 0)
            def _():
                job.relay(turn)

            @pl.when(turn >= 2)
            def _():
                for copy in leave(slot, 0):
                    copy.wait()

            job.arrived(origin)
            at = pl.ds(pl.multiple_of(origin * tile, tile), tile)
            normed = job.dst.at[pl.ds(2 * origin, 2)]

            def forward(index, carry):
                left = pl.ds(pl.multiple_of(index * step, step), step)
                right = pl.ds(pl.multiple_of(units + index * step, step), step)
                value = normed[...].reshape(tile, width)
                gate = product(value, gate_w[:, left])
                up = product(value, up_w[:, left])
                act_grad = act_grads[at, left]
                sigmoid = jax.nn.sigmoid(gate)
                silu = gate * sigmoid
                acts[slot, :, left] = (silu * up).astype(LOW)
                gate_grad = act_grad * up * sigmoid * (1.0 + gate * (1.0 - sigmoid))
                backs[slot, :, left] = gate_grad.astype(LOW)
                backs[slot, :, right] = (act_grad * silu).astype(LOW)
                return carry

            lax.fori_loop(0, units // step, forward, 0)

            def backward(index, carry):
                where = pl.ds(pl.multiple_of(index * span, span), span)
                value = times_transposed(backs[slot, :, :units], gate_w[where, :])
                value += times_transposed(backs[slot, :, units:], up_w[where, :])
                terms[slot, :, where] = value.astype(LOW)
                return carry

            lax.fori_loop(0, width // span, backward, 0)
            for copy in leave(slot, origin):
                copy.start()
            return carry

        lax.fori_loop(0, chips, one_chip, 0)
        for slot in range(min(2, chips)):
            for copy in leave(slot, 0):
                copy.wait()


class Plan:
    def __init__(self, parts, groups, width):
        self.parts, self.groups = parts, groups
        self.shard = width // (parts * groups)
        self.run = HEAD_DIM // self.shard
        self.heads = HEADS // parts

    def qkv_starts(self, part):
        at, index = part // self.run, lax.rem(part, self.run)
        return [
            (kind * HEADS + (index * self.heads + head) * (self.parts // self.run) + at) * HEAD_DIM
            for kind in range(3)
            for head in range(self.heads)
        ]

    def unit_source(self, weight, kind):
        rows, columns = weight.shape
        half = columns // 2
        step = half // (self.groups * self.parts)
        if step % HEAD_DIM == 0:
            return weight, lambda part: [
                kind * half + (at * self.parts + part) * step for at in range(self.groups)
            ]
        pieces = weight[:, kind * half : (kind + 1) * half]
        pieces = pieces.reshape(rows, self.groups, self.parts, step).transpose(2, 0, 1, 3)
        return pieces.reshape(self.parts, rows, self.groups * step), None

    def unit_job(self, shape):
        step = shape[1] // (2 * self.groups)
        if step % HEAD_DIM:
            return Exchange(self.parts, shape)
        return Deliver(
            self.parts,
            shape,
            lambda part: [(at * self.parts + part) * step for at in range(2 * self.groups)],
        )

    def unit_rows(self, pieces):
        if pieces.ndim == 2:
            return pieces
        parts, rows, columns = pieces.shape
        outer = 2 * self.groups
        pieces = pieces.reshape(parts, rows, outer, columns // outer).transpose(1, 2, 0, 3)
        return pieces.reshape(rows, parts * columns).astype(jnp.float32)


def per_device(tokens, w_qkv, w_out, w_gate_up, w_down, seq_lengths, block_order, cotangent):
    lengths = seq_lengths[0]
    order_row = block_order[0]
    parts = lax.axis_size("ctx")
    groups = lax.axis_size("fsdp")
    rows, width = tokens.shape
    length = rows * parts
    plan = Plan(parts, groups, width)
    heads, shard, run = plan.heads, plan.shard, plan.run
    head_width = heads * HEAD_DIM
    line = (("ctx", parts),)
    plane = (("ctx", parts), ("fsdp", groups))
    block = (rows, width)

    down_rows = gather(w_down, "fsdp")
    unit_columns = w_gate_up.shape[1] // (2 * parts)
    unit_shape = (w_gate_up.shape[0], unit_columns)
    both_shape = (w_gate_up.shape[0], 2 * unit_columns)
    qkv_shape = (w_qkv.shape[0], 3 * head_width)
    gate_source, gate_starts = plan.unit_source(w_gate_up, 0)
    up_source, up_starts = plan.unit_source(w_gate_up, 1)
    inputs = tokens.astype(jnp.float32)
    normed_in, root_in = normalize(inputs)
    qkv_cols, normed_in_full, gate_cols, out_rows = call(
        [
            Spread(parts, groups, qkv_shape, plan.qkv_starts),
            Gather(parts, block, cuts=1),
            Exchange(parts, unit_shape, 2, gate_starts),
            Fan(groups, w_out.shape),
        ],
        [w_qkv, normed_in.astype(LOW), gate_source, w_out],
        "start",
        2,
        plane,
        micros=90,
    )
    gate_cols = gather(gate_cols.reshape(width // groups, -1), "fsdp")
    qkv_cols = qkv_cols.reshape(width, 3 * head_width)
    normed_in_full = normed_in_full.reshape(length, width)

    row_index = jnp.arange(length, dtype=jnp.int32)
    packed = initial_index(row_index, order_row)
    _, pos = places(packed, lengths)
    cosine_table, sine_table = angle_tables(pos)
    half_sign = jnp.where(jnp.arange(HEAD_DIM) < HEAD_DIM // 2, -1.0, 1.0)
    tables = (
        cosine_table[:, 0, :],
        sine_table[:, 0, :] * half_sign,
        packed[:, None] - jnp.where(jnp.arange(HEAD_DIM) < HEAD_DIM // 2, pos[:, None], 0),
        jnp.broadcast_to(packed[None, :], (8, length)),
    )
    up_cols, out_cols, qkv_low, mix_low = call(
        [
            Exchange(parts, unit_shape, 0, up_starts),
            Exchange(run, (heads, shard, width), second="out"),
        ],
        [up_source, out_rows.reshape(run, heads, shard, width)],
        "attend",
        1,
        line,
        Attend(normed_in_full, qkv_cols, tables, heads),
        micros=40,
    )
    up_cols = gather(up_cols.reshape(width // groups, -1), "fsdp")
    out_cols = out_cols.reshape(head_width, width)

    out_terms = dot(mix_low, out_cols).astype(LOW)
    attn_out, cot_full = call(
        [Scatter(parts, block, cuts=1), Gather(parts, block, cuts=1)],
        [out_terms.reshape((parts,) + block), cotangent],
        "out",
        3,
        line,
        micros=64,
    )
    cot_full = cot_full.reshape(length, width)
    residual = inputs + attn_out
    normed_mid, root_mid = normalize(residual)
    act_grad = times_transposed(cot_full, down_rows)
    mid_job = Gather(parts, block, watched=True)
    normed_mid_full, activated, gate_up_back, mid_back_terms = call(
        [mid_job],
        [normed_mid.astype(LOW)],
        "mid",
        4,
        line,
        FeedForward(mid_job, act_grad, gate_cols, up_cols),
        micros=60,
    )
    normed_mid_full = normed_mid_full.reshape(length, width)
    mid_back, gate_up_grad, down_grad = call(
        [Scatter(parts, block)],
        [mid_back_terms.reshape((parts,) + block)],
        "mid_back",
        5,
        line,
        Grads([(normed_mid_full, gate_up_back), (activated, cot_full)]),
    )
    gate_up_grad = scatter(gate_up_grad, "fsdp")
    down_grad = scatter(down_grad, "fsdp")
    residual_back = cotangent.astype(jnp.float32) + norm_back(mid_back, normed_mid, root_mid)
    proj_back = residual_back.astype(LOW)

    proj_job = Gather(parts, block, watched=True)
    _, down_terms, back_heads, out_grad = call(
        [proj_job],
        [proj_back],
        "proj_back",
        6,
        line,
        ProjectBack(proj_job, activated, down_rows, out_cols, mix_low),
        micros=45,
    )
    down_out, out_grad, in_back_terms, qkv_grad = call(
        [
            Scatter(parts, block),
            Exchange(run, (heads, shard, width), second="in"),
        ],
        [
            down_terms.reshape((parts,) + block),
            out_grad.reshape(heads, run, shard, width),
        ],
        "attend_back",
        8,
        line,
        AttendBack(back_heads, qkv_low, normed_in_full, qkv_cols, tables, heads),
        micros=60,
    )
    layer_out = (residual + down_out).astype(LOW)
    out_grad, gate_up_grad = lax.optimization_barrier((out_grad, gate_up_grad))
    out_grad = scatter(out_grad.reshape(groups * shard, width), "fsdp")
    in_back, qkv_grad, gate_up_grad = call(
        [
            Scatter(parts, block),
            Collect(parts, groups, qkv_shape, plan.qkv_starts),
            plan.unit_job(both_shape),
        ],
        [
            in_back_terms.reshape((parts,) + block),
            qkv_grad.reshape((groups, parts) + qkv_shape),
            gate_up_grad.reshape((parts,) + both_shape),
        ],
        "in_back",
        7,
        plane,
        micros=90,
    )
    in_back, down_grad, out_grad = lax.optimization_barrier((in_back, down_grad, out_grad))
    tokens_grad = residual_back + norm_back(in_back, normed_in, root_in)
    return (
        layer_out,
        tokens_grad,
        qkv_grad,
        out_grad.astype(jnp.float32),
        plan.unit_rows(gate_up_grad),
        down_grad.astype(jnp.float32),
    )


def solution(mesh):
    both = P(("fsdp", "ctx"), None)
    one = P("fsdp", None)
    return jax.shard_map(
        per_device,
        mesh=mesh,
        in_specs=(both, both, both, both, both, one, one, both),
        out_specs=(both,) * 6,
        check_vma=False,
    )
```

```python
import jax
import jax.numpy as jnp
from jax import lax
from jax.experimental import pallas as pl
from jax.experimental.pallas import tpu as pltpu
from jax.sharding import PartitionSpec as P

HEADS = 16
HEAD_DIM = 128
BLOCK = 128
LOW = jnp.bfloat16


def normalize(values):
    average = jnp.mean(values, axis=-1, keepdims=True)
    centered = values - average
    variance = jnp.mean(centered * centered, axis=-1, keepdims=True)
    inv_root = lax.rsqrt(variance + 1e-05)
    return (centered * inv_root, inv_root)


def norm_back(upstream, normed, inv_root):
    first_mean = jnp.mean(upstream, axis=-1, keepdims=True)
    second_mean = jnp.mean(upstream * normed, axis=-1, keepdims=True)
    return inv_root * (upstream - first_mean - normed * second_mean)


def places(token_index, lengths):
    seq_ends = jnp.cumsum(lengths)
    sequence = jnp.sum((token_index[:, None] >= seq_ends[None, :]).astype(jnp.int32), axis=1)
    before = jnp.arange(lengths.shape[0], dtype=jnp.int32)
    seq_start = jnp.sum(jnp.where(before[None, :] < sequence[:, None], lengths[None, :], 0), axis=1)
    return (sequence, token_index - seq_start)


def initial_index(row_index, order_row):
    slot_index = row_index // BLOCK
    slot_table = jnp.arange(order_row.shape[0], dtype=jnp.int32)
    picked = jnp.sum(
        jnp.where(slot_table[None, :] == slot_index[:, None], order_row[None, :], 0), axis=1
    )
    return picked * BLOCK + row_index % BLOCK


def angle_tables(position):
    half_dim = HEAD_DIM // 2
    frequency = 10000.0 ** (-jnp.arange(half_dim, dtype=jnp.float32) * 2.0 / HEAD_DIM)
    angle_table = position.astype(jnp.float32)[:, None] * frequency[None, :]
    angle_table = jnp.concatenate([angle_table, angle_table], axis=-1)
    return (jnp.cos(angle_table)[:, None, :], jnp.sin(angle_table)[:, None, :])


def rotate(values, cosine_table, sine_table):
    half_dim = values.shape[-1] // 2
    turned = jnp.concatenate([-values[..., half_dim:], values[..., :half_dim]], axis=-1)
    return values * cosine_table + turned * sine_table


def unrotate(values, cosine_table, sine_table):
    half_dim = values.shape[-1] // 2
    scaled = values * sine_table
    turned = jnp.concatenate([scaled[..., half_dim:], -scaled[..., :half_dim]], axis=-1)
    return values * cosine_table + turned


def dot(left, right):
    return jnp.dot(left, right, preferred_element_type=jnp.float32)


def times_transposed(left, right):
    return lax.dot_general(
        left, right, (((1,), (1,)), ((), ())), preferred_element_type=jnp.float32
    )


def column_product(left, right):
    return lax.dot_general(
        left, right, (((0,), (0,)), ((), ())), preferred_element_type=jnp.float32
    )


def gather(values, axes):
    return lax.all_gather(values, axes, axis=0, tiled=True)


def scatter(values, axes):
    return lax.psum_scatter(values, axes, scatter_dimension=0, tiled=True)


def enter(axes):
    barrier = pltpu.get_barrier_semaphore()
    count = 0
    for axis, size in axes:
        me = lax.axis_index(axis)
        for step in range(1, size):
            pl.semaphore_signal(barrier, inc=1, device_id={axis: lax.rem(me + step, size)})
        count += size - 1
    pl.semaphore_wait(barrier, count)


def remote(src, dst, send, recv, axis, peer):
    return pltpu.make_async_remote_copy(
        src_ref=src, dst_ref=dst, send_sem=send, recv_sem=recv, device_id={axis: peer}
    )


class Exchange:
    def __init__(self, parts, shape, delay=0, columns=None, second=""):
        self.parts, self.delay, self.columns, self.second = parts, delay, columns, second
        self.outside = () if second else ("in", "out")
        placed = shape[:1] + (parts,) + shape[1:] if second == "out" else (parts,) + shape
        self.out = jax.ShapeDtypeStruct(placed, LOW)
        self.scratch = [
            pltpu.SemaphoreType.DMA((parts - 1,)),
            pltpu.SemaphoreType.DMA((parts - 1,)),
            pltpu.SemaphoreType.DMA,
        ]

    def run(self, src, dst, send, recv, local):
        for _ in range(self.delay):
            yield
        place = lax.axis_index("ctx")
        me = lax.rem(place, self.parts)
        slot = dst.at[:, me] if self.second == "out" else dst.at[me]

        def blocks(part):
            if self.second == "in":
                return [(src.at[:, part], slot)]
            return blocks_of(src, part, slot, self.columns)

        copies = []
        for step in range(1, self.parts):
            peer = lax.rem(me + step, self.parts)
            whole = (send.at[step - 1], recv.at[step - 1], "ctx", place - me + peer)
            for block, target in blocks(peer):
                copies.append(remote(block, target, *whole))
                copies[-1].start()
            if self.columns:
                del copies[step - 1 :]
                copies.append(remote(slot, slot, *whole))
        for block, target in blocks(me):
            pltpu.make_async_copy(block, target, local).start()
        yield
        for copy in copies:
            copy.wait()
            yield
        pltpu.make_async_copy(slot, slot, local).wait()


def blocks_of(src, part, slot, columns):
    if columns is None:
        return [(src.at[part], slot)]
    starts = columns(part)
    wide = slot.shape[1] // len(starts)
    return [
        (
            src.at[:, pl.ds(pl.multiple_of(start, HEAD_DIM), wide)],
            slot.at[:, pl.ds(index * wide, wide)],
        )
        for index, start in enumerate(starts)
    ]


class Gather:
    def __init__(self, parts, shape, watched=False, cuts=2):
        self.outside = ("in", "out")
        self.parts, self.watched, self.shape, self.cuts = parts, watched, shape, cuts
        self.out = jax.ShapeDtypeStruct((parts,) + shape, LOW)
        chips = parts // 2
        self.scratch = [
            pltpu.SemaphoreType.DMA((2, chips, self.cuts)),
            pltpu.SemaphoreType.DMA((chips, self.cuts)),
            pltpu.SemaphoreType.DMA((chips, self.cuts)),
            pltpu.SemaphoreType.DMA((chips, self.cuts)),
            pltpu.SemaphoreType.DMA,
        ]
        if watched:
            self.scratch += [pltpu.VMEM(self.out.shape, LOW), pltpu.SemaphoreType.DMA((chips,))]

    def run(self, src, out, send, recv, pair_send, pair_recv, local, *watch):
        dst = watch[0] if self.watched else out
        chips, cuts = self.parts // 2, self.cuts
        rows = self.shape[0] // cuts
        me = lax.axis_index("ctx")
        chip, core = me // 2, lax.rem(me, 2)
        partner = me + 1 - 2 * core

        def piece(block, cut):
            return block.at[pl.ds(cut * rows, rows)]

        def line(block, slot, origin, way, cut):
            return remote(
                piece(block, cut),
                piece(slot, cut),
                send.at[way, origin, cut],
                recv.at[origin, cut],
                "ctx",
                me + 2 - 4 * way,
            )

        def across(block, slot, origin, cut):
            return remote(
                piece(block, cut),
                piece(slot, cut),
                pair_send.at[origin, cut],
                pair_recv.at[origin, cut],
                "ctx",
                partner,
            )

        mine = dst.at[me]
        own = pltpu.make_async_copy(src, mine, local)

        def arrived(origin):
            other = dst.at[2 * origin + 1 - core]
            for cut in range(cuts):
                across(other, other, origin, cut).wait_recv()

            @pl.when(origin == chip)
            def _():
                own.wait()

            if self.watched:
                kept(origin).start()

        def kept(origin):
            rows = pl.ds(2 * origin, 2)
            return pltpu.make_async_copy(dst.at[rows], out.at[rows], watch[1].at[origin])

        def relay(step):
            for cut in range(cuts):
                for way in range(2):
                    origin = chip - step if way == 0 else chip + step

                    @pl.when((origin >= 0) & (origin < chips))
                    def _():
                        slot = dst.at[2 * origin + core]
                        line(slot, slot, origin, way, cut).wait_recv()

                        @pl.when((chip < chips - 1) if way == 0 else (chip > 0))
                        def _():
                            line(slot, slot, origin, way, cut).start()

                        across(slot, slot, origin, cut).start()

        self.dst, self.arrived, self.relay = dst, arrived, relay
        for cut in range(cuts):

            @pl.when(chip < chips - 1)
            def _():
                line(src, mine, chip, 0, cut).start()

            @pl.when(chip > 0)
            def _():
                line(src, mine, chip, 1, cut).start()

        for cut in range(cuts):
            across(src, mine, chip, cut).start()
        own.start()
        yield
        if self.watched:
            yield
        for step in range(1, chips):
            if not self.watched:
                relay(step)
                yield
        for step in range(chips):
            for way in range(2):
                origin = chip - step if way == 0 else chip + step
                ahead = (chip < chips - 1) if way == 0 else (chip > 0)

                @pl.when((origin >= 0) & (origin < chips) & ahead)
                def _():
                    slot = dst.at[2 * origin + core]
                    for cut in range(cuts):
                        line(slot, slot, origin, way, cut).wait_send()

        for origin in range(chips):
            slot = dst.at[2 * origin + core]
            for cut in range(cuts):
                across(slot, slot, origin, cut).wait_send()
            if self.watched:
                kept(origin).wait()
            else:
                arrived(origin)


class Scatter:
    outside = ()

    def __init__(self, parts, shape, cuts=2):
        self.parts, self.shape, self.cuts = parts, shape, cuts
        self.out = jax.ShapeDtypeStruct(shape, jnp.float32)
        chips = parts // 2
        piece = (self.cuts, shape[0] // self.cuts, shape[1])
        self.scratch = [
            pltpu.VMEM((chips,) + shape, LOW),
            pltpu.VMEM((2, chips) + piece, LOW),
            pltpu.VMEM((chips,) + piece, LOW),
            pltpu.SemaphoreType.DMA((chips,)),
            pltpu.SemaphoreType.DMA((chips,)),
            pltpu.SemaphoreType.DMA((chips, self.cuts)),
            pltpu.SemaphoreType.DMA((2, chips, self.cuts)),
        ]

    def run(self, src, out, pair, come, stage, pair_send, pair_recv, send, recv):
        chips, cuts = self.parts // 2, self.cuts
        me = lax.axis_index("ctx")
        chip, core = me // 2, lax.rem(me, 2)
        partner = me + 1 - 2 * core
        rows = self.shape[0] // cuts
        slab = min(rows, 16)
        last = chips - 1

        def across(goal):
            return remote(
                src.at[2 * goal + 1 - core],
                pair.at[goal],
                pair_send.at[goal],
                pair_recv.at[goal],
                "ctx",
                partner,
            )

        def line(goal, cut, way):
            return remote(
                stage.at[goal, cut],
                come.at[way, goal, cut],
                send.at[goal, cut],
                recv.at[way, goal, cut],
                "ctx",
                me + 2 - 4 * way,
            )

        def wide(ref, *index):
            return ref[index].astype(jnp.float32)

        def slabs(part):
            def one(index, carry):
                part(pl.multiple_of(index * slab, slab))
                return carry

            lax.fori_loop(0, rows // slab, one, 0)

        def both(goal, cut, at):
            at = pl.ds(cut * rows + at, slab)
            return wide(src, 2 * goal + core, at) + wide(pair, goal, at)

        order = []
        for step in range((chips + 1) // 2):
            order += sorted({step, last - step})
        for goal in order:
            across(goal).start()
        yield
        for step in range(last * cuts):
            for way in range(2):
                turn = step - (chip if way == 0 else last - chip)
                goal = (last - turn // cuts) if way == 0 else turn // cuts
                cut = step - (chip if way == 0 else last - chip) - (turn // cuts) * cuts
                first = (chip == 0) if way == 0 else (chip == last)
                ahead = last - chip if way == 0 else chip

                def begin(at):
                    value = both(goal, cut, at)
                    stage[goal, cut, pl.ds(at, slab), :] = value.astype(LOW)

                def middle(at):
                    value = both(goal, cut, at) + wide(come, way, goal, cut, pl.ds(at, slab))
                    stage[goal, cut, pl.ds(at, slab), :] = value.astype(LOW)

                @pl.when((turn >= 0) & (turn < ahead * cuts))
                def _():
                    @pl.when(cut == 0)
                    def _():
                        across(goal).wait_recv()

                    @pl.when(first)
                    def _():
                        slabs(begin)

                    @pl.when(jnp.logical_not(first))
                    def _():
                        line(goal, cut, way).wait_recv()
                        slabs(middle)

                    line(goal, cut, way).start()

            yield
        across(chip).wait_recv()
        for cut in range(cuts):

            def own(at):
                out[pl.ds(cut * rows + at, slab), :] = both(chip, cut, at)

            slabs(own)
        yield
        for cut in range(cuts):
            for way in range(2):

                def final(at):
                    out[pl.ds(cut * rows + at, slab), :] += wide(
                        come, way, chip, cut, pl.ds(at, slab)
                    )

                @pl.when((chip > 0) if way == 0 else (chip < last))
                def _():
                    line(chip, cut, way).wait_recv()
                    slabs(final)

            yield
        for goal in range(chips):
            across(goal).wait_send()

            @pl.when(chip != goal)
            def _():
                for cut in range(cuts):
                    line(goal, cut, 0).wait_send()


class Fan:
    outside = ("in", "out")

    def __init__(self, groups, shape):
        self.groups = groups
        self.out = jax.ShapeDtypeStruct((groups,) + shape, LOW)
        self.scratch = [
            pltpu.SemaphoreType.DMA((groups - 1,)),
            pltpu.SemaphoreType.DMA((groups - 1,)),
            pltpu.SemaphoreType.DMA,
        ]

    def run(self, src, dst, send, recv, local):
        groups = self.groups
        group = lax.axis_index("fsdp")
        copies = []
        for hop in range(1, groups):
            peer = lax.rem(group + hop, groups)
            copies.append(
                remote(src, dst.at[group], send.at[hop - 1], recv.at[hop - 1], "fsdp", peer)
            )
            copies[-1].start()
        own = pltpu.make_async_copy(src, dst.at[group], local)
        own.start()
        yield
        yield
        yield
        for copy in copies:
            copy.wait()
        own.wait()


class Spread:
    outside = ("in", "out")

    def __init__(self, parts, groups, shape, columns=None):
        self.parts, self.groups, self.columns = parts, groups, columns
        self.out = jax.ShapeDtypeStruct((groups, parts) + shape, LOW)
        self.scratch = [
            pltpu.SemaphoreType.DMA((parts - 1,)),
            pltpu.SemaphoreType.DMA((parts - 1,)),
            pltpu.SemaphoreType.DMA((groups - 1, parts)),
            pltpu.SemaphoreType.DMA((groups - 1, parts)),
            pltpu.SemaphoreType.DMA,
        ]

    def run(self, src, dst, send, recv, far_send, far_recv, local):
        parts, groups = self.parts, self.groups
        me, group = lax.axis_index("ctx"), lax.axis_index("fsdp")
        slot = dst.at[group, me]
        for block, target in blocks_of(src, me, slot, self.columns):
            pltpu.make_async_copy(block, target, local).start()
        copies = []
        for step in range(1, parts):
            peer = lax.rem(me + step, parts)
            whole = (send.at[step - 1], recv.at[step - 1], "ctx", peer)
            for block, target in blocks_of(src, peer, slot, self.columns):
                remote(block, target, *whole).start()
            copies.append(remote(slot, slot, *whole))
        pltpu.make_async_copy(slot, slot, local).wait()

        def pass_on(block, origin, step):
            out = []
            for hop in range(1, groups):
                copy = remote(
                    block,
                    dst.at[group, origin],
                    far_send.at[hop - 1, step],
                    far_recv.at[hop - 1, step],
                    "fsdp",
                    lax.rem(group + hop, groups),
                )
                copy.start()
                out.append(copy)
            return out

        far = pass_on(slot, me, 0)
        eager = -(-parts // 2)
        yield
        for step in range(1, parts):
            copies[step - 1].wait_recv()
            origin = lax.rem(me - step + parts, parts)
            far += pass_on(dst.at[group, origin], origin, step)
            if step % eager == 0:
                yield
        for at, copy in enumerate(far):
            copy.wait()
            if at % 6 == 5:
                yield
        for copy in copies:
            copy.wait_send()


class Sum:
    outside = ()

    def __init__(self, groups, shape):
        self.groups = groups
        self.out = jax.ShapeDtypeStruct(shape, jnp.float32)
        self.scratch = [
            pltpu.VMEM((groups - 1,) + shape, LOW),
            pltpu.SemaphoreType.DMA((groups - 1,)),
            pltpu.SemaphoreType.DMA((groups - 1,)),
        ]

    def run(self, src, out, far, send, recv):
        groups = self.groups
        group = lax.axis_index("fsdp")
        copies = []
        for hop in range(1, groups):
            peer = lax.rem(group + hop, groups)
            copies.append(
                remote(
                    src.at[peer], far.at[hop - 1], send.at[hop - 1], recv.at[hop - 1], "fsdp", peer
                )
            )
            copies[-1].start()
        for _ in range(8):
            yield
        for copy in copies:
            copy.wait_recv()
        value = src[group].astype(jnp.float32)
        for hop in range(groups - 1):
            value += far[hop].astype(jnp.float32)
        out[...] = value
        for copy in copies:
            copy.wait_send()


class Deliver:
    outside = ("in",)

    def __init__(self, parts, shape, offsets, delay=0, eager=1):
        self.parts, self.shape, self.offsets = parts, shape, offsets
        self.delay, self.eager = delay, eager
        self.out = jax.ShapeDtypeStruct((shape[0], parts * shape[1]), jnp.float32)
        self.scratch = [
            pltpu.VMEM((parts,) + shape, LOW),
            pltpu.SemaphoreType.DMA((parts - 1,)),
            pltpu.SemaphoreType.DMA((parts,)),
        ]

    def place(self, out, origin, read):
        starts = self.offsets(origin)
        step = self.shape[1] // len(starts)
        for index, start in enumerate(starts):
            out[:, pl.ds(pl.multiple_of(start, HEAD_DIM), step)] = read(
                index * step, (index + 1) * step
            )

    def send(self, me, step, block, came, send, recv):
        return remote(
            block,
            came.at[step - 1],
            send.at[step - 1],
            recv.at[step - 1],
            "ctx",
            lax.rem(me + step, self.parts),
        )

    def run(self, src, out, came, send, recv):
        for _ in range(self.delay):
            yield
        me = lax.axis_index("ctx")
        copies = []
        for step in range(1, self.parts):
            block = src.at[lax.rem(me + step, self.parts)]
            copies.append(self.send(me, step, block, came, send, recv))
            copies[-1].start()
        last = self.parts - 1
        own = pltpu.make_async_copy(src.at[me], came.at[last], recv.at[last])
        own.start()
        yield
        own.wait()
        self.place(out, me, lambda lo, hi: came[last, :, lo:hi].astype(jnp.float32))
        yield from self.finish(me, out, copies, came)

    def finish(self, me, out, copies, came):
        for step in range(1, self.parts):
            copies[step - 1].wait_recv()
            origin = lax.rem(me - step + self.parts, self.parts)
            self.place(out, origin, lambda lo, hi: came[step - 1, :, lo:hi].astype(jnp.float32))
            if step % self.eager == 0:
                yield
        for copy in copies:
            copy.wait_send()


class Collect(Deliver):
    outside = ()

    def __init__(self, parts, groups, shape, offsets, delay=0, eager=1):
        super().__init__(parts, shape, offsets, delay, eager)
        self.groups = groups
        self.scratch = self.scratch + [
            pltpu.VMEM((groups - 1, parts) + shape, LOW),
            pltpu.VMEM((parts,) + shape, LOW),
            pltpu.VMEM(shape, jnp.float32),
            pltpu.SemaphoreType.DMA((groups - 1, parts)),
            pltpu.SemaphoreType.DMA((groups - 1, parts)),
        ]

    def run(self, src, out, came, send, recv, far, stage, mine, far_send, far_recv):
        parts, groups = self.parts, self.groups
        me, group = lax.axis_index("ctx"), lax.axis_index("fsdp")
        goals = [lax.rem(me + step, parts) for step in range(1, parts + 1)]
        hops = []
        for goal in goals:
            for hop in range(1, groups):
                peer = lax.rem(group + hop, groups)
                hops.append(
                    remote(
                        src.at[peer, goal],
                        far.at[hop - 1, goal],
                        far_send.at[hop - 1, goal],
                        far_recv.at[hop - 1, goal],
                        "fsdp",
                        peer,
                    )
                )
                hops[-1].start()
        yield
        copies = []
        for step in range(1, parts + 1):
            goal = goals[step - 1]
            for copy in hops[(step - 1) * (groups - 1) : step * (groups - 1)]:
                copy.wait_recv()
            value = src[group, goal].astype(jnp.float32)
            for hop in range(groups - 1):
                value += far[hop, goal].astype(jnp.float32)
            if step < parts:
                stage[goal] = value.astype(LOW)
                copies.append(self.send(me, step, stage.at[goal], came, send, recv))
                copies[-1].start()
            else:
                mine[...] = value
            if step % self.eager == 0:
                yield
        self.place(out, me, lambda lo, hi: mine[:, lo:hi])
        yield from self.finish(me, out, copies, came)
        for copy in hops:
            copy.wait_send()


def product(left, right):
    return jnp.dot(left, right, preferred_element_type=jnp.float32)


class Puts:
    def __init__(self, made, put):
        self.made, self.put, self.copies = made, put, []

    def pair(self, fill, columns, out, at, tile):
        for copy in self.copies:
            copy.wait()
        lax.fori_loop(0, 2, fill, 0)
        self.copies = []
        for half in range(2):
            begin = at + half * tile
            copy = pltpu.make_async_copy(
                self.made.at[half, :, pl.ds(0, columns)],
                out.at[begin : begin + tile, :],
                self.put.at[half],
            )
            copy.start()
            self.copies.append(copy)

    def finish(self):
        for copy in self.copies:
            copy.wait()


def call(jobs, operands, name, identity, axes, work=None, micros=50):
    counts = [len(job.scratch) for job in jobs]
    jobs_n = len(jobs)
    extra = work.operands if work else []
    extra_out = work.outs if work else []
    extra_scratch = work.scratch if work else []

    def kernel(*refs):
        refs = list(refs)

        def take(count):
            taken = refs[:count]
            del refs[:count]
            return taken

        ins, more = take(jobs_n), take(len(extra))
        outs, more_outs = take(jobs_n), take(len(extra_out))
        runs = []
        for job, src, dst, count in zip(jobs, ins, outs, counts):
            runs.append(job.run(src, dst, *take(count)))
        if work:
            runs.append(work.run(*more, *more_outs, *refs))
        enter(axes)
        while runs:
            going = []
            for run in runs:
                try:
                    next(run)
                    going.append(run)
                except StopIteration:
                    pass
            runs = going

    vmem = pl.BlockSpec(memory_space=pltpu.VMEM)
    anywhere = pl.BlockSpec(memory_space=pl.ANY)
    in_specs = [anywhere if "in" in job.outside else vmem for job in jobs]
    out_specs = [anywhere if "out" in job.outside else vmem for job in jobs]
    return pl.pallas_call(
        kernel,
        out_shape=tuple(job.out for job in jobs) + tuple(extra_out),
        in_specs=in_specs + [anywhere] * len(extra),
        out_specs=tuple(out_specs) + (anywhere,) * len(extra_out),
        scratch_shapes=[shape for job in jobs for shape in job.scratch] + list(extra_scratch),
        compiler_params=pltpu.CompilerParams(
            collective_id=identity, has_side_effects=True, vmem_limit_bytes=62 << 20
        ),
        cost_estimate=pl.CostEstimate(
            flops=0, bytes_accessed=micros * 3_000_000, transcendentals=0
        ),
        name=name,
    )(*operands, *extra)


class Grads:
    tile = 256

    def __init__(self, pairs):
        self.pairs = pairs
        length, wide = pairs[0][0].shape[0], max(right.shape[1] for _, right in pairs)
        self.operands = [array for pair in pairs for array in pair]
        self.outs = [jax.ShapeDtypeStruct((l.shape[1], r.shape[1]), LOW) for l, r in pairs]
        self.slots = [[id(array) for array in self.operands].index(id(a)) for a in self.operands]
        self.operands = [a for i, a in enumerate(self.operands) if self.slots[i] == i]
        self.slots = [sorted(set(self.slots)).index(slot) for slot in self.slots]
        self.scratch = [pltpu.VMEM(array.shape, LOW) for array in self.operands]
        self.scratch += [
            pltpu.VMEM((self.tile, length), LOW),
            pltpu.VMEM((2, self.tile, wide), LOW),
            pltpu.SemaphoreType.DMA((len(self.operands),)),
            pltpu.SemaphoreType.DMA((2,)),
        ]

    def run(self, *refs):
        n, tile, count = len(self.pairs), self.tile, len(self.operands)
        sources, outs = refs[:count], refs[count : count + n]
        held = refs[count + n : 2 * count + n]
        turned, made, get, put = refs[2 * count + n :]
        gets = [pltpu.make_async_copy(s, h, get.at[i]) for i, (s, h) in enumerate(zip(sources, held))]
        for copy in gets:
            copy.start()
        yield
        puts = Puts(made, put)
        for which in range(n):
            first, second = self.slots[2 * which : 2 * which + 2]
            left, right, out = held[first], held[second], outs[which]
            for slot in (first, second):
                if slot not in self.slots[: 2 * which]:
                    gets[slot].wait()
            columns = right.shape[1]
            step = min(columns, 512)
            for at in range(0, left.shape[1], 2 * tile):

                def pair(half, carry):
                    begin = pl.multiple_of(at + half * tile, tile)
                    turned[...] = left[:, pl.ds(begin, tile)].T

                    def one(index, carry):
                        where = pl.ds(pl.multiple_of(index * step, step), step)
                        made[half, :, where] = product(turned[...], right[:, where]).astype(LOW)
                        return carry

                    return lax.fori_loop(0, columns // step, one, carry)

                puts.pair(pair, columns, out, at, tile)
                yield
        puts.finish()


def softmax_block(query, keys, ok):
    scores = times_transposed(query, keys) * HEAD_DIM ** (-0.5)
    scores = jnp.where(ok, scores, -1e30)
    weights = jnp.exp(scores - jnp.max(scores, axis=-1, keepdims=True))
    weights = jnp.where(ok, weights, 0.0)
    return weights, jnp.sum(weights, axis=-1, keepdims=True)


class Attend:
    tile = 256

    def __init__(self, rows, weight, tables, heads):
        self.heads = heads
        self.operands = [rows, weight] + list(tables)
        length, wide = rows.shape[0], weight.shape[1]
        self.outs = [
            jax.ShapeDtypeStruct((length, wide), LOW),
            jax.ShapeDtypeStruct((length, wide // 3), LOW),
        ]
        self.scratch = [pltpu.VMEM(array.shape, array.dtype) for array in self.operands]
        self.scratch += [pltpu.VMEM(out.shape, out.dtype) for out in self.outs]
        self.scratch += [
            pltpu.SemaphoreType.DMA((len(self.operands),)),
            pltpu.SemaphoreType.DMA((2,)),
        ]

    def run(self, *refs):
        n, tile, heads = len(self.operands), self.tile, self.heads
        sources, results, held = refs[:n], refs[n : n + 2], refs[n + 2 : 2 * n + 2]
        qkv, mix, get, put = refs[2 * n + 2 :]
        rows, weight, cosine, sine, ends, keys = held
        gets = [pltpu.make_async_copy(s, h, get.at[i]) for i, (s, h) in enumerate(zip(sources, held))]
        for copy in gets:
            copy.start()
        yield
        for copy in gets:
            copy.wait()
        width = heads * HEAD_DIM

        def project(index, carry):
            at = pl.ds(pl.multiple_of(index * tile, tile), tile)
            value = product(rows[at, :], weight[...])
            for head in range(3 * heads):
                block = value[:, head * HEAD_DIM : (head + 1) * HEAD_DIM]
                if head < 2 * heads:
                    turned = pltpu.roll(block, HEAD_DIM // 2, 1)
                    block = block * cosine[at, :] + turned * sine[at, :]
                qkv[at, head * HEAD_DIM : (head + 1) * HEAD_DIM] = block.astype(LOW)
            return carry

        lax.fori_loop(0, rows.shape[0] // tile, project, 0)
        send = pltpu.make_async_copy(qkv, results[0], put.at[0])
        send.start()
        yield

        half = HEAD_DIM // 2

        def attend(index, carry):
            at = pl.ds(pl.multiple_of(index * tile, tile), tile)
            ok = (keys[:1, :] >= ends[at, :1]) & (keys[:1, :] <= ends[at, half : half + 1])
            for head in range(heads):
                lo = head * HEAD_DIM
                weights, total = softmax_block(
                    qkv[at, lo : lo + HEAD_DIM], qkv[:, width + lo : width + lo + HEAD_DIM], ok
                )
                value = qkv[:, 2 * width + lo : 2 * width + lo + HEAD_DIM]
                mixed = product(weights.astype(LOW), value) / total
                mix[at, lo : lo + HEAD_DIM] = mixed.astype(LOW)
            return carry

        lax.fori_loop(0, rows.shape[0] // tile, attend, 0)
        send_mix = pltpu.make_async_copy(mix, results[1], put.at[1])
        send_mix.start()
        yield
        send.wait()
        send_mix.wait()


class AttendBack:
    tile = 256

    def __init__(self, back, qkv, rows, weight, tables, heads):
        self.heads = heads
        self.operands = [back, qkv] + list(tables) + [weight, rows]
        length, wide, width = rows.shape[0], weight.shape[1], rows.shape[1]
        self.outs = [
            jax.ShapeDtypeStruct((length, width), LOW),
            jax.ShapeDtypeStruct((width, wide), LOW),
        ]
        self.scratch = [pltpu.VMEM(array.shape, array.dtype) for array in self.operands]
        self.scratch += [
            pltpu.VMEM((length, wide), LOW),
            pltpu.VMEM((2, length, HEAD_DIM), jnp.float32),
            pltpu.VMEM((self.tile, length), LOW),
            pltpu.VMEM((2, self.tile, width), LOW),
            pltpu.SemaphoreType.DMA((len(self.operands),)),
            pltpu.SemaphoreType.DMA((2,)),
        ]

    def run(self, *refs):
        n, tile, heads = len(self.operands), self.tile, self.heads
        sources, results, held = refs[:n], refs[n : n + 2], refs[n + 2 : 2 * n + 2]
        grads, sums, turned, made, get, put = refs[2 * n + 2 :]
        back, qkv, cosine, sine, ends, keys, weight, rows = held
        length, width = back.shape
        gets = [pltpu.make_async_copy(s, h, get.at[i]) for i, (s, h) in enumerate(zip(sources, held))]
        for copy in gets:
            copy.start()
        yield
        for copy in gets[:-2]:
            copy.wait()

        def unrotated(value, at):
            return value * cosine[at, :] - pltpu.roll(value, HEAD_DIM // 2, 1) * sine[at, :]

        half = HEAD_DIM // 2
        for head in range(heads):
            lo = head * HEAD_DIM
            mine = slice(lo, lo + HEAD_DIM)
            key = slice(width + lo, width + lo + HEAD_DIM)
            val = slice(2 * width + lo, 2 * width + lo + HEAD_DIM)
            sums[...] = jnp.zeros_like(sums)

            def attend(index, carry):
                at = pl.ds(pl.multiple_of(index * tile, tile), tile)
                ok = (keys[:1, :] >= ends[at, :1]) & (keys[:1, :] <= ends[at, half : half + 1])
                weights, total = softmax_block(qkv[at, mine], qkv[:, key], ok)
                probs = weights / total
                upper = back[at, mine]
                prob_back = times_transposed(upper, qkv[:, val])
                delta = jnp.sum(probs * prob_back, axis=-1, keepdims=True)
                score_back = HEAD_DIM ** (-0.5) * probs * (prob_back - delta)
                score_low = score_back.astype(LOW)
                query_back = product(score_low, qkv[:, key])
                grads[at, mine] = unrotated(query_back, at).astype(LOW)
                sums[0] += product(score_low.T, qkv[at, mine])
                sums[1] += product(probs.astype(LOW).T, upper)
                return carry

            lax.fori_loop(0, length // tile, attend, 0)
            yield

            def settle(index, carry):
                at = pl.ds(pl.multiple_of(index * tile, tile), tile)
                grads[at, key] = unrotated(sums[0, at, :], at).astype(LOW)
                grads[at, val] = sums[1, at, :].astype(LOW)
                return carry

            lax.fori_loop(0, length // tile, settle, 0)
        puts = Puts(made, put)
        wide = grads.shape[1]
        part = tile if wide % tile == 0 else HEAD_DIM
        gets[-2].wait()
        for at in range(0, length, 2 * tile):

            def terms(half, carry):
                where = pl.ds(pl.multiple_of(at + half * tile, tile), tile)

                def one(index, carry):
                    span = pl.ds(pl.multiple_of(index * tile, tile), tile)
                    value = times_transposed(grads[where, :], weight[span, :])
                    made[half, :, span] = value.astype(LOW)
                    return carry

                return lax.fori_loop(0, made.shape[2] // tile, one, carry)

            puts.pair(terms, made.shape[2], results[0], at, tile)
            yield
        gets[-1].wait()
        for at in range(0, rows.shape[1], 2 * tile):

            def weights(half, carry):
                where = pl.ds(pl.multiple_of(at + half * tile, tile), tile)
                turned[...] = rows[:, where].T

                def one(index, carry):
                    span = pl.ds(pl.multiple_of(index * part, part), part)
                    made[half, :, span] = product(turned[...], grads[:, span]).astype(LOW)
                    return carry

                return lax.fori_loop(0, wide // part, one, carry)

            puts.pair(weights, wide, results[1], at, tile)
            yield
        puts.finish()


def near_first(chips):
    table = []
    for chip in range(chips):
        order = [chip]
        for step in range(1, chips):
            order += [at for at in (chip + step, chip - step) if 0 <= at < chips]
        table.append(order)
    return table


def next_chip(chips, turn):
    chip = lax.axis_index("ctx") // 2
    return sum(
        jnp.where((chip == at) & (turn == when), order[when], 0)
        for at, order in enumerate(near_first(chips))
        for when in range(chips)
    )


class ProjectBack:
    tile = 256

    def __init__(self, job, activated, down, out_rows, mix):
        self.job = job
        self.operands = [activated, down, out_rows, mix]
        length, heads_width = mix.shape
        width = down.shape[1]
        self.outs = [
            jax.ShapeDtypeStruct((length, width), LOW),
            jax.ShapeDtypeStruct((length, heads_width), LOW),
            jax.ShapeDtypeStruct((heads_width, width), LOW),
        ]
        self.scratch = [pltpu.VMEM(array.shape, array.dtype) for array in self.operands]
        self.scratch += [
            pltpu.VMEM((2, self.tile, width), LOW),
            pltpu.VMEM((length, heads_width), LOW),
            pltpu.VMEM((heads_width, width), jnp.float32),
            pltpu.VMEM((heads_width, width), LOW),
            pltpu.SemaphoreType.DMA((4,)),
            pltpu.SemaphoreType.DMA((2,)),
            pltpu.SemaphoreType.DMA((2,)),
        ]

    def run(self, *refs):
        job, tile = self.job, self.tile
        sources, results, held = refs[:4], refs[4:7], refs[7:11]
        made, back, total, total_low, get, put, leave = refs[11:]
        activated, down, out_rows, mix = held
        length, width = mix.shape[0], down.shape[1]
        gets = [pltpu.make_async_copy(s, h, get.at[i]) for i, (s, h) in enumerate(zip(sources, held))]
        for copy in gets:
            copy.start()
        yield
        for copy in gets:
            copy.wait()
        total[...] = jnp.zeros_like(total)
        puts = Puts(made, put)
        for at in range(0, length, 2 * tile):

            def terms(half, carry):
                where = pl.ds(pl.multiple_of(at + half * tile, tile), tile)

                def one(index, carry):
                    span = pl.ds(pl.multiple_of(index * tile, tile), tile)
                    value = product(activated[where, :], down[:, span])
                    made[half, :, span] = value.astype(LOW)
                    return carry

                return lax.fori_loop(0, width // tile, one, carry)

            puts.pair(terms, width, results[0], at, tile)
        chips = job.parts // 2
        rows = length // chips

        def one_chip(turn, carry):
            origin = next_chip(chips, turn)

            @pl.when(turn > 0)
            def _():
                job.relay(turn)

            job.arrived(origin)
            at = pl.ds(pl.multiple_of(origin * rows, rows), rows)
            block = job.dst.at[pl.ds(2 * origin, 2)]
            value = block[...].reshape(rows, width)
            back[at, :] = times_transposed(value, out_rows[...]).astype(LOW)
            total[...] += product(mix[at, :].T, value)
            return carry

        lax.fori_loop(0, chips, one_chip, 0)
        total_low[...] = total[...].astype(LOW)
        out = [
            pltpu.make_async_copy(back, results[1], leave.at[0]),
            pltpu.make_async_copy(total_low, results[2], leave.at[1]),
        ]
        for copy in out:
            copy.start()
        puts.finish()
        for copy in out:
            copy.wait()


class FeedForward:
    def __init__(self, job, act_grad, gate, up):
        self.job = job
        self.operands = [act_grad, gate, up]
        length = act_grad.shape[0]
        width, units = gate.shape
        self.outs = [
            jax.ShapeDtypeStruct((length, units), LOW),
            jax.ShapeDtypeStruct((length, 2 * units), LOW),
            jax.ShapeDtypeStruct((length, width), LOW),
        ]
        self.tile = length // (job.parts // 2)
        self.scratch = [pltpu.VMEM(array.shape, array.dtype) for array in self.operands]
        self.scratch += [pltpu.VMEM((2, self.tile) + out.shape[1:], LOW) for out in self.outs]
        self.scratch += [pltpu.SemaphoreType.DMA((3,)), pltpu.SemaphoreType.DMA((3, 2))]

    def run(self, *refs):
        job, tile = self.job, self.tile
        sources, results, held, made = refs[:3], refs[3:6], refs[6:9], refs[9:12]
        get, put = refs[12:]
        act_grads, gate_w, up_w = held
        acts, backs, terms = made
        width, units = gate_w.shape
        step = min(units, 256)
        span = min(width, 512)
        gets = [pltpu.make_async_copy(sources[i], held[i], get.at[i]) for i in (1, 2, 0)]
        for copy in gets:
            copy.start()
        yield
        for copy in gets:
            copy.wait()
        chips = job.parts // 2

        def leave(slot, origin):
            at = pl.ds(pl.multiple_of(origin * tile, tile), tile)
            return [
                pltpu.make_async_copy(made[i].at[slot], results[i].at[at, :], put.at[i, slot])
                for i in range(3)
            ]

        def one_chip(turn, carry):
            origin = next_chip(chips, turn)
            slot = lax.rem(turn, 2)

            @pl.when(turn > 0)
            def _():
                job.relay(turn)

            @pl.when(turn >= 2)
            def _():
                for copy in leave(slot, 0):
                    copy.wait()

            job.arrived(origin)
            at = pl.ds(pl.multiple_of(origin * tile, tile), tile)
            normed = job.dst.at[pl.ds(2 * origin, 2)]

            def forward(index, carry):
                left = pl.ds(pl.multiple_of(index * step, step), step)
                right = pl.ds(pl.multiple_of(units + index * step, step), step)
                value = normed[...].reshape(tile, width)
                gate = product(value, gate_w[:, left])
                up = product(value, up_w[:, left])
                act_grad = act_grads[at, left]
                sigmoid = jax.nn.sigmoid(gate)
                silu = gate * sigmoid
                acts[slot, :, left] = (silu * up).astype(LOW)
                gate_grad = act_grad * up * sigmoid * (1.0 + gate * (1.0 - sigmoid))
                backs[slot, :, left] = gate_grad.astype(LOW)
                backs[slot, :, right] = (act_grad * silu).astype(LOW)
                return carry

            lax.fori_loop(0, units // step, forward, 0)

            def backward(index, carry):
                where = pl.ds(pl.multiple_of(index * span, span), span)
                value = times_transposed(backs[slot, :, :units], gate_w[where, :])
                value += times_transposed(backs[slot, :, units:], up_w[where, :])
                terms[slot, :, where] = value.astype(LOW)
                return carry

            lax.fori_loop(0, width // span, backward, 0)
            for copy in leave(slot, origin):
                copy.start()
            return carry

        lax.fori_loop(0, chips, one_chip, 0)
        for slot in range(min(2, chips)):
            for copy in leave(slot, 0):
                copy.wait()


class Plan:
    def __init__(self, parts, groups, width):
        self.parts, self.groups = parts, groups
        self.shard = width // (parts * groups)
        self.run = HEAD_DIM // self.shard
        self.heads = HEADS // parts

    def qkv_starts(self, part):
        at, index = part // self.run, lax.rem(part, self.run)
        return [
            (kind * HEADS + (index * self.heads + head) * (self.parts // self.run) + at) * HEAD_DIM
            for kind in range(3)
            for head in range(self.heads)
        ]

    def unit_source(self, weight, kind):
        rows, columns = weight.shape
        half = columns // 2
        step = half // (self.groups * self.parts)
        if step % HEAD_DIM == 0:
            return weight, lambda part: [
                kind * half + (at * self.parts + part) * step for at in range(self.groups)
            ]
        pieces = weight[:, kind * half : (kind + 1) * half]
        pieces = pieces.reshape(rows, self.groups, self.parts, step).transpose(2, 0, 1, 3)
        return pieces.reshape(self.parts, rows, self.groups * step), None

    def unit_job(self, shape):
        step = shape[1] // (2 * self.groups)
        if step % HEAD_DIM:
            return Exchange(self.parts, shape)
        return Deliver(
            self.parts,
            shape,
            lambda part: [(at * self.parts + part) * step for at in range(2 * self.groups)],
        )

    def unit_rows(self, pieces):
        if pieces.ndim == 2:
            return pieces
        parts, rows, columns = pieces.shape
        outer = 2 * self.groups
        pieces = pieces.reshape(parts, rows, outer, columns // outer).transpose(1, 2, 0, 3)
        return pieces.reshape(rows, parts * columns).astype(jnp.float32)


def per_device(tokens, w_qkv, w_out, w_gate_up, w_down, seq_lengths, block_order, cotangent):
    lengths = seq_lengths[0]
    order_row = block_order[0]
    parts = lax.axis_size("ctx")
    groups = lax.axis_size("fsdp")
    rows, width = tokens.shape
    length = rows * parts
    plan = Plan(parts, groups, width)
    heads, shard, run = plan.heads, plan.shard, plan.run
    head_width = heads * HEAD_DIM
    line = (("ctx", parts),)
    plane = (("ctx", parts), ("fsdp", groups))
    block = (rows, width)

    down_rows = gather(w_down, "fsdp")
    unit_columns = w_gate_up.shape[1] // (2 * parts)
    unit_shape = (w_gate_up.shape[0], unit_columns)
    both_shape = (w_gate_up.shape[0], 2 * unit_columns)
    qkv_shape = (w_qkv.shape[0], 3 * head_width)
    gate_source, gate_starts = plan.unit_source(w_gate_up, 0)
    up_source, up_starts = plan.unit_source(w_gate_up, 1)
    inputs = tokens.astype(jnp.float32)
    normed_in, root_in = normalize(inputs)
    qkv_cols, normed_in_full, gate_cols, out_rows = call(
        [
            Spread(parts, groups, qkv_shape, plan.qkv_starts),
            Gather(parts, block, cuts=1),
            Exchange(parts, unit_shape, 2, gate_starts),
            Fan(groups, w_out.shape),
        ],
        [w_qkv, normed_in.astype(LOW), gate_source, w_out],
        "start",
        2,
        plane,
        micros=90,
    )
    gate_cols = gather(gate_cols.reshape(width // groups, -1), "fsdp")
    qkv_cols = qkv_cols.reshape(width, 3 * head_width)
    normed_in_full = normed_in_full.reshape(length, width)

    row_index = jnp.arange(length, dtype=jnp.int32)
    packed = initial_index(row_index, order_row)
    _, pos = places(packed, lengths)
    cosine_table, sine_table = angle_tables(pos)
    half_sign = jnp.where(jnp.arange(HEAD_DIM) < HEAD_DIM // 2, -1.0, 1.0)
    tables = (
        cosine_table[:, 0, :],
        sine_table[:, 0, :] * half_sign,
        packed[:, None] - jnp.where(jnp.arange(HEAD_DIM) < HEAD_DIM // 2, pos[:, None], 0),
        jnp.broadcast_to(packed[None, :], (8, length)),
    )
    up_cols, out_cols, qkv_low, mix_low = call(
        [
            Exchange(parts, unit_shape, 0, up_starts),
            Exchange(run, (heads, shard, width), second="out"),
        ],
        [up_source, out_rows.reshape(run, heads, shard, width)],
        "attend",
        1,
        line,
        Attend(normed_in_full, qkv_cols, tables, heads),
        micros=40,
    )
    up_cols = gather(up_cols.reshape(width // groups, -1), "fsdp")
    out_cols = out_cols.reshape(head_width, width)

    out_terms = dot(mix_low, out_cols).astype(LOW)
    attn_out, cot_full = call(
        [Scatter(parts, block, cuts=1), Gather(parts, block, cuts=1)],
        [out_terms.reshape((parts,) + block), cotangent],
        "out",
        3,
        line,
        micros=64,
    )
    cot_full = cot_full.reshape(length, width)
    residual = inputs + attn_out
    normed_mid, root_mid = normalize(residual)
    act_grad = times_transposed(cot_full, down_rows)
    mid_job = Gather(parts, block, watched=True)
    normed_mid_full, activated, gate_up_back, mid_back_terms = call(
        [mid_job],
        [normed_mid.astype(LOW)],
        "mid",
        4,
        line,
        FeedForward(mid_job, act_grad, gate_cols, up_cols),
        micros=60,
    )
    normed_mid_full = normed_mid_full.reshape(length, width)
    mid_back, gate_up_grad, down_grad = call(
        [Scatter(parts, block)],
        [mid_back_terms.reshape((parts,) + block)],
        "mid_back",
        5,
        line,
        Grads([(normed_mid_full, gate_up_back), (activated, cot_full)]),
    )
    gate_up_grad = scatter(gate_up_grad, "fsdp")
    down_grad = scatter(down_grad, "fsdp")
    residual_back = cotangent.astype(jnp.float32) + norm_back(mid_back, normed_mid, root_mid)
    proj_back = residual_back.astype(LOW)

    proj_job = Gather(parts, block, watched=True)
    _, down_terms, back_heads, out_grad = call(
        [proj_job],
        [proj_back],
        "proj_back",
        6,
        line,
        ProjectBack(proj_job, activated, down_rows, out_cols, mix_low),
        micros=45,
    )
    down_out, out_grad, in_back_terms, qkv_grad = call(
        [
            Scatter(parts, block),
            Exchange(run, (heads, shard, width), second="in"),
        ],
        [
            down_terms.reshape((parts,) + block),
            out_grad.reshape(heads, run, shard, width),
        ],
        "attend_back",
        8,
        line,
        AttendBack(back_heads, qkv_low, normed_in_full, qkv_cols, tables, heads),
        micros=60,
    )
    layer_out = (residual + down_out).astype(LOW)
    in_back, qkv_grad, gate_up_grad, out_grad = call(
        [
            Scatter(parts, block),
            Collect(parts, groups, qkv_shape, plan.qkv_starts),
            plan.unit_job(both_shape),
            Sum(groups, w_out.shape),
        ],
        [
            in_back_terms.reshape((parts,) + block),
            qkv_grad.reshape((groups, parts) + qkv_shape),
            gate_up_grad.reshape((parts,) + both_shape),
            out_grad.reshape((groups,) + w_out.shape),
        ],
        "in_back",
        7,
        plane,
        micros=90,
    )
    in_back, down_grad = lax.optimization_barrier((in_back, down_grad))
    tokens_grad = residual_back + norm_back(in_back, normed_in, root_in)
    return (
        layer_out,
        tokens_grad,
        qkv_grad,
        out_grad,
        plan.unit_rows(gate_up_grad),
        down_grad.astype(jnp.float32),
    )


def solution(mesh):
    both = P(("fsdp", "ctx"), None)
    one = P("fsdp", None)
    return jax.shard_map(
        per_device,
        mesh=mesh,
        in_specs=(both, both, both, both, both, one, one, both),
        out_specs=(both,) * 6,
        check_vma=False,
    )
```

```python
import jax
import jax.numpy as jnp
from jax import lax
from jax.experimental import pallas as pl
from jax.experimental.pallas import tpu as pltpu
from jax.sharding import PartitionSpec as P

HEADS = 16
HEAD_DIM = 128
BLOCK = 128
LOW = jnp.bfloat16


def normalize(values):
    average = jnp.mean(values, axis=-1, keepdims=True)
    centered = values - average
    variance = jnp.mean(centered * centered, axis=-1, keepdims=True)
    inv_root = lax.rsqrt(variance + 1e-05)
    return (centered * inv_root, inv_root)


def norm_back(upstream, normed, inv_root):
    first_mean = jnp.mean(upstream, axis=-1, keepdims=True)
    second_mean = jnp.mean(upstream * normed, axis=-1, keepdims=True)
    return inv_root * (upstream - first_mean - normed * second_mean)


def places(token_index, lengths):
    seq_ends = jnp.cumsum(lengths)
    sequence = jnp.sum((token_index[:, None] >= seq_ends[None, :]).astype(jnp.int32), axis=1)
    before = jnp.arange(lengths.shape[0], dtype=jnp.int32)
    seq_start = jnp.sum(jnp.where(before[None, :] < sequence[:, None], lengths[None, :], 0), axis=1)
    return (sequence, token_index - seq_start)


def initial_index(row_index, order_row):
    slot_index = row_index // BLOCK
    slot_table = jnp.arange(order_row.shape[0], dtype=jnp.int32)
    picked = jnp.sum(
        jnp.where(slot_table[None, :] == slot_index[:, None], order_row[None, :], 0), axis=1
    )
    return picked * BLOCK + row_index % BLOCK


def angle_tables(position):
    half_dim = HEAD_DIM // 2
    frequency = 10000.0 ** (-jnp.arange(half_dim, dtype=jnp.float32) * 2.0 / HEAD_DIM)
    angle_table = position.astype(jnp.float32)[:, None] * frequency[None, :]
    angle_table = jnp.concatenate([angle_table, angle_table], axis=-1)
    return (jnp.cos(angle_table)[:, None, :], jnp.sin(angle_table)[:, None, :])


def rotate(values, cosine_table, sine_table):
    half_dim = values.shape[-1] // 2
    turned = jnp.concatenate([-values[..., half_dim:], values[..., :half_dim]], axis=-1)
    return values * cosine_table + turned * sine_table


def unrotate(values, cosine_table, sine_table):
    half_dim = values.shape[-1] // 2
    scaled = values * sine_table
    turned = jnp.concatenate([scaled[..., half_dim:], -scaled[..., :half_dim]], axis=-1)
    return values * cosine_table + turned


def dot(left, right):
    return jnp.dot(left, right, preferred_element_type=jnp.float32)


def times_transposed(left, right):
    return lax.dot_general(
        left, right, (((1,), (1,)), ((), ())), preferred_element_type=jnp.float32
    )


def column_product(left, right):
    return lax.dot_general(
        left, right, (((0,), (0,)), ((), ())), preferred_element_type=jnp.float32
    )


def gather(values, axes):
    return lax.all_gather(values, axes, axis=0, tiled=True)


def scatter(values, axes):
    return lax.psum_scatter(values, axes, scatter_dimension=0, tiled=True)


def enter(axes):
    barrier = pltpu.get_barrier_semaphore()
    count = 0
    for axis, size in axes:
        me = lax.axis_index(axis)
        for step in range(1, size):
            pl.semaphore_signal(barrier, inc=1, device_id={axis: lax.rem(me + step, size)})
        count += size - 1
    pl.semaphore_wait(barrier, count)


def remote(src, dst, send, recv, axis, peer):
    return pltpu.make_async_remote_copy(
        src_ref=src, dst_ref=dst, send_sem=send, recv_sem=recv, device_id={axis: peer}
    )


class Exchange:
    def __init__(self, parts, shape, delay=0, columns=None, second=""):
        self.parts, self.delay, self.columns, self.second = parts, delay, columns, second
        self.outside = () if second else ("in", "out")
        placed = shape[:1] + (parts,) + shape[1:] if second == "out" else (parts,) + shape
        self.out = jax.ShapeDtypeStruct(placed, LOW)
        self.scratch = [
            pltpu.SemaphoreType.DMA((parts - 1,)),
            pltpu.SemaphoreType.DMA((parts - 1,)),
            pltpu.SemaphoreType.DMA,
        ]

    def run(self, src, dst, send, recv, local):
        for _ in range(self.delay):
            yield
        place = lax.axis_index("ctx")
        me = lax.rem(place, self.parts)
        slot = dst.at[:, me] if self.second == "out" else dst.at[me]

        def blocks(part):
            if self.second == "in":
                return [(src.at[:, part], slot)]
            return blocks_of(src, part, slot, self.columns)

        copies = []
        for step in range(1, self.parts):
            peer = lax.rem(me + step, self.parts)
            whole = (send.at[step - 1], recv.at[step - 1], "ctx", place - me + peer)
            for block, target in blocks(peer):
                copies.append(remote(block, target, *whole))
                copies[-1].start()
            if self.columns:
                del copies[step - 1 :]
                copies.append(remote(slot, slot, *whole))
        for block, target in blocks(me):
            pltpu.make_async_copy(block, target, local).start()
        yield
        for copy in copies:
            copy.wait()
            yield
        pltpu.make_async_copy(slot, slot, local).wait()


def blocks_of(src, part, slot, columns):
    if columns is None:
        return [(src.at[part], slot)]
    starts = columns(part)
    wide = slot.shape[1] // len(starts)
    return [
        (
            src.at[:, pl.ds(pl.multiple_of(start, HEAD_DIM), wide)],
            slot.at[:, pl.ds(index * wide, wide)],
        )
        for index, start in enumerate(starts)
    ]


class Gather:
    def __init__(self, parts, shape, watched=False, cuts=2):
        self.outside = ("in", "out")
        self.parts, self.watched, self.shape, self.cuts = parts, watched, shape, cuts
        self.out = jax.ShapeDtypeStruct((parts,) + shape, LOW)
        chips = parts // 2
        self.scratch = [
            pltpu.SemaphoreType.DMA((2, chips, self.cuts)),
            pltpu.SemaphoreType.DMA((chips, self.cuts)),
            pltpu.SemaphoreType.DMA((chips, self.cuts)),
            pltpu.SemaphoreType.DMA((chips, self.cuts)),
            pltpu.SemaphoreType.DMA,
        ]
        if watched:
            self.scratch += [pltpu.VMEM(self.out.shape, LOW), pltpu.SemaphoreType.DMA((chips,))]

    def run(self, src, out, send, recv, pair_send, pair_recv, local, *watch):
        dst = watch[0] if self.watched else out
        chips, cuts = self.parts // 2, self.cuts
        rows = self.shape[0] // cuts
        me = lax.axis_index("ctx")
        chip, core = me // 2, lax.rem(me, 2)
        partner = me + 1 - 2 * core

        def piece(block, cut):
            return block.at[pl.ds(cut * rows, rows)]

        def line(block, slot, origin, way, cut):
            return remote(
                piece(block, cut),
                piece(slot, cut),
                send.at[way, origin, cut],
                recv.at[origin, cut],
                "ctx",
                me + 2 - 4 * way,
            )

        def across(block, slot, origin, cut):
            return remote(
                piece(block, cut),
                piece(slot, cut),
                pair_send.at[origin, cut],
                pair_recv.at[origin, cut],
                "ctx",
                partner,
            )

        mine = dst.at[me]
        own = pltpu.make_async_copy(src, mine, local)

        def arrived(origin):
            other = dst.at[2 * origin + 1 - core]
            for cut in range(cuts):
                across(other, other, origin, cut).wait_recv()

            @pl.when(origin == chip)
            def _():
                own.wait()

            if self.watched:
                kept(origin).start()

        def kept(origin):
            rows = pl.ds(2 * origin, 2)
            return pltpu.make_async_copy(dst.at[rows], out.at[rows], watch[1].at[origin])

        def relay(step):
            for cut in range(cuts):
                for way in range(2):
                    origin = chip - step if way == 0 else chip + step

                    @pl.when((origin >= 0) & (origin < chips))
                    def _():
                        slot = dst.at[2 * origin + core]
                        line(slot, slot, origin, way, cut).wait_recv()

                        @pl.when((chip < chips - 1) if way == 0 else (chip > 0))
                        def _():
                            line(slot, slot, origin, way, cut).start()

                        across(slot, slot, origin, cut).start()

        self.dst, self.arrived, self.relay = dst, arrived, relay
        for cut in range(cuts):

            @pl.when(chip < chips - 1)
            def _():
                line(src, mine, chip, 0, cut).start()

            @pl.when(chip > 0)
            def _():
                line(src, mine, chip, 1, cut).start()

        for cut in range(cuts):
            across(src, mine, chip, cut).start()
        own.start()
        yield
        if self.watched:
            yield
        for step in range(1, chips):
            if not self.watched:
                relay(step)
                yield
        for step in range(chips):
            for way in range(2):
                origin = chip - step if way == 0 else chip + step
                ahead = (chip < chips - 1) if way == 0 else (chip > 0)

                @pl.when((origin >= 0) & (origin < chips) & ahead)
                def _():
                    slot = dst.at[2 * origin + core]
                    for cut in range(cuts):
                        line(slot, slot, origin, way, cut).wait_send()

        for origin in range(chips):
            slot = dst.at[2 * origin + core]
            for cut in range(cuts):
                across(slot, slot, origin, cut).wait_send()
            if self.watched:
                kept(origin).wait()
            else:
                arrived(origin)


class Scatter:
    outside = ()

    def __init__(self, parts, shape, cuts=2):
        self.parts, self.shape, self.cuts = parts, shape, cuts
        self.out = jax.ShapeDtypeStruct(shape, jnp.float32)
        chips = parts // 2
        piece = (self.cuts, shape[0] // self.cuts, shape[1])
        self.scratch = [
            pltpu.VMEM((chips,) + shape, LOW),
            pltpu.VMEM((2, chips) + piece, LOW),
            pltpu.VMEM((chips,) + piece, LOW),
            pltpu.SemaphoreType.DMA((chips,)),
            pltpu.SemaphoreType.DMA((chips,)),
            pltpu.SemaphoreType.DMA((chips, self.cuts)),
            pltpu.SemaphoreType.DMA((2, chips, self.cuts)),
        ]

    def run(self, src, out, pair, come, stage, pair_send, pair_recv, send, recv):
        chips, cuts = self.parts // 2, self.cuts
        me = lax.axis_index("ctx")
        chip, core = me // 2, lax.rem(me, 2)
        partner = me + 1 - 2 * core
        rows = self.shape[0] // cuts
        slab = min(rows, 16)
        last = chips - 1

        def across(goal):
            return remote(
                src.at[2 * goal + 1 - core],
                pair.at[goal],
                pair_send.at[goal],
                pair_recv.at[goal],
                "ctx",
                partner,
            )

        def line(goal, cut, way):
            return remote(
                stage.at[goal, cut],
                come.at[way, goal, cut],
                send.at[goal, cut],
                recv.at[way, goal, cut],
                "ctx",
                me + 2 - 4 * way,
            )

        def wide(ref, *index):
            return ref[index].astype(jnp.float32)

        def slabs(part):
            def one(index, carry):
                part(pl.multiple_of(index * slab, slab))
                return carry

            lax.fori_loop(0, rows // slab, one, 0)

        def both(goal, cut, at):
            at = pl.ds(cut * rows + at, slab)
            return wide(src, 2 * goal + core, at) + wide(pair, goal, at)

        order = []
        for step in range((chips + 1) // 2):
            order += sorted({step, last - step})
        for goal in order:
            across(goal).start()
        yield
        for step in range(last * cuts):
            for way in range(2):
                turn = step - (chip if way == 0 else last - chip)
                goal = (last - turn // cuts) if way == 0 else turn // cuts
                cut = step - (chip if way == 0 else last - chip) - (turn // cuts) * cuts
                first = (chip == 0) if way == 0 else (chip == last)
                ahead = last - chip if way == 0 else chip

                def begin(at):
                    value = both(goal, cut, at)
                    stage[goal, cut, pl.ds(at, slab), :] = value.astype(LOW)

                def middle(at):
                    value = both(goal, cut, at) + wide(come, way, goal, cut, pl.ds(at, slab))
                    stage[goal, cut, pl.ds(at, slab), :] = value.astype(LOW)

                @pl.when((turn >= 0) & (turn < ahead * cuts))
                def _():
                    @pl.when(cut == 0)
                    def _():
                        across(goal).wait_recv()

                    @pl.when(first)
                    def _():
                        slabs(begin)

                    @pl.when(jnp.logical_not(first))
                    def _():
                        line(goal, cut, way).wait_recv()
                        slabs(middle)

                    line(goal, cut, way).start()

            yield
        across(chip).wait_recv()
        for cut in range(cuts):

            def own(at):
                out[pl.ds(cut * rows + at, slab), :] = both(chip, cut, at)

            slabs(own)
        yield
        for cut in range(cuts):
            for way in range(2):

                def final(at):
                    out[pl.ds(cut * rows + at, slab), :] += wide(
                        come, way, chip, cut, pl.ds(at, slab)
                    )

                @pl.when((chip > 0) if way == 0 else (chip < last))
                def _():
                    line(chip, cut, way).wait_recv()
                    slabs(final)

            yield
        for goal in range(chips):
            across(goal).wait_send()

            @pl.when(chip != goal)
            def _():
                for cut in range(cuts):
                    line(goal, cut, 0).wait_send()


class Fan:
    outside = ("in", "out")

    def __init__(self, groups, shape):
        self.groups = groups
        self.out = jax.ShapeDtypeStruct((groups,) + shape, LOW)
        self.scratch = [
            pltpu.SemaphoreType.DMA((groups - 1,)),
            pltpu.SemaphoreType.DMA((groups - 1,)),
            pltpu.SemaphoreType.DMA,
        ]

    def run(self, src, dst, send, recv, local):
        groups = self.groups
        group = lax.axis_index("fsdp")
        copies = []
        for hop in range(1, groups):
            peer = lax.rem(group + hop, groups)
            copies.append(
                remote(src, dst.at[group], send.at[hop - 1], recv.at[hop - 1], "fsdp", peer)
            )
            copies[-1].start()
        own = pltpu.make_async_copy(src, dst.at[group], local)
        own.start()
        yield
        yield
        yield
        for copy in copies:
            copy.wait()
        own.wait()


class Spread:
    outside = ("in", "out")

    def __init__(self, parts, groups, shape, columns=None):
        self.parts, self.groups, self.columns = parts, groups, columns
        self.out = jax.ShapeDtypeStruct((groups, parts) + shape, LOW)
        self.scratch = [
            pltpu.SemaphoreType.DMA((parts - 1,)),
            pltpu.SemaphoreType.DMA((parts - 1,)),
            pltpu.SemaphoreType.DMA((groups - 1, parts)),
            pltpu.SemaphoreType.DMA((groups - 1, parts)),
            pltpu.SemaphoreType.DMA,
        ]

    def run(self, src, dst, send, recv, far_send, far_recv, local):
        parts, groups = self.parts, self.groups
        me, group = lax.axis_index("ctx"), lax.axis_index("fsdp")
        slot = dst.at[group, me]
        for block, target in blocks_of(src, me, slot, self.columns):
            pltpu.make_async_copy(block, target, local).start()
        copies = []
        for step in range(1, parts):
            peer = lax.rem(me + step, parts)
            whole = (send.at[step - 1], recv.at[step - 1], "ctx", peer)
            for block, target in blocks_of(src, peer, slot, self.columns):
                remote(block, target, *whole).start()
            copies.append(remote(slot, slot, *whole))
        pltpu.make_async_copy(slot, slot, local).wait()

        def pass_on(block, origin, step):
            out = []
            for hop in range(1, groups):
                copy = remote(
                    block,
                    dst.at[group, origin],
                    far_send.at[hop - 1, step],
                    far_recv.at[hop - 1, step],
                    "fsdp",
                    lax.rem(group + hop, groups),
                )
                copy.start()
                out.append(copy)
            return out

        far = pass_on(slot, me, 0)
        eager = -(-parts // 2)
        yield
        for step in range(1, parts):
            copies[step - 1].wait_recv()
            origin = lax.rem(me - step + parts, parts)
            far += pass_on(dst.at[group, origin], origin, step)
            if step % eager == 0:
                yield
        for at, copy in enumerate(far):
            copy.wait()
            if at % 6 == 5:
                yield
        for copy in copies:
            copy.wait_send()


class Sum:
    outside = ()

    def __init__(self, groups, shape):
        self.groups = groups
        self.out = jax.ShapeDtypeStruct(shape, jnp.float32)
        self.scratch = [
            pltpu.VMEM((groups - 1,) + shape, LOW),
            pltpu.SemaphoreType.DMA((groups - 1,)),
            pltpu.SemaphoreType.DMA((groups - 1,)),
        ]

    def run(self, src, out, far, send, recv):
        groups = self.groups
        group = lax.axis_index("fsdp")
        copies = []
        for hop in range(1, groups):
            peer = lax.rem(group + hop, groups)
            copies.append(
                remote(
                    src.at[peer], far.at[hop - 1], send.at[hop - 1], recv.at[hop - 1], "fsdp", peer
                )
            )
            copies[-1].start()
        for _ in range(8):
            yield
        for copy in copies:
            copy.wait_recv()
        value = src[group].astype(jnp.float32)
        for hop in range(groups - 1):
            value += far[hop].astype(jnp.float32)
        out[...] = value
        for copy in copies:
            copy.wait_send()


class Deliver:
    outside = ("in",)

    def __init__(self, parts, shape, offsets, delay=0, eager=1):
        self.parts, self.shape, self.offsets = parts, shape, offsets
        self.delay, self.eager = delay, eager
        self.out = jax.ShapeDtypeStruct((shape[0], parts * shape[1]), jnp.float32)
        self.scratch = [
            pltpu.VMEM((parts,) + shape, LOW),
            pltpu.SemaphoreType.DMA((parts - 1,)),
            pltpu.SemaphoreType.DMA((parts,)),
        ]

    def place(self, out, origin, read):
        starts = self.offsets(origin)
        step = self.shape[1] // len(starts)
        for index, start in enumerate(starts):
            out[:, pl.ds(pl.multiple_of(start, HEAD_DIM), step)] = read(
                index * step, (index + 1) * step
            )

    def send(self, me, step, block, came, send, recv):
        return remote(
            block,
            came.at[step - 1],
            send.at[step - 1],
            recv.at[step - 1],
            "ctx",
            lax.rem(me + step, self.parts),
        )

    def run(self, src, out, came, send, recv):
        for _ in range(self.delay):
            yield
        me = lax.axis_index("ctx")
        copies = []
        for step in range(1, self.parts):
            block = src.at[lax.rem(me + step, self.parts)]
            copies.append(self.send(me, step, block, came, send, recv))
            copies[-1].start()
        last = self.parts - 1
        own = pltpu.make_async_copy(src.at[me], came.at[last], recv.at[last])
        own.start()
        yield
        own.wait()
        self.place(out, me, lambda lo, hi: came[last, :, lo:hi].astype(jnp.float32))
        yield from self.finish(me, out, copies, came)

    def finish(self, me, out, copies, came):
        for step in range(1, self.parts):
            copies[step - 1].wait_recv()
            origin = lax.rem(me - step + self.parts, self.parts)
            self.place(out, origin, lambda lo, hi: came[step - 1, :, lo:hi].astype(jnp.float32))
            if step % self.eager == 0:
                yield
        for copy in copies:
            copy.wait_send()


class Collect(Deliver):
    outside = ()

    def __init__(self, parts, groups, shape, offsets, delay=0, eager=1):
        super().__init__(parts, shape, offsets, delay, eager)
        self.groups = groups
        self.scratch = self.scratch + [
            pltpu.VMEM((groups - 1, parts) + shape, LOW),
            pltpu.VMEM((parts,) + shape, LOW),
            pltpu.VMEM(shape, jnp.float32),
            pltpu.SemaphoreType.DMA((groups - 1, parts)),
            pltpu.SemaphoreType.DMA((groups - 1, parts)),
        ]

    def run(self, src, out, came, send, recv, far, stage, mine, far_send, far_recv):
        parts, groups = self.parts, self.groups
        me, group = lax.axis_index("ctx"), lax.axis_index("fsdp")
        goals = [lax.rem(me + step, parts) for step in range(1, parts + 1)]
        hops = []
        for goal in goals:
            for hop in range(1, groups):
                peer = lax.rem(group + hop, groups)
                hops.append(
                    remote(
                        src.at[peer, goal],
                        far.at[hop - 1, goal],
                        far_send.at[hop - 1, goal],
                        far_recv.at[hop - 1, goal],
                        "fsdp",
                        peer,
                    )
                )
                hops[-1].start()
        yield
        copies = []
        for step in range(1, parts + 1):
            goal = goals[step - 1]
            for copy in hops[(step - 1) * (groups - 1) : step * (groups - 1)]:
                copy.wait_recv()
            value = src[group, goal].astype(jnp.float32)
            for hop in range(groups - 1):
                value += far[hop, goal].astype(jnp.float32)
            if step < parts:
                stage[goal] = value.astype(LOW)
                copies.append(self.send(me, step, stage.at[goal], came, send, recv))
                copies[-1].start()
            else:
                mine[...] = value
            if step % self.eager == 0:
                yield
        self.place(out, me, lambda lo, hi: mine[:, lo:hi])
        yield from self.finish(me, out, copies, came)
        for copy in hops:
            copy.wait_send()


def product(left, right):
    return jnp.dot(left, right, preferred_element_type=jnp.float32)


class Puts:
    def __init__(self, made, put):
        self.made, self.put, self.copies = made, put, []

    def pair(self, fill, columns, out, at, tile):
        for copy in self.copies:
            copy.wait()
        lax.fori_loop(0, 2, fill, 0)
        self.copies = []
        for half in range(2):
            begin = at + half * tile
            copy = pltpu.make_async_copy(
                self.made.at[half, :, pl.ds(0, columns)],
                out.at[begin : begin + tile, :],
                self.put.at[half],
            )
            copy.start()
            self.copies.append(copy)

    def finish(self):
        for copy in self.copies:
            copy.wait()


def call(jobs, operands, name, identity, axes, work=None, micros=50):
    counts = [len(job.scratch) for job in jobs]
    jobs_n = len(jobs)
    extra = work.operands if work else []
    extra_out = work.outs if work else []
    extra_scratch = work.scratch if work else []

    def kernel(*refs):
        refs = list(refs)

        def take(count):
            taken = refs[:count]
            del refs[:count]
            return taken

        ins, more = take(jobs_n), take(len(extra))
        outs, more_outs = take(jobs_n), take(len(extra_out))
        runs = []
        for job, src, dst, count in zip(jobs, ins, outs, counts):
            runs.append(job.run(src, dst, *take(count)))
        if work:
            runs.append(work.run(*more, *more_outs, *refs))
        enter(axes)
        while runs:
            going = []
            for run in runs:
                try:
                    next(run)
                    going.append(run)
                except StopIteration:
                    pass
            runs = going

    vmem = pl.BlockSpec(memory_space=pltpu.VMEM)
    anywhere = pl.BlockSpec(memory_space=pl.ANY)
    in_specs = [anywhere if "in" in job.outside else vmem for job in jobs]
    out_specs = [anywhere if "out" in job.outside else vmem for job in jobs]
    return pl.pallas_call(
        kernel,
        out_shape=tuple(job.out for job in jobs) + tuple(extra_out),
        in_specs=in_specs + [anywhere] * len(extra),
        out_specs=tuple(out_specs) + (anywhere,) * len(extra_out),
        scratch_shapes=[shape for job in jobs for shape in job.scratch] + list(extra_scratch),
        compiler_params=pltpu.CompilerParams(
            collective_id=identity, has_side_effects=True, vmem_limit_bytes=62 << 20
        ),
        cost_estimate=pl.CostEstimate(
            flops=0, bytes_accessed=micros * 3_000_000, transcendentals=0
        ),
        name=name,
    )(*operands, *extra)


class Grads:
    tile = 256

    def __init__(self, pairs):
        self.pairs = pairs
        length, wide = pairs[0][0].shape[0], max(right.shape[1] for _, right in pairs)
        self.operands = [array for pair in pairs for array in pair]
        self.outs = [jax.ShapeDtypeStruct((l.shape[1], r.shape[1]), LOW) for l, r in pairs]
        self.slots = [[id(array) for array in self.operands].index(id(a)) for a in self.operands]
        self.operands = [a for i, a in enumerate(self.operands) if self.slots[i] == i]
        self.slots = [sorted(set(self.slots)).index(slot) for slot in self.slots]
        self.scratch = [pltpu.VMEM(array.shape, LOW) for array in self.operands]
        self.scratch += [
            pltpu.VMEM((self.tile, length), LOW),
            pltpu.VMEM((2, self.tile, wide), LOW),
            pltpu.SemaphoreType.DMA((len(self.operands),)),
            pltpu.SemaphoreType.DMA((2,)),
        ]

    def run(self, *refs):
        n, tile, count = len(self.pairs), self.tile, len(self.operands)
        sources, outs = refs[:count], refs[count : count + n]
        held = refs[count + n : 2 * count + n]
        turned, made, get, put = refs[2 * count + n :]
        gets = [pltpu.make_async_copy(s, h, get.at[i]) for i, (s, h) in enumerate(zip(sources, held))]
        for copy in gets:
            copy.start()
        yield
        puts = Puts(made, put)
        for which in range(n):
            first, second = self.slots[2 * which : 2 * which + 2]
            left, right, out = held[first], held[second], outs[which]
            for slot in (first, second):
                if slot not in self.slots[: 2 * which]:
                    gets[slot].wait()
            columns = right.shape[1]
            step = min(columns, 512)
            for at in range(0, left.shape[1], 2 * tile):

                def pair(half, carry):
                    begin = pl.multiple_of(at + half * tile, tile)
                    turned[...] = left[:, pl.ds(begin, tile)].T

                    def one(index, carry):
                        where = pl.ds(pl.multiple_of(index * step, step), step)
                        made[half, :, where] = product(turned[...], right[:, where]).astype(LOW)
                        return carry

                    return lax.fori_loop(0, columns // step, one, carry)

                puts.pair(pair, columns, out, at, tile)
                yield
        puts.finish()


def softmax_block(query, keys, ok):
    scores = times_transposed(query, keys) * HEAD_DIM ** (-0.5)
    scores = jnp.where(ok, scores, -1e30)
    weights = jnp.exp(scores - jnp.max(scores, axis=-1, keepdims=True))
    weights = jnp.where(ok, weights, 0.0)
    return weights, jnp.sum(weights, axis=-1, keepdims=True)


class Attend:
    tile = 256

    def __init__(self, rows, weight, tables, heads):
        self.heads = heads
        self.operands = [rows, weight] + list(tables)
        length, wide = rows.shape[0], weight.shape[1]
        self.outs = [
            jax.ShapeDtypeStruct((length, wide), LOW),
            jax.ShapeDtypeStruct((length, wide // 3), LOW),
        ]
        self.scratch = [pltpu.VMEM(array.shape, array.dtype) for array in self.operands]
        self.scratch += [pltpu.VMEM(out.shape, out.dtype) for out in self.outs]
        self.scratch += [
            pltpu.SemaphoreType.DMA((len(self.operands),)),
            pltpu.SemaphoreType.DMA((2,)),
        ]

    def run(self, *refs):
        n, tile, heads = len(self.operands), self.tile, self.heads
        sources, results, held = refs[:n], refs[n : n + 2], refs[n + 2 : 2 * n + 2]
        qkv, mix, get, put = refs[2 * n + 2 :]
        rows, weight, cosine, sine, ends, keys = held
        gets = [pltpu.make_async_copy(s, h, get.at[i]) for i, (s, h) in enumerate(zip(sources, held))]
        for copy in gets:
            copy.start()
        yield
        for copy in gets:
            copy.wait()
        width = heads * HEAD_DIM

        def project(index, carry):
            at = pl.ds(pl.multiple_of(index * tile, tile), tile)
            value = product(rows[at, :], weight[...])
            for head in range(3 * heads):
                block = value[:, head * HEAD_DIM : (head + 1) * HEAD_DIM]
                if head < 2 * heads:
                    turned = pltpu.roll(block, HEAD_DIM // 2, 1)
                    block = block * cosine[at, :] + turned * sine[at, :]
                qkv[at, head * HEAD_DIM : (head + 1) * HEAD_DIM] = block.astype(LOW)
            return carry

        lax.fori_loop(0, rows.shape[0] // tile, project, 0)
        send = pltpu.make_async_copy(qkv, results[0], put.at[0])
        send.start()
        yield

        half = HEAD_DIM // 2

        def attend(index, carry):
            at = pl.ds(pl.multiple_of(index * tile, tile), tile)
            ok = (keys[:1, :] >= ends[at, :1]) & (keys[:1, :] <= ends[at, half : half + 1])
            for head in range(heads):
                lo = head * HEAD_DIM
                weights, total = softmax_block(
                    qkv[at, lo : lo + HEAD_DIM], qkv[:, width + lo : width + lo + HEAD_DIM], ok
                )
                value = qkv[:, 2 * width + lo : 2 * width + lo + HEAD_DIM]
                mixed = product(weights.astype(LOW), value) / total
                mix[at, lo : lo + HEAD_DIM] = mixed.astype(LOW)
            return carry

        lax.fori_loop(0, rows.shape[0] // tile, attend, 0)
        send_mix = pltpu.make_async_copy(mix, results[1], put.at[1])
        send_mix.start()
        yield
        send.wait()
        send_mix.wait()


class AttendBack:
    tile = 256

    def __init__(self, back, qkv, rows, weight, tables, heads):
        self.heads = heads
        self.operands = [back, qkv] + list(tables) + [weight, rows]
        length, wide, width = rows.shape[0], weight.shape[1], rows.shape[1]
        self.outs = [
            jax.ShapeDtypeStruct((length, width), LOW),
            jax.ShapeDtypeStruct((width, wide), LOW),
        ]
        self.scratch = [pltpu.VMEM(array.shape, array.dtype) for array in self.operands]
        self.scratch += [
            pltpu.VMEM((length, wide), LOW),
            pltpu.VMEM((2, length, HEAD_DIM), jnp.float32),
            pltpu.VMEM((self.tile, length), LOW),
            pltpu.VMEM((2, self.tile, width), LOW),
            pltpu.SemaphoreType.DMA((len(self.operands),)),
            pltpu.SemaphoreType.DMA((2,)),
        ]

    def run(self, *refs):
        n, tile, heads = len(self.operands), self.tile, self.heads
        sources, results, held = refs[:n], refs[n : n + 2], refs[n + 2 : 2 * n + 2]
        grads, sums, turned, made, get, put = refs[2 * n + 2 :]
        back, qkv, cosine, sine, ends, keys, weight, rows = held
        length, width = back.shape
        gets = [pltpu.make_async_copy(s, h, get.at[i]) for i, (s, h) in enumerate(zip(sources, held))]
        for copy in gets:
            copy.start()
        yield
        for copy in gets[:-2]:
            copy.wait()

        def unrotated(value, at):
            return value * cosine[at, :] - pltpu.roll(value, HEAD_DIM // 2, 1) * sine[at, :]

        half = HEAD_DIM // 2
        for head in range(heads):
            lo = head * HEAD_DIM
            mine = slice(lo, lo + HEAD_DIM)
            key = slice(width + lo, width + lo + HEAD_DIM)
            val = slice(2 * width + lo, 2 * width + lo + HEAD_DIM)
            sums[...] = jnp.zeros_like(sums)

            def attend(index, carry):
                at = pl.ds(pl.multiple_of(index * tile, tile), tile)
                ok = (keys[:1, :] >= ends[at, :1]) & (keys[:1, :] <= ends[at, half : half + 1])
                weights, total = softmax_block(qkv[at, mine], qkv[:, key], ok)
                probs = weights / total
                upper = back[at, mine]
                prob_back = times_transposed(upper, qkv[:, val])
                delta = jnp.sum(probs * prob_back, axis=-1, keepdims=True)
                score_back = HEAD_DIM ** (-0.5) * probs * (prob_back - delta)
                score_low = score_back.astype(LOW)
                query_back = product(score_low, qkv[:, key])
                grads[at, mine] = unrotated(query_back, at).astype(LOW)
                sums[0] += product(score_low.T, qkv[at, mine])
                sums[1] += product(probs.astype(LOW).T, upper)
                return carry

            lax.fori_loop(0, length // tile, attend, 0)
            yield

            def settle(index, carry):
                at = pl.ds(pl.multiple_of(index * tile, tile), tile)
                grads[at, key] = unrotated(sums[0, at, :], at).astype(LOW)
                grads[at, val] = sums[1, at, :].astype(LOW)
                return carry

            lax.fori_loop(0, length // tile, settle, 0)
        puts = Puts(made, put)
        wide = grads.shape[1]
        part = tile if wide % tile == 0 else HEAD_DIM
        gets[-2].wait()
        for at in range(0, length, 2 * tile):

            def terms(half, carry):
                where = pl.ds(pl.multiple_of(at + half * tile, tile), tile)

                def one(index, carry):
                    span = pl.ds(pl.multiple_of(index * tile, tile), tile)
                    value = times_transposed(grads[where, :], weight[span, :])
                    made[half, :, span] = value.astype(LOW)
                    return carry

                return lax.fori_loop(0, made.shape[2] // tile, one, carry)

            puts.pair(terms, made.shape[2], results[0], at, tile)
            yield
        gets[-1].wait()
        for at in range(0, rows.shape[1], 2 * tile):

            def weights(half, carry):
                where = pl.ds(pl.multiple_of(at + half * tile, tile), tile)
                turned[...] = rows[:, where].T

                def one(index, carry):
                    span = pl.ds(pl.multiple_of(index * part, part), part)
                    made[half, :, span] = product(turned[...], grads[:, span]).astype(LOW)
                    return carry

                return lax.fori_loop(0, wide // part, one, carry)

            puts.pair(weights, wide, results[1], at, tile)
            yield
        puts.finish()


def near_first(chips):
    table = []
    for chip in range(chips):
        order = [chip]
        for step in range(1, chips):
            order += [at for at in (chip + step, chip - step) if 0 <= at < chips]
        table.append(order)
    return table


def next_chip(chips, turn):
    chip = lax.axis_index("ctx") // 2
    return sum(
        jnp.where((chip == at) & (turn == when), order[when], 0)
        for at, order in enumerate(near_first(chips))
        for when in range(chips)
    )


class ProjectBack:
    tile = 256

    def __init__(self, job, activated, down, out_rows, mix):
        self.job = job
        self.operands = [activated, down, out_rows, mix]
        length, heads_width = mix.shape
        width = down.shape[1]
        self.outs = [
            jax.ShapeDtypeStruct((length, width), LOW),
            jax.ShapeDtypeStruct((length, heads_width), LOW),
            jax.ShapeDtypeStruct((heads_width, width), LOW),
        ]
        self.scratch = [pltpu.VMEM(array.shape, array.dtype) for array in self.operands]
        self.scratch += [
            pltpu.VMEM((2, self.tile, width), LOW),
            pltpu.VMEM((length, heads_width), LOW),
            pltpu.VMEM((heads_width, width), jnp.float32),
            pltpu.VMEM((heads_width, width), LOW),
            pltpu.SemaphoreType.DMA((4,)),
            pltpu.SemaphoreType.DMA((2,)),
            pltpu.SemaphoreType.DMA((2,)),
        ]

    def run(self, *refs):
        job, tile = self.job, self.tile
        sources, results, held = refs[:4], refs[4:7], refs[7:11]
        made, back, total, total_low, get, put, leave = refs[11:]
        activated, down, out_rows, mix = held
        length, width = mix.shape[0], down.shape[1]
        gets = [pltpu.make_async_copy(s, h, get.at[i]) for i, (s, h) in enumerate(zip(sources, held))]
        for copy in gets:
            copy.start()
        yield
        for copy in gets:
            copy.wait()
        total[...] = jnp.zeros_like(total)
        puts = Puts(made, put)
        for at in range(0, length, 2 * tile):

            def terms(half, carry):
                where = pl.ds(pl.multiple_of(at + half * tile, tile), tile)

                def one(index, carry):
                    span = pl.ds(pl.multiple_of(index * tile, tile), tile)
                    value = product(activated[where, :], down[:, span])
                    made[half, :, span] = value.astype(LOW)
                    return carry

                return lax.fori_loop(0, width // tile, one, carry)

            puts.pair(terms, width, results[0], at, tile)
        chips = job.parts // 2
        rows = length // chips

        def one_chip(turn, carry):
            origin = next_chip(chips, turn)

            @pl.when(turn > 0)
            def _():
                job.relay(turn)

            job.arrived(origin)
            at = pl.ds(pl.multiple_of(origin * rows, rows), rows)
            block = job.dst.at[pl.ds(2 * origin, 2)]
            value = block[...].reshape(rows, width)
            back[at, :] = times_transposed(value, out_rows[...]).astype(LOW)
            total[...] += product(mix[at, :].T, value)
            return carry

        lax.fori_loop(0, chips, one_chip, 0)
        total_low[...] = total[...].astype(LOW)
        out = [
            pltpu.make_async_copy(back, results[1], leave.at[0]),
            pltpu.make_async_copy(total_low, results[2], leave.at[1]),
        ]
        for copy in out:
            copy.start()
        puts.finish()
        for copy in out:
            copy.wait()


class FeedForward:
    def __init__(self, job, act_grad, gate, up):
        self.job = job
        self.operands = [act_grad, gate, up]
        length = act_grad.shape[0]
        width, units = gate.shape
        self.outs = [
            jax.ShapeDtypeStruct((length, units), LOW),
            jax.ShapeDtypeStruct((length, 2 * units), LOW),
            jax.ShapeDtypeStruct((length, width), LOW),
        ]
        self.tile = length // (job.parts // 2)
        self.scratch = [pltpu.VMEM(array.shape, array.dtype) for array in self.operands]
        self.scratch += [pltpu.VMEM((2, self.tile) + out.shape[1:], LOW) for out in self.outs]
        self.scratch += [pltpu.SemaphoreType.DMA((3,)), pltpu.SemaphoreType.DMA((3, 2))]

    def run(self, *refs):
        job, tile = self.job, self.tile
        sources, results, held, made = refs[:3], refs[3:6], refs[6:9], refs[9:12]
        get, put = refs[12:]
        act_grads, gate_w, up_w = held
        acts, backs, terms = made
        width, units = gate_w.shape
        step = min(units, 256)
        span = min(width, 512)
        gets = [pltpu.make_async_copy(sources[i], held[i], get.at[i]) for i in (1, 2, 0)]
        for copy in gets:
            copy.start()
        yield
        for copy in gets:
            copy.wait()
        chips = job.parts // 2

        def leave(slot, origin):
            at = pl.ds(pl.multiple_of(origin * tile, tile), tile)
            return [
                pltpu.make_async_copy(made[i].at[slot], results[i].at[at, :], put.at[i, slot])
                for i in range(3)
            ]

        def one_chip(turn, carry):
            origin = next_chip(chips, turn)
            slot = lax.rem(turn, 2)

            @pl.when(turn > 0)
            def _():
                job.relay(turn)

            @pl.when(turn >= 2)
            def _():
                for copy in leave(slot, 0):
                    copy.wait()

            job.arrived(origin)
            at = pl.ds(pl.multiple_of(origin * tile, tile), tile)
            normed = job.dst.at[pl.ds(2 * origin, 2)]

            def forward(index, carry):
                left = pl.ds(pl.multiple_of(index * step, step), step)
                right = pl.ds(pl.multiple_of(units + index * step, step), step)
                value = normed[...].reshape(tile, width)
                gate = product(value, gate_w[:, left])
                up = product(value, up_w[:, left])
                act_grad = act_grads[at, left]
                sigmoid = jax.nn.sigmoid(gate)
                silu = gate * sigmoid
                acts[slot, :, left] = (silu * up).astype(LOW)
                gate_grad = act_grad * up * sigmoid * (1.0 + gate * (1.0 - sigmoid))
                backs[slot, :, left] = gate_grad.astype(LOW)
                backs[slot, :, right] = (act_grad * silu).astype(LOW)
                return carry

            lax.fori_loop(0, units // step, forward, 0)

            def backward(index, carry):
                where = pl.ds(pl.multiple_of(index * span, span), span)
                value = times_transposed(backs[slot, :, :units], gate_w[where, :])
                value += times_transposed(backs[slot, :, units:], up_w[where, :])
                terms[slot, :, where] = value.astype(LOW)
                return carry

            lax.fori_loop(0, width // span, backward, 0)
            for copy in leave(slot, origin):
                copy.start()
            return carry

        lax.fori_loop(0, chips, one_chip, 0)
        for slot in range(min(2, chips)):
            for copy in leave(slot, 0):
                copy.wait()


class Plan:
    def __init__(self, parts, groups, width):
        self.parts, self.groups = parts, groups
        self.shard = width // (parts * groups)
        self.run = HEAD_DIM // self.shard
        self.heads = HEADS // parts

    def qkv_starts(self, part):
        at, index = part // self.run, lax.rem(part, self.run)
        return [
            (kind * HEADS + (index * self.heads + head) * (self.parts // self.run) + at) * HEAD_DIM
            for kind in range(3)
            for head in range(self.heads)
        ]

    def unit_source(self, weight, kind):
        rows, columns = weight.shape
        half = columns // 2
        step = half // (self.groups * self.parts)
        if step % HEAD_DIM == 0:
            return weight, lambda part: [
                kind * half + (at * self.parts + part) * step for at in range(self.groups)
            ]
        pieces = weight[:, kind * half : (kind + 1) * half]
        pieces = pieces.reshape(rows, self.groups, self.parts, step).transpose(2, 0, 1, 3)
        return pieces.reshape(self.parts, rows, self.groups * step), None

    def unit_job(self, shape):
        step = shape[1] // (2 * self.groups)
        if step % HEAD_DIM:
            return Exchange(self.parts, shape)
        return Deliver(
            self.parts,
            shape,
            lambda part: [(at * self.parts + part) * step for at in range(2 * self.groups)],
        )

    def unit_rows(self, pieces):
        if pieces.ndim == 2:
            return pieces
        parts, rows, columns = pieces.shape
        outer = 2 * self.groups
        pieces = pieces.reshape(parts, rows, outer, columns // outer).transpose(1, 2, 0, 3)
        return pieces.reshape(rows, parts * columns).astype(jnp.float32)


def per_device(tokens, w_qkv, w_out, w_gate_up, w_down, seq_lengths, block_order, cotangent):
    lengths = seq_lengths[0]
    order_row = block_order[0]
    parts = lax.axis_size("ctx")
    groups = lax.axis_size("fsdp")
    rows, width = tokens.shape
    length = rows * parts
    plan = Plan(parts, groups, width)
    heads, shard, run = plan.heads, plan.shard, plan.run
    head_width = heads * HEAD_DIM
    line = (("ctx", parts),)
    plane = (("ctx", parts), ("fsdp", groups))
    block = (rows, width)

    down_rows = gather(w_down, "fsdp")
    unit_columns = w_gate_up.shape[1] // (2 * parts)
    unit_shape = (w_gate_up.shape[0], unit_columns)
    both_shape = (w_gate_up.shape[0], 2 * unit_columns)
    qkv_shape = (w_qkv.shape[0], 3 * head_width)
    gate_source, gate_starts = plan.unit_source(w_gate_up, 0)
    up_source, up_starts = plan.unit_source(w_gate_up, 1)
    inputs = tokens.astype(jnp.float32)
    normed_in, root_in = normalize(inputs)
    qkv_cols, normed_in_full, gate_cols, out_rows = call(
        [
            Spread(parts, groups, qkv_shape, plan.qkv_starts),
            Gather(parts, block, cuts=1),
            Exchange(parts, unit_shape, 2, gate_starts),
            Fan(groups, w_out.shape),
        ],
        [w_qkv, normed_in.astype(LOW), gate_source, w_out],
        "start",
        2,
        plane,
        micros=90,
    )
    gate_cols = gather(gate_cols.reshape(width // groups, -1), "fsdp")
    qkv_cols = qkv_cols.reshape(width, 3 * head_width)
    normed_in_full = normed_in_full.reshape(length, width)

    row_index = jnp.arange(length, dtype=jnp.int32)
    packed = initial_index(row_index, order_row)
    _, pos = places(packed, lengths)
    cosine_table, sine_table = angle_tables(pos)
    half_sign = jnp.where(jnp.arange(HEAD_DIM) < HEAD_DIM // 2, -1.0, 1.0)
    tables = (
        cosine_table[:, 0, :],
        sine_table[:, 0, :] * half_sign,
        packed[:, None] - jnp.where(jnp.arange(HEAD_DIM) < HEAD_DIM // 2, pos[:, None], 0),
        jnp.broadcast_to(packed[None, :], (8, length)),
    )
    up_cols, out_cols, qkv_low, mix_low = call(
        [
            Exchange(parts, unit_shape, 0, up_starts),
            Exchange(run, (heads, shard, width), second="out"),
        ],
        [up_source, out_rows.reshape(run, heads, shard, width)],
        "attend",
        1,
        line,
        Attend(normed_in_full, qkv_cols, tables, heads),
        micros=40,
    )
    up_cols = gather(up_cols.reshape(width // groups, -1), "fsdp")
    out_cols = out_cols.reshape(head_width, width)

    out_terms = dot(mix_low, out_cols).astype(LOW)
    attn_out, cot_full = call(
        [Scatter(parts, block, cuts=1), Gather(parts, block, cuts=1)],
        [out_terms.reshape((parts,) + block), cotangent],
        "out",
        3,
        line,
        micros=64,
    )
    cot_full = cot_full.reshape(length, width)
    residual = inputs + attn_out
    normed_mid, root_mid = normalize(residual)
    act_grad = times_transposed(cot_full, down_rows)
    mid_job = Gather(parts, block, watched=True)
    normed_mid_full, activated, gate_up_back, mid_back_terms = call(
        [mid_job],
        [normed_mid.astype(LOW)],
        "mid",
        4,
        line,
        FeedForward(mid_job, act_grad, gate_cols, up_cols),
        micros=60,
    )
    normed_mid_full = normed_mid_full.reshape(length, width)
    mid_back, gate_up_grad, down_grad = call(
        [Scatter(parts, block)],
        [mid_back_terms.reshape((parts,) + block)],
        "mid_back",
        5,
        line,
        Grads([(normed_mid_full, gate_up_back), (activated, cot_full)]),
    )
    gate_up_grad = scatter(gate_up_grad, "fsdp")
    down_grad = scatter(down_grad, "fsdp")
    residual_back = cotangent.astype(jnp.float32) + norm_back(mid_back, normed_mid, root_mid)
    proj_back = residual_back.astype(LOW)

    proj_job = Gather(parts, block, watched=True)
    _, down_terms, back_heads, out_grad = call(
        [proj_job],
        [proj_back],
        "proj_back",
        6,
        line,
        ProjectBack(proj_job, activated, down_rows, out_cols, mix_low),
        micros=45,
    )
    down_out, out_grad, in_back_terms, qkv_grad = call(
        [
            Scatter(parts, block, cuts=1),
            Exchange(run, (heads, shard, width), second="in"),
        ],
        [
            down_terms.reshape((parts,) + block),
            out_grad.reshape(heads, run, shard, width),
        ],
        "attend_back",
        8,
        line,
        AttendBack(back_heads, qkv_low, normed_in_full, qkv_cols, tables, heads),
        micros=60,
    )
    layer_out = (residual + down_out).astype(LOW)
    in_back, qkv_grad, gate_up_grad, out_grad = call(
        [
            Scatter(parts, block),
            Collect(parts, groups, qkv_shape, plan.qkv_starts),
            plan.unit_job(both_shape),
            Sum(groups, w_out.shape),
        ],
        [
            in_back_terms.reshape((parts,) + block),
            qkv_grad.reshape((groups, parts) + qkv_shape),
            gate_up_grad.reshape((parts,) + both_shape),
            out_grad.reshape((groups,) + w_out.shape),
        ],
        "in_back",
        7,
        plane,
        micros=90,
    )
    in_back, down_grad = lax.optimization_barrier((in_back, down_grad))
    tokens_grad = residual_back + norm_back(in_back, normed_in, root_in)
    return (
        layer_out,
        tokens_grad,
        qkv_grad,
        out_grad,
        plan.unit_rows(gate_up_grad),
        down_grad.astype(jnp.float32),
    )


def solution(mesh):
    both = P(("fsdp", "ctx"), None)
    one = P("fsdp", None)
    return jax.shard_map(
        per_device,
        mesh=mesh,
        in_specs=(both, both, both, both, both, one, one, both),
        out_specs=(both,) * 6,
        check_vma=False,
    )
```
